32 devices in a mesh: gx: 8 (over y, x, core), gy: 4 (over z).
Axes of the slice: x: 2, y: 2, z: 4, core: 2. Of those that a mesh axis runs over, the one named last changes fastest.
Arguments:
- velocity: float32 [3, 512, 128, 128], P(None, 'gx', 'gy'), may hold values from -6 to 6
- host_cell: int32 [3, 16384], P(None, ('gx', 'gy')), may hold values from 0 to 126, as said below
- host_frac: float32 [3, 16384], P(None, ('gx', 'gy')), may hold values from 0 to 1
- host_dst: int32 [16384], P(('gx', 'gy')), may hold values from -1 to 8191, as said below
- owner_src: int32 [8192], P(('gx', 'gy')), may hold values from 0 to 16383, as said below
- rotor_speed: float32 [32], P(('gx', 'gy')), may hold values from 1.5 to 4
- blade_radius: float32 [8192], P(('gx', 'gy')), may hold values from 0.1 to 1
- blade_chord: float32 [8192], P(('gx', 'gy')), may hold values from 0.2 to 0.8
- blade_twist: float32 [8192], P(('gx', 'gy')), may hold values from -0.4 to 0.4
- blade_angle: float32 [8192], P(('gx', 'gy')), may hold values from -3.140625 to 3.140625
Outputs:
- velocity_next: float32 [3, 512, 128, 128], P(None, 'gx', 'gy')
- point_force: float32 [3, 8192], P(None, ('gx', 'gy'))
The draws below stay inside these ranges and needn't reach their ends.
Inputs may be any that keep to these rules, and one draw needn't show every extreme that they name: `host_cell`: row 0 of a slot is its anchor cell streamwise inside its brick (below 64), row 1 spanwise (below 32), row 2 vertically (below 127). `host_dst`: each point number appears in exactly one slot; all other slots hold -1. The points of one turbine lie in slots of two bricks whose streamwise indices differ in the lowest bit (same spanwise index); those two bricks hold the points of two turbines. A brick may use all of its 512 slots, and some brick does. host_dst[owner_src[r]] = r for every point r.
All inputs are finite; a program needn't handle non-finite values.
Results may differ from the reference program's by a relative error of at most 0.00011.
Values sent between devices are 32-bit elements; how exact they have to be, the bound alone decides.
No kernel may reach another device: no remote copies, remote signals or barrier semaphores. Data moves between devices by JAX's collectives and lax.ppermute only.
A program may use at most 128 MiB of HBM per device.

```python
import math
import jax
import jax.numpy as jnp
from jax import lax

CX = 64
CY = 32
CZ = 128
P_SIZE = 256
HOST = 512
NX = 512
NY = 128
NZ = 128
NT = 32
NPTS = 8192
SLOTS = 16384
N_GX = 8
N_GY = 4


def place_label(labels, position, wanted):
    found = jnp.argmax((labels == wanted).astype(jnp.int32)).astype(jnp.int32)
    previous = labels[position]
    return labels.at[found].set(previous).at[position].set(wanted)


def route_tables(key):
    base_key = jax.random.fold_in(key, 101)
    key_orient, key_brick, key_point, key_label = jax.random.split(base_key, 4)
    devices = N_GX * N_GY
    pairs = devices // 2
    slot_total = devices * HOST
    point_total = devices * P_SIZE
    labels = jax.random.permutation(key_label, devices).astype(jnp.int32)
    labels = place_label(labels, 0, devices // 2)
    labels = place_label(labels, N_GY, N_GY + 1)
    labels = place_label(labels, 1, 0)
    pair_ids = jnp.arange(pairs, dtype=jnp.int32)
    lower = 2 * (pair_ids // N_GY) * N_GY + pair_ids % N_GY
    upper = lower + N_GY
    flip_bits = jax.random.randint(key_orient, (pairs,), 0, 2)
    wake_brick = jnp.where(flip_bits == 1, lower, upper)
    drawn_brick = jnp.where(flip_bits == 1, upper, lower)
    wake_count = jnp.where(pair_ids == 0, 2 * P_SIZE, 3 * P_SIZE // 2).astype(jnp.int32)
    brick_keys = jax.random.split(key_brick, devices)
    brick_perm = jax.vmap(lambda one_key: jax.random.permutation(one_key, HOST))(brick_keys).astype(jnp.int32)
    slot_ids = jnp.arange(devices, dtype=jnp.int32)[:, None] * HOST + brick_perm
    wake_slots = slot_ids[wake_brick]
    drawn_slots = slot_ids[drawn_brick]
    column = jnp.arange(2 * P_SIZE, dtype=jnp.int32)[None, :]
    from_wake = jnp.take_along_axis(wake_slots, jnp.broadcast_to(column, (pairs, 2 * P_SIZE)), axis=1)
    drawn_index = jnp.clip(column - wake_count[:, None], 0, HOST - 1)
    from_drawn = jnp.take_along_axis(drawn_slots, drawn_index, axis=1)
    used_slots = jnp.where(column < wake_count[:, None], from_wake, from_drawn)
    point_ids = jnp.arange(P_SIZE, dtype=jnp.int32)[None, :]
    pair_points = jnp.concatenate([labels[lower][:, None] * P_SIZE + point_ids, labels[upper][:, None] * P_SIZE + point_ids], axis=1)
    point_keys = jax.random.split(key_point, pairs)
    point_perm = jax.vmap(lambda one_key: jax.random.permutation(one_key, 2 * P_SIZE))(point_keys).astype(jnp.int32)
    pair_points = jnp.take_along_axis(pair_points, point_perm, axis=1)
    flat_slots = used_slots.reshape(-1).astype(jnp.int32)
    flat_points = pair_points.reshape(-1).astype(jnp.int32)
    host_table = jnp.full((slot_total,), -1, jnp.int32).at[flat_slots].set(flat_points)
    owner_table = jnp.zeros((point_total,), jnp.int32).at[flat_points].set(flat_slots)
    return (host_table, owner_table)


def draw_host_dst(key, part):
    return route_tables(key)[0]


def draw_owner_src(key, part):
    return route_tables(key)[1]


def draw_host_cell(key, part):
    key_x, key_y, key_z = jax.random.split(jax.random.fold_in(key, 202), 3)
    slot_total = N_GX * N_GY * HOST
    cell_x = jax.random.randint(key_x, (slot_total,), 0, CX)
    cell_y = jax.random.randint(key_y, (slot_total,), 0, CY)
    cell_z = jax.random.randint(key_z, (slot_total,), 0, CZ - 1)
    cells = jnp.stack([cell_x, cell_y, cell_z]).astype(jnp.int32)
    cells = cells.at[:, 0].set(jnp.array([CX - 1, CY - 1, CZ - 2], jnp.int32))
    cells = cells.at[:, 1].set(jnp.zeros((3,), jnp.int32))
    return cells


def steps_of(key, shape, cuts, smallest, largest):
    factor_of, own = 1.0, jax.random.fold_in(key, 6)
    for dim, shards_of in cuts:
        steps = jnp.exp(jax.random.uniform(jax.random.fold_in(own, dim), (shards_of,), jnp.float32, smallest / len(cuts), largest / len(cuts)))
        factor_of = factor_of * jnp.repeat(steps, shape[dim] // shards_of).reshape([-1 if axis == dim else 1 for axis in range(len(shape))])
    return factor_of


def scatter_about(stream_key, extent, spread, most, cuts=(), held_as=jnp.bfloat16):
    values = jax.random.normal(stream_key, extent, jnp.float32) * spread
    if len(cuts) > 0:
        values = steps_of(stream_key, extent, cuts, -0.22, 0.18) * values
    return jnp.clip(values, min=-most, max=most).astype(held_as)


def setup_inputs(seed: int = 0) -> dict:
    streams_of = jax.random.split(jax.random.key(seed), 11)
    return {
        "velocity": scatter_about(streams_of[0], (3, NX, NY, NZ), 1.0, 6.0, ((1, 8), (2, 4)), jnp.float32),
        "host_cell": draw_host_cell(jax.random.fold_in(streams_of[10], 71), 0),
        "host_frac": jnp.clip(1.0 * jax.random.uniform(streams_of[2], (3, SLOTS), jnp.float32) ** steps_of(streams_of[2], (3, SLOTS), ((1, 32),), -0.2, 0.2), 0.0, 1.0),
        "host_dst": draw_host_dst(jax.random.fold_in(streams_of[10], 71), 0),
        "owner_src": draw_owner_src(jax.random.fold_in(streams_of[10], 71), 0),
        "rotor_speed": jnp.clip(jnp.exp(math.log(4.0) - 0.98082925 * jax.random.uniform(streams_of[5], (NT,), jnp.float32) ** steps_of(streams_of[5], (NT,), ((0, 32),), -0.2, 0.2)), 1.5, 4.0),
        "blade_radius": jnp.clip(0.1 + 0.9 * jax.random.uniform(streams_of[6], (NPTS,), jnp.float32) ** steps_of(streams_of[6], (NPTS,), ((0, 32),), -0.2, 0.2), 0.1, 1.0),
        "blade_chord": jnp.clip(0.2 + 0.6 * jax.random.uniform(streams_of[7], (NPTS,), jnp.float32) ** steps_of(streams_of[7], (NPTS,), ((0, 32),), -0.2, 0.2), 0.2, 0.8),
        "blade_twist": jnp.clip(jax.random.uniform(streams_of[8], (NPTS,), jnp.float32, -0.4, 0.4) * steps_of(streams_of[8], (NPTS,), ((0, 32),), -0.4, 0.0), -0.4, 0.4),
        "blade_angle": jnp.clip(jax.random.uniform(streams_of[9], (NPTS,), jnp.float32, -3.140625, 3.140625), -3.140625, 3.140625),
    }


DT_STEP = 0.2
NU_VISC = 0.5
EPS_SQ = 1.44
CORE_SQ = 0.01

def offset_weights(fraction):
    offsets = jnp.arange(-1, 3).astype(jnp.float32)
    kernel_raw = jnp.exp(-(offsets[:, None] - fraction[None, :]) ** 2 / EPS_SQ)
    return kernel_raw / lax.optimization_barrier(jnp.sum(kernel_raw, axis=0, keepdims=True))

def attack(axial_flow, tangent, pitch_twist):
    rel_speed = jnp.sqrt(axial_flow * axial_flow + tangent * tangent + 1.0)
    cos_phi = tangent / rel_speed
    sin_phi = axial_flow / rel_speed
    sin_alpha = sin_phi * jnp.cos(pitch_twist) - cos_phi * jnp.sin(pitch_twist)
    cos_alpha = cos_phi * jnp.cos(pitch_twist) + sin_phi * jnp.sin(pitch_twist)
    lift_coef = 2.0 * jnp.pi * sin_alpha * cos_alpha / (1.0 + 4.0 * sin_alpha * sin_alpha)
    drag_coef = 0.02 + 0.8 * sin_alpha * sin_alpha
    return (rel_speed, cos_phi, sin_phi, lift_coef, drag_coef)

def blade_loads(sampled, spin_rate, radius, blade_chord, pitch_twist, azimuth):
    cos_angle = jnp.cos(azimuth)
    sin_angle = jnp.sin(azimuth)
    axial_flow = sampled[0]
    tangent = spin_rate * radius - (cos_angle * sampled[2] - sin_angle * sampled[1])
    rel_speed, cos_phi, sin_phi, lift_coef, drag_coef = attack(axial_flow, tangent, pitch_twist)
    circulation = 0.5 * blade_chord * rel_speed * lift_coef
    spacing = radius[:, :, None] - radius[:, None, :]
    alignment = cos_angle[:, :, None] * cos_angle[:, None, :] + sin_angle[:, :, None] * sin_angle[:, None, :]
    kernel = spacing / (spacing * spacing + CORE_SQ) * alignment / (4.0 * jnp.pi)
    induced = jnp.einsum('tij,tj->ti', kernel, circulation, precision=lax.Precision.HIGHEST)
    rel_speed, cos_phi, sin_phi, lift_coef, drag_coef = attack(axial_flow + induced, tangent, pitch_twist)
    dynamic = 0.5 * blade_chord * rel_speed * rel_speed
    lift_force = dynamic * lift_coef
    drag_force = dynamic * drag_coef
    thrust_part = lift_force * cos_phi + drag_force * sin_phi
    torque_part = lift_force * sin_phi - drag_force * cos_phi
    return jnp.stack([-thrust_part, torque_part * sin_angle, -torque_part * cos_angle])

def advance(velocity_pad, force_field):
    center = velocity_pad[:, 1:-1, 1:-1, 1:-1]
    outputs = []
    for component in range(3):
        one_field = velocity_pad[component]
        plus_x = one_field[2:, 1:-1, 1:-1]
        minus_x = one_field[:-2, 1:-1, 1:-1]
        plus_y = one_field[1:-1, 2:, 1:-1]
        minus_y = one_field[1:-1, :-2, 1:-1]
        plus_z = one_field[1:-1, 1:-1, 2:]
        minus_z = one_field[1:-1, 1:-1, :-2]
        middle = one_field[1:-1, 1:-1, 1:-1]
        transport = center[0] * (plus_x - minus_x) * 0.5 + center[1] * (plus_y - minus_y) * 0.5 + center[2] * (plus_z - minus_z) * 0.5
        diffusion = plus_x + minus_x + plus_y + minus_y + plus_z + minus_z - 6.0 * middle
        outputs.append(middle + DT_STEP * (-transport + NU_VISC * diffusion + force_field[component]))
    return jnp.stack(outputs)

def reference(velocity, host_cell, host_frac, host_dst, owner_src, rotor_speed, blade_radius, blade_chord, blade_twist, blade_angle):
    devices = N_GX * N_GY
    slot_total = devices * HOST
    slot_brick = jnp.arange(slot_total).astype(jnp.int32) // HOST
    base_x = slot_brick // N_GY * CX + host_cell[0]
    base_y = slot_brick % N_GY * CY + host_cell[1]
    base_z = host_cell[2]
    padded = jnp.pad(velocity, ((0, 0), (1, 1), (1, 1), (0, 0)))
    sampled = jnp.zeros((3, slot_total), jnp.float32)
    for step_x in range(2):
        weight_x = host_frac[0] if step_x else 1.0 - host_frac[0]
        for step_y in range(2):
            weight_y = host_frac[1] if step_y else 1.0 - host_frac[1]
            for step_z in range(2):
                weight_z = host_frac[2] if step_z else 1.0 - host_frac[2]
                weight = weight_x * weight_y * weight_z
                sampled = sampled + weight * padded[:, base_x + 1 + step_x, base_y + 1 + step_y, base_z + step_z]
    owned_rows = sampled[:, owner_src].reshape(3, devices, P_SIZE)
    point_force = blade_loads(owned_rows, rotor_speed[:, None], blade_radius.reshape(devices, P_SIZE), blade_chord.reshape(devices, P_SIZE), blade_twist.reshape(devices, P_SIZE), blade_angle.reshape(devices, P_SIZE))
    point_force = point_force.reshape(3, devices * P_SIZE)
    host_force = jnp.where(host_dst[None, :] >= 0, point_force[:, jnp.maximum(host_dst, 0)], 0.0)
    weights_x = offset_weights(host_frac[0])
    weights_y = offset_weights(host_frac[1])
    weights_z = offset_weights(host_frac[2])
    index_x, index_y, index_z, values = ([], [], [], [])
    for off_x in range(4):
        for off_y in range(4):
            for off_z in range(4):
                index_x.append(base_x + off_x + 1)
                index_y.append(base_y + off_y + 1)
                index_z.append(base_z + off_z + 1)
                values.append(host_force * (weights_x[off_x] * weights_y[off_y] * weights_z[off_z])[None, :])
    force_grid = jnp.zeros((3, NX + 4, NY + 4, NZ + 4), jnp.float32)
    force_grid = force_grid.at[:, jnp.concatenate(index_x), jnp.concatenate(index_y), jnp.concatenate(index_z)].add(jnp.concatenate(values, axis=1))
    force_field = force_grid[:, 2:NX + 2, 2:NY + 2, 2:NZ + 2]
    velocity_pad = jnp.pad(velocity, ((0, 0), (1, 1), (1, 1), (1, 1)))
    velocity_next = advance(velocity_pad, force_field)
    return (velocity_next, point_force)
```

```python
import math

import jax
import jax.numpy as jnp
from jax import lax
from jax.experimental import pallas as pl
from jax.experimental.pallas import tpu as pltpu
from jax.sharding import PartitionSpec as P

CX = 64
CY = 32
CZ = 128
P_SIZE = 256
HOST = 512
PTS = 2 * P_SIZE

DT_STEP = 0.2
NU_VISC = 0.5
EPS_SQ = 1.44
CORE_SQ = 0.01

ROWS = 16
YROWS = 72
FACE_X = 3 * CY
FACE_Y = 3 * YROWS
RIM_Y = 2 * 3 * YROWS
RIM_X = 2 * 3 * CY

F32 = jnp.float32
BF16 = jnp.bfloat16
VM = pl.BlockSpec(memory_space=pltpu.MemorySpace.VMEM)
SM = pl.BlockSpec(memory_space=pltpu.MemorySpace.SMEM)
PARAMS = pltpu.CompilerParams(vmem_limit_bytes=48 * 1024 * 1024)

S_PX, S_PY, S_OKD, S_BRICK, S_B0, S_B1, S_KEY = range(7)


def call(body, outs, n_in, name, scratch=()):
    return pl.pallas_call(
        body,
        out_shape=[jax.ShapeDtypeStruct(s, F32) for s in outs],
        in_specs=[SM] + [VM] * (n_in - 1),
        out_specs=[VM] * len(outs),
        scratch_shapes=list(scratch),
        compiler_params=PARAMS,
        name=name,
    )


def split(value):
    high = value.astype(BF16)
    low = (value - high.astype(F32)).astype(BF16)
    return high, low


def dot3(a_high, a_low, b_high, b_low):
    def one(a, b):
        return jnp.dot(a, b, preferred_element_type=F32)

    return one(a_high, b_high) + (one(a_high, b_low) + one(a_low, b_high))


def stencil_body(scal, v_ref, out_ref, ylo_ref, yhi_ref):
    row = lax.broadcasted_iota(jnp.int32, (CY, CZ), 0)
    lane = lax.broadcasted_iota(jnp.int32, (CY, CZ), 1)

    def step(x, carry):
        has_plus = jnp.where(x < CX - 1, 1.0, 0.0)
        has_minus = jnp.where(x > 0, 1.0, 0.0)
        up = jnp.minimum(x + 1, CX - 1)
        down = jnp.maximum(x - 1, 0)
        v0 = v_ref[0, x]
        v1 = v_ref[1, x]
        v2 = v_ref[2, x]
        for c in range(3):
            mid = (v0, v1, v2)[c]
            xp = v_ref[c, up] * has_plus
            xm = v_ref[c, down] * has_minus
            yp = jnp.where(row == CY - 1, 0.0, pltpu.roll(mid, CY - 1, 0))
            ym = jnp.where(row == 0, 0.0, pltpu.roll(mid, 1, 0))
            zp = jnp.where(lane == CZ - 1, 0.0, pltpu.roll(mid, CZ - 1, 1))
            zm = jnp.where(lane == 0, 0.0, pltpu.roll(mid, 1, 1))
            transport = v0 * (xp - xm) * 0.5 + v1 * (yp - ym) * 0.5 + v2 * (zp - zm) * 0.5
            diffusion = xp + xm + yp + ym + zp + zm - 6.0 * mid
            out_ref[c, x] = mid + DT_STEP * (NU_VISC * diffusion - transport)
            ylo_ref[c, pl.ds(x, 1)] = mid[0:1]
            yhi_ref[c, pl.ds(x, 1)] = mid[CY - 1 : CY]
        return carry

    lax.fori_loop(0, CX, step, 0)


def ypack_body(n_gx, scal, ylo_ref, yhi_ref, face_a, face_b, own_ref, *rest):
    gathered, (pay_c, pay_d, blk_ref) = rest[:n_gx], rest[n_gx:]
    even_x = scal[S_PX] == 0
    even_y = scal[S_PY] == 0
    tail = jnp.zeros((YROWS - CX - 1, CZ), F32)
    for c in range(3):
        x_high = jnp.where(even_x, face_a[c * CY : c * CY + 1], face_b[c * CY : c * CY + 1])
        low = jnp.concatenate([ylo_ref[c], x_high, tail], axis=0)
        high = jnp.concatenate([yhi_ref[c], x_high, tail], axis=0)
        pay_c[c * YROWS : (c + 1) * YROWS] = jnp.where(even_y, high, low)
        pay_d[c * YROWS : (c + 1) * YROWS] = jnp.where(even_y, low, high)
    pieces = [own_ref[...], face_a[FACE_X : FACE_X + ROWS]] + [g[...] for g in gathered]
    blocks = jnp.concatenate(pieces, axis=0)
    blk_ref[...] = blocks
    pay_c[FACE_Y:] = blocks
    pay_d[FACE_Y:] = blocks


def sample_body(n_blk, scal, v_ref, cell_ref, frac_ref, face_a, face_b, rec_c, rec_d, blk_ref, *rest):
    others, (samp_ref, sel_ref, pts_ref) = rest[:n_blk], rest[n_blk:]
    b0, b1, brick = scal[S_B0], scal[S_B1], scal[S_BRICK]
    sources = [(blk_ref, 0), (rec_c, FACE_Y)]
    if rec_d.shape[0] > FACE_Y:
        sources.append((rec_d, FACE_Y))
    sources += [(o, 0) for o in others]
    keys, members, values = [], [], []
    for ref, first in sources:
        for k in range((ref.shape[0] - first) // ROWS):
            value = ref[first + k * ROWS : first + (k + 1) * ROWS]
            key = value[14:15, 0:1]
            home = key.astype(jnp.int32) // HOST
            keys.append(key)
            members.append((home == b0) | (home == b1))
            values.append(value)
    low_key = functools_min([jnp.where(m, k, 1e9) for k, m in zip(keys, members)], jnp.minimum)
    high_key = functools_min([jnp.where(m, k, -1.0) for k, m in zip(keys, members)], jnp.maximum)
    turbine_a = jnp.zeros((ROWS, CZ), F32)
    turbine_b = jnp.zeros((ROWS, CZ), F32)
    for key, value in zip(keys, values):
        turbine_a = jnp.where(key == low_key, value, turbine_a)
        turbine_b = jnp.where(key == high_key, value, turbine_b)
    sel = jnp.concatenate([turbine_a, turbine_b], axis=0)
    sel_ref[...] = sel
    turned = jnp.concatenate([sel, jnp.zeros((CZ - 2 * ROWS, CZ), F32)], axis=0).T

    def column(k):
        picks = (2 * k, 2 * k + 1, ROWS + 2 * k, ROWS + 2 * k + 1)
        return jnp.concatenate([turned[:, j : j + 1] for j in picks], axis=0)

    slot = column(7).astype(jnp.int32)
    mine = (slot // HOST) == brick
    local = jnp.where(mine, slot % HOST, -1)
    lane_s = lax.broadcasted_iota(jnp.int32, (PTS, HOST), 1)
    hit = lane_s == local
    code = ((cell_ref[0:1] * CY + cell_ref[1:2]) * CZ + cell_ref[2:3]).astype(F32)

    def pull(row):
        return jnp.sum(jnp.where(hit, row, 0.0), axis=1, keepdims=True)

    code_col = pull(code).astype(jnp.int32)
    fx, fy, fz = pull(frac_ref[0:1]), pull(frac_ref[1:2]), pull(frac_ref[2:3])
    x_col = jnp.where(mine, code_col // (CY * CZ), -100)
    y_col = (code_col // CZ) % CY
    z_col = code_col % CZ
    lane = lax.broadcasted_iota(jnp.int32, (PTS, CZ), 1)
    columns = (x_col.astype(F32), y_col.astype(F32), z_col.astype(F32), fx, fy, fz, column(0))
    table = jnp.zeros((PTS, CZ), F32)
    for k, col in enumerate(columns):
        table = jnp.where(lane == k, col, table)
    pts_ref[...] = table

    def weight(coord, base, frac):
        return jnp.where(coord == base, 1.0 - frac, jnp.where(coord == base + 1, frac, 0.0))

    wy = weight(lane % CY, y_col, fy)
    x_lane = lane // CY - x_col
    acc = None
    per = 4
    for j in range(CX * CY // (CZ * per)):
        parts = []
        for i in range(per):
            shift = (CZ // CY) * (j * per + i)
            wx = jnp.where(x_lane == -shift, 1.0 - fx, jnp.where(x_lane == 1 - shift, fx, 0.0))
            parts.append(wx * wy)
        w_high, w_low = split(jnp.concatenate(parts, axis=1))
        nx = CZ * per // CY
        rows = [v_ref[c, j * nx : (j + 1) * nx].reshape(nx * CY, CZ) for c in range(3)]
        f_high, f_low = split(jnp.concatenate(rows, axis=1))
        part = dot3(w_high, w_low, f_high, f_low)
        acc = part if acc is None else acc + part
    edge_x = jnp.where(lane < CY, CX, lane - CY)
    edge_y = jnp.where(lane < CY, lane, CY)
    edge_w = jnp.where(lane < CY + YROWS, weight(edge_x, x_col, fx) * weight(edge_y, y_col, fy), 0.0)
    even_x = scal[S_PX] == 0
    even_y = scal[S_PY] == 0
    ok_d = scal[S_OKD] == 1
    rows = []
    for c in range(3):
        plane = jnp.where(even_x, face_a[c * CY : (c + 1) * CY], face_b[c * CY : (c + 1) * CY])
        from_d = jnp.where(ok_d, rec_d[c * YROWS : (c + 1) * YROWS], 0.0)
        line = jnp.where(even_y, rec_c[c * YROWS : (c + 1) * YROWS], from_d)
        rows.append(jnp.concatenate([plane, line, jnp.zeros((CZ - CY - YROWS, CZ), F32)], axis=0))
    w_high, w_low = split(edge_w)
    f_high, f_low = split(jnp.concatenate(rows, axis=1))
    acc = acc + dot3(w_high, w_low, f_high, f_low)
    wz = weight(lane, z_col, fz)
    out = jnp.zeros((PTS, CZ), F32)
    for c in range(3):
        value = jnp.sum(acc[:, c * CZ : (c + 1) * CZ] * wz, axis=1, keepdims=True)
        out = jnp.where(lane == c, value, out)
    samp_ref[...] = out.T[0:8]


def functools_min(items, op):
    result = items[0]
    for item in items[1:]:
        result = op(result, item)
    return result


def weights_body(scal, pts_ref, gx_ref, gy_ref, pz_ref):
    table = pts_ref[...].T

    def offsets(frac):
        raw = [jnp.exp(-((o - frac) ** 2) / EPS_SQ) for o in (-1.0, 0.0, 1.0, 2.0)]
        total = (raw[0] + raw[1]) + (raw[2] + raw[3])
        return [value / total for value in raw]

    def profile(rows, inner, base, frac):
        index = lax.broadcasted_iota(jnp.int32, (rows, PTS), 0)
        late = index - inner
        index = jnp.where(index < inner, index, jnp.where(late < 2, late - 2, late - 2 + inner))
        rel = index - base.astype(jnp.int32)
        result = jnp.zeros((rows, PTS), F32)
        for k, w in enumerate(offsets(frac)):
            result = jnp.where(rel == k - 1, w, result)
        return result

    gx_ref[...] = profile(YROWS, CX, table[0:1], table[3:4])
    gy_ref[...] = profile(CY + 8, CY, table[1:2], table[4:5])
    wz = offsets(table[5:6])
    stack = jnp.concatenate(wz + [jnp.zeros((CZ - 4, PTS), F32)], axis=0).T
    z_rel = lax.broadcasted_iota(jnp.int32, (PTS, CZ), 1) - pts_ref[:, 2:3].astype(jnp.int32)
    pz = jnp.zeros((PTS, CZ), F32)
    for k in range(4):
        pz = jnp.where(z_rel == k - 1, stack[:, k : k + 1], pz)
    pz_ref[...] = pz


def attack(axial_flow, tangent, cos_twist, sin_twist):
    rel_speed = jnp.sqrt(axial_flow * axial_flow + tangent * tangent + 1.0)
    cos_phi = tangent / rel_speed
    sin_phi = axial_flow / rel_speed
    sin_alpha = sin_phi * cos_twist - cos_phi * sin_twist
    cos_alpha = cos_phi * cos_twist + sin_phi * sin_twist
    lift_coef = 2.0 * jnp.pi * sin_alpha * cos_alpha / (1.0 + 4.0 * sin_alpha * sin_alpha)
    drag_coef = 0.02 + 0.8 * sin_alpha * sin_alpha
    return rel_speed, cos_phi, sin_phi, lift_coef, drag_coef


def loads_body(scal, samp_ref, other_ref, sel_ref, pts_ref, gx_ref, gy_ref, pz_ref, lh_ref, pay_c, pay_d, ret_ref, xrim_ref):
    def row(k):
        picks = (2 * k, 2 * k + 1, ROWS + 2 * k, ROWS + 2 * k + 1)
        return jnp.concatenate([sel_ref[j : j + 1] for j in picks], axis=1)

    radius, chord, spin, cos_t, sin_t, cos_a, sin_a = [row(k) for k in range(7)]
    flow = samp_ref[...] + other_ref[...]
    axial = flow[0:1]
    tangent = spin - (cos_a * flow[2:3] - sin_a * flow[1:2])
    rel_speed, cos_phi, sin_phi, lift_coef, drag_coef = attack(axial, tangent, cos_t, sin_t)
    circ = 0.5 * chord * rel_speed * lift_coef
    parts = []
    for t in range(2):
        seg = slice(t * P_SIZE, (t + 1) * P_SIZE)
        spacing = radius[:, seg] - pts_ref[seg, 6:7]
        kernel = spacing / (spacing * spacing + CORE_SQ)
        lhs = jnp.concatenate([cos_a[:, seg] * circ[:, seg], sin_a[:, seg] * circ[:, seg], jnp.zeros((6, P_SIZE), F32)], axis=0)
        both = jnp.dot(lhs, kernel, preferred_element_type=F32, precision=lax.Precision.HIGHEST)
        parts.append((cos_a[:, seg] * both[0:1] + sin_a[:, seg] * both[1:2]) / (4.0 * math.pi))
    induced = jnp.concatenate(parts, axis=1)
    rel_speed, cos_phi, sin_phi, lift_coef, drag_coef = attack(axial + induced, tangent, cos_t, sin_t)
    dynamic = 0.5 * chord * rel_speed * rel_speed
    lift = dynamic * lift_coef
    drag = dynamic * drag_coef
    thrust = lift * cos_phi + drag * sin_phi
    torque = lift * sin_phi - drag * cos_phi
    force = [-thrust, torque * sin_a, -torque * cos_a]
    pieces = []
    for t in range(2):
        for c in range(3):
            for h in range(2):
                at = t * P_SIZE + h * CZ
                pieces.append(force[c][:, at : at + CZ])
        key = sel_ref[t * ROWS + 14 : t * ROWS + 15, 0:1]
        pieces.append(jnp.broadcast_to(key, (2, CZ)))
    blocks = jnp.concatenate(pieces, axis=0)
    ret_ref[...] = blocks
    pay_c[RIM_Y:] = blocks
    pay_d[RIM_Y:] = blocks
    cols = jnp.concatenate(force + [jnp.zeros((CZ - 3, PTS), F32)], axis=0).T
    pz = pz_ref[...] * DT_STEP
    lines = jnp.concatenate([cols[:, c : c + 1] * pz for c in range(3)], axis=1)
    l_high, l_low = split(lines)
    lh_ref[...] = lines
    gx = gx_ref[...]
    gy = gy_ref[...]
    planes = [gx * gy[CY + k : CY + k + 1] for k in range(4)]
    planes += [gx[CX + k : CX + k + 1] * gy[0:CY] for k in range(4)]
    w_high, w_low = split(jnp.concatenate(planes, axis=0))
    rim = dot3(w_high, w_low, l_high, l_low)
    even_y = scal[S_PY] == 0
    for k in range(2):
        for c in range(3):
            low = rim[k * YROWS : (k + 1) * YROWS, c * CZ : (c + 1) * CZ]
            high = rim[(k + 2) * YROWS : (k + 3) * YROWS, c * CZ : (c + 1) * CZ]
            at = (k * 3 + c) * YROWS
            pay_c[at : at + YROWS] = jnp.where(even_y, high, low)
            pay_d[at : at + YROWS] = jnp.where(even_y, low, high)
    first = 4 * YROWS
    for k in range(4):
        for c in range(3):
            at = (k * 3 + c) * CY
            xrim_ref[at : at + CY] = rim[first + k * CY : first + (k + 1) * CY, c * CZ : (c + 1) * CZ]


SPREAD_X = 16


def spread_body(lines_ref, gx_ref, gy_ref, base_ref, out_ref, lh, ll):
    @pl.when(pl.program_id(0) == 0)
    def _():
        high, low = split(lines_ref[...])
        lh[...] = high
        ll[...] = low

    first = pl.multiple_of(pl.program_id(0) * SPREAD_X, SPREAD_X)
    gx = gx_ref[pl.ds(first, SPREAD_X)]
    gy = gy_ref[0:CY]
    planes = jnp.concatenate([gx[i : i + 1] * gy for i in range(SPREAD_X)], axis=0)
    w_high, w_low = split(planes)
    value = dot3(w_high, w_low, lh[...], ll[...])
    for c in range(3):
        out_ref[c] = base_ref[c] + value[:, c * CZ : (c + 1) * CZ].reshape(SPREAD_X, CY, CZ)


def spread(lines, gx, gy, base):
    whole = lambda i: (0, 0)
    block = pl.BlockSpec((3, SPREAD_X, CY, CZ), lambda i: (0, i, 0, 0))
    return pl.pallas_call(
        spread_body,
        out_shape=jax.ShapeDtypeStruct(base.shape, F32),
        grid=(CX // SPREAD_X,),
        in_specs=[
            pl.BlockSpec(lines.shape, whole),
            pl.BlockSpec(gx.shape, whole),
            pl.BlockSpec(gy.shape, whole),
            block,
        ],
        out_specs=block,
        scratch_shapes=[pltpu.VMEM((PTS, 3 * CZ), BF16)] * 2,
        compiler_params=PARAMS,
        name="spread",
    )(lines, gx, gy, base)


def xpack_body(scal, xrim_ref, rec_c, rec_d, pay_a, pay_b):
    even_x = scal[S_PX] == 0
    even_y = scal[S_PY] == 0
    ok_d = scal[S_OKD] == 1
    zero = jnp.zeros((CY - 4, CZ), F32)
    for k in range(2):
        sides = []
        for s in range(2):
            sides.append([])
            for c in range(3):
                near, far = [], []
                for y in range(2):
                    at = (y * 3 + c) * YROWS + CX + 2 * s + k
                    from_c = rec_c[at : at + 1]
                    from_d = jnp.where(ok_d, rec_d[at : at + 1], 0.0)
                    near.append(jnp.where(even_y, from_d, from_c))
                    far.append(jnp.where(even_y, from_c, from_d))
                at = ((2 * s + k) * 3 + c) * CY
                sides[s].append(xrim_ref[at : at + CY] + jnp.concatenate(near + [zero] + far, axis=0))
        for c in range(3):
            at = (k * 3 + c) * CY
            pay_a[at : at + CY] = jnp.where(even_x, sides[1][c], sides[0][c])
            pay_b[at : at + CY] = jnp.where(even_x, sides[0][c], sides[1][c])


def final_body(n_ret, scal, main_ref, v_ref, face_a, face_b, yc_ref, yd_ref, rim_a, rim_b, rim_c, rim_d, *rest):
    rets, (out_ref, pf_ref) = rest[:n_ret], rest[n_ret:]
    even_x = scal[S_PX] == 0
    even_y = scal[S_PY] == 0
    ok_d = scal[S_OKD] == 1
    coef = DT_STEP * 0.5
    out_ref[...] = main_ref[...]
    for c in range(3):
        rows = slice(c * CY, (c + 1) * CY)
        a, b = face_a[rows], face_b[rows]
        x_low = jnp.where(even_x, b, a)
        x_high = jnp.where(even_x, a, b)
        out_ref[c, 0] += coef * x_low * (2.0 * NU_VISC + v_ref[0, 0])
        out_ref[c, CX - 1] += coef * x_high * (2.0 * NU_VISC - v_ref[0, CX - 1])
        for k in range(2):
            rows = slice((k * 3 + c) * CY, (k * 3 + c + 1) * CY)
            a, b = rim_a[rows], rim_b[rows]
            out_ref[c, k] += jnp.where(even_x, b, a)
            out_ref[c, CX - 2 + k] += jnp.where(even_x, a, b)
        rows = slice(c * YROWS, c * YROWS + CX)
        a, b = yc_ref[rows], jnp.where(ok_d, yd_ref[rows], 0.0)
        y_low = jnp.where(even_y, b, a)
        y_high = jnp.where(even_y, a, b)
        out_ref[c, :, 0, :] += coef * y_low * (2.0 * NU_VISC + v_ref[1, :, 0, :])
        out_ref[c, :, CY - 1, :] += coef * y_high * (2.0 * NU_VISC - v_ref[1, :, CY - 1, :])
        for k in range(2):
            at = (k * 3 + c) * YROWS
            a, b = rim_c[at : at + CX], jnp.where(ok_d, rim_d[at : at + CX], 0.0)
            out_ref[c, :, k, :] += jnp.where(even_y, b, a)
            out_ref[c, :, CY - 2 + k, :] += jnp.where(even_y, a, b)
    mine = scal[S_KEY].astype(F32)
    found = jnp.zeros((8, CZ), F32)
    for ref in rets:
        for k in range(ref.shape[0] // 8):
            value = ref[8 * k : 8 * k + 8]
            found = jnp.where(value[6:7, 0:1] == mine, value, found)
    for c in range(3):
        pf_ref[c : c + 1] = jnp.concatenate([found[2 * c : 2 * c + 1], found[2 * c + 1 : 2 * c + 2]], axis=1)


def per_device(
    velocity,
    host_cell,
    host_frac,
    host_dst,
    owner_src,
    rotor_speed,
    blade_radius,
    blade_chord,
    blade_twist,
    blade_angle,
):
    nx, ny = lax.axis_size("gx"), lax.axis_size("gy")
    ix, iy = lax.axis_index("gx"), lax.axis_index("gy")
    px, py = ix % 2, iy % 2
    merged = ny == 4

    def flip(n, bits):
        return [(i, i ^ bits) for i in range(n)]

    def odd_pairs(n):
        up = [(i, i + 1) for i in range(1, n - 1, 2)]
        return up + [(t, s) for s, t in up]

    ok_d = jnp.where(py == 0, iy > 0, iy < ny - 1).astype(jnp.int32)
    low_brick = (ix - px) * ny + iy
    scal = jnp.stack([px, py, ok_d, ix * ny + iy, low_brick, low_brick + ny, owner_src[0]]).astype(jnp.int32)

    block = jnp.concatenate(
        [
            value.reshape(2, CZ)
            for value in (
                blade_radius,
                blade_chord,
                rotor_speed * blade_radius,
                jnp.cos(blade_twist),
                jnp.sin(blade_twist),
                jnp.cos(blade_angle),
                jnp.sin(blade_angle),
                owner_src.astype(F32),
            )
        ],
        axis=0,
    )
    edge_a = lax.dynamic_slice_in_dim(velocity, (CX - 1) * (1 - px), 1, axis=1).reshape(FACE_X, CZ)
    edge_b = lax.dynamic_slice_in_dim(velocity, (CX - 1) * px, 1, axis=1).reshape(FACE_X, CZ)
    face_a = lax.ppermute(jnp.concatenate([edge_a, block], axis=0), "gx", flip(nx, 1))
    face_b = lax.ppermute(edge_b, "gx", odd_pairs(nx))
    base, ylo, yhi = call(stencil_body, [velocity.shape, (3, CX, CZ), (3, CX, CZ)], 2, "stencil")(scal, velocity)
    pair = jnp.concatenate([block, face_a[FACE_X:]], axis=0)
    gathered = [lax.ppermute(pair, "gx", flip(nx, 2 * o)) for o in range(1, nx // 2)]
    n_rows = nx * ROWS
    pay_c, pay_d, blocks = call(
        lambda *refs: ypack_body(len(gathered), *refs),
        [(FACE_Y + n_rows, CZ), (FACE_Y + n_rows, CZ), (n_rows, CZ)],
        6 + len(gathered),
        "ypack",
    )(scal, ylo, yhi, face_a, face_b, block, *gathered)
    rec_c = lax.ppermute(pay_c, "gy", flip(ny, 1))
    if merged:
        rec_d = lax.ppermute(pay_d, "gy", flip(ny, 3))
    else:
        rec_d = lax.ppermute(pay_d[:FACE_Y], "gy", odd_pairs(ny))
    bits = [o for o in range(2, ny) if not (merged and o == 3)]
    others = [lax.ppermute(blocks, "gy", flip(ny, o)) for o in bits]
    samp, sel, pts = call(
        lambda *refs: sample_body(len(others), *refs),
        [(8, PTS), (2 * ROWS, CZ), (PTS, CZ)],
        9 + len(others),
        "sample",
    )(scal, velocity, host_cell, host_frac, face_a, face_b, rec_c, rec_d, blocks, *others)
    other = lax.ppermute(samp, "gx", flip(nx, 1))
    gx, gy, pz = call(weights_body, [(YROWS, PTS), (CY + 8, PTS), (PTS, CZ)], 2, "weights")(scal, pts)
    lines, pay_c, pay_d, ret, xrim = call(
        loads_body,
        [(PTS, 3 * CZ), (RIM_Y + ROWS, CZ), (RIM_Y + ROWS, CZ), (ROWS, CZ), (2 * RIM_X, CZ)],
        8,
        "loads",
    )(scal, samp, other, sel, pts, gx, gy, pz)
    rim_c = lax.ppermute(pay_c, "gy", flip(ny, 1))
    if merged:
        rim_d = lax.ppermute(pay_d, "gy", flip(ny, 3))
        back = [ret, rim_c[RIM_Y:], rim_d[RIM_Y:]]
    else:
        rim_d = lax.ppermute(pay_d[:RIM_Y], "gy", odd_pairs(ny))
        back = [ret, rim_c[RIM_Y:]]
    back += [lax.ppermute(ret, "gy", flip(ny, o)) for o in bits]
    back = jnp.concatenate(back, axis=0)
    main = spread(lines, gx, gy, base)
    pay_a, pay_b = call(xpack_body, [(RIM_X, CZ)] * 2, 4, "xpack")(scal, xrim, rim_c, rim_d)
    rim_a = lax.ppermute(pay_a, "gx", flip(nx, 1))
    rim_b = lax.ppermute(pay_b, "gx", odd_pairs(nx))
    rets = [back] + [lax.ppermute(back, "gx", flip(nx, 2 * o)) for o in range(1, nx // 2)]
    return tuple(
        call(lambda *refs: final_body(len(rets), *refs), [velocity.shape, (3, P_SIZE)], 11 + len(rets), "final")(
            scal, main, velocity, face_a, face_b, rec_c, rec_d, rim_a, rim_b, rim_c, rim_d, *rets
        )
    )


def solution(mesh):
    return jax.shard_map(
        per_device,
        mesh=mesh,
        in_specs=(
            P(None, "gx", "gy", None),
            P(None, ("gx", "gy")),
            P(None, ("gx", "gy")),
            P(("gx", "gy")),
            P(("gx", "gy")),
            P(("gx", "gy")),
            P(("gx", "gy")),
            P(("gx", "gy")),
            P(("gx", "gy")),
            P(("gx", "gy")),
        ),
        out_specs=(P(None, "gx", "gy", None), P(None, ("gx", "gy"))),
        check_vma=False,
    )
```

```python
import math

import jax
import jax.numpy as jnp
from jax import lax
from jax.experimental import pallas as pl
from jax.experimental.pallas import tpu as pltpu
from jax.sharding import PartitionSpec as P

CX = 64
CY = 32
CZ = 128
P_SIZE = 256
HOST = 512
PTS = 2 * P_SIZE

DT_STEP = 0.2
NU_VISC = 0.5
EPS_SQ = 1.44
CORE_SQ = 0.01

ROWS = 16
BACK = 8
YROWS = 72
XROWS = 40
FACE_Y = 3 * CX
FACE_X = 3 * XROWS
RIM_Y = 2 * 3 * YROWS
RIM_X = 2 * 3 * CY
CHUNK = 8
N_CHUNK = CX // CHUNK

F32 = jnp.float32
BF16 = jnp.bfloat16
VM = pl.BlockSpec(memory_space=pltpu.MemorySpace.VMEM)
SM = pl.BlockSpec(memory_space=pltpu.MemorySpace.SMEM)
HB = pl.BlockSpec(memory_space=pltpu.MemorySpace.HBM)
PARAMS = pltpu.CompilerParams(vmem_limit_bytes=48 * 1024 * 1024)


def call(body, outs, n_in, name, scratch=(), first=VM, second=VM, out_specs=None, aliases=None):
    return pl.pallas_call(
        body,
        out_shape=[jax.ShapeDtypeStruct(s, F32) for s in outs],
        in_specs=([first, second] + [VM] * n_in)[:n_in],
        out_specs=out_specs or [VM] * len(outs),
        scratch_shapes=list(scratch),
        input_output_aliases=aliases or {},
        compiler_params=PARAMS,
        name=name,
    )


def place():
    ny = lax.axis_size("gy")
    ix, iy = lax.axis_index("gx"), lax.axis_index("gy")
    px, py = lax.rem(ix, 2), lax.rem(iy, 2)
    return px == 0, py == 0, ix * ny + iy, (ix - px) * ny + iy, ny


def split(value):
    high = value.astype(BF16)
    low = (value - high.astype(F32)).astype(BF16)
    return high, low


def dot3(a_high, a_low, b_high, b_low):
    def one(a, b):
        return jnp.dot(a, b, preferred_element_type=F32)

    return one(a_high, b_high) + (one(a_high, b_low) + one(a_low, b_high))


def reduce_list(items, op):
    result = items[0]
    for item in items[1:]:
        result = op(result, item)
    return result


def pack_body(v_ref, spin_ref, radius, chord, twist, angle, source, pay_c, pay_d, blk_ref, low, high, sems):
    _, even_y, _, _, _ = place()
    copies = [
        pltpu.make_async_copy(v_ref.at[:, :, pl.ds(0, 8)], low, sems.at[0]),
        pltpu.make_async_copy(v_ref.at[:, :, pl.ds(CY - 8, 8)], high, sems.at[1]),
    ]
    for copy in copies:
        copy.start()
    parts = [
        radius[...],
        chord[...],
        radius[...] * spin_ref[0],
        jnp.cos(twist[...]),
        jnp.sin(twist[...]),
        jnp.cos(angle[...]),
        jnp.sin(angle[...]),
        source[...].astype(F32),
    ]
    block = jnp.concatenate(parts, axis=0)
    blk_ref[...] = block
    pay_c[FACE_Y:] = block
    for copy in copies:
        copy.wait()
    for c in range(3):
        y_low = low[c, :, 0, :]
        y_high = high[c, :, 7, :]
        pay_c[c * CX : (c + 1) * CX] = jnp.where(even_y, y_high, y_low)
        pay_d[c * CX : (c + 1) * CX] = jnp.where(even_y, y_low, y_high)


def stencil_body(v_ref, out_ref, y_ref, x_ref, buf, sems):
    row = lax.broadcasted_iota(jnp.int32, (CY, CZ), 0)
    lane = lax.broadcasted_iota(jnp.int32, (CY, CZ), 1)
    copies = []
    for k in range(N_CHUNK):
        part = pl.ds(k * CHUNK, CHUNK)
        copies.append(pltpu.make_async_copy(v_ref.at[:, part], buf.at[:, part], sems.at[k]))
        copies[-1].start()
    half = 0.5 * DT_STEP
    visc = DT_STEP * NU_VISC
    not_last_y, not_first_y = row < CY - 1, row > 0
    not_last_z, not_first_z = lane < CZ - 1, lane > 0

    def step(x, carry):
        up = jnp.minimum(x + 1, CX - 1)
        down = jnp.maximum(x - 1, 0)
        v0, v1, v2 = v_ref_of(buf, x)
        a_x = jnp.where(x < CX - 1, visc - half * v0, 0.0)
        b_x = jnp.where(x > 0, visc + half * v0, 0.0)
        a_y = jnp.where(not_last_y, visc - half * v1, 0.0)
        b_y = jnp.where(not_first_y, visc + half * v1, 0.0)
        a_z = jnp.where(not_last_z, visc - half * v2, 0.0)
        b_z = jnp.where(not_first_z, visc + half * v2, 0.0)
        for c in range(3):
            mid = (v0, v1, v2)[c]
            along_x = a_x * buf[c, up] + b_x * buf[c, down]
            along_y = a_y * pltpu.roll(mid, CY - 1, 0) + b_y * pltpu.roll(mid, 1, 0)
            along_z = a_z * pltpu.roll(mid, CZ - 1, 1) + b_z * pltpu.roll(mid, 1, 1)
            out_ref[c, x] = (1.0 - 6.0 * visc) * mid + along_x + (along_y + along_z)
            y_ref[c, pl.ds(x, 1)] = mid[0:1]
            y_ref[c + 3, pl.ds(x, 1)] = mid[CY - 1 : CY]
        return carry

    copies[0].wait()
    for k in range(N_CHUNK):
        if k + 1 < N_CHUNK:
            copies[k + 1].wait()
        lax.fori_loop(k * CHUNK, (k + 1) * CHUNK, step, 0, unroll=2)
    for c in range(3):
        x_ref[c] = buf[c, 0]
        x_ref[c + 3] = buf[c, CX - 1]


def v_ref_of(buf, x):
    return buf[0, x], buf[1, x], buf[2, x]


def weight(coord, base, frac):
    return jnp.where(coord == base, 1.0 - frac, jnp.where(coord == base + 1, frac, 0.0))


def sample_body(v_ref, cell_ref, frac_ref, tab_ref):
    rows = jnp.concatenate([cell_ref[...].astype(F32), frac_ref[...], jnp.zeros((CZ - 6, HOST), F32)], axis=0)
    turned = rows.T
    x_col, y_col, z_col = [turned[:, k : k + 1].astype(jnp.int32) for k in range(3)]
    fx, fy, fz = [turned[:, k : k + 1] for k in range(3, 6)]
    lane = lax.broadcasted_iota(jnp.int32, (HOST, CZ), 1)
    wy = weight(lane % CY, y_col, fy)
    x_lane = lane // CY - x_col
    acc = None
    per = 4
    nx = CZ * per // CY
    for j in range(CX // nx):
        parts = []
        for i in range(per):
            shift = (CZ // CY) * (j * per + i)
            wx = jnp.where(x_lane == -shift, 1.0 - fx, jnp.where(x_lane == 1 - shift, fx, 0.0))
            parts.append(wx * wy)
        w_high, w_low = split(jnp.concatenate(parts, axis=1))
        field = [v_ref[c, j * nx : (j + 1) * nx].reshape(nx * CY, CZ) for c in range(3)]
        f_high, f_low = split(jnp.concatenate(field, axis=1))
        part = dot3(w_high, w_low, f_high, f_low)
        acc = part if acc is None else acc + part
    wz = weight(lane, z_col, fz)
    out = turned
    for c in range(3):
        value = jnp.sum(acc[:, c * CZ : (c + 1) * CZ] * wz, axis=1, keepdims=True)
        out = jnp.where(lane == 6 + c, value, out)
    tab_ref[...] = out


def xpack_body(n_z, x_ref, own_ref, rec_c, rec_d, *rest):
    others, (pay_a, pay_b, blk_ref) = rest[:n_z], rest[n_z:]
    even_x, even_y, _, _, _ = place()
    for c in range(3):
        at = c * CX
        y_high = jnp.where(even_y, rec_c[at : at + 1], rec_d[at : at + 1])
        tail = jnp.concatenate([y_high, jnp.zeros((XROWS - CY - 1, CZ), F32)], axis=0)
        low, high = x_ref[c], x_ref[c + 3]
        at = c * XROWS
        pay_a[at : at + CY] = jnp.where(even_x, high, low)
        pay_b[at : at + CY] = jnp.where(even_x, low, high)
        pay_a[at + CY : at + XROWS] = tail
        pay_b[at + CY : at + XROWS] = tail
    blocks = jnp.concatenate([own_ref[...], rec_c[FACE_Y:]] + [o[...] for o in others], axis=0)
    blk_ref[...] = blocks
    pay_a[FACE_X:] = blocks


def select_body(n_blk, tab_ref, face_a, face_b, rec_c, rec_d, blk_ref, *rest):
    others, (samp_ref, sel_ref, pts_ref) = rest[:n_blk], rest[n_blk:]
    even_x, even_y, brick, b0, ny = place()
    b1 = b0 + ny
    keys, members, values = [], [], []
    for ref, first in [(blk_ref, 0), (face_a, FACE_X)] + [(o, 0) for o in others]:
        for k in range((ref.shape[0] - first) // ROWS):
            value = ref[first + k * ROWS : first + (k + 1) * ROWS]
            key = value[14:15, 0:1]
            home = key.astype(jnp.int32) // HOST
            keys.append(key)
            members.append((home == b0) | (home == b1))
            values.append(value)
    low_key = reduce_list([jnp.where(m, k, 1e9) for k, m in zip(keys, members)], jnp.minimum)
    high_key = reduce_list([jnp.where(m, k, -1.0) for k, m in zip(keys, members)], jnp.maximum)
    turbine_a = jnp.zeros((ROWS, CZ), F32)
    turbine_b = jnp.zeros((ROWS, CZ), F32)
    for key, value in zip(keys, values):
        turbine_a = jnp.where(key == low_key, value, turbine_a)
        turbine_b = jnp.where(key == high_key, value, turbine_b)
    sel = jnp.concatenate([turbine_a, turbine_b], axis=0)
    sel_ref[...] = sel
    turned = jnp.concatenate([sel, jnp.zeros((CZ - 2 * ROWS, CZ), F32)], axis=0).T

    def column(k):
        picks = (2 * k, 2 * k + 1, ROWS + 2 * k, ROWS + 2 * k + 1)
        return jnp.concatenate([turned[:, j : j + 1] for j in picks], axis=0)

    table = tab_ref[...]
    lane = lax.broadcasted_iota(jnp.int32, (PTS, CZ), 1)
    x_col, y_col, z_col = [table[:, k : k + 1].astype(jnp.int32) for k in range(3)]
    fx, fy, fz = [table[:, k : k + 1] for k in range(3, 6)]
    on_line = lane >= CX
    edge_x = jnp.where(on_line, lane - CX, CX)
    edge_y = jnp.where(on_line, CY, lane)
    edge_w = jnp.where(on_line | (lane <= CY), weight(edge_x, x_col, fx) * weight(edge_y, y_col, fy), 0.0)
    field = []
    for c in range(3):
        at = c * XROWS
        plane = jnp.where(even_x, face_a[at : at + XROWS], face_b[at : at + XROWS])
        at = c * CX
        line = jnp.where(even_y, rec_c[at : at + CX], rec_d[at : at + CX])
        field.append(jnp.concatenate([plane, jnp.zeros((CX - XROWS, CZ), F32), line], axis=0))
    w_high, w_low = split(edge_w)
    f_high, f_low = split(jnp.concatenate(field, axis=1))
    acc = dot3(w_high, w_low, f_high, f_low)
    wz = weight(lane, z_col, fz)
    for c in range(3):
        value = jnp.sum(acc[:, c * CZ : (c + 1) * CZ] * wz, axis=1, keepdims=True)
        table = table + jnp.where(lane == 6 + c, value, 0.0)
    by_slot = table.T[0:16]
    slot = column(7).astype(jnp.int32)
    mine = (slot // HOST) == brick
    local = jnp.where(mine, slot % HOST, -1)
    hit = lax.broadcasted_iota(jnp.int32, (PTS, HOST), 1) == local
    code = (by_slot[0:1] * CY + by_slot[1:2]) * CZ + by_slot[2:3]

    def pull(row):
        return jnp.sum(jnp.where(hit, row, 0.0), axis=1, keepdims=True)

    code_col = pull(code).astype(jnp.int32)
    pulled = [pull(by_slot[k : k + 1]) for k in range(3, 9)]
    columns = [
        jnp.where(mine, code_col // (CY * CZ), -100).astype(F32),
        ((code_col // CZ) % CY).astype(F32),
        (code_col % CZ).astype(F32),
        *pulled[0:3],
        column(0),
        *pulled[3:6],
    ]
    points = jnp.zeros((PTS, CZ), F32)
    for k, col in enumerate(columns):
        points = jnp.where(lane == k, col, points)
    pts_ref[...] = points
    samp_ref[...] = points.T[7:15]


def weights_body(pts_ref, gx_ref, gy_ref, pz_ref):
    table = pts_ref[...].T

    def offsets(frac):
        raw = [jnp.exp(-((o - frac) ** 2) / EPS_SQ) for o in (-1.0, 0.0, 1.0, 2.0)]
        total = (raw[0] + raw[1]) + (raw[2] + raw[3])
        return [value / total for value in raw]

    def profile(rows, inner, base, frac):
        index = lax.broadcasted_iota(jnp.int32, (rows, PTS), 0)
        late = index - inner
        index = jnp.where(index < inner, index, jnp.where(late < 2, late - 2, late - 2 + inner))
        rel = index - base.astype(jnp.int32)
        result = jnp.zeros((rows, PTS), F32)
        for k, w in enumerate(offsets(frac)):
            result = jnp.where(rel == k - 1, w, result)
        return result

    gx_ref[...] = profile(YROWS, CX, table[0:1], table[3:4])
    gy_ref[...] = profile(CY + 8, CY, table[1:2], table[4:5])
    wz = offsets(table[5:6])
    stack = jnp.concatenate(wz + [jnp.zeros((CZ - 4, PTS), F32)], axis=0).T
    z_rel = lax.broadcasted_iota(jnp.int32, (PTS, CZ), 1) - pts_ref[:, 2:3].astype(jnp.int32)
    pz = jnp.zeros((PTS, CZ), F32)
    for k in range(4):
        pz = jnp.where(z_rel == k - 1, stack[:, k : k + 1], pz)
    pz_ref[...] = pz


def attack(axial_flow, tangent, cos_twist, sin_twist):
    rel_speed = jnp.sqrt(axial_flow * axial_flow + tangent * tangent + 1.0)
    cos_phi = tangent / rel_speed
    sin_phi = axial_flow / rel_speed
    sin_alpha = sin_phi * cos_twist - cos_phi * sin_twist
    cos_alpha = cos_phi * cos_twist + sin_phi * sin_twist
    lift_coef = 2.0 * jnp.pi * sin_alpha * cos_alpha / (1.0 + 4.0 * sin_alpha * sin_alpha)
    drag_coef = 0.02 + 0.8 * sin_alpha * sin_alpha
    return rel_speed, cos_phi, sin_phi, lift_coef, drag_coef


def loads_body(samp_ref, other_ref, sel_ref, pts_ref, gx_ref, gy_ref, pz_ref, lh_ref, pay_c, pay_d, ret_ref, xrim_ref):
    even_x, even_y, _, _, _ = place()

    def row(k):
        picks = (2 * k, 2 * k + 1, ROWS + 2 * k, ROWS + 2 * k + 1)
        return jnp.concatenate([sel_ref[j : j + 1] for j in picks], axis=1)

    radius, chord, spin, cos_t, sin_t, cos_a, sin_a = [row(k) for k in range(7)]
    flow = samp_ref[...] + other_ref[...]
    axial = flow[0:1]
    tangent = spin - (cos_a * flow[2:3] - sin_a * flow[1:2])
    rel_speed, cos_phi, sin_phi, lift_coef, drag_coef = attack(axial, tangent, cos_t, sin_t)
    circ = 0.5 * chord * rel_speed * lift_coef
    parts = []
    for t in range(2):
        seg = slice(t * P_SIZE, (t + 1) * P_SIZE)
        spacing = radius[:, seg] - pts_ref[seg, 6:7]
        kernel = spacing / (spacing * spacing + CORE_SQ)
        lhs = jnp.concatenate([cos_a[:, seg] * circ[:, seg], sin_a[:, seg] * circ[:, seg], jnp.zeros((6, P_SIZE), F32)], axis=0)
        both = jnp.dot(lhs, kernel, preferred_element_type=F32, precision=lax.Precision.HIGHEST)
        parts.append((cos_a[:, seg] * both[0:1] + sin_a[:, seg] * both[1:2]) / (4.0 * math.pi))
    induced = jnp.concatenate(parts, axis=1)
    rel_speed, cos_phi, sin_phi, lift_coef, drag_coef = attack(axial + induced, tangent, cos_t, sin_t)
    dynamic = 0.5 * chord * rel_speed * rel_speed
    lift = dynamic * lift_coef
    drag = dynamic * drag_coef
    thrust = lift * cos_phi + drag * sin_phi
    torque = lift * sin_phi - drag * cos_phi
    force = [-thrust, torque * sin_a, -torque * cos_a]
    pieces = []
    for c in range(3):
        chosen = jnp.where(even_x, force[c][:, 0:P_SIZE], force[c][:, P_SIZE:])
        pieces += [chosen[:, 0:CZ], chosen[:, CZ:]]
    key = jnp.where(even_x, sel_ref[14:15, 0:1], sel_ref[ROWS + 14 : ROWS + 15, 0:1])
    pieces.append(jnp.broadcast_to(key, (2, CZ)))
    blocks = jnp.concatenate(pieces, axis=0)
    ret_ref[...] = blocks
    pay_c[RIM_Y:] = blocks
    cols = jnp.concatenate(force + [jnp.zeros((CZ - 3, PTS), F32)], axis=0).T
    pz = pz_ref[...] * DT_STEP
    lines = jnp.concatenate([cols[:, c : c + 1] * pz for c in range(3)], axis=1)
    l_high, l_low = split(lines)
    lh_ref[...] = lines
    gx = gx_ref[...]
    gy = gy_ref[...]
    planes = [gx * gy[CY + k : CY + k + 1] for k in range(4)]
    planes += [gx[CX + k : CX + k + 1] * gy[0:CY] for k in range(4)]
    w_high, w_low = split(jnp.concatenate(planes, axis=0))
    rim = dot3(w_high, w_low, l_high, l_low)
    for k in range(2):
        for c in range(3):
            low = rim[k * YROWS : (k + 1) * YROWS, c * CZ : (c + 1) * CZ]
            high = rim[(k + 2) * YROWS : (k + 3) * YROWS, c * CZ : (c + 1) * CZ]
            at = (k * 3 + c) * YROWS
            pay_c[at : at + YROWS] = jnp.where(even_y, high, low)
            pay_d[at : at + YROWS] = jnp.where(even_y, low, high)
    first = 4 * YROWS
    for k in range(4):
        for c in range(3):
            at = (k * 3 + c) * CY
            xrim_ref[at : at + CY] = rim[first + k * CY : first + (k + 1) * CY, c * CZ : (c + 1) * CZ]


SPREAD_X = 8


def spread_body(lines_ref, gx_ref, gy_ref, base_ref, out_ref):
    l_high, l_low = split(lines_ref[...])
    gy = gy_ref[0:CY]
    for k in range(CX // SPREAD_X):
        first = k * SPREAD_X
        planes = jnp.concatenate([gx_ref[first + i : first + i + 1] * gy for i in range(SPREAD_X)], axis=0)
        w_high, w_low = split(planes)
        value = dot3(w_high, w_low, l_high, l_low)
        for c in range(3):
            part = value[:, c * CZ : (c + 1) * CZ].reshape(SPREAD_X, CY, CZ)
            out_ref[c, first : first + SPREAD_X] = base_ref[c, first : first + SPREAD_X] + part


def rimpack_body(n_z, xrim_ref, ret_ref, rec_c, rec_d, *rest):
    others, (pay_a, pay_b, back_ref) = rest[:n_z], rest[n_z:]
    even_x, even_y, _, _, _ = place()
    zero = jnp.zeros((CY - 4, CZ), F32)
    for k in range(2):
        for c in range(3):
            sides = []
            for s in range(2):
                near, far = [], []
                for y in range(2):
                    at = (y * 3 + c) * YROWS + CX + 2 * s + k
                    from_c, from_d = rec_c[at : at + 1], rec_d[at : at + 1]
                    near.append(jnp.where(even_y, from_d, from_c))
                    far.append(jnp.where(even_y, from_c, from_d))
                at = ((2 * s + k) * 3 + c) * CY
                sides.append(xrim_ref[at : at + CY] + jnp.concatenate(near + [zero] + far, axis=0))
            at = (k * 3 + c) * CY
            pay_a[at : at + CY] = jnp.where(even_x, sides[1], sides[0])
            pay_b[at : at + CY] = jnp.where(even_x, sides[0], sides[1])
    back = jnp.concatenate([ret_ref[...], rec_c[RIM_Y:]] + [o[...] for o in others], axis=0)
    back_ref[...] = back
    pay_a[RIM_X:] = back


def final_body(n_ret, main_ref, x_ref, y_ref, own_ref, face_a, face_b, yc_ref, yd_ref, rim_a, rim_b, rim_c, rim_d, back_ref, *rest):
    rets, (out_ref, pf_ref, buf, sems) = rest[:n_ret], rest[n_ret:]
    even_x, even_y, _, _, _ = place()
    half = 0.5 * DT_STEP
    visc = DT_STEP * NU_VISC
    copies = []
    for k in range(N_CHUNK):
        first = k * CHUNK
        part = slice(first, first + CHUNK)
        for c in range(3):
            buf[c, part] = main_ref[c, part]
            if k in (0, N_CHUNK - 1):
                a, b = face_a[c * XROWS : c * XROWS + CY], face_b[c * XROWS : c * XROWS + CY]
                if k == 0:
                    buf[c, 0] += jnp.where(even_x, b, a) * (visc + half * x_ref[0])
                else:
                    buf[c, CX - 1] += jnp.where(even_x, a, b) * (visc - half * x_ref[3])
                for i in range(2):
                    rows = slice((i * 3 + c) * CY, (i * 3 + c + 1) * CY)
                    a, b = rim_a[rows], rim_b[rows]
                    if k == 0:
                        buf[c, i] += jnp.where(even_x, b, a)
                    else:
                        buf[c, CX - 2 + i] += jnp.where(even_x, a, b)
            rows = slice(c * CX + first, c * CX + first + CHUNK)
            a, b = yc_ref[rows], yd_ref[rows]
            low = [jnp.where(even_y, b, a) * (visc + half * y_ref[1, part]), 0.0]
            high = [0.0, jnp.where(even_y, a, b) * (visc - half * y_ref[4, part])]
            for i in range(2):
                at = (i * 3 + c) * YROWS + first
                a, b = rim_c[at : at + CHUNK], rim_d[at : at + CHUNK]
                buf[c, part, i, :] += jnp.where(even_y, b, a) + low[i]
                buf[c, part, CY - 2 + i, :] += jnp.where(even_y, a, b) + high[i]
        copies.append(pltpu.make_async_copy(buf.at[:, pl.ds(first, CHUNK)], out_ref.at[:, pl.ds(first, CHUNK)], sems.at[k]))
        copies[-1].start()
    mine = own_ref[14:15, 0:1]
    found = jnp.zeros((BACK, CZ), F32)
    for ref, first in [(back_ref, 0), (rim_a, RIM_X)] + [(r, 0) for r in rets]:
        for k in range((ref.shape[0] - first) // BACK):
            value = ref[first + BACK * k : first + BACK * k + BACK]
            found = jnp.where(value[6:7, 0:1] == mine, value, found)
    for c in range(3):
        pf_ref[c : c + 1] = jnp.concatenate([found[2 * c : 2 * c + 1], found[2 * c + 1 : 2 * c + 2]], axis=1)
    for copy in copies:
        copy.wait()


def per_device(
    velocity,
    host_cell,
    host_frac,
    host_dst,
    owner_src,
    rotor_speed,
    blade_radius,
    blade_chord,
    blade_twist,
    blade_angle,
):
    nx, ny = lax.axis_size("gx"), lax.axis_size("gy")

    def flip(n, bits):
        return [(i, i ^ bits) for i in range(n)]

    def odd_pairs(n):
        up = [(i, i + 1) for i in range(1, n - 1, 2)]
        return up + [(t, s) for s, t in up]

    def gather_y(block):
        return [lax.ppermute(block, "gy", flip(ny, o)) for o in range(2, ny)]

    def gather_x(block):
        return [lax.ppermute(block, "gx", flip(nx, 2 * o)) for o in range(1, nx // 2)]

    def swap(blocks):
        return [lax.ppermute(block, "gx", flip(nx, 1)) for block in blocks]

    dma = pltpu.SemaphoreType.DMA
    tiles = pltpu.VMEM((3, CX, 8, CZ), F32)
    pay_c, pay_d, block = call(
        pack_body,
        [(FACE_Y + ROWS, CZ), (FACE_Y, CZ), (ROWS, CZ)],
        7,
        "pack",
        scratch=[tiles, tiles, dma((2,))],
        first=HB,
        second=SM,
    )(velocity, rotor_speed, *[a.reshape(2, CZ) for a in (blade_radius, blade_chord, blade_twist, blade_angle, owner_src)])
    rec_c = lax.ppermute(pay_c, "gy", flip(ny, 1))
    rec_d = lax.ppermute(pay_d, "gy", odd_pairs(ny))
    from_y = gather_y(block)
    base, y_faces, x_faces = call(
        stencil_body,
        [velocity.shape, (6, CX, CZ), (6, CY, CZ)],
        1,
        "stencil",
        scratch=[pltpu.VMEM(velocity.shape, F32), dma((N_CHUNK,))],
        first=HB,
    )(velocity)
    n_rows = ny * ROWS
    pay_a, pay_b, blocks = call(
        lambda *refs: xpack_body(len(from_y), *refs),
        [(FACE_X + n_rows, CZ), (FACE_X, CZ), (n_rows, CZ)],
        4 + len(from_y),
        "xpack",
    )(x_faces, block, rec_c, rec_d, *from_y)
    face_a = lax.ppermute(pay_a, "gx", flip(nx, 1))
    face_b = lax.ppermute(pay_b, "gx", odd_pairs(nx))
    from_x = gather_x(blocks)
    table = call(sample_body, [(HOST, CZ)], 3, "sample")(velocity, host_cell, host_frac)[0]
    from_x += swap(from_x)
    samp, sel, pts = call(
        lambda *refs: select_body(len(from_x), *refs),
        [(8, PTS), (2 * ROWS, CZ), (PTS, CZ)],
        6 + len(from_x),
        "select",
    )(table, face_a, face_b, rec_c, rec_d, blocks, *from_x)
    other = swap([samp])[0]
    gx, gy, pz = call(weights_body, [(YROWS, PTS), (CY + 8, PTS), (PTS, CZ)], 1, "weights")(pts)
    lines, pay_c, pay_d, ret, xrim = call(
        loads_body,
        [(PTS, 3 * CZ), (RIM_Y + BACK, CZ), (RIM_Y, CZ), (BACK, CZ), (2 * RIM_X, CZ)],
        7,
        "loads",
    )(samp, other, sel, pts, gx, gy, pz)
    rim_c = lax.ppermute(pay_c, "gy", flip(ny, 1))
    rim_d = lax.ppermute(pay_d, "gy", odd_pairs(ny))
    ret_y = gather_y(ret)
    main = call(spread_body, [velocity.shape], 4, "spread")(lines, gx, gy, base)[0]
    pay_a, pay_b, back = call(
        lambda *refs: rimpack_body(len(ret_y), *refs),
        [(RIM_X + ny * BACK, CZ), (RIM_X, CZ), (ny * BACK, CZ)],
        4 + len(ret_y),
        "rimpack",
    )(xrim, ret, rim_c, rim_d, *ret_y)
    rim_a = lax.ppermute(pay_a, "gx", flip(nx, 1))
    rim_b = lax.ppermute(pay_b, "gx", odd_pairs(nx))
    rets = gather_x(back)
    rets += swap(rets)
    return tuple(
        call(
            lambda *refs: final_body(len(rets), *refs),
            [velocity.shape, (3, P_SIZE)],
            13 + len(rets),
            "final",
            scratch=[pltpu.VMEM(velocity.shape, F32), dma((N_CHUNK,))],
            out_specs=[HB, VM],
        )(main, x_faces, y_faces, block, face_a, face_b, rec_c, rec_d, rim_a, rim_b, rim_c, rim_d, back, *rets)
    )


def solution(mesh):
    return jax.shard_map(
        per_device,
        mesh=mesh,
        in_specs=(
            P(None, "gx", "gy", None),
            P(None, ("gx", "gy")),
            P(None, ("gx", "gy")),
            P(("gx", "gy")),
            P(("gx", "gy")),
            P(("gx", "gy")),
            P(("gx", "gy")),
            P(("gx", "gy")),
            P(("gx", "gy")),
            P(("gx", "gy")),
        ),
        out_specs=(P(None, "gx", "gy", None), P(None, ("gx", "gy"))),
        check_vma=False,
    )
```

```python
import math

import jax
import jax.numpy as jnp
from jax import lax
from jax.experimental import pallas as pl
from jax.experimental.pallas import tpu as pltpu
from jax.sharding import PartitionSpec as P

CX = 64
CY = 32
CZ = 128
P_SIZE = 256
HOST = 512
PTS = 2 * P_SIZE

DT_STEP = 0.2
NU_VISC = 0.5
EPS_SQ = 1.44
CORE_SQ = 0.01

ROWS = 16
BACK = 8
YROWS = 72
XROWS = 40
FACE_Y = 3 * CX
FACE_X = 3 * XROWS
RIM_Y = 2 * 3 * YROWS
RIM_X = 2 * 3 * CY
CHUNK = 8
N_CHUNK = CX // CHUNK

F32 = jnp.float32
BF16 = jnp.bfloat16
VM = pl.BlockSpec(memory_space=pltpu.MemorySpace.VMEM)
SM = pl.BlockSpec(memory_space=pltpu.MemorySpace.SMEM)
HB = pl.BlockSpec(memory_space=pltpu.MemorySpace.HBM)
MIB = 1024 * 1024


def call(body, outs, n_in, name, scratch=(), first=VM, second=VM, out_specs=None, in_specs=None, vmem=12):
    return pl.pallas_call(
        body,
        out_shape=[jax.ShapeDtypeStruct(s, F32) for s in outs],
        in_specs=in_specs or ([first, second] + [VM] * n_in)[:n_in],
        out_specs=out_specs or [VM] * len(outs),
        scratch_shapes=list(scratch),
        compiler_params=pltpu.CompilerParams(vmem_limit_bytes=vmem * MIB),
        name=name,
    )


def place():
    nx, ny = lax.axis_size("gx"), lax.axis_size("gy")
    ix, iy = lax.axis_index("gx"), lax.axis_index("gy")
    px, py = lax.rem(ix, 2), lax.rem(iy, 2)
    inner = (ix + px > 0) & (ix + px < nx)
    return px == 0, py == 0, inner, ix * ny + iy, (ix - px) * ny + iy, ny


def split(value):
    high = value.astype(BF16)
    low = (value - high.astype(F32)).astype(BF16)
    return high, low


def dot3(a_high, a_low, b_high, b_low):
    def one(a, b):
        return jnp.dot(a, b, preferred_element_type=F32)

    return one(a_high, b_high) + (one(a_high, b_low) + one(a_low, b_high))


def reduce_list(items, op):
    result = items[0]
    for item in items[1:]:
        result = op(result, item)
    return result


def pack_body(v_ref, spin_hbm, *rest):
    params, (pay_c, pay_d, blk_ref, low, high, held, held_int, spin_ref, sems) = rest[:5], rest[5:]
    _, even_y, _, _, _, _ = place()
    small = [pltpu.make_async_copy(spin_hbm, spin_ref, sems.at[2])]
    small += [pltpu.make_async_copy(p, held.at[k], sems.at[3 + k]) for k, p in enumerate(params[:4])]
    small.append(pltpu.make_async_copy(params[4], held_int, sems.at[7]))
    copies = [
        pltpu.make_async_copy(v_ref.at[:, :, pl.ds(0, 8)], low, sems.at[0]),
        pltpu.make_async_copy(v_ref.at[:, :, pl.ds(CY - 8, 8)], high, sems.at[1]),
    ]
    for copy in small + copies:
        copy.start()
    for copy in small:
        copy.wait()
    radius, chord, twist, angle = [held[k] for k in range(4)]
    parts = [
        radius,
        chord,
        radius * spin_ref[0],
        jnp.cos(twist),
        jnp.sin(twist),
        jnp.cos(angle),
        jnp.sin(angle),
        held_int[...].astype(F32),
    ]
    block = jnp.concatenate(parts, axis=0)
    blk_ref[...] = block
    pay_c[FACE_Y:] = block
    for copy in copies:
        copy.wait()
    for c in range(3):
        y_low = low[c, :, 0, :]
        y_high = high[c, :, 7, :]
        pay_c[c * CX : (c + 1) * CX] = jnp.where(even_y, y_high, y_low)
        pay_d[c * CX : (c + 1) * CX] = jnp.where(even_y, y_low, y_high)


def stencil_body(v_ref, out_ref, y_ref, x_ref, buf, sems):
    row = lax.broadcasted_iota(jnp.int32, (CY, CZ), 0)
    lane = lax.broadcasted_iota(jnp.int32, (CY, CZ), 1)
    copies = []
    for k in range(N_CHUNK):
        part = pl.ds(k * CHUNK, CHUNK)
        copies.append(pltpu.make_async_copy(v_ref.at[:, part], buf.at[:, part], sems.at[k]))
        copies[-1].start()
    half = 0.5 * DT_STEP
    visc = DT_STEP * NU_VISC
    not_last_y, not_first_y = row < CY - 1, row > 0
    not_last_z, not_first_z = lane < CZ - 1, lane > 0

    def step(x, carry):
        up = jnp.minimum(x + 1, CX - 1)
        down = jnp.maximum(x - 1, 0)
        v0, v1, v2 = v_ref_of(buf, x)
        a_x = jnp.where(x < CX - 1, visc - half * v0, 0.0)
        b_x = jnp.where(x > 0, visc + half * v0, 0.0)
        a_y = jnp.where(not_last_y, visc - half * v1, 0.0)
        b_y = jnp.where(not_first_y, visc + half * v1, 0.0)
        a_z = jnp.where(not_last_z, visc - half * v2, 0.0)
        b_z = jnp.where(not_first_z, visc + half * v2, 0.0)
        for c in range(3):
            mid = (v0, v1, v2)[c]
            along_x = a_x * buf[c, up] + b_x * buf[c, down]
            along_y = a_y * pltpu.roll(mid, CY - 1, 0) + b_y * pltpu.roll(mid, 1, 0)
            along_z = a_z * pltpu.roll(mid, CZ - 1, 1) + b_z * pltpu.roll(mid, 1, 1)
            out_ref[c, x] = (1.0 - 6.0 * visc) * mid + along_x + (along_y + along_z)
            y_ref[c, pl.ds(x, 1)] = mid[0:1]
            y_ref[c + 3, pl.ds(x, 1)] = mid[CY - 1 : CY]
        return carry

    copies[0].wait()
    for k in range(N_CHUNK):
        if k + 1 < N_CHUNK:
            copies[k + 1].wait()
        lax.fori_loop(k * CHUNK, (k + 1) * CHUNK, step, 0, unroll=2)
    for c in range(3):
        x_ref[c] = buf[c, 0]
        x_ref[c + 3] = buf[c, CX - 1]


def v_ref_of(buf, x):
    return buf[0, x], buf[1, x], buf[2, x]


def weight(coord, base, frac):
    return jnp.where(coord == base, 1.0 - frac, jnp.where(coord == base + 1, frac, 0.0))


def sample_body(v_ref, cell_ref, frac_ref, tab_ref):
    rows = jnp.concatenate([cell_ref[...].astype(F32), frac_ref[...], jnp.zeros((CZ - 6, HOST), F32)], axis=0)
    turned = rows.T
    x_col, y_col, z_col = [turned[:, k : k + 1].astype(jnp.int32) for k in range(3)]
    fx, fy, fz = [turned[:, k : k + 1] for k in range(3, 6)]
    lane = lax.broadcasted_iota(jnp.int32, (HOST, CZ), 1)
    wy = weight(lane % CY, y_col, fy)
    x_lane = lane // CY - x_col
    acc = None
    per = 4
    nx = CZ * per // CY
    for j in range(CX // nx):
        parts = []
        for i in range(per):
            shift = (CZ // CY) * (j * per + i)
            wx = jnp.where(x_lane == -shift, 1.0 - fx, jnp.where(x_lane == 1 - shift, fx, 0.0))
            parts.append(wx * wy)
        w_high, w_low = split(jnp.concatenate(parts, axis=1))
        field = [v_ref[c, j * nx : (j + 1) * nx].reshape(nx * CY, CZ) for c in range(3)]
        f_high, f_low = split(jnp.concatenate(field, axis=1))
        part = dot3(w_high, w_low, f_high, f_low)
        acc = part if acc is None else acc + part
    wz = weight(lane, z_col, fz)
    out = turned
    for c in range(3):
        value = jnp.sum(acc[:, c * CZ : (c + 1) * CZ] * wz, axis=1, keepdims=True)
        out = jnp.where(lane == 6 + c, value, out)
    tab_ref[...] = out


def xpack_body(n_blk, x_ref, rec_c, rec_d, *rest):
    pieces, (pay_a, pay_b, blk_ref) = rest[:n_blk], rest[n_blk:]
    even_x, even_y, inner, _, _, _ = place()
    for c in range(3):
        at = c * CX
        y_high = jnp.where(even_y, rec_c[at : at + 1], rec_d[at : at + 1])
        tail = jnp.concatenate([y_high, jnp.zeros((XROWS - CY - 1, CZ), F32)], axis=0)
        low, high = x_ref[c], x_ref[c + 3]
        at = c * XROWS
        pay_a[at : at + CY] = jnp.where(even_x, high, low)
        pay_b[at : at + CY] = jnp.where(even_x, low, high)
        pay_a[at + CY : at + XROWS] = tail
        pay_b[at + CY : at + XROWS] = tail
    blocks = jnp.concatenate([p[...] for p in pieces], axis=0)
    blk_ref[...] = blocks
    if pay_b.shape[0] > FACE_X:
        pay_b[FACE_X:] = blocks


def select_body(n_blk, tab_ref, face_a, face_b, rec_c, rec_d, blk_ref, *rest):
    others, (samp_ref, sel_ref, pts_ref) = rest[:n_blk], rest[n_blk:]
    even_x, even_y, inner, brick, b0, ny = place()
    b1 = b0 + ny
    keys, members, values = [], [], []
    for ref, first in [(blk_ref, 0), (face_b, FACE_X)] + [(o, 0) for o in others]:
        for k in range((ref.shape[0] - first) // ROWS):
            value = ref[first + k * ROWS : first + (k + 1) * ROWS]
            key = value[14:15, 0:1]
            home = key.astype(jnp.int32) // HOST
            keys.append(key)
            members.append((home == b0) | (home == b1))
            values.append(value)
    low_key = reduce_list([jnp.where(m, k, 1e9) for k, m in zip(keys, members)], jnp.minimum)
    high_key = reduce_list([jnp.where(m, k, -1.0) for k, m in zip(keys, members)], jnp.maximum)
    turbine_a = jnp.zeros((ROWS, CZ), F32)
    turbine_b = jnp.zeros((ROWS, CZ), F32)
    for key, value in zip(keys, values):
        turbine_a = jnp.where(key == low_key, value, turbine_a)
        turbine_b = jnp.where(key == high_key, value, turbine_b)
    sel = jnp.concatenate([turbine_a, turbine_b], axis=0)
    sel_ref[...] = sel
    turned = jnp.concatenate([sel, jnp.zeros((CZ - 2 * ROWS, CZ), F32)], axis=0).T

    def column(k):
        picks = (2 * k, 2 * k + 1, ROWS + 2 * k, ROWS + 2 * k + 1)
        return jnp.concatenate([turned[:, j : j + 1] for j in picks], axis=0)

    table = tab_ref[...]
    lane = lax.broadcasted_iota(jnp.int32, (PTS, CZ), 1)
    x_col, y_col, z_col = [table[:, k : k + 1].astype(jnp.int32) for k in range(3)]
    fx, fy, fz = [table[:, k : k + 1] for k in range(3, 6)]
    on_line = lane >= CX
    edge_x = jnp.where(on_line, lane - CX, CX)
    edge_y = jnp.where(on_line, CY, lane)
    edge_w = jnp.where(on_line | (lane <= CY), weight(edge_x, x_col, fx) * weight(edge_y, y_col, fy), 0.0)
    field = []
    for c in range(3):
        at = c * XROWS
        past = jnp.where(inner, face_b[at : at + XROWS], 0.0)
        plane = jnp.where(even_x, face_a[at : at + XROWS], past)
        at = c * CX
        line = jnp.where(even_y, rec_c[at : at + CX], rec_d[at : at + CX])
        field.append(jnp.concatenate([plane, jnp.zeros((CX - XROWS, CZ), F32), line], axis=0))
    w_high, w_low = split(edge_w)
    f_high, f_low = split(jnp.concatenate(field, axis=1))
    acc = dot3(w_high, w_low, f_high, f_low)
    wz = weight(lane, z_col, fz)
    for c in range(3):
        value = jnp.sum(acc[:, c * CZ : (c + 1) * CZ] * wz, axis=1, keepdims=True)
        table = table + jnp.where(lane == 6 + c, value, 0.0)
    slot = column(7).astype(jnp.int32)
    mine = (slot // HOST) == brick
    local = jnp.where(mine, slot % HOST, -1)
    hit = (lax.broadcasted_iota(jnp.int32, (PTS, HOST), 1) == local).astype(F32).astype(BF16)
    first, second = split(table)
    third = (table - first.astype(F32) - second.astype(F32)).astype(BF16)
    pulled = [jnp.dot(hit, part, preferred_element_type=F32) for part in (first, second, third)]
    points = pulled[0] + pulled[1] + pulled[2]
    points = jnp.where(lane == 9, column(0), points)
    pts_ref[...] = jnp.where((lane == 0) & jnp.logical_not(mine), -100.0, points)
    samp_ref[...] = points.T[6:14]


def weights_body(pts_ref, gx_ref, gy_ref, pz_ref):
    table = pts_ref[...].T

    def offsets(frac):
        raw = [jnp.exp(-((o - frac) ** 2) / EPS_SQ) for o in (-1.0, 0.0, 1.0, 2.0)]
        total = (raw[0] + raw[1]) + (raw[2] + raw[3])
        return [value / total for value in raw]

    def profile(rows, inner, base, frac):
        index = lax.broadcasted_iota(jnp.int32, (rows, PTS), 0)
        late = index - inner
        index = jnp.where(index < inner, index, jnp.where(late < 2, late - 2, late - 2 + inner))
        rel = index - base.astype(jnp.int32)
        result = jnp.zeros((rows, PTS), F32)
        for k, w in enumerate(offsets(frac)):
            result = jnp.where(rel == k - 1, w, result)
        return result

    gx_ref[...] = profile(YROWS, CX, table[0:1], table[3:4])
    gy_ref[...] = profile(CY + 8, CY, table[1:2], table[4:5])
    wz = offsets(table[5:6])
    stack = jnp.concatenate(wz + [jnp.zeros((CZ - 4, PTS), F32)], axis=0).T
    z_rel = lax.broadcasted_iota(jnp.int32, (PTS, CZ), 1) - pts_ref[:, 2:3].astype(jnp.int32)
    pz = jnp.zeros((PTS, CZ), F32)
    for k in range(4):
        pz = jnp.where(z_rel == k - 1, stack[:, k : k + 1], pz)
    pz_ref[...] = pz


def attack(axial_flow, tangent, cos_twist, sin_twist):
    rel_speed = jnp.sqrt(axial_flow * axial_flow + tangent * tangent + 1.0)
    cos_phi = tangent / rel_speed
    sin_phi = axial_flow / rel_speed
    sin_alpha = sin_phi * cos_twist - cos_phi * sin_twist
    cos_alpha = cos_phi * cos_twist + sin_phi * sin_twist
    lift_coef = 2.0 * jnp.pi * sin_alpha * cos_alpha / (1.0 + 4.0 * sin_alpha * sin_alpha)
    drag_coef = 0.02 + 0.8 * sin_alpha * sin_alpha
    return rel_speed, cos_phi, sin_phi, lift_coef, drag_coef


def loads_body(samp_ref, other_ref, sel_ref, pts_ref, gx_ref, gy_ref, pz_ref, lh_ref, pay_c, pay_d, ret_ref, xrim_ref):
    even_x, even_y, inner, _, _, _ = place()

    def row(k):
        picks = (2 * k, 2 * k + 1, ROWS + 2 * k, ROWS + 2 * k + 1)
        return jnp.concatenate([sel_ref[j : j + 1] for j in picks], axis=1)

    radius, chord, spin, cos_t, sin_t, cos_a, sin_a = [row(k) for k in range(7)]
    flow = samp_ref[...] + other_ref[...]
    axial = flow[0:1]
    tangent = spin - (cos_a * flow[2:3] - sin_a * flow[1:2])
    rel_speed, cos_phi, sin_phi, lift_coef, drag_coef = attack(axial, tangent, cos_t, sin_t)
    circ = 0.5 * chord * rel_speed * lift_coef
    parts = []
    for t in range(2):
        seg = slice(t * P_SIZE, (t + 1) * P_SIZE)
        spacing = radius[:, seg] - pts_ref[seg, 9:10]
        kernel = spacing / (spacing * spacing + CORE_SQ)
        lhs = jnp.concatenate([cos_a[:, seg] * circ[:, seg], sin_a[:, seg] * circ[:, seg], jnp.zeros((6, P_SIZE), F32)], axis=0)
        both = jnp.dot(lhs, kernel, preferred_element_type=F32, precision=lax.Precision.HIGHEST)
        parts.append((cos_a[:, seg] * both[0:1] + sin_a[:, seg] * both[1:2]) / (4.0 * math.pi))
    induced = jnp.concatenate(parts, axis=1)
    rel_speed, cos_phi, sin_phi, lift_coef, drag_coef = attack(axial + induced, tangent, cos_t, sin_t)
    dynamic = 0.5 * chord * rel_speed * rel_speed
    lift = dynamic * lift_coef
    drag = dynamic * drag_coef
    thrust = lift * cos_phi + drag * sin_phi
    torque = lift * sin_phi - drag * cos_phi
    force = [-thrust, torque * sin_a, -torque * cos_a]
    pieces = []
    for t in range(2):
        for c in range(3):
            for h in range(2):
                at = t * P_SIZE + h * CZ
                pieces.append(force[c][:, at : at + CZ])
        key = sel_ref[t * ROWS + 14 : t * ROWS + 15, 0:1]
        pieces.append(jnp.broadcast_to(key, (2, CZ)))
    blocks = jnp.concatenate(pieces, axis=0)
    ret_ref[...] = blocks
    pay_c[RIM_Y:] = blocks
    cols = jnp.concatenate(force + [jnp.zeros((CZ - 3, PTS), F32)], axis=0).T
    pz = pz_ref[...] * DT_STEP
    lines = jnp.concatenate([cols[:, c : c + 1] * pz for c in range(3)], axis=1)
    l_high, l_low = split(lines)
    lh_ref[...] = lines
    gx = gx_ref[...]
    gy = gy_ref[...]
    planes = [gx * gy[CY + k : CY + k + 1] for k in range(4)]
    planes += [gx[CX + k : CX + k + 1] * gy[0:CY] for k in range(4)]
    w_high, w_low = split(jnp.concatenate(planes, axis=0))
    rim = dot3(w_high, w_low, l_high, l_low)
    for k in range(2):
        for c in range(3):
            low = rim[k * YROWS : (k + 1) * YROWS, c * CZ : (c + 1) * CZ]
            high = rim[(k + 2) * YROWS : (k + 3) * YROWS, c * CZ : (c + 1) * CZ]
            at = (k * 3 + c) * YROWS
            pay_c[at : at + YROWS] = jnp.where(even_y, high, low)
            pay_d[at : at + YROWS] = jnp.where(even_y, low, high)
    first = 4 * YROWS
    for k in range(4):
        for c in range(3):
            at = (k * 3 + c) * CY
            xrim_ref[at : at + CY] = rim[first + k * CY : first + (k + 1) * CY, c * CZ : (c + 1) * CZ]


SPREAD_X = 8


def spread_body(start, lines_ref, gx_ref, gy_ref, base_ref, out_ref):
    l_high, l_low = split(lines_ref[...])
    gy = gy_ref[0:CY]
    for k in range(out_ref.shape[1] // SPREAD_X):
        at = k * SPREAD_X
        first = start + at
        planes = jnp.concatenate([gx_ref[first + i : first + i + 1] * gy for i in range(SPREAD_X)], axis=0)
        w_high, w_low = split(planes)
        value = dot3(w_high, w_low, l_high, l_low)
        for c in range(3):
            part = value[:, c * CZ : (c + 1) * CZ].reshape(SPREAD_X, CY, CZ)
            out_ref[c, at : at + SPREAD_X] = base_ref[c, first : first + SPREAD_X] + part


def rimpack_body(n_blk, xrim_ref, rec_c, rec_d, *rest):
    pieces, (pay_a, pay_b, back_ref) = rest[:n_blk], rest[n_blk:]
    even_x, even_y, inner, _, _, _ = place()
    zero = jnp.zeros((CY - 4, CZ), F32)
    for k in range(2):
        for c in range(3):
            sides = []
            for s in range(2):
                near, far = [], []
                for y in range(2):
                    at = (y * 3 + c) * YROWS + CX + 2 * s + k
                    from_c, from_d = rec_c[at : at + 1], rec_d[at : at + 1]
                    near.append(jnp.where(even_y, from_d, from_c))
                    far.append(jnp.where(even_y, from_c, from_d))
                at = ((2 * s + k) * 3 + c) * CY
                sides.append(xrim_ref[at : at + CY] + jnp.concatenate(near + [zero] + far, axis=0))
            at = (k * 3 + c) * CY
            pay_a[at : at + CY] = jnp.where(even_x, sides[1], sides[0])
            pay_b[at : at + CY] = jnp.where(even_x, sides[0], sides[1])
    back = jnp.concatenate([p[...] for p in pieces], axis=0)
    back_ref[...] = back
    if pay_b.shape[0] > RIM_X:
        pay_b[RIM_X:] = back


def final_body(n_ret, main_low, main_high, x_ref, y_ref, own_ref, face_a, face_b, yc_ref, yd_ref, rim_a, rim_b, rim_c, rim_d, back_ref, *rest):
    rets, (out_ref, pf_ref, buf, sems) = rest[:n_ret], rest[n_ret:]
    even_x, even_y, inner, _, _, _ = place()
    half = 0.5 * DT_STEP
    visc = DT_STEP * NU_VISC
    copies = []
    for k in range(N_CHUNK):
        first = k * CHUNK
        part = slice(first, first + CHUNK)
        for c in range(3):
            half_of = main_low if k < N_CHUNK // 2 else main_high
            at = first % (CX // 2)
            buf[c, part] = half_of[c, at : at + CHUNK]
            if k in (0, N_CHUNK - 1):
                a = face_a[c * XROWS : c * XROWS + CY]
                b = jnp.where(inner, face_b[c * XROWS : c * XROWS + CY], 0.0)
                if k == 0:
                    buf[c, 0] += jnp.where(even_x, b, a) * (visc + half * x_ref[0])
                else:
                    buf[c, CX - 1] += jnp.where(even_x, a, b) * (visc - half * x_ref[3])
                for i in range(2):
                    rows = slice((i * 3 + c) * CY, (i * 3 + c + 1) * CY)
                    a, b = rim_a[rows], jnp.where(inner, rim_b[rows], 0.0)
                    if k == 0:
                        buf[c, i] += jnp.where(even_x, b, a)
                    else:
                        buf[c, CX - 2 + i] += jnp.where(even_x, a, b)
            rows = slice(c * CX + first, c * CX + first + CHUNK)
            a, b = yc_ref[rows], yd_ref[rows]
            low = [jnp.where(even_y, b, a) * (visc + half * y_ref[1, part]), 0.0]
            high = [0.0, jnp.where(even_y, a, b) * (visc - half * y_ref[4, part])]
            for i in range(2):
                at = (i * 3 + c) * YROWS + first
                a, b = rim_c[at : at + CHUNK], rim_d[at : at + CHUNK]
                buf[c, part, i, :] += jnp.where(even_y, b, a) + low[i]
                buf[c, part, CY - 2 + i, :] += jnp.where(even_y, a, b) + high[i]
        copies.append(pltpu.make_async_copy(buf.at[:, pl.ds(first, CHUNK)], out_ref.at[:, pl.ds(first, CHUNK)], sems.at[k]))
        copies[-1].start()
    mine = own_ref[14:15, 0:1]
    found = jnp.zeros((BACK, CZ), F32)
    for ref, first in [(back_ref, 0), (rim_b, RIM_X)] + [(r, 0) for r in rets]:
        for k in range((ref.shape[0] - first) // BACK):
            value = ref[first + BACK * k : first + BACK * k + BACK]
            found = jnp.where(value[6:7, 0:1] == mine, value, found)
    for c in range(3):
        pf_ref[c : c + 1] = jnp.concatenate([found[2 * c : 2 * c + 1], found[2 * c + 1 : 2 * c + 2]], axis=1)
    for copy in copies:
        copy.wait()


def per_device(
    velocity,
    host_cell,
    host_frac,
    host_dst,
    owner_src,
    rotor_speed,
    blade_radius,
    blade_chord,
    blade_twist,
    blade_angle,
):
    nx, ny = lax.axis_size("gx"), lax.axis_size("gy")
    ring = nx == 8

    def flip(n, bits):
        return [(i, i ^ bits) for i in range(n)]

    def odd_pairs(n, closed=False):
        up = [(i, (i + 1) % n) for i in range(1, n if closed else n - 1, 2)]
        return up + [(t, s) for s, t in up]

    def swap(block):
        return lax.ppermute(block, "gx", flip(nx, 1))

    def join(pieces):
        return pieces[0] if len(pieces) == 1 else jnp.concatenate(pieces, axis=0)

    def after(values, other):
        return lax.optimization_barrier((values, other))

    def gather_y(first, filler):
        pieces = [first]
        for bit in [b for b in (2, 4, 8) if b < ny]:
            got = lax.ppermute(join(pieces), "gy", flip(ny, bit))
            if filler is not None:
                got, filler = after(got, filler())
                yield filler
                filler = None
            pieces.append(got)
        yield pieces

    def gather_x(blocks):
        pieces = []
        for bit in [4] if ring else [b for b in (2, 4, 8, 16) if b < nx]:
            pieces.append(lax.ppermute(join([blocks] + pieces) if not ring else blocks, "gx", flip(nx, bit)))
        return pieces

    dma = pltpu.SemaphoreType.DMA
    tiles = pltpu.VMEM((3, CX, 8, CZ), F32)
    pay_c, pay_d, block = call(
        pack_body,
        [(FACE_Y + ROWS, CZ), (FACE_Y, CZ), (ROWS, CZ)],
        7,
        "pack",
        scratch=[tiles, tiles, pltpu.VMEM((4, 2, CZ), F32), pltpu.VMEM((2, CZ), jnp.int32), pltpu.SMEM((1,), F32), dma((8,))],
        in_specs=[HB] * 7,
    )(velocity, rotor_speed, *[a.reshape(2, CZ) for a in (blade_radius, blade_chord, blade_twist, blade_angle, owner_src)])
    rec_c = lax.ppermute(pay_c, "gy", flip(ny, 1))
    rec_d = lax.ppermute(pay_d, "gy", odd_pairs(ny))
    base, y_faces, x_faces = call(
        stencil_body,
        [velocity.shape, (6, CX, CZ), (6, CY, CZ)],
        1,
        "stencil",
        scratch=[pltpu.VMEM(velocity.shape, F32), dma((N_CHUNK,))],
        in_specs=[HB],
    )(velocity)
    rec_c, base = after(rec_c, base)
    sampled = lambda: call(sample_body, [(HOST, CZ)], 3, "sample", vmem=24)(velocity, host_cell, host_frac)[0]
    table, pieces = list(gather_y(join([block, rec_c[FACE_Y:]]), sampled))
    pieces = pieces + [swap(p) for p in pieces]
    n_rows = 2 * ny * ROWS
    pay_a, pay_b, blocks = call(
        lambda *refs: xpack_body(len(pieces), *refs),
        [(FACE_X, CZ), (FACE_X + (n_rows if ring else 0), CZ), (n_rows, CZ)],
        3 + len(pieces),
        "xpack",
    )(x_faces, rec_c, rec_d, *pieces)
    face_b = lax.ppermute(pay_b, "gx", odd_pairs(nx, ring))
    from_x = gather_x(blocks)
    face_a = swap(pay_a)
    if ring:
        from_x.append(swap(face_b[FACE_X:]))
    samp, sel, pts = call(
        lambda *refs: select_body(len(from_x), *refs),
        [(8, PTS), (2 * ROWS, CZ), (PTS, CZ)],
        6 + len(from_x),
        "select",
    )(table, face_a, face_b, rec_c, rec_d, blocks, *from_x)
    other = swap(samp)
    gx, gy, pz = call(weights_body, [(YROWS, PTS), (CY + 8, PTS), (PTS, CZ)], 1, "weights")(pts)
    lines, pay_c, pay_d, ret, xrim = call(
        loads_body,
        [(PTS, 3 * CZ), (RIM_Y + 2 * BACK, CZ), (RIM_Y, CZ), (2 * BACK, CZ), (2 * RIM_X, CZ)],
        7,
        "loads",
    )(samp, other, sel, pts, gx, gy, pz)
    rim_c = lax.ppermute(pay_c, "gy", flip(ny, 1))
    rim_d = lax.ppermute(pay_d, "gy", odd_pairs(ny))

    def spread(start):
        return call(
            lambda *refs: spread_body(start, *refs), [(3, CX // 2, CY, CZ)], 4, "spread"
        )(lines, gx, gy, base)[0]

    rim_c, main_low = after(rim_c, spread(0))
    main_high, pieces = list(gather_y(join([ret, rim_c[RIM_Y:]]), lambda: spread(CX // 2)))
    n_rows = 2 * ny * BACK
    pay_a, pay_b, back = call(
        lambda *refs: rimpack_body(len(pieces), *refs),
        [(RIM_X, CZ), (RIM_X + (n_rows if ring else 0), CZ), (n_rows, CZ)],
        3 + len(pieces),
        "rimpack",
    )(xrim, rim_c, rim_d, *pieces)
    rim_b = lax.ppermute(pay_b, "gx", odd_pairs(nx, ring))
    rets = gather_x(back)
    rim_a = swap(pay_a)
    if ring:
        rets.append(swap(rim_b[RIM_X:]))
    return tuple(
        call(
            lambda *refs: final_body(len(rets), *refs),
            [velocity.shape, (3, P_SIZE)],
            14 + len(rets),
            "final",
            scratch=[pltpu.VMEM(velocity.shape, F32), dma((N_CHUNK,))],
            out_specs=[HB, VM],
        )(main_low, main_high, x_faces, y_faces, block, face_a, face_b, rec_c, rec_d, rim_a, rim_b, rim_c, rim_d, back, *rets)
    )


def solution(mesh):
    return jax.shard_map(
        per_device,
        mesh=mesh,
        in_specs=(
            P(None, "gx", "gy", None),
            P(None, ("gx", "gy")),
            P(None, ("gx", "gy")),
            P(("gx", "gy")),
            P(("gx", "gy")),
            P(("gx", "gy")),
            P(("gx", "gy")),
            P(("gx", "gy")),
            P(("gx", "gy")),
            P(("gx", "gy")),
        ),
        out_specs=(P(None, "gx", "gy", None), P(None, ("gx", "gy"))),
        check_vma=False,
    )
```

```python
import math

import jax
import jax.numpy as jnp
from jax import lax
from jax.experimental import pallas as pl
from jax.experimental.pallas import tpu as pltpu
from jax.sharding import PartitionSpec as P

CX = 64
CY = 32
CZ = 128
P_SIZE = 256
HOST = 512
PTS = 2 * P_SIZE

DT_STEP = 0.2
NU_VISC = 0.5
EPS_SQ = 1.44
CORE_SQ = 0.01

ROWS = 16
BACK = 8
YROWS = 72
XROWS = 40
FACE_Y = 3 * CX
FACE_X = 3 * XROWS
RIM_Y = 2 * 3 * YROWS
RIM_X = 2 * 3 * CY
CHUNK = 8
N_CHUNK = CX // CHUNK

F32 = jnp.float32
BF16 = jnp.bfloat16
VM = pl.BlockSpec(memory_space=pltpu.MemorySpace.VMEM)
SM = pl.BlockSpec(memory_space=pltpu.MemorySpace.SMEM)
HB = pl.BlockSpec(memory_space=pltpu.MemorySpace.HBM)
MIB = 1024 * 1024


def call(body, outs, n_in, name, scratch=(), first=VM, second=VM, out_specs=None, in_specs=None, vmem=12):
    return pl.pallas_call(
        body,
        out_shape=[jax.ShapeDtypeStruct(s, F32) for s in outs],
        in_specs=in_specs or ([first, second] + [VM] * n_in)[:n_in],
        out_specs=out_specs or [VM] * len(outs),
        scratch_shapes=list(scratch),
        compiler_params=pltpu.CompilerParams(vmem_limit_bytes=vmem * MIB),
        name=name,
    )


def place():
    nx, ny = lax.axis_size("gx"), lax.axis_size("gy")
    ix, iy = lax.axis_index("gx"), lax.axis_index("gy")
    px, py = lax.rem(ix, 2), lax.rem(iy, 2)
    inner = (ix + px > 0) & (ix + px < nx)
    return px == 0, py == 0, inner, ix * ny + iy, (ix - px) * ny + iy, ny


def split(value):
    high = value.astype(BF16)
    low = (value - high.astype(F32)).astype(BF16)
    return high, low


def dot3(a_high, a_low, b_high, b_low):
    def one(a, b):
        return jnp.dot(a, b, preferred_element_type=F32)

    return one(a_high, b_high) + (one(a_high, b_low) + one(a_low, b_high))


def reduce_list(items, op):
    result = items[0]
    for item in items[1:]:
        result = op(result, item)
    return result


def pack_body(v_ref, spin_hbm, *rest):
    params, (pay_c, pay_d, blk_ref, x_ref, y_ref, low, high, held, held_int, spin_ref, sems) = rest[:5], rest[5:]
    _, even_y, _, brick, _, _ = place()
    small = [pltpu.make_async_copy(spin_hbm, spin_ref, sems.at[2])]
    small += [pltpu.make_async_copy(p, held.at[k], sems.at[3 + k]) for k, p in enumerate(params[:4])]
    small.append(pltpu.make_async_copy(params[4], held_int, sems.at[7]))
    copies = [
        pltpu.make_async_copy(v_ref.at[:, :, pl.ds(0, 8)], low, sems.at[0]),
        pltpu.make_async_copy(v_ref.at[:, :, pl.ds(CY - 8, 8)], high, sems.at[1]),
        pltpu.make_async_copy(v_ref.at[:, 0], x_ref.at[pl.ds(0, 3)], sems.at[8]),
        pltpu.make_async_copy(v_ref.at[:, CX - 1], x_ref.at[pl.ds(3, 3)], sems.at[9]),
    ]
    for copy in small + copies:
        copy.start()
    for copy in small:
        copy.wait()
    radius, chord, twist, angle = [held[k] for k in range(4)]
    parts = [
        radius,
        chord,
        jnp.cos(twist),
        jnp.sin(twist),
        jnp.cos(angle),
        jnp.sin(angle),
        held_int[...].astype(F32),
        jnp.full((1, CZ), spin_ref[0], F32),
        jnp.full((1, CZ), brick.astype(F32), F32),
    ]
    block = jnp.concatenate(parts, axis=0)
    blk_ref[...] = block
    pay_c[FACE_Y:] = block
    for copy in copies:
        copy.wait()
    for c in range(3):
        y_low = low[c, :, 0, :]
        y_high = high[c, :, 7, :]
        y_ref[c] = y_low
        y_ref[c + 3] = y_high
        pay_c[c * CX : (c + 1) * CX] = jnp.where(even_y, y_high, y_low)
        pay_d[c * CX : (c + 1) * CX] = jnp.where(even_y, y_low, y_high)


def stencil_body(start, v_ref, out_ref):
    row = lax.broadcasted_iota(jnp.int32, (CY, CZ), 0)
    lane = lax.broadcasted_iota(jnp.int32, (CY, CZ), 1)
    half = 0.5 * DT_STEP
    visc = DT_STEP * NU_VISC
    not_last_y, not_first_y = row < CY - 1, row > 0
    not_last_z, not_first_z = lane < CZ - 1, lane > 0

    def step(k, carry):
        x = start + k
        up = jnp.minimum(x + 1, CX - 1)
        down = jnp.maximum(x - 1, 0)
        v0, v1, v2 = v_ref[0, x], v_ref[1, x], v_ref[2, x]
        a_x = jnp.where(x < CX - 1, visc - half * v0, 0.0)
        b_x = jnp.where(x > 0, visc + half * v0, 0.0)
        a_y = jnp.where(not_last_y, visc - half * v1, 0.0)
        b_y = jnp.where(not_first_y, visc + half * v1, 0.0)
        a_z = jnp.where(not_last_z, visc - half * v2, 0.0)
        b_z = jnp.where(not_first_z, visc + half * v2, 0.0)
        for c in range(3):
            mid = (v0, v1, v2)[c]
            along_x = a_x * v_ref[c, up] + b_x * v_ref[c, down]
            along_y = a_y * pltpu.roll(mid, CY - 1, 0) + b_y * pltpu.roll(mid, 1, 0)
            along_z = a_z * pltpu.roll(mid, CZ - 1, 1) + b_z * pltpu.roll(mid, 1, 1)
            out_ref[c, k] = (1.0 - 6.0 * visc) * mid + along_x + (along_y + along_z)
        return carry

    lax.fori_loop(0, CX // 2, step, 0, unroll=2)


def weight(coord, base, frac):
    return jnp.where(coord == base, 1.0 - frac, jnp.where(coord == base + 1, frac, 0.0))


def sample_body(v_ref, cell_ref, frac_ref, tab_ref):
    rows = jnp.concatenate([cell_ref[...].astype(F32), frac_ref[...], jnp.zeros((CZ - 6, HOST), F32)], axis=0)
    turned = rows.T
    x_col, y_col, z_col = [turned[:, k : k + 1].astype(jnp.int32) for k in range(3)]
    fx, fy, fz = [turned[:, k : k + 1] for k in range(3, 6)]
    lane = lax.broadcasted_iota(jnp.int32, (HOST, CZ), 1)
    wy = weight(lane % CY, y_col, fy)
    x_lane = lane // CY - x_col
    acc = None
    per = 4
    nx = CZ * per // CY
    for j in range(CX // nx):
        parts = []
        for i in range(per):
            shift = (CZ // CY) * (j * per + i)
            wx = jnp.where(x_lane == -shift, 1.0 - fx, jnp.where(x_lane == 1 - shift, fx, 0.0))
            parts.append(wx * wy)
        w_high, w_low = split(jnp.concatenate(parts, axis=1))
        field = [v_ref[c, j * nx : (j + 1) * nx].reshape(nx * CY, CZ) for c in range(3)]
        f_high, f_low = split(jnp.concatenate(field, axis=1))
        part = dot3(w_high, w_low, f_high, f_low)
        acc = part if acc is None else acc + part
    wz = weight(lane, z_col, fz)
    out = turned
    for c in range(3):
        value = jnp.sum(acc[:, c * CZ : (c + 1) * CZ] * wz, axis=1, keepdims=True)
        out = jnp.where(lane == 6 + c, value, out)
    tab_ref[...] = out


def split_blocks(sources):
    return [
        ref[first + k * ROWS : first + (k + 1) * ROWS]
        for ref, first in sources
        for k in range((ref.shape[0] - first) // ROWS)
    ]


def pick_pair(values, b0, ny):
    keys = [value[12:13, 0:1] for value in values]
    members = []
    for key in keys:
        home = jnp.floor(key * (1.0 / HOST)).astype(jnp.int32)
        members.append((home == b0) | (home == b0 + ny))
    low_key = reduce_list([jnp.where(m, k, 1e9) for k, m in zip(keys, members)], jnp.minimum)
    high_key = reduce_list([jnp.where(m, k, -9.0) for k, m in zip(keys, members)], jnp.maximum)
    low = jnp.full((ROWS, CZ), -1.0, F32)
    high = low
    for key, value in zip(keys, values):
        low = jnp.where(key == low_key, value, low)
        high = jnp.where(key == high_key, value, high)
    return low, high


def xpack_body(n_blk, x_ref, rec_c, rec_d, *rest):
    pieces, (pay_a, pay_b, own_ref, *others) = rest[:n_blk], rest[n_blk:]
    even_x, even_y, inner, _, b0, ny = place()
    for c in range(3):
        at = c * CX
        y_high = jnp.where(even_y, rec_c[at : at + 1], rec_d[at : at + 1])
        tail = jnp.concatenate([y_high, jnp.zeros((XROWS - CY - 1, CZ), F32)], axis=0)
        low, high = x_ref[c], x_ref[c + 3]
        at = c * XROWS
        pay_a[at : at + CY] = jnp.where(even_x, high, low)
        pay_b[at : at + CY] = jnp.where(even_x, low, high)
        pay_a[at + CY : at + XROWS] = tail
        pay_b[at + CY : at + XROWS] = tail
    if not others:
        own_ref[...] = jnp.concatenate([p[...] for p in pieces], axis=0)
        return
    values = split_blocks([(p, 0) for p in pieces])
    chips = ny * 2
    side = jnp.where(even_x, -chips, chips)
    total = lax.axis_size("gx") * ny
    own_ref[...] = jnp.concatenate(pick_pair(values, b0, ny), axis=0)
    pay_b[FACE_X:] = jnp.concatenate(pick_pair(values, lax.rem(b0 + side + total, total), ny), axis=0)
    others[0][...] = jnp.concatenate(pick_pair(values, lax.rem(b0 + 2 * chips, total), ny), axis=0)


def select_body(n_blk, tab_ref, face_a, face_b, rec_c, rec_d, blk_ref, *rest):
    others, (samp_ref, sel_ref, pts_ref) = rest[:n_blk], rest[n_blk:]
    even_x, even_y, inner, brick, b0, ny = place()
    sources = [(blk_ref, 0), (face_b, FACE_X)] + [(o, 0) for o in others]
    turbine_a, turbine_b = pick_pair(split_blocks(sources), b0, ny)
    sel = jnp.concatenate([turbine_a, turbine_b], axis=0)
    sel_ref[...] = sel
    turned = jnp.concatenate([sel, jnp.zeros((CZ - 2 * ROWS, CZ), F32)], axis=0).T

    def column(k):
        picks = (2 * k, 2 * k + 1, ROWS + 2 * k, ROWS + 2 * k + 1)
        return jnp.concatenate([turned[:, j : j + 1] for j in picks], axis=0)

    table = tab_ref[...]
    lane = lax.broadcasted_iota(jnp.int32, (PTS, CZ), 1)
    x_col, y_col, z_col = [table[:, k : k + 1].astype(jnp.int32) for k in range(3)]
    fx, fy, fz = [table[:, k : k + 1] for k in range(3, 6)]
    on_line = lane >= CX
    edge_x = jnp.where(on_line, lane - CX, CX)
    edge_y = jnp.where(on_line, CY, lane)
    edge_w = jnp.where(on_line | (lane <= CY), weight(edge_x, x_col, fx) * weight(edge_y, y_col, fy), 0.0)
    field = []
    for c in range(3):
        at = c * XROWS
        past = jnp.where(inner, face_b[at : at + XROWS], 0.0)
        plane = jnp.where(even_x, face_a[at : at + XROWS], past)
        at = c * CX
        line = jnp.where(even_y, rec_c[at : at + CX], rec_d[at : at + CX])
        field.append(jnp.concatenate([plane, jnp.zeros((CX - XROWS, CZ), F32), line], axis=0))
    w_high, w_low = split(edge_w)
    f_high, f_low = split(jnp.concatenate(field, axis=1))
    acc = dot3(w_high, w_low, f_high, f_low)
    wz = weight(lane, z_col, fz)
    for c in range(3):
        value = jnp.sum(acc[:, c * CZ : (c + 1) * CZ] * wz, axis=1, keepdims=True)
        table = table + jnp.where(lane == 6 + c, value, 0.0)
    slot = column(6).astype(jnp.int32)
    mine = (slot // HOST) == brick
    local = jnp.where(mine, slot % HOST, -1)
    hit = (lax.broadcasted_iota(jnp.int32, (PTS, HOST), 1) == local).astype(F32).astype(BF16)
    first, second = split(table)
    third = (table - first.astype(F32) - second.astype(F32)).astype(BF16)
    pulled = [jnp.dot(hit, part, preferred_element_type=F32) for part in (first, second, third)]
    points = pulled[0] + pulled[1] + pulled[2]
    points = jnp.where(lane == 9, column(0), points)
    pts_ref[...] = jnp.where((lane == 0) & jnp.logical_not(mine), -100.0, points)
    samp_ref[...] = points.T[6:14]


def weights_body(pts_ref, gx_ref, gy_ref, pz_ref):
    table = pts_ref[...].T

    def offsets(frac):
        raw = [jnp.exp(-((o - frac) ** 2) / EPS_SQ) for o in (-1.0, 0.0, 1.0, 2.0)]
        total = (raw[0] + raw[1]) + (raw[2] + raw[3])
        return [value / total for value in raw]

    def profile(rows, inner, base, frac):
        index = lax.broadcasted_iota(jnp.int32, (rows, PTS), 0)
        late = index - inner
        index = jnp.where(index < inner, index, jnp.where(late < 2, late - 2, late - 2 + inner))
        rel = index - base.astype(jnp.int32)
        result = jnp.zeros((rows, PTS), F32)
        for k, w in enumerate(offsets(frac)):
            result = jnp.where(rel == k - 1, w, result)
        return result

    gx_ref[...] = profile(YROWS, CX, table[0:1], table[3:4])
    gy_ref[...] = profile(CY + 8, CY, table[1:2], table[4:5])
    wz = offsets(table[5:6])
    stack = jnp.concatenate(wz + [jnp.zeros((CZ - 4, PTS), F32)], axis=0).T
    z_rel = lax.broadcasted_iota(jnp.int32, (PTS, CZ), 1) - pts_ref[:, 2:3].astype(jnp.int32)
    pz = jnp.zeros((PTS, CZ), F32)
    for k in range(4):
        pz = jnp.where(z_rel == k - 1, stack[:, k : k + 1], pz)
    pz_ref[...] = pz


def attack(axial_flow, tangent, cos_twist, sin_twist):
    rel_speed = jnp.sqrt(axial_flow * axial_flow + tangent * tangent + 1.0)
    cos_phi = tangent / rel_speed
    sin_phi = axial_flow / rel_speed
    sin_alpha = sin_phi * cos_twist - cos_phi * sin_twist
    cos_alpha = cos_phi * cos_twist + sin_phi * sin_twist
    lift_coef = 2.0 * jnp.pi * sin_alpha * cos_alpha / (1.0 + 4.0 * sin_alpha * sin_alpha)
    drag_coef = 0.02 + 0.8 * sin_alpha * sin_alpha
    return rel_speed, cos_phi, sin_phi, lift_coef, drag_coef


def loads_body(samp_ref, other_ref, sel_ref, pts_ref, gx_ref, gy_ref, pz_ref, lh_ref, pay_c, pay_d, ret_ref, xrim_ref):
    even_x, even_y, inner, _, _, _ = place()

    def row(k):
        picks = (2 * k, 2 * k + 1, ROWS + 2 * k, ROWS + 2 * k + 1)
        return jnp.concatenate([sel_ref[j : j + 1] for j in picks], axis=1)

    radius, chord, cos_t, sin_t, cos_a, sin_a = [row(k) for k in range(6)]
    spin = radius * jnp.concatenate([sel_ref[j : j + 1] for j in (14, 14, ROWS + 14, ROWS + 14)], axis=1)
    flow = samp_ref[...] + other_ref[...]
    axial = flow[0:1]
    tangent = spin - (cos_a * flow[2:3] - sin_a * flow[1:2])
    rel_speed, cos_phi, sin_phi, lift_coef, drag_coef = attack(axial, tangent, cos_t, sin_t)
    circ = 0.5 * chord * rel_speed * lift_coef
    parts = []
    for t in range(2):
        seg = slice(t * P_SIZE, (t + 1) * P_SIZE)
        spacing = radius[:, seg] - pts_ref[seg, 9:10]
        kernel = spacing / (spacing * spacing + CORE_SQ)
        lhs = jnp.concatenate([cos_a[:, seg] * circ[:, seg], sin_a[:, seg] * circ[:, seg], jnp.zeros((6, P_SIZE), F32)], axis=0)
        both = jnp.dot(lhs, kernel, preferred_element_type=F32, precision=lax.Precision.HIGHEST)
        parts.append((cos_a[:, seg] * both[0:1] + sin_a[:, seg] * both[1:2]) / (4.0 * math.pi))
    induced = jnp.concatenate(parts, axis=1)
    rel_speed, cos_phi, sin_phi, lift_coef, drag_coef = attack(axial + induced, tangent, cos_t, sin_t)
    dynamic = 0.5 * chord * rel_speed * rel_speed
    lift = dynamic * lift_coef
    drag = dynamic * drag_coef
    thrust = lift * cos_phi + drag * sin_phi
    torque = lift * sin_phi - drag * cos_phi
    force = [-thrust, torque * sin_a, -torque * cos_a]
    pieces = []
    for t in range(2):
        for c in range(3):
            for h in range(2):
                at = t * P_SIZE + h * CZ
                pieces.append(force[c][:, at : at + CZ])
        pieces += [sel_ref[t * ROWS + 15 : t * ROWS + 16]] * 2
    blocks = jnp.concatenate(pieces, axis=0)
    ret_ref[...] = blocks
    cols = jnp.concatenate(force + [jnp.zeros((CZ - 3, PTS), F32)], axis=0).T
    pz = pz_ref[...] * DT_STEP
    lines = jnp.concatenate([cols[:, c : c + 1] * pz for c in range(3)], axis=1)
    l_high, l_low = split(lines)
    lh_ref[...] = lines
    gx = gx_ref[...]
    gy = gy_ref[...]
    planes = [gx * gy[CY + k : CY + k + 1] for k in range(4)]
    planes += [gx[CX + k : CX + k + 1] * gy[0:CY] for k in range(4)]
    w_high, w_low = split(jnp.concatenate(planes, axis=0))
    rim = dot3(w_high, w_low, l_high, l_low)
    for k in range(2):
        for c in range(3):
            low = rim[k * YROWS : (k + 1) * YROWS, c * CZ : (c + 1) * CZ]
            high = rim[(k + 2) * YROWS : (k + 3) * YROWS, c * CZ : (c + 1) * CZ]
            at = (k * 3 + c) * YROWS
            pay_c[at : at + YROWS] = jnp.where(even_y, high, low)
            pay_d[at : at + YROWS] = jnp.where(even_y, low, high)
    first = 4 * YROWS
    for k in range(4):
        for c in range(3):
            at = (k * 3 + c) * CY
            xrim_ref[at : at + CY] = rim[first + k * CY : first + (k + 1) * CY, c * CZ : (c + 1) * CZ]


SPREAD_X = 8


def spread_body(start, lines_ref, gx_ref, gy_ref, base_ref, out_ref):
    l_high, l_low = split(lines_ref[...])
    gy = gy_ref[0:CY]
    for k in range(out_ref.shape[1] // SPREAD_X):
        at = k * SPREAD_X
        first = start + at
        planes = jnp.concatenate([gx_ref[first + i : first + i + 1] * gy for i in range(SPREAD_X)], axis=0)
        w_high, w_low = split(planes)
        value = dot3(w_high, w_low, l_high, l_low)
        for c in range(3):
            part = value[:, c * CZ : (c + 1) * CZ].reshape(SPREAD_X, CY, CZ)
            out_ref[c, at : at + SPREAD_X] = base_ref[c, at : at + SPREAD_X] + part


def rimpack_body(n_blk, xrim_ref, rec_c, rec_d, *rest):
    pieces, (pay_a, pay_b, back_ref, *others) = rest[:n_blk], rest[n_blk:]
    even_x, even_y, inner, _, b0, ny = place()
    zero = jnp.zeros((CY - 4, CZ), F32)
    for k in range(2):
        for c in range(3):
            sides = []
            for s in range(2):
                near, far = [], []
                for y in range(2):
                    at = (y * 3 + c) * YROWS + CX + 2 * s + k
                    from_c, from_d = rec_c[at : at + 1], rec_d[at : at + 1]
                    near.append(jnp.where(even_y, from_d, from_c))
                    far.append(jnp.where(even_y, from_c, from_d))
                at = ((2 * s + k) * 3 + c) * CY
                sides.append(xrim_ref[at : at + CY] + jnp.concatenate(near + [zero] + far, axis=0))
            at = (k * 3 + c) * CY
            pay_a[at : at + CY] = jnp.where(even_x, sides[1], sides[0])
            pay_b[at : at + CY] = jnp.where(even_x, sides[0], sides[1])
    back = jnp.concatenate([p[...] for p in pieces], axis=0)
    back_ref[...] = back
    if others:
        chips = ny * 2
        side = jnp.where(even_x, -chips, chips)
        total = lax.axis_size("gx") * ny
        for ref, at, target in (
            (pay_b, RIM_X, lax.rem(b0 + side + total, total)),
            (others[0], 0, lax.rem(b0 + 2 * chips, total)),
        ):
            for core in range(2):
                wanted = (target + core * ny).astype(F32)
                found = jnp.full((BACK, CZ), -1.0, F32)
                for k in range(back.shape[0] // BACK):
                    value = back[k * BACK : (k + 1) * BACK]
                    found = jnp.where(value[6:7, 0:1] == wanted, value, found)
                ref[at + core * BACK : at + (core + 1) * BACK] = found


def final_body(n_ret, main_low, main_high, x_ref, y_ref, face_a, face_b, yc_ref, yd_ref, rim_a, rim_b, rim_c, rim_d, back_ref, *rest):
    rets, (out_ref, pf_ref, buf, sems) = rest[:n_ret], rest[n_ret:]
    even_x, even_y, inner, brick, _, _ = place()
    half = 0.5 * DT_STEP
    visc = DT_STEP * NU_VISC
    copies = []
    for k in range(N_CHUNK):
        first = k * CHUNK
        part = slice(first, first + CHUNK)
        for c in range(3):
            half_of = main_low if k < N_CHUNK // 2 else main_high
            at = first % (CX // 2)
            buf[c, part] = half_of[c, at : at + CHUNK]
            if k in (0, N_CHUNK - 1):
                a = face_a[c * XROWS : c * XROWS + CY]
                b = jnp.where(inner, face_b[c * XROWS : c * XROWS + CY], 0.0)
                if k == 0:
                    buf[c, 0] += jnp.where(even_x, b, a) * (visc + half * x_ref[0])
                else:
                    buf[c, CX - 1] += jnp.where(even_x, a, b) * (visc - half * x_ref[3])
                for i in range(2):
                    rows = slice((i * 3 + c) * CY, (i * 3 + c + 1) * CY)
                    a, b = rim_a[rows], jnp.where(inner, rim_b[rows], 0.0)
                    if k == 0:
                        buf[c, i] += jnp.where(even_x, b, a)
                    else:
                        buf[c, CX - 2 + i] += jnp.where(even_x, a, b)
            rows = slice(c * CX + first, c * CX + first + CHUNK)
            a, b = yc_ref[rows], yd_ref[rows]
            low = [jnp.where(even_y, b, a) * (visc + half * y_ref[1, part]), 0.0]
            high = [0.0, jnp.where(even_y, a, b) * (visc - half * y_ref[4, part])]
            for i in range(2):
                at = (i * 3 + c) * YROWS + first
                a, b = rim_c[at : at + CHUNK], rim_d[at : at + CHUNK]
                buf[c, part, i, :] += jnp.where(even_y, b, a) + low[i]
                buf[c, part, CY - 2 + i, :] += jnp.where(even_y, a, b) + high[i]
        copies.append(pltpu.make_async_copy(buf.at[:, pl.ds(first, CHUNK)], out_ref.at[:, pl.ds(first, CHUNK)], sems.at[k]))
        copies[-1].start()
    mine = brick.astype(F32)
    found = jnp.zeros((BACK, CZ), F32)
    for ref, first in [(back_ref, 0), (rim_b, RIM_X)] + [(r, 0) for r in rets]:
        for k in range((ref.shape[0] - first) // BACK):
            value = ref[first + BACK * k : first + BACK * k + BACK]
            found = jnp.where(value[6:7, 0:1] == mine, value, found)
    for c in range(3):
        pf_ref[c : c + 1] = jnp.concatenate([found[2 * c : 2 * c + 1], found[2 * c + 1 : 2 * c + 2]], axis=1)
    for copy in copies:
        copy.wait()


def per_device(
    velocity,
    host_cell,
    host_frac,
    host_dst,
    owner_src,
    rotor_speed,
    blade_radius,
    blade_chord,
    blade_twist,
    blade_angle,
):
    nx, ny = lax.axis_size("gx"), lax.axis_size("gy")
    ring = nx == 8

    def flip(n, bits):
        return [(i, i ^ bits) for i in range(n)]

    def odd_pairs(n, closed=False):
        up = [(i, (i + 1) % n) for i in range(1, n if closed else n - 1, 2)]
        return up + [(t, s) for s, t in up]

    def swap(block):
        return lax.ppermute(block, "gx", flip(nx, 1))

    def join(pieces):
        return pieces[0] if len(pieces) == 1 else jnp.concatenate(pieces, axis=0)

    def after(values, other):
        return lax.optimization_barrier((values, other))

    def gather_y(first, filler):
        pieces = [first]
        for bit in [b for b in (2, 4, 8) if b < ny]:
            got = lax.ppermute(join(pieces), "gy", flip(ny, bit))
            if filler is not None:
                got, filler = after(got, filler())
                yield filler
                filler = None
            pieces.append(got)
        yield pieces

    def gather_x(blocks):
        pieces = []
        for bit in [b for b in (2, 4, 8, 16) if b < nx]:
            pieces.append(lax.ppermute(join([blocks] + pieces), "gx", flip(nx, bit)))
        return pieces

    dma = pltpu.SemaphoreType.DMA
    tiles = pltpu.VMEM((3, CX, 8, CZ), F32)
    pay_c, pay_d, block, x_faces, y_faces = call(
        pack_body,
        [(FACE_Y + ROWS, CZ), (FACE_Y, CZ), (ROWS, CZ), (6, CY, CZ), (6, CX, CZ)],
        7,
        "pack",
        scratch=[tiles, tiles, pltpu.VMEM((4, 2, CZ), F32), pltpu.VMEM((2, CZ), jnp.int32), pltpu.SMEM((1,), F32), dma((10,))],
        in_specs=[HB] * 7,
        vmem=56,
    )(velocity, rotor_speed, *[a.reshape(2, CZ) for a in (blade_radius, blade_chord, blade_twist, blade_angle, owner_src)])
    rec_c = lax.ppermute(pay_c, "gy", flip(ny, 1))
    rec_d = lax.ppermute(pay_d, "gy", odd_pairs(ny))

    def stencil(start):
        return call(lambda *refs: stencil_body(start, *refs), [(3, CX // 2, CY, CZ)], 1, "stencil")(velocity)[0]

    rec_c, base_low = after(rec_c, stencil(0))
    sampled = lambda: call(sample_body, [(HOST, CZ)], 3, "sample", vmem=24)(velocity, host_cell, host_frac)[0]
    table, pieces = list(gather_y(join([block, rec_c[FACE_Y:]]), sampled))
    pieces = pieces + [swap(p) for p in pieces]
    n_rows = 2 * ny * ROWS
    pair = (2 * ROWS, CZ)
    pay_a, pay_b, blocks, *across = call(
        lambda *refs: xpack_body(len(pieces), *refs),
        [(FACE_X, CZ), (FACE_X + 2 * ROWS, CZ), pair, pair] if ring else [(FACE_X, CZ), (FACE_X, CZ), (n_rows, CZ)],
        3 + len(pieces),
        "xpack",
    )(x_faces, rec_c, rec_d, *pieces)
    face_b = lax.ppermute(pay_b, "gx", odd_pairs(nx, ring))
    from_x = [lax.ppermute(across[0], "gx", flip(nx, 4))] if ring else gather_x(blocks)
    face_a = swap(pay_a)
    base_high = stencil(CX // 2)
    face_b, base_high = after(face_b, base_high)
    if ring:
        from_x.append(swap(face_b[FACE_X:]))
    samp, sel, pts = call(
        lambda *refs: select_body(len(from_x), *refs),
        [(8, PTS), (2 * ROWS, CZ), (PTS, CZ)],
        6 + len(from_x),
        "select",
    )(table, face_a, face_b, rec_c, rec_d, blocks, *from_x)
    other = swap(samp)
    gx, gy, pz = call(weights_body, [(YROWS, PTS), (CY + 8, PTS), (PTS, CZ)], 1, "weights")(pts)
    lines, pay_c, pay_d, ret, xrim = call(
        loads_body,
        [(PTS, 3 * CZ), (RIM_Y, CZ), (RIM_Y, CZ), (2 * BACK, CZ), (2 * RIM_X, CZ)],
        7,
        "loads",
    )(samp, other, sel, pts, gx, gy, pz)
    ret_c = lax.ppermute(ret, "gy", flip(ny, 1))
    rim_c = lax.ppermute(pay_c, "gy", flip(ny, 1))
    rim_d = lax.ppermute(pay_d, "gy", odd_pairs(ny))

    def spread(start, base):
        return call(
            lambda *refs: spread_body(start, *refs), [(3, CX // 2, CY, CZ)], 4, "spread"
        )(lines, gx, gy, base)[0]

    ret_c, main_low = after(ret_c, spread(0, base_low))
    main_high, pieces = list(gather_y(join([ret, ret_c]), lambda: spread(CX // 2, base_high)))
    rim_c, main_high = after(rim_c, main_high)
    n_rows = 2 * ny * BACK
    pair = (2 * BACK, CZ)
    pay_a, pay_b, back, *across = call(
        lambda *refs: rimpack_body(len(pieces), *refs),
        [(RIM_X, CZ), (RIM_X + 2 * BACK, CZ), (n_rows, CZ), pair] if ring else [(RIM_X, CZ), (RIM_X, CZ), (n_rows, CZ)],
        3 + len(pieces),
        "rimpack",
    )(xrim, rim_c, rim_d, *pieces)
    rim_b = lax.ppermute(pay_b, "gx", odd_pairs(nx, ring))
    rets = [lax.ppermute(across[0], "gx", flip(nx, 4))] if ring else gather_x(back)
    rim_a = swap(pay_a)
    if ring:
        rets.append(swap(rim_b[RIM_X:]))
    return tuple(
        call(
            lambda *refs: final_body(len(rets), *refs),
            [velocity.shape, (3, P_SIZE)],
            13 + len(rets),
            "final",
            scratch=[pltpu.VMEM(velocity.shape, F32), dma((N_CHUNK,))],
            out_specs=[HB, VM],
        )(main_low, main_high, x_faces, y_faces, face_a, face_b, rec_c, rec_d, rim_a, rim_b, rim_c, rim_d, back, *rets)
    )


def solution(mesh):
    return jax.shard_map(
        per_device,
        mesh=mesh,
        in_specs=(
            P(None, "gx", "gy", None),
            P(None, ("gx", "gy")),
            P(None, ("gx", "gy")),
            P(("gx", "gy")),
            P(("gx", "gy")),
            P(("gx", "gy")),
            P(("gx", "gy")),
            P(("gx", "gy")),
            P(("gx", "gy")),
            P(("gx", "gy")),
        ),
        out_specs=(P(None, "gx", "gy", None), P(None, ("gx", "gy"))),
        check_vma=False,
    )
```

```python
import math

import jax
import jax.numpy as jnp
from jax import lax
from jax.experimental import pallas as pl
from jax.experimental.pallas import tpu as pltpu
from jax.sharding import PartitionSpec as P

CX = 64
CY = 32
CZ = 128
P_SIZE = 256
HOST = 512
PTS = 2 * P_SIZE

DT_STEP = 0.2
NU_VISC = 0.5
EPS_SQ = 1.44
CORE_SQ = 0.01

ROWS = 16
BACK = 8
YROWS = 72
XROWS = 40
FACE_Y = 3 * CX
FACE_X = 3 * XROWS
RIM_Y = 2 * 3 * YROWS
RIM_X = 2 * 3 * CY
CHUNK = 8
N_CHUNK = CX // CHUNK

F32 = jnp.float32
BF16 = jnp.bfloat16
VM = pl.BlockSpec(memory_space=pltpu.MemorySpace.VMEM)
SM = pl.BlockSpec(memory_space=pltpu.MemorySpace.SMEM)
HB = pl.BlockSpec(memory_space=pltpu.MemorySpace.HBM)
MIB = 1024 * 1024


def call(body, outs, n_in, name, scratch=(), first=VM, second=VM, out_specs=None, in_specs=None, vmem=12, aliases=None):
    return pl.pallas_call(
        body,
        out_shape=[jax.ShapeDtypeStruct(s, F32) for s in outs],
        in_specs=in_specs or ([first, second] + [VM] * n_in)[:n_in],
        out_specs=out_specs or [VM] * len(outs),
        scratch_shapes=list(scratch),
        input_output_aliases=aliases or {},
        compiler_params=pltpu.CompilerParams(vmem_limit_bytes=vmem * MIB),
        name=name,
    )


def place():
    nx, ny = lax.axis_size("gx"), lax.axis_size("gy")
    ix, iy = lax.axis_index("gx"), lax.axis_index("gy")
    px, py = lax.rem(ix, 2), lax.rem(iy, 2)
    inner = (ix + px > 0) & (ix + px < nx)
    return px == 0, py == 0, inner, ix * ny + iy, (ix - px) * ny + iy, ny


def split(value):
    high = value.astype(BF16)
    low = (value - high.astype(F32)).astype(BF16)
    return high, low


def dot3(a_high, a_low, b_high, b_low):
    def one(a, b):
        return jnp.dot(a, b, preferred_element_type=F32)

    return one(a_high, b_high) + (one(a_high, b_low) + one(a_low, b_high))


def reduce_list(items, op):
    result = items[0]
    for item in items[1:]:
        result = op(result, item)
    return result


def pack_body(v_ref, spin_hbm, *rest):
    params, (pay_c, pay_d, blk_ref, x_ref, y_ref, low, high, held, held_int, spin_ref, sems) = rest[:5], rest[5:]
    _, even_y, _, brick, _, _ = place()
    small = [pltpu.make_async_copy(spin_hbm, spin_ref, sems.at[2])]
    small += [pltpu.make_async_copy(p, held.at[k], sems.at[3 + k]) for k, p in enumerate(params[:4])]
    small.append(pltpu.make_async_copy(params[4], held_int, sems.at[7]))
    copies = [
        pltpu.make_async_copy(v_ref.at[:, :, pl.ds(0, 8)], low, sems.at[0]),
        pltpu.make_async_copy(v_ref.at[:, :, pl.ds(CY - 8, 8)], high, sems.at[1]),
        pltpu.make_async_copy(v_ref.at[:, 0], x_ref.at[pl.ds(0, 3)], sems.at[8]),
        pltpu.make_async_copy(v_ref.at[:, CX - 1], x_ref.at[pl.ds(3, 3)], sems.at[9]),
    ]
    for copy in small + copies:
        copy.start()
    for copy in small:
        copy.wait()
    radius, chord, twist, angle = [held[k] for k in range(4)]
    parts = [
        radius,
        chord,
        jnp.cos(twist),
        jnp.sin(twist),
        jnp.cos(angle),
        jnp.sin(angle),
        held_int[...].astype(F32),
        jnp.full((1, CZ), spin_ref[0], F32),
        jnp.full((1, CZ), brick.astype(F32), F32),
    ]
    block = jnp.concatenate(parts, axis=0)
    blk_ref[...] = block
    pay_c[FACE_Y:] = block
    for copy in copies:
        copy.wait()
    for c in range(3):
        y_low = low[c, :, 0, :]
        y_high = high[c, :, 7, :]
        y_ref[c] = y_low
        y_ref[c + 3] = y_high
        pay_c[c * CX : (c + 1) * CX] = jnp.where(even_y, y_high, y_low)
        pay_d[c * CX : (c + 1) * CX] = jnp.where(even_y, y_low, y_high)


def stencil_body(start, v_ref, out_ref):
    row = lax.broadcasted_iota(jnp.int32, (CY, CZ), 0)
    lane = lax.broadcasted_iota(jnp.int32, (CY, CZ), 1)
    half = 0.5 * DT_STEP
    visc = DT_STEP * NU_VISC
    not_last_y, not_first_y = row < CY - 1, row > 0
    not_last_z, not_first_z = lane < CZ - 1, lane > 0

    def step(k, carry):
        x = start + k
        up = jnp.minimum(x + 1, CX - 1)
        down = jnp.maximum(x - 1, 0)
        v0, v1, v2 = v_ref[0, x], v_ref[1, x], v_ref[2, x]
        a_x = jnp.where(x < CX - 1, visc - half * v0, 0.0)
        b_x = jnp.where(x > 0, visc + half * v0, 0.0)
        a_y = jnp.where(not_last_y, visc - half * v1, 0.0)
        b_y = jnp.where(not_first_y, visc + half * v1, 0.0)
        a_z = jnp.where(not_last_z, visc - half * v2, 0.0)
        b_z = jnp.where(not_first_z, visc + half * v2, 0.0)
        for c in range(3):
            mid = (v0, v1, v2)[c]
            along_x = a_x * v_ref[c, up] + b_x * v_ref[c, down]
            along_y = a_y * pltpu.roll(mid, CY - 1, 0) + b_y * pltpu.roll(mid, 1, 0)
            along_z = a_z * pltpu.roll(mid, CZ - 1, 1) + b_z * pltpu.roll(mid, 1, 1)
            out_ref[c, k] = (1.0 - 6.0 * visc) * mid + along_x + (along_y + along_z)
        return carry

    lax.fori_loop(0, CX // 2, step, 0, unroll=2)


def weight(coord, base, frac):
    return jnp.where(coord == base, 1.0 - frac, jnp.where(coord == base + 1, frac, 0.0))


def sample_body(v_ref, cell_ref, frac_ref, tab_ref):
    rows = jnp.concatenate([cell_ref[...].astype(F32), frac_ref[...], jnp.zeros((CZ - 6, HOST), F32)], axis=0)
    turned = rows.T
    x_col, y_col, z_col = [turned[:, k : k + 1].astype(jnp.int32) for k in range(3)]
    fx, fy, fz = [turned[:, k : k + 1] for k in range(3, 6)]
    lane = lax.broadcasted_iota(jnp.int32, (HOST, CZ), 1)
    wy = weight(lane % CY, y_col, fy)
    x_lane = lane // CY - x_col
    acc = None
    per = 4
    nx = CZ * per // CY
    for j in range(CX // nx):
        parts = []
        for i in range(per):
            shift = (CZ // CY) * (j * per + i)
            wx = jnp.where(x_lane == -shift, 1.0 - fx, jnp.where(x_lane == 1 - shift, fx, 0.0))
            parts.append(wx * wy)
        w_high, w_low = split(jnp.concatenate(parts, axis=1))
        field = [v_ref[c, j * nx : (j + 1) * nx].reshape(nx * CY, CZ) for c in range(3)]
        f_high, f_low = split(jnp.concatenate(field, axis=1))
        part = dot3(w_high, w_low, f_high, f_low)
        acc = part if acc is None else acc + part
    wz = weight(lane, z_col, fz)
    out = turned
    for c in range(3):
        value = jnp.sum(acc[:, c * CZ : (c + 1) * CZ] * wz, axis=1, keepdims=True)
        out = jnp.where(lane == 6 + c, value, out)
    tab_ref[...] = out


def split_blocks(sources):
    return [
        ref[first + k * ROWS : first + (k + 1) * ROWS]
        for ref, first in sources
        for k in range((ref.shape[0] - first) // ROWS)
    ]


def pick_pair(values, b0, ny):
    keys = [value[12:13, 0:1] for value in values]
    members = []
    for key in keys:
        home = jnp.floor(key * (1.0 / HOST)).astype(jnp.int32)
        members.append((home == b0) | (home == b0 + ny))
    low_key = reduce_list([jnp.where(m, k, 1e9) for k, m in zip(keys, members)], jnp.minimum)
    high_key = reduce_list([jnp.where(m, k, -9.0) for k, m in zip(keys, members)], jnp.maximum)
    low = jnp.full((ROWS, CZ), -1.0, F32)
    high = low
    for key, value in zip(keys, values):
        low = jnp.where(key == low_key, value, low)
        high = jnp.where(key == high_key, value, high)
    return low, high


def xpack_body(n_blk, x_ref, rec_c, rec_d, *rest):
    pieces, (pay_a, pay_b, own_ref, *others) = rest[:n_blk], rest[n_blk:]
    even_x, even_y, inner, _, b0, ny = place()
    for c in range(3):
        at = c * CX
        y_high = jnp.where(even_y, rec_c[at : at + 1], rec_d[at : at + 1])
        tail = jnp.concatenate([y_high, jnp.zeros((XROWS - CY - 1, CZ), F32)], axis=0)
        low, high = x_ref[c], x_ref[c + 3]
        at = c * XROWS
        pay_a[at : at + CY] = jnp.where(even_x, high, low)
        pay_b[at : at + CY] = jnp.where(even_x, low, high)
        pay_a[at + CY : at + XROWS] = tail
        pay_b[at + CY : at + XROWS] = tail
    if not others:
        own_ref[...] = jnp.concatenate([p[...] for p in pieces], axis=0)
        return
    values = split_blocks([(p, 0) for p in pieces])
    chips = ny * 2
    side = jnp.where(even_x, -chips, chips)
    total = lax.axis_size("gx") * ny
    own_ref[...] = jnp.concatenate(pick_pair(values, b0, ny), axis=0)
    beside = jnp.concatenate(pick_pair(values, lax.rem(b0 + side + total, total), ny), axis=0)
    pay_b[FACE_X:] = beside
    others[1][...] = beside
    others[0][...] = jnp.concatenate(pick_pair(values, lax.rem(b0 + 2 * chips, total), ny), axis=0)


def select_body(n_blk, tab_ref, face_a, face_b, rec_c, rec_d, blk_ref, *rest):
    others, (samp_ref, sel_ref, pts_ref) = rest[:n_blk], rest[n_blk:]
    even_x, even_y, inner, brick, b0, ny = place()
    sources = [(blk_ref, 0), (face_b, FACE_X)] + [(o, 0) for o in others]
    turbine_a, turbine_b = pick_pair(split_blocks(sources), b0, ny)
    sel = jnp.concatenate([turbine_a, turbine_b], axis=0)
    sel_ref[...] = sel
    turned = jnp.concatenate([sel, jnp.zeros((CZ - 2 * ROWS, CZ), F32)], axis=0).T

    def column(k):
        picks = (2 * k, 2 * k + 1, ROWS + 2 * k, ROWS + 2 * k + 1)
        return jnp.concatenate([turned[:, j : j + 1] for j in picks], axis=0)

    table = tab_ref[...]
    lane = lax.broadcasted_iota(jnp.int32, (PTS, CZ), 1)
    x_col, y_col, z_col = [table[:, k : k + 1].astype(jnp.int32) for k in range(3)]
    fx, fy, fz = [table[:, k : k + 1] for k in range(3, 6)]
    on_line = lane >= CX
    edge_x = jnp.where(on_line, lane - CX, CX)
    edge_y = jnp.where(on_line, CY, lane)
    edge_w = jnp.where(on_line | (lane <= CY), weight(edge_x, x_col, fx) * weight(edge_y, y_col, fy), 0.0)
    field = []
    for c in range(3):
        at = c * XROWS
        past = jnp.where(inner, face_b[at : at + XROWS], 0.0)
        plane = jnp.where(even_x, face_a[at : at + XROWS], past)
        at = c * CX
        line = jnp.where(even_y, rec_c[at : at + CX], rec_d[at : at + CX])
        field.append(jnp.concatenate([plane, jnp.zeros((CX - XROWS, CZ), F32), line], axis=0))
    w_high, w_low = split(edge_w)
    f_high, f_low = split(jnp.concatenate(field, axis=1))
    acc = dot3(w_high, w_low, f_high, f_low)
    wz = weight(lane, z_col, fz)
    for c in range(3):
        value = jnp.sum(acc[:, c * CZ : (c + 1) * CZ] * wz, axis=1, keepdims=True)
        table = table + jnp.where(lane == 6 + c, value, 0.0)
    slot = column(6).astype(jnp.int32)
    mine = (slot // HOST) == brick
    local = jnp.where(mine, slot % HOST, -1)
    hit = (lax.broadcasted_iota(jnp.int32, (PTS, HOST), 1) == local).astype(F32).astype(BF16)
    first, second = split(table)
    third = (table - first.astype(F32) - second.astype(F32)).astype(BF16)
    pulled = [jnp.dot(hit, part, preferred_element_type=F32) for part in (first, second, third)]
    points = pulled[0] + pulled[1] + pulled[2]
    points = jnp.where(lane == 9, column(0), points)
    pts_ref[...] = jnp.where((lane == 0) & jnp.logical_not(mine), -100.0, points)
    samp_ref[...] = points.T[6:14]


def weights_body(pts_ref, gx_ref, gy_ref, pz_ref):
    table = pts_ref[...].T

    def offsets(frac):
        raw = [jnp.exp(-((o - frac) ** 2) / EPS_SQ) for o in (-1.0, 0.0, 1.0, 2.0)]
        total = (raw[0] + raw[1]) + (raw[2] + raw[3])
        return [value / total for value in raw]

    def profile(rows, inner, base, frac):
        index = lax.broadcasted_iota(jnp.int32, (rows, PTS), 0)
        late = index - inner
        index = jnp.where(index < inner, index, jnp.where(late < 2, late - 2, late - 2 + inner))
        rel = index - base.astype(jnp.int32)
        result = jnp.zeros((rows, PTS), F32)
        for k, w in enumerate(offsets(frac)):
            result = jnp.where(rel == k - 1, w, result)
        return result

    gx_ref[...] = profile(YROWS, CX, table[0:1], table[3:4])
    gy_ref[...] = profile(CY + 8, CY, table[1:2], table[4:5])
    wz = offsets(table[5:6])
    stack = jnp.concatenate(wz + [jnp.zeros((CZ - 4, PTS), F32)], axis=0).T
    z_rel = lax.broadcasted_iota(jnp.int32, (PTS, CZ), 1) - pts_ref[:, 2:3].astype(jnp.int32)
    pz = jnp.zeros((PTS, CZ), F32)
    for k in range(4):
        pz = jnp.where(z_rel == k - 1, stack[:, k : k + 1], pz)
    pz_ref[...] = pz


def attack(axial_flow, tangent, cos_twist, sin_twist):
    rel_speed = jnp.sqrt(axial_flow * axial_flow + tangent * tangent + 1.0)
    cos_phi = tangent / rel_speed
    sin_phi = axial_flow / rel_speed
    sin_alpha = sin_phi * cos_twist - cos_phi * sin_twist
    cos_alpha = cos_phi * cos_twist + sin_phi * sin_twist
    lift_coef = 2.0 * jnp.pi * sin_alpha * cos_alpha / (1.0 + 4.0 * sin_alpha * sin_alpha)
    drag_coef = 0.02 + 0.8 * sin_alpha * sin_alpha
    return rel_speed, cos_phi, sin_phi, lift_coef, drag_coef


def loads_body(samp_ref, other_ref, sel_ref, pts_ref, gx_ref, gy_ref, pz_ref, lh_ref, pay_c, pay_d, ret_ref, xrim_ref):
    even_x, even_y, inner, _, _, _ = place()

    def row(k):
        picks = (2 * k, 2 * k + 1, ROWS + 2 * k, ROWS + 2 * k + 1)
        return jnp.concatenate([sel_ref[j : j + 1] for j in picks], axis=1)

    radius, chord, cos_t, sin_t, cos_a, sin_a = [row(k) for k in range(6)]
    spin = radius * jnp.concatenate([sel_ref[j : j + 1] for j in (14, 14, ROWS + 14, ROWS + 14)], axis=1)
    flow = samp_ref[...] + other_ref[...]
    axial = flow[0:1]
    tangent = spin - (cos_a * flow[2:3] - sin_a * flow[1:2])
    rel_speed, cos_phi, sin_phi, lift_coef, drag_coef = attack(axial, tangent, cos_t, sin_t)
    circ = 0.5 * chord * rel_speed * lift_coef
    parts = []
    for t in range(2):
        seg = slice(t * P_SIZE, (t + 1) * P_SIZE)
        spacing = radius[:, seg] - pts_ref[seg, 9:10]
        kernel = spacing / (spacing * spacing + CORE_SQ)
        lhs = jnp.concatenate([cos_a[:, seg] * circ[:, seg], sin_a[:, seg] * circ[:, seg], jnp.zeros((6, P_SIZE), F32)], axis=0)
        both = jnp.dot(lhs, kernel, preferred_element_type=F32, precision=lax.Precision.HIGHEST)
        parts.append((cos_a[:, seg] * both[0:1] + sin_a[:, seg] * both[1:2]) / (4.0 * math.pi))
    induced = jnp.concatenate(parts, axis=1)
    rel_speed, cos_phi, sin_phi, lift_coef, drag_coef = attack(axial + induced, tangent, cos_t, sin_t)
    dynamic = 0.5 * chord * rel_speed * rel_speed
    lift = dynamic * lift_coef
    drag = dynamic * drag_coef
    thrust = lift * cos_phi + drag * sin_phi
    torque = lift * sin_phi - drag * cos_phi
    force = [-thrust, torque * sin_a, -torque * cos_a]
    pieces = []
    for t in range(2):
        for c in range(3):
            for h in range(2):
                at = t * P_SIZE + h * CZ
                pieces.append(force[c][:, at : at + CZ])
        pieces += [sel_ref[t * ROWS + 15 : t * ROWS + 16]] * 2
    blocks = jnp.concatenate(pieces, axis=0)
    ret_ref[...] = blocks
    cols = jnp.concatenate(force + [jnp.zeros((CZ - 3, PTS), F32)], axis=0).T
    pz = pz_ref[...] * DT_STEP
    lines = jnp.concatenate([cols[:, c : c + 1] * pz for c in range(3)], axis=1)
    l_high, l_low = split(lines)
    lh_ref[...] = lines
    gx = gx_ref[...]
    gy = gy_ref[...]
    planes = [gx * gy[CY + k : CY + k + 1] for k in range(4)]
    planes += [gx[CX + k : CX + k + 1] * gy[0:CY] for k in range(4)]
    w_high, w_low = split(jnp.concatenate(planes, axis=0))
    rim = dot3(w_high, w_low, l_high, l_low)
    for k in range(2):
        for c in range(3):
            low = rim[k * YROWS : (k + 1) * YROWS, c * CZ : (c + 1) * CZ]
            high = rim[(k + 2) * YROWS : (k + 3) * YROWS, c * CZ : (c + 1) * CZ]
            at = (k * 3 + c) * YROWS
            pay_c[at : at + YROWS] = jnp.where(even_y, high, low)
            pay_d[at : at + YROWS] = jnp.where(even_y, low, high)
    first = 4 * YROWS
    for k in range(4):
        for c in range(3):
            at = (k * 3 + c) * CY
            xrim_ref[at : at + CY] = rim[first + k * CY : first + (k + 1) * CY, c * CZ : (c + 1) * CZ]


SPREAD_X = 8


def spread_body(start, lines_ref, gx_ref, gy_ref, base_ref, out_ref):
    l_high, l_low = split(lines_ref[...])
    gy = gy_ref[0:CY]
    for k in range(out_ref.shape[1] // SPREAD_X):
        at = k * SPREAD_X
        first = start + at
        planes = jnp.concatenate([gx_ref[first + i : first + i + 1] * gy for i in range(SPREAD_X)], axis=0)
        w_high, w_low = split(planes)
        value = dot3(w_high, w_low, l_high, l_low)
        for c in range(3):
            part = value[:, c * CZ : (c + 1) * CZ].reshape(SPREAD_X, CY, CZ)
            out_ref[c, at : at + SPREAD_X] = base_ref[c, at : at + SPREAD_X] + part


def rimpack_body(n_blk, xrim_ref, rec_c, rec_d, *rest):
    pieces, (pay_a, pay_b, back_ref, *others) = rest[:n_blk], rest[n_blk:]
    even_x, even_y, inner, _, b0, ny = place()
    zero = jnp.zeros((CY - 4, CZ), F32)
    for k in range(2):
        for c in range(3):
            sides = []
            for s in range(2):
                near, far = [], []
                for y in range(2):
                    at = (y * 3 + c) * YROWS + CX + 2 * s + k
                    from_c, from_d = rec_c[at : at + 1], rec_d[at : at + 1]
                    near.append(jnp.where(even_y, from_d, from_c))
                    far.append(jnp.where(even_y, from_c, from_d))
                at = ((2 * s + k) * 3 + c) * CY
                sides.append(xrim_ref[at : at + CY] + jnp.concatenate(near + [zero] + far, axis=0))
            at = (k * 3 + c) * CY
            pay_a[at : at + CY] = jnp.where(even_x, sides[1], sides[0])
            pay_b[at : at + CY] = jnp.where(even_x, sides[0], sides[1])
    back = jnp.concatenate([p[...] for p in pieces], axis=0)
    back_ref[...] = back
    if others:
        chips = ny * 2
        side = jnp.where(even_x, -chips, chips)
        total = lax.axis_size("gx") * ny
        for ref, at, target in (
            (pay_b, RIM_X, lax.rem(b0 + side + total, total)),
            (others[0], 0, lax.rem(b0 + 2 * chips, total)),
        ):
            for core in range(2):
                wanted = (target + core * ny).astype(F32)
                found = jnp.full((BACK, CZ), -1.0, F32)
                for k in range(back.shape[0] // BACK):
                    value = back[k * BACK : (k + 1) * BACK]
                    found = jnp.where(value[6:7, 0:1] == wanted, value, found)
                ref[at + core * BACK : at + (core + 1) * BACK] = found
        others[1][...] = pay_b[RIM_X:]


def face_terms(buf, at, first, main_low, main_high, y_ref, rec_c, rec_d, rim_c, rim_d, even_y):
    half = 0.5 * DT_STEP
    visc = DT_STEP * NU_VISC
    part = slice(first, first + CHUNK)
    here = slice(at, at + CHUNK)
    half_of = main_low if first < CX // 2 else main_high
    inner = first % (CX // 2)
    for c in range(3):
        buf[c, here] = half_of[c, inner : inner + CHUNK]
        rows = slice(c * CX + first, c * CX + first + CHUNK)
        a, b = rec_c[rows], rec_d[rows]
        low = [jnp.where(even_y, b, a) * (visc + half * y_ref[1, part]), 0.0]
        high = [0.0, jnp.where(even_y, a, b) * (visc - half * y_ref[4, part])]
        for i in range(2):
            row = (i * 3 + c) * YROWS + first
            a, b = rim_c[row : row + CHUNK], rim_d[row : row + CHUNK]
            buf[c, here, i, :] += jnp.where(even_y, b, a) + low[i]
            buf[c, here, CY - 2 + i, :] += jnp.where(even_y, a, b) + high[i]


def chunk_copy(buf, at, out_ref, first, sem):
    return pltpu.make_async_copy(buf.at[:, pl.ds(at, CHUNK)], out_ref.at[:, pl.ds(first, CHUNK)], sem)


def inside_body(main_low, main_high, y_ref, rec_c, rec_d, rim_c, rim_d, out_ref, buf, sems):
    _, even_y, _, _, _, _ = place()
    copies = []
    for k in range(N_CHUNK - 2):
        first = (k + 1) * CHUNK
        face_terms(buf, k * CHUNK, first, main_low, main_high, y_ref, rec_c, rec_d, rim_c, rim_d, even_y)
        copies.append(chunk_copy(buf, k * CHUNK, out_ref, first, sems.at[k]))
        copies[-1].start()
    for copy in copies:
        copy.wait()


def final_body(n_ret, _, main_low, main_high, x_ref, y_ref, face_a, face_b, rec_c, rec_d, rim_a, rim_b, rim_c, rim_d, back_ref, *rest):
    rets, (out_ref, pf_ref, buf, sems) = rest[:n_ret], rest[n_ret:]
    even_x, even_y, inner, brick, _, _ = place()
    half = 0.5 * DT_STEP
    visc = DT_STEP * NU_VISC
    copies = []
    for k in range(2):
        first, at = k * (CX - CHUNK), k * CHUNK
        face_terms(buf, at, first, main_low, main_high, y_ref, rec_c, rec_d, rim_c, rim_d, even_y)
        for c in range(3):
            a = face_a[c * XROWS : c * XROWS + CY]
            b = jnp.where(inner, face_b[c * XROWS : c * XROWS + CY], 0.0)
            if k == 0:
                buf[c, 0] += jnp.where(even_x, b, a) * (visc + half * x_ref[0])
            else:
                buf[c, 2 * CHUNK - 1] += jnp.where(even_x, a, b) * (visc - half * x_ref[3])
            for i in range(2):
                rows = slice((i * 3 + c) * CY, (i * 3 + c + 1) * CY)
                a, b = rim_a[rows], jnp.where(inner, rim_b[rows], 0.0)
                if k == 0:
                    buf[c, i] += jnp.where(even_x, b, a)
                else:
                    buf[c, 2 * CHUNK - 2 + i] += jnp.where(even_x, a, b)
        copies.append(chunk_copy(buf, at, out_ref, first, sems.at[k]))
        copies[-1].start()
    mine = brick.astype(F32)
    found = jnp.zeros((BACK, CZ), F32)
    for ref, first in [(back_ref, 0), (rim_b, RIM_X)] + [(r, 0) for r in rets]:
        for k in range((ref.shape[0] - first) // BACK):
            value = ref[first + BACK * k : first + BACK * k + BACK]
            found = jnp.where(value[6:7, 0:1] == mine, value, found)
    for c in range(3):
        pf_ref[c : c + 1] = jnp.concatenate([found[2 * c : 2 * c + 1], found[2 * c + 1 : 2 * c + 2]], axis=1)
    for copy in copies:
        copy.wait()


def per_device(
    velocity,
    host_cell,
    host_frac,
    host_dst,
    owner_src,
    rotor_speed,
    blade_radius,
    blade_chord,
    blade_twist,
    blade_angle,
):
    nx, ny = lax.axis_size("gx"), lax.axis_size("gy")
    ring = nx == 8

    def flip(n, bits):
        return [(i, i ^ bits) for i in range(n)]

    def odd_pairs(n, closed=False):
        up = [(i, (i + 1) % n) for i in range(1, n if closed else n - 1, 2)]
        return up + [(t, s) for s, t in up]

    def same_side(n):
        return [(i, (i + (2 if i % 2 else n - 2)) % n) for i in range(n)]

    def across_x(blocks):
        return [lax.ppermute(b, "gx", p) for b, p in zip(blocks, (flip(nx, 4), same_side(nx)))]

    def swap(block):
        return lax.ppermute(block, "gx", flip(nx, 1))

    def join(pieces):
        return pieces[0] if len(pieces) == 1 else jnp.concatenate(pieces, axis=0)

    def after(values, other):
        return lax.optimization_barrier((values, other))

    def gather_y(first, filler):
        pieces = [first]
        for bit in [b for b in (2, 4, 8) if b < ny]:
            got = lax.ppermute(join(pieces), "gy", flip(ny, bit))
            if filler is not None:
                got, filler = after(got, filler())
                yield filler
                filler = None
            pieces.append(got)
        yield pieces

    def gather_x(blocks):
        pieces = []
        for bit in [b for b in (2, 4, 8, 16) if b < nx]:
            pieces.append(lax.ppermute(join([blocks] + pieces), "gx", flip(nx, bit)))
        return pieces

    dma = pltpu.SemaphoreType.DMA
    tiles = pltpu.VMEM((3, CX, 8, CZ), F32)
    pay_c, pay_d, block, x_faces, y_faces = call(
        pack_body,
        [(FACE_Y + ROWS, CZ), (FACE_Y, CZ), (ROWS, CZ), (6, CY, CZ), (6, CX, CZ)],
        7,
        "pack",
        scratch=[tiles, tiles, pltpu.VMEM((4, 2, CZ), F32), pltpu.VMEM((2, CZ), jnp.int32), pltpu.SMEM((1,), F32), dma((10,))],
        in_specs=[HB] * 7,
        vmem=56,
    )(velocity, rotor_speed, *[a.reshape(2, CZ) for a in (blade_radius, blade_chord, blade_twist, blade_angle, owner_src)])
    rec_c = lax.ppermute(pay_c, "gy", flip(ny, 1))
    rec_d = lax.ppermute(pay_d, "gy", odd_pairs(ny))

    def stencil(start):
        return call(lambda *refs: stencil_body(start, *refs), [(3, CX // 2, CY, CZ)], 1, "stencil")(velocity)[0]

    rec_c, base_low = after(rec_c, stencil(0))
    two = join([block, rec_c[FACE_Y:]])
    beside = swap(two)
    cells, beside = after(host_cell, beside)
    sampled = lambda: call(sample_body, [(HOST, CZ)], 3, "sample", vmem=24)(velocity, cells, host_frac)[0]
    table, pieces = list(gather_y(two, sampled))
    pieces = pieces + [beside] + [swap(p) for p in pieces[1:]]
    n_rows = 2 * ny * ROWS
    pair = (2 * ROWS, CZ)
    pay_a, pay_b, blocks, *across = call(
        lambda *refs: xpack_body(len(pieces), *refs),
        [(FACE_X, CZ), (FACE_X + 2 * ROWS, CZ), pair, pair, pair] if ring else [(FACE_X, CZ), (FACE_X, CZ), (n_rows, CZ)],
        3 + len(pieces),
        "xpack",
    )(x_faces, rec_c, rec_d, *pieces)
    face_b = lax.ppermute(pay_b, "gx", odd_pairs(nx, ring))
    from_x = across_x(across) if ring else gather_x(blocks)
    face_a = swap(pay_a)
    (face_a, face_b), base_high = after((face_a, face_b), stencil(CX // 2))
    samp, sel, pts = call(
        lambda *refs: select_body(len(from_x), *refs),
        [(8, PTS), (2 * ROWS, CZ), (PTS, CZ)],
        6 + len(from_x),
        "select",
    )(table, face_a, face_b, rec_c, rec_d, blocks, *from_x)
    other = swap(samp)
    gx, gy, pz = call(weights_body, [(YROWS, PTS), (CY + 8, PTS), (PTS, CZ)], 1, "weights")(pts)
    lines, pay_c, pay_d, ret, xrim = call(
        loads_body,
        [(PTS, 3 * CZ), (RIM_Y, CZ), (RIM_Y, CZ), (2 * BACK, CZ), (2 * RIM_X, CZ)],
        7,
        "loads",
    )(samp, other, sel, pts, gx, gy, pz)
    ret_c = lax.ppermute(ret, "gy", flip(ny, 1))
    rim_c = lax.ppermute(pay_c, "gy", flip(ny, 1))
    rim_d = lax.ppermute(pay_d, "gy", odd_pairs(ny))

    def spread(start, base):
        return call(
            lambda *refs: spread_body(start, *refs), [(3, CX // 2, CY, CZ)], 4, "spread"
        )(lines, gx, gy, base)[0]

    ret_c, main_low = after(ret_c, spread(0, base_low))
    main_high, pieces = list(gather_y(join([ret, ret_c]), lambda: spread(CX // 2, base_high)))
    rim_c, main_high = after(rim_c, main_high)
    n_rows = 2 * ny * BACK
    pair = (2 * BACK, CZ)
    pay_a, pay_b, back, *across = call(
        lambda *refs: rimpack_body(len(pieces), *refs),
        [(RIM_X, CZ), (RIM_X + 2 * BACK, CZ), (n_rows, CZ), pair, pair] if ring else [(RIM_X, CZ), (RIM_X, CZ), (n_rows, CZ)],
        3 + len(pieces),
        "rimpack",
    )(xrim, rim_c, rim_d, *pieces)
    rim_b = lax.ppermute(pay_b, "gx", odd_pairs(nx, ring))
    rets = across_x(across) if ring else gather_x(back)
    rim_a = swap(pay_a)
    inside = call(
        inside_body,
        [velocity.shape],
        7,
        "inside",
        scratch=[pltpu.VMEM((3, CX - 2 * CHUNK, CY, CZ), F32), dma((N_CHUNK - 2,))],
        out_specs=[HB],
        vmem=16,
    )(main_low, main_high, y_faces, rec_c, rec_d, rim_c, rim_d)[0]
    (rim_a, rim_b), inside = after((rim_a, rim_b), inside)
    return tuple(
        call(
            lambda *refs: final_body(len(rets), *refs),
            [velocity.shape, (3, P_SIZE)],
            14 + len(rets),
            "final",
            scratch=[pltpu.VMEM((3, 2 * CHUNK, CY, CZ), F32), dma((2,))],
            first=HB,
            out_specs=[HB, VM],
            aliases={0: 0},
        )(inside, main_low, main_high, x_faces, y_faces, face_a, face_b, rec_c, rec_d, rim_a, rim_b, rim_c, rim_d, back, *rets)
    )


def solution(mesh):
    return jax.shard_map(
        per_device,
        mesh=mesh,
        in_specs=(
            P(None, "gx", "gy", None),
            P(None, ("gx", "gy")),
            P(None, ("gx", "gy")),
            P(("gx", "gy")),
            P(("gx", "gy")),
            P(("gx", "gy")),
            P(("gx", "gy")),
            P(("gx", "gy")),
            P(("gx", "gy")),
            P(("gx", "gy")),
        ),
        out_specs=(P(None, "gx", "gy", None), P(None, ("gx", "gy"))),
        check_vma=False,
    )
```

```python
import math

import jax
import jax.numpy as jnp
from jax import lax
from jax.experimental import pallas as pl
from jax.experimental.pallas import tpu as pltpu
from jax.sharding import PartitionSpec as P

CX = 64
CY = 32
CZ = 128
P_SIZE = 256
HOST = 512
PTS = 2 * P_SIZE

DT_STEP = 0.2
NU_VISC = 0.5
EPS_SQ = 1.44
CORE_SQ = 0.01

ROWS = 16
BACK = 8
YROWS = 72
XROWS = 40
FACE_Y = 3 * CX
FACE_X = 3 * XROWS
RIM_Y = 2 * 3 * YROWS
RIM_X = 2 * 3 * CY
CHUNK = 8
N_CHUNK = CX // CHUNK

F32 = jnp.float32
BF16 = jnp.bfloat16
VM = pl.BlockSpec(memory_space=pltpu.MemorySpace.VMEM)
SM = pl.BlockSpec(memory_space=pltpu.MemorySpace.SMEM)
HB = pl.BlockSpec(memory_space=pltpu.MemorySpace.HBM)
MIB = 1024 * 1024


def call(body, outs, n_in, name, scratch=(), first=VM, second=VM, out_specs=None, in_specs=None, vmem=12, aliases=None):
    return pl.pallas_call(
        body,
        out_shape=[jax.ShapeDtypeStruct(s, F32) for s in outs],
        in_specs=in_specs or ([first, second] + [VM] * n_in)[:n_in],
        out_specs=out_specs or [VM] * len(outs),
        scratch_shapes=list(scratch),
        input_output_aliases=aliases or {},
        compiler_params=pltpu.CompilerParams(vmem_limit_bytes=vmem * MIB),
        name=name,
    )


def place():
    nx, ny = lax.axis_size("gx"), lax.axis_size("gy")
    ix, iy = lax.axis_index("gx"), lax.axis_index("gy")
    px, py = lax.rem(ix, 2), lax.rem(iy, 2)
    inner = (ix + px > 0) & (ix + px < nx)
    return px == 0, py == 0, inner, ix * ny + iy, (ix - px) * ny + iy, ny


def split(value):
    high = value.astype(BF16)
    low = (value - high.astype(F32)).astype(BF16)
    return high, low


def dot3(a_high, a_low, b_high, b_low):
    def one(a, b):
        return jnp.dot(a, b, preferred_element_type=F32)

    return one(a_high, b_high) + (one(a_high, b_low) + one(a_low, b_high))


def reduce_list(items, op):
    result = items[0]
    for item in items[1:]:
        result = op(result, item)
    return result


def pack_body(v_ref, spin_hbm, *rest):
    params, (pay_c, pay_d, blk_ref, held, held_int, spin_ref, sems) = rest[:5], rest[5:]
    _, even_y, _, brick, _, _ = place()

    def faces(first, second):
        made = []
        for k, (ref, y) in enumerate(((pay_c, first), (pay_d, second))):
            for c in range(3):
                made.append(pltpu.make_async_copy(v_ref.at[c, :, y], ref.at[pl.ds(c * CX, CX)], sems.at[3 * k + c]))
        return made

    @pl.when(even_y)
    def _():
        for copy in faces(CY - 1, 0):
            copy.start()

    @pl.when(jnp.logical_not(even_y))
    def _():
        for copy in faces(0, CY - 1):
            copy.start()

    small = [pltpu.make_async_copy(spin_hbm, spin_ref, sems.at[6])]
    small += [pltpu.make_async_copy(p, held.at[k], sems.at[7 + k]) for k, p in enumerate(params[:4])]
    small.append(pltpu.make_async_copy(params[4], held_int, sems.at[11]))
    for copy in small:
        copy.start()
    for copy in small:
        copy.wait()
    radius, chord, twist, angle = [held[k] for k in range(4)]
    parts = [
        radius,
        chord,
        jnp.cos(twist),
        jnp.sin(twist),
        jnp.cos(angle),
        jnp.sin(angle),
        held_int[...].astype(F32),
        jnp.full((1, CZ), spin_ref[0], F32),
        jnp.full((1, CZ), brick.astype(F32), F32),
    ]
    block = jnp.concatenate(parts, axis=0)
    blk_ref[...] = block
    pay_c[FACE_Y:] = block
    for copy in faces(0, 0):
        copy.wait()


def stencil_body(start, v_ref, out_ref):
    row = lax.broadcasted_iota(jnp.int32, (CY, CZ), 0)
    lane = lax.broadcasted_iota(jnp.int32, (CY, CZ), 1)
    half = 0.5 * DT_STEP
    visc = DT_STEP * NU_VISC
    not_last_y, not_first_y = row < CY - 1, row > 0
    not_last_z, not_first_z = lane < CZ - 1, lane > 0

    def step(k, carry):
        x = start + k
        up = jnp.minimum(x + 1, CX - 1)
        down = jnp.maximum(x - 1, 0)
        v0, v1, v2 = v_ref[0, x], v_ref[1, x], v_ref[2, x]
        a_x = jnp.where(x < CX - 1, visc - half * v0, 0.0)
        b_x = jnp.where(x > 0, visc + half * v0, 0.0)
        a_y = jnp.where(not_last_y, visc - half * v1, 0.0)
        b_y = jnp.where(not_first_y, visc + half * v1, 0.0)
        a_z = jnp.where(not_last_z, visc - half * v2, 0.0)
        b_z = jnp.where(not_first_z, visc + half * v2, 0.0)
        for c in range(3):
            mid = (v0, v1, v2)[c]
            along_x = a_x * v_ref[c, up] + b_x * v_ref[c, down]
            along_y = a_y * pltpu.roll(mid, CY - 1, 0) + b_y * pltpu.roll(mid, 1, 0)
            along_z = a_z * pltpu.roll(mid, CZ - 1, 1) + b_z * pltpu.roll(mid, 1, 1)
            out_ref[c, k] = (1.0 - 6.0 * visc) * mid + along_x + (along_y + along_z)
        return carry

    lax.fori_loop(0, CX // 2, step, 0, unroll=2)


def weight(coord, base, frac):
    return jnp.where(coord == base, 1.0 - frac, jnp.where(coord == base + 1, frac, 0.0))


def sample_body(v_ref, cell_ref, frac_ref, tab_ref, x_ref, y_ref):
    for c in range(3):
        x_ref[c] = v_ref[c, 0]
        x_ref[c + 3] = v_ref[c, CX - 1]
    y_ref[0] = v_ref[1, :, 0, :]
    y_ref[1] = v_ref[1, :, CY - 1, :]
    rows = jnp.concatenate([cell_ref[...].astype(F32), frac_ref[...], jnp.zeros((CZ - 6, HOST), F32)], axis=0)
    turned = rows.T
    x_col, y_col, z_col = [turned[:, k : k + 1].astype(jnp.int32) for k in range(3)]
    fx, fy, fz = [turned[:, k : k + 1] for k in range(3, 6)]
    lane = lax.broadcasted_iota(jnp.int32, (HOST, CZ), 1)
    wy = weight(lane % CY, y_col, fy)
    x_lane = lane // CY - x_col
    acc = None
    per = 4
    nx = CZ * per // CY
    for j in range(CX // nx):
        parts = []
        for i in range(per):
            shift = (CZ // CY) * (j * per + i)
            wx = jnp.where(x_lane == -shift, 1.0 - fx, jnp.where(x_lane == 1 - shift, fx, 0.0))
            parts.append(wx * wy)
        w_high, w_low = split(jnp.concatenate(parts, axis=1))
        field = [v_ref[c, j * nx : (j + 1) * nx].reshape(nx * CY, CZ) for c in range(3)]
        f_high, f_low = split(jnp.concatenate(field, axis=1))
        part = dot3(w_high, w_low, f_high, f_low)
        acc = part if acc is None else acc + part
    wz = weight(lane, z_col, fz)
    out = turned
    for c in range(3):
        value = jnp.sum(acc[:, c * CZ : (c + 1) * CZ] * wz, axis=1, keepdims=True)
        out = jnp.where(lane == 6 + c, value, out)
    tab_ref[...] = out


def split_blocks(sources):
    return [
        ref[first + k * ROWS : first + (k + 1) * ROWS]
        for ref, first in sources
        for k in range((ref.shape[0] - first) // ROWS)
    ]


def pick_pair(values, b0, ny):
    keys = [value[12:13, 0:1] for value in values]
    members = []
    for key in keys:
        home = jnp.floor(key * (1.0 / HOST)).astype(jnp.int32)
        members.append((home == b0) | (home == b0 + ny))
    low_key = reduce_list([jnp.where(m, k, 1e9) for k, m in zip(keys, members)], jnp.minimum)
    high_key = reduce_list([jnp.where(m, k, -9.0) for k, m in zip(keys, members)], jnp.maximum)
    low = jnp.full((ROWS, CZ), -1.0, F32)
    high = low
    for key, value in zip(keys, values):
        low = jnp.where(key == low_key, value, low)
        high = jnp.where(key == high_key, value, high)
    return low, high


def xpack_body(n_blk, x_ref, rec_c, rec_d, *rest):
    pieces, (pay_a, pay_b, own_ref, *others) = rest[:n_blk], rest[n_blk:]
    even_x, even_y, inner, _, b0, ny = place()
    for c in range(3):
        at = c * CX
        y_high = jnp.where(even_y, rec_c[at : at + 1], rec_d[at : at + 1])
        tail = jnp.concatenate([y_high, jnp.zeros((XROWS - CY - 1, CZ), F32)], axis=0)
        low, high = x_ref[c], x_ref[c + 3]
        at = c * XROWS
        pay_a[at : at + CY] = jnp.where(even_x, high, low)
        pay_b[at : at + CY] = jnp.where(even_x, low, high)
        pay_a[at + CY : at + XROWS] = tail
        pay_b[at + CY : at + XROWS] = tail
    if not others:
        own_ref[...] = jnp.concatenate([p[...] for p in pieces], axis=0)
        return
    values = split_blocks([(p, 0) for p in pieces])
    chips = ny * 2
    side = jnp.where(even_x, -chips, chips)
    total = lax.axis_size("gx") * ny
    own_ref[...] = jnp.concatenate(pick_pair(values, b0, ny), axis=0)
    beside = jnp.concatenate(pick_pair(values, lax.rem(b0 + side + total, total), ny), axis=0)
    pay_b[FACE_X:] = beside
    others[1][...] = beside
    others[0][...] = jnp.concatenate(pick_pair(values, lax.rem(b0 + 2 * chips, total), ny), axis=0)


def select_body(n_blk, tab_ref, face_a, face_b, rec_c, rec_d, blk_ref, *rest):
    others, (samp_ref, sel_ref, pts_ref) = rest[:n_blk], rest[n_blk:]
    even_x, even_y, inner, brick, b0, ny = place()
    sources = [(blk_ref, 0), (face_b, FACE_X)] + [(o, 0) for o in others]
    turbine_a, turbine_b = pick_pair(split_blocks(sources), b0, ny)
    sel = jnp.concatenate([turbine_a, turbine_b], axis=0)
    sel_ref[...] = sel
    turned = jnp.concatenate([sel, jnp.zeros((CZ - 2 * ROWS, CZ), F32)], axis=0).T

    def column(k):
        picks = (2 * k, 2 * k + 1, ROWS + 2 * k, ROWS + 2 * k + 1)
        return jnp.concatenate([turned[:, j : j + 1] for j in picks], axis=0)

    table = tab_ref[...]
    lane = lax.broadcasted_iota(jnp.int32, (PTS, CZ), 1)
    x_col, y_col, z_col = [table[:, k : k + 1].astype(jnp.int32) for k in range(3)]
    fx, fy, fz = [table[:, k : k + 1] for k in range(3, 6)]
    on_line = lane >= CX
    edge_x = jnp.where(on_line, lane - CX, CX)
    edge_y = jnp.where(on_line, CY, lane)
    edge_w = jnp.where(on_line | (lane <= CY), weight(edge_x, x_col, fx) * weight(edge_y, y_col, fy), 0.0)
    field = []
    for c in range(3):
        at = c * XROWS
        past = jnp.where(inner, face_b[at : at + XROWS], 0.0)
        plane = jnp.where(even_x, face_a[at : at + XROWS], past)
        at = c * CX
        line = jnp.where(even_y, rec_c[at : at + CX], rec_d[at : at + CX])
        field.append(jnp.concatenate([plane, jnp.zeros((CX - XROWS, CZ), F32), line], axis=0))
    w_high, w_low = split(edge_w)
    f_high, f_low = split(jnp.concatenate(field, axis=1))
    acc = dot3(w_high, w_low, f_high, f_low)
    wz = weight(lane, z_col, fz)
    for c in range(3):
        value = jnp.sum(acc[:, c * CZ : (c + 1) * CZ] * wz, axis=1, keepdims=True)
        table = table + jnp.where(lane == 6 + c, value, 0.0)
    slot = column(6).astype(jnp.int32)
    mine = (slot // HOST) == brick
    local = jnp.where(mine, slot % HOST, -1)
    hit = (lax.broadcasted_iota(jnp.int32, (PTS, HOST), 1) == local).astype(F32).astype(BF16)
    first, second = split(table)
    third = (table - first.astype(F32) - second.astype(F32)).astype(BF16)
    pulled = [jnp.dot(hit, part, preferred_element_type=F32) for part in (first, second, third)]
    points = pulled[0] + pulled[1] + pulled[2]
    points = jnp.where(lane == 9, column(0), points)
    pts_ref[...] = jnp.where((lane == 0) & jnp.logical_not(mine), -100.0, points)
    samp_ref[...] = points.T[6:14]


def offsets(frac):
    raw = [jnp.exp(-((o - frac) ** 2) / EPS_SQ) for o in (-1.0, 0.0, 1.0, 2.0)]
    total = (raw[0] + raw[1]) + (raw[2] + raw[3])
    return [value / total for value in raw]


def profile(rows, inner, base, frac):
    index = lax.broadcasted_iota(jnp.int32, (rows, PTS), 0)
    late = index - inner
    index = jnp.where(index < inner, index, jnp.where(late < 2, late - 2, late - 2 + inner))
    rel = index - base.astype(jnp.int32)
    result = jnp.zeros((rows, PTS), F32)
    for k, w in enumerate(offsets(frac)):
        result = jnp.where(rel == k - 1, w, result)
    return result


def line_profile(base, frac, extra):
    stack = jnp.concatenate(offsets(frac) + [base] + extra + [jnp.zeros((CZ - 5 - len(extra), PTS), F32)], axis=0).T
    rel = lax.broadcasted_iota(jnp.int32, (PTS, CZ), 1) - stack[:, 4:5].astype(jnp.int32)
    result = jnp.zeros((PTS, CZ), F32)
    for k in range(4):
        result = jnp.where(rel == k - 1, stack[:, k : k + 1], result)
    return result, [stack[:, 5 + k : 6 + k] for k in range(len(extra))]


def weights_body(pts_ref, gx_ref, gy_ref, pz_ref, pos_ref):
    table = pts_ref[...].T
    gx_ref[...] = profile(YROWS, CX, table[0:1], table[3:4])
    gy_ref[...] = profile(CY, CY, table[1:2], table[4:5])
    pz_ref[...] = line_profile(table[2:3], table[5:6], [])[0]
    pos_ref[...] = jnp.concatenate([table[q : q + 1, k * CZ : (k + 1) * CZ] for q in range(6) for k in range(4)], axis=0)


def attack(axial_flow, tangent, cos_twist, sin_twist):
    rel_speed = jnp.sqrt(axial_flow * axial_flow + tangent * tangent + 1.0)
    cos_phi = tangent / rel_speed
    sin_phi = axial_flow / rel_speed
    sin_alpha = sin_phi * cos_twist - cos_phi * sin_twist
    cos_alpha = cos_phi * cos_twist + sin_phi * sin_twist
    lift_coef = 2.0 * jnp.pi * sin_alpha * cos_alpha / (1.0 + 4.0 * sin_alpha * sin_alpha)
    drag_coef = 0.02 + 0.8 * sin_alpha * sin_alpha
    return rel_speed, cos_phi, sin_phi, lift_coef, drag_coef


def loads_body(samp_ref, other_ref, sel_ref, pts_ref, gx_ref, gy_ref, pz_ref, pos_ref, lh_ref, pay_ref, xrim_ref):
    def row(k):
        picks = (2 * k, 2 * k + 1, ROWS + 2 * k, ROWS + 2 * k + 1)
        return jnp.concatenate([sel_ref[j : j + 1] for j in picks], axis=1)

    radius, chord, cos_t, sin_t, cos_a, sin_a = [row(k) for k in range(6)]
    spin = radius * jnp.concatenate([sel_ref[j : j + 1] for j in (14, 14, ROWS + 14, ROWS + 14)], axis=1)
    flow = samp_ref[...] + other_ref[...]
    axial = flow[0:1]
    tangent = spin - (cos_a * flow[2:3] - sin_a * flow[1:2])
    rel_speed, cos_phi, sin_phi, lift_coef, drag_coef = attack(axial, tangent, cos_t, sin_t)
    circ = 0.5 * chord * rel_speed * lift_coef
    parts = []
    for t in range(2):
        seg = slice(t * P_SIZE, (t + 1) * P_SIZE)
        spacing = radius[:, seg] - pts_ref[seg, 9:10]
        kernel = spacing / (spacing * spacing + CORE_SQ)
        lhs = jnp.concatenate([cos_a[:, seg] * circ[:, seg], sin_a[:, seg] * circ[:, seg], jnp.zeros((6, P_SIZE), F32)], axis=0)
        both = jnp.dot(lhs, kernel, preferred_element_type=F32, precision=lax.Precision.HIGHEST)
        parts.append((cos_a[:, seg] * both[0:1] + sin_a[:, seg] * both[1:2]) / (4.0 * math.pi))
    induced = jnp.concatenate(parts, axis=1)
    rel_speed, cos_phi, sin_phi, lift_coef, drag_coef = attack(axial + induced, tangent, cos_t, sin_t)
    dynamic = 0.5 * chord * rel_speed * rel_speed
    lift = dynamic * lift_coef
    drag = dynamic * drag_coef
    thrust = lift * cos_phi + drag * sin_phi
    torque = lift * sin_phi - drag * cos_phi
    force = [-thrust, torque * sin_a, -torque * cos_a]
    pieces = []
    for t in range(2):
        for c in range(3):
            for h in range(2):
                at = t * P_SIZE + h * CZ
                pieces.append(force[c][:, at : at + CZ])
        pieces += [sel_ref[t * ROWS + 15 : t * ROWS + 16]] * 2
    blocks = jnp.concatenate(pieces, axis=0)
    pay_ref[0 : 2 * BACK] = blocks
    pay_ref[2 * BACK :] = pos_ref[...]
    cols = jnp.concatenate(force + [jnp.zeros((CZ - 3, PTS), F32)], axis=0).T
    pz = pz_ref[...] * DT_STEP
    lines = jnp.concatenate([cols[:, c : c + 1] * pz for c in range(3)], axis=1)
    l_high, l_low = split(lines)
    lh_ref[...] = lines
    gx = gx_ref[...]
    gy = gy_ref[...]
    planes = [gx[CX + k : CX + k + 1] * gy for k in range(4)]
    w_high, w_low = split(jnp.concatenate(planes, axis=0))
    rim = dot3(w_high, w_low, l_high, l_low)
    for k in range(4):
        for c in range(3):
            at = (k * 3 + c) * CY
            xrim_ref[at : at + CY] = rim[k * CY : (k + 1) * CY, c * CZ : (c + 1) * CZ]


def near_body(rec_c, rec_d, low_ref, high_ref):
    _, even_y, _, _, _, _ = place()
    c_all, d_all = rec_c[...], rec_d[...]
    for side, out_ref in ((0, low_ref), (1, high_ref)):
        got = jnp.where(even_y, d_all, c_all) if side == 0 else jnp.where(even_y, c_all, d_all)

        def wide(first, picks):
            return jnp.concatenate([got[first + j : first + j + 1] for j in picks], axis=1)

        x, y, z, fx, fy, fz = [wide(2 * BACK + 4 * q, range(4)) for q in range(6)]
        force = [wide(2 * c, (0, 1, BACK, BACK + 1)) * DT_STEP for c in range(3)]
        pz, columns = line_profile(z, fz, force)
        l_high, l_low = split(jnp.concatenate([col * pz for col in columns], axis=1))
        gx = profile(YROWS, CX, x, fx)
        wy = offsets(fy)
        planes = []
        for i in range(2):
            rel = (CY + i if side == 0 else i - 2) - y.astype(jnp.int32)
            gy = jnp.zeros((1, PTS), F32)
            for k in range(4):
                gy = jnp.where(rel == k - 1, wy[k], gy)
            planes.append(gx * gy)
        w_high, w_low = split(jnp.concatenate(planes, axis=0))
        rim = dot3(w_high, w_low, l_high, l_low)
        for i in range(2):
            for c in range(3):
                at = (i * 3 + c) * YROWS
                out_ref[at : at + YROWS] = rim[i * YROWS : (i + 1) * YROWS, c * CZ : (c + 1) * CZ]


SPREAD_X = 8


def spread_body(start, lines_ref, gx_ref, gy_ref, base_ref, out_ref):
    l_high, l_low = split(lines_ref[...])
    gy = gy_ref[0:CY]
    for k in range(out_ref.shape[1] // SPREAD_X):
        at = k * SPREAD_X
        first = start + at
        planes = jnp.concatenate([gx_ref[first + i : first + i + 1] * gy for i in range(SPREAD_X)], axis=0)
        w_high, w_low = split(planes)
        value = dot3(w_high, w_low, l_high, l_low)
        for c in range(3):
            part = value[:, c * CZ : (c + 1) * CZ].reshape(SPREAD_X, CY, CZ)
            out_ref[c, at : at + SPREAD_X] = base_ref[c, at : at + SPREAD_X] + part


def rimpack_body(n_blk, xrim_ref, low_ref, high_ref, *rest):
    pieces, (pay_a, pay_b, back_ref, *others) = rest[:n_blk], rest[n_blk:]
    even_x, even_y, inner, _, b0, ny = place()
    zero = jnp.zeros((CY - 4, CZ), F32)
    for k in range(2):
        for c in range(3):
            sides = []
            for s in range(2):
                near, far = [], []
                for y in range(2):
                    at = (y * 3 + c) * YROWS + CX + 2 * s + k
                    near.append(low_ref[at : at + 1])
                    far.append(high_ref[at : at + 1])
                at = ((2 * s + k) * 3 + c) * CY
                sides.append(xrim_ref[at : at + CY] + jnp.concatenate(near + [zero] + far, axis=0))
            at = (k * 3 + c) * CY
            pay_a[at : at + CY] = jnp.where(even_x, sides[1], sides[0])
            pay_b[at : at + CY] = jnp.where(even_x, sides[0], sides[1])
    back = jnp.concatenate([p[...] for p in pieces], axis=0)
    back_ref[...] = back
    if others:
        chips = ny * 2
        side = jnp.where(even_x, -chips, chips)
        total = lax.axis_size("gx") * ny
        for ref, at, target in (
            (pay_b, RIM_X, lax.rem(b0 + side + total, total)),
            (others[0], 0, lax.rem(b0 + 2 * chips, total)),
        ):
            for core in range(2):
                wanted = (target + core * ny).astype(F32)
                found = jnp.full((BACK, CZ), -1.0, F32)
                for k in range(back.shape[0] // BACK):
                    value = back[k * BACK : (k + 1) * BACK]
                    found = jnp.where(value[6:7, 0:1] == wanted, value, found)
                ref[at + core * BACK : at + (core + 1) * BACK] = found
        others[1][...] = pay_b[RIM_X:]


def face_terms(buf, at, first, main_low, main_high, y_ref, rec_c, rec_d, rim_low, rim_high, even_y):
    half = 0.5 * DT_STEP
    visc = DT_STEP * NU_VISC
    part = slice(first, first + CHUNK)
    here = slice(at, at + CHUNK)
    half_of = main_low if first < CX // 2 else main_high
    inner = first % (CX // 2)
    for c in range(3):
        buf[c, here] = half_of[c, inner : inner + CHUNK]
        rows = slice(c * CX + first, c * CX + first + CHUNK)
        a, b = rec_c[rows], rec_d[rows]
        low = [jnp.where(even_y, b, a) * (visc + half * y_ref[0, part]), 0.0]
        high = [0.0, jnp.where(even_y, a, b) * (visc - half * y_ref[1, part])]
        for i in range(2):
            row = (i * 3 + c) * YROWS + first
            buf[c, here, i, :] += rim_low[row : row + CHUNK] + low[i]
            buf[c, here, CY - 2 + i, :] += rim_high[row : row + CHUNK] + high[i]


def chunk_copy(buf, at, out_ref, first, sem):
    return pltpu.make_async_copy(buf.at[:, pl.ds(at, CHUNK)], out_ref.at[:, pl.ds(first, CHUNK)], sem)


def inside_body(main_low, main_high, y_ref, rec_c, rec_d, rim_low, rim_high, out_ref, buf, sems):
    _, even_y, _, _, _, _ = place()
    copies = []
    for k in range(N_CHUNK - 2):
        first = (k + 1) * CHUNK
        face_terms(buf, k * CHUNK, first, main_low, main_high, y_ref, rec_c, rec_d, rim_low, rim_high, even_y)
        copies.append(chunk_copy(buf, k * CHUNK, out_ref, first, sems.at[k]))
        copies[-1].start()
    for copy in copies:
        copy.wait()


def final_body(n_ret, _, main_low, main_high, x_ref, y_ref, face_a, face_b, rec_c, rec_d, rim_a, rim_b, rim_low, rim_high, back_ref, *rest):
    rets, (out_ref, pf_ref, buf, sems) = rest[:n_ret], rest[n_ret:]
    even_x, even_y, inner, brick, _, _ = place()
    half = 0.5 * DT_STEP
    visc = DT_STEP * NU_VISC
    copies = []
    for k in range(2):
        first, at = k * (CX - CHUNK), k * CHUNK
        face_terms(buf, at, first, main_low, main_high, y_ref, rec_c, rec_d, rim_low, rim_high, even_y)
        for c in range(3):
            a = face_a[c * XROWS : c * XROWS + CY]
            b = jnp.where(inner, face_b[c * XROWS : c * XROWS + CY], 0.0)
            if k == 0:
                buf[c, 0] += jnp.where(even_x, b, a) * (visc + half * x_ref[0])
            else:
                buf[c, 2 * CHUNK - 1] += jnp.where(even_x, a, b) * (visc - half * x_ref[3])
            for i in range(2):
                rows = slice((i * 3 + c) * CY, (i * 3 + c + 1) * CY)
                a, b = rim_a[rows], jnp.where(inner, rim_b[rows], 0.0)
                if k == 0:
                    buf[c, i] += jnp.where(even_x, b, a)
                else:
                    buf[c, 2 * CHUNK - 2 + i] += jnp.where(even_x, a, b)
        copies.append(chunk_copy(buf, at, out_ref, first, sems.at[k]))
        copies[-1].start()
    mine = brick.astype(F32)
    found = jnp.zeros((BACK, CZ), F32)
    for ref, first in [(back_ref, 0), (rim_b, RIM_X)] + [(r, 0) for r in rets]:
        for k in range((ref.shape[0] - first) // BACK):
            value = ref[first + BACK * k : first + BACK * k + BACK]
            found = jnp.where(value[6:7, 0:1] == mine, value, found)
    for c in range(3):
        pf_ref[c : c + 1] = jnp.concatenate([found[2 * c : 2 * c + 1], found[2 * c + 1 : 2 * c + 2]], axis=1)
    for copy in copies:
        copy.wait()


def per_device(
    velocity,
    host_cell,
    host_frac,
    host_dst,
    owner_src,
    rotor_speed,
    blade_radius,
    blade_chord,
    blade_twist,
    blade_angle,
):
    nx, ny = lax.axis_size("gx"), lax.axis_size("gy")
    ring = nx == 8

    def flip(n, bits):
        return [(i, i ^ bits) for i in range(n)]

    def odd_pairs(n, closed=False):
        up = [(i, (i + 1) % n) for i in range(1, n if closed else n - 1, 2)]
        return up + [(t, s) for s, t in up]

    def same_side(n):
        return [(i, (i + (2 if i % 2 else n - 2)) % n) for i in range(n)]

    def across_x(blocks):
        return [lax.ppermute(b, "gx", p) for b, p in zip(blocks, (flip(nx, 4), same_side(nx)))]

    def swap(block):
        return lax.ppermute(block, "gx", flip(nx, 1))

    def join(pieces):
        return pieces[0] if len(pieces) == 1 else jnp.concatenate(pieces, axis=0)

    def after(values, other):
        return lax.optimization_barrier((values, other))

    def gather_y(first, filler):
        pieces = [first]
        for bit in [b for b in (2, 4, 8) if b < ny]:
            got = lax.ppermute(join(pieces), "gy", flip(ny, bit))
            if filler is not None:
                got, filler = after(got, filler())
                yield filler
                filler = None
            pieces.append(got)
        yield pieces

    def gather_x(blocks):
        pieces = []
        for bit in [b for b in (2, 4, 8, 16) if b < nx]:
            pieces.append(lax.ppermute(join([blocks] + pieces), "gx", flip(nx, bit)))
        return pieces

    dma = pltpu.SemaphoreType.DMA
    pay_c, pay_d, block = call(
        pack_body,
        [(FACE_Y + ROWS, CZ), (FACE_Y, CZ), (ROWS, CZ)],
        7,
        "pack",
        scratch=[pltpu.VMEM((4, 2, CZ), F32), pltpu.VMEM((2, CZ), jnp.int32), pltpu.SMEM((1,), F32), dma((12,))],
        in_specs=[HB] * 7,
        vmem=56,
    )(velocity, rotor_speed, *[a.reshape(2, CZ) for a in (blade_radius, blade_chord, blade_twist, blade_angle, owner_src)])
    rec_c = lax.ppermute(pay_c, "gy", flip(ny, 1))
    rec_d = lax.ppermute(pay_d, "gy", odd_pairs(ny))

    def stencil(start):
        return call(lambda *refs: stencil_body(start, *refs), [(3, CX // 2, CY, CZ)], 1, "stencil")(velocity)[0]

    rec_c, base_low = after(rec_c, stencil(0))
    two = join([block, rec_c[FACE_Y:]])
    beside = swap(two)
    cells, beside = after(host_cell, beside)
    sampled = lambda: call(sample_body, [(HOST, CZ), (6, CY, CZ), (2, CX, CZ)], 3, "sample", vmem=24)(velocity, cells, host_frac)
    (table, x_faces, y_faces), pieces = list(gather_y(two, sampled))
    pieces = pieces + [beside] + [swap(p) for p in pieces[1:]]
    n_rows = 2 * ny * ROWS
    pair = (2 * ROWS, CZ)
    pay_a, pay_b, blocks, *across = call(
        lambda *refs: xpack_body(len(pieces), *refs),
        [(FACE_X, CZ), (FACE_X + 2 * ROWS, CZ), pair, pair, pair] if ring else [(FACE_X, CZ), (FACE_X, CZ), (n_rows, CZ)],
        3 + len(pieces),
        "xpack",
    )(x_faces, rec_c, rec_d, *pieces)
    face_b = lax.ppermute(pay_b, "gx", odd_pairs(nx, ring))
    from_x = across_x(across) if ring else gather_x(blocks)
    face_a = swap(pay_a)
    (face_a, face_b), base_high = after((face_a, face_b), stencil(CX // 2))
    samp, sel, pts = call(
        lambda *refs: select_body(len(from_x), *refs),
        [(8, PTS), (2 * ROWS, CZ), (PTS, CZ)],
        6 + len(from_x),
        "select",
    )(table, face_a, face_b, rec_c, rec_d, blocks, *from_x)
    other = swap(samp)
    gx, gy, pz, pos = call(weights_body, [(YROWS, PTS), (CY, PTS), (PTS, CZ), (24, CZ)], 1, "weights")(pts)
    lines, points, xrim = call(
        loads_body,
        [(PTS, 3 * CZ), (2 * BACK + 24, CZ), (2 * RIM_X, CZ)],
        8,
        "loads",
    )(samp, other, sel, pts, gx, gy, pz, pos)
    near_d = lax.ppermute(points, "gy", odd_pairs(ny))
    near_c = lax.ppermute(points, "gy", flip(ny, 1))

    def spread(start, base):
        return call(
            lambda *refs: spread_body(start, *refs), [(3, CX // 2, CY, CZ)], 4, "spread"
        )(lines, gx, gy, base)[0]

    (near_c, near_d), main_low = after((near_c, near_d), spread(0, base_low))
    nearby = lambda: call(near_body, [(RIM_Y, CZ)] * 2, 2, "near")(near_c, near_d)
    (rim_low, rim_high), pieces = list(gather_y(join([points[: 2 * BACK], near_c[: 2 * BACK]]), nearby))
    n_rows = 2 * ny * BACK
    pair = (2 * BACK, CZ)
    pay_a, pay_b, back, *across = call(
        lambda *refs: rimpack_body(len(pieces), *refs),
        [(RIM_X, CZ), (RIM_X + 2 * BACK, CZ), (n_rows, CZ), pair, pair] if ring else [(RIM_X, CZ), (RIM_X, CZ), (n_rows, CZ)],
        3 + len(pieces),
        "rimpack",
    )(xrim, rim_low, rim_high, *pieces)
    rim_b = lax.ppermute(pay_b, "gx", odd_pairs(nx, ring))
    rets = across_x(across) if ring else gather_x(back)
    rim_a = swap(pay_a)
    main_high = spread(CX // 2, base_high)
    (main_low, main_high) = lax.optimization_barrier((main_low, main_high))
    inside = call(
        inside_body,
        [velocity.shape],
        7,
        "inside",
        scratch=[pltpu.VMEM((3, CX - 2 * CHUNK, CY, CZ), F32), dma((N_CHUNK - 2,))],
        out_specs=[HB],
        vmem=16,
    )(main_low, main_high, y_faces, rec_c, rec_d, rim_low, rim_high)[0]
    (rim_a, rim_b), inside = after((rim_a, rim_b), inside)
    return tuple(
        call(
            lambda *refs: final_body(len(rets), *refs),
            [velocity.shape, (3, P_SIZE)],
            14 + len(rets),
            "final",
            scratch=[pltpu.VMEM((3, 2 * CHUNK, CY, CZ), F32), dma((2,))],
            first=HB,
            out_specs=[HB, VM],
            aliases={0: 0},
        )(inside, main_low, main_high, x_faces, y_faces, face_a, face_b, rec_c, rec_d, rim_a, rim_b, rim_low, rim_high, back, *rets)
    )


def solution(mesh):
    return jax.shard_map(
        per_device,
        mesh=mesh,
        in_specs=(
            P(None, "gx", "gy", None),
            P(None, ("gx", "gy")),
            P(None, ("gx", "gy")),
            P(("gx", "gy")),
            P(("gx", "gy")),
            P(("gx", "gy")),
            P(("gx", "gy")),
            P(("gx", "gy")),
            P(("gx", "gy")),
            P(("gx", "gy")),
        ),
        out_specs=(P(None, "gx", "gy", None), P(None, ("gx", "gy"))),
        check_vma=False,
    )
```

```python
import math

import jax
import jax.numpy as jnp
from jax import lax
from jax.experimental import pallas as pl
from jax.experimental.pallas import tpu as pltpu
from jax.sharding import PartitionSpec as P

CX = 64
CY = 32
CZ = 128
P_SIZE = 256
HOST = 512
PTS = 2 * P_SIZE

DT_STEP = 0.2
NU_VISC = 0.5
EPS_SQ = 1.44
CORE_SQ = 0.01

ROWS = 16
BACK = 8
YROWS = 72
XROWS = 40
FACE_Y = 3 * CX
FACE_X = 3 * XROWS
RIM_Y = 2 * 3 * YROWS
RIM_X = 2 * 3 * CY
CHUNK = 8
N_CHUNK = CX // CHUNK

F32 = jnp.float32
BF16 = jnp.bfloat16
VM = pl.BlockSpec(memory_space=pltpu.MemorySpace.VMEM)
SM = pl.BlockSpec(memory_space=pltpu.MemorySpace.SMEM)
HB = pl.BlockSpec(memory_space=pltpu.MemorySpace.HBM)
MIB = 1024 * 1024


def call(body, outs, n_in, name, scratch=(), first=VM, second=VM, out_specs=None, in_specs=None, vmem=12, aliases=None):
    return pl.pallas_call(
        body,
        out_shape=[jax.ShapeDtypeStruct(s, F32) for s in outs],
        in_specs=in_specs or ([first, second] + [VM] * n_in)[:n_in],
        out_specs=out_specs or [VM] * len(outs),
        scratch_shapes=list(scratch),
        input_output_aliases=aliases or {},
        compiler_params=pltpu.CompilerParams(vmem_limit_bytes=vmem * MIB),
        name=name,
    )


def place():
    nx, ny = lax.axis_size("gx"), lax.axis_size("gy")
    ix, iy = lax.axis_index("gx"), lax.axis_index("gy")
    px, py = lax.rem(ix, 2), lax.rem(iy, 2)
    inner = (ix + px > 0) & (ix + px < nx)
    return px == 0, py == 0, inner, ix * ny + iy, (ix - px) * ny + iy, ny


def odd_side():
    ny, iy = lax.axis_size("gy"), lax.axis_index("gy")
    py = lax.rem(iy, 2)
    return (iy + py > 0) & (iy + py < ny)


def split(value):
    high = value.astype(BF16)
    low = (value - high.astype(F32)).astype(BF16)
    return high, low


def dot3(a_high, a_low, b_high, b_low):
    def one(a, b):
        return jnp.dot(a, b, preferred_element_type=F32)

    return one(a_high, b_high) + (one(a_high, b_low) + one(a_low, b_high))


def reduce_list(items, op):
    result = items[0]
    for item in items[1:]:
        result = op(result, item)
    return result


def pack_body(v_ref, spin_hbm, *rest):
    params, (pay_c, pay_d, blk_ref, held, held_int, spin_ref, sems) = rest[:5], rest[5:]
    _, even_y, _, brick, _, _ = place()

    def faces(first, second):
        made = []
        for k, (ref, y) in enumerate(((pay_c, first), (pay_d, second))):
            for c in range(3):
                made.append(pltpu.make_async_copy(v_ref.at[c, :, y], ref.at[pl.ds(c * CX, CX)], sems.at[3 * k + c]))
        return made

    @pl.when(even_y)
    def _():
        for copy in faces(CY - 1, 0):
            copy.start()

    @pl.when(jnp.logical_not(even_y))
    def _():
        for copy in faces(0, CY - 1):
            copy.start()

    small = [pltpu.make_async_copy(spin_hbm, spin_ref, sems.at[6])]
    small += [pltpu.make_async_copy(p, held.at[k], sems.at[7 + k]) for k, p in enumerate(params[:4])]
    small.append(pltpu.make_async_copy(params[4], held_int, sems.at[11]))
    for copy in small:
        copy.start()
    for copy in small:
        copy.wait()
    radius, chord, twist, angle = [held[k] for k in range(4)]
    parts = [
        radius,
        chord,
        jnp.cos(twist),
        jnp.sin(twist),
        jnp.cos(angle),
        jnp.sin(angle),
        held_int[...].astype(F32),
        jnp.full((1, CZ), spin_ref[0], F32),
        jnp.full((1, CZ), brick.astype(F32), F32),
    ]
    block = jnp.concatenate(parts, axis=0)
    blk_ref[...] = block
    pay_c[FACE_Y:] = block
    pay_d[FACE_Y:] = block
    for copy in faces(0, 0):
        copy.wait()


def stencil_body(start, v_ref, out_ref):
    row = lax.broadcasted_iota(jnp.int32, (CY, CZ), 0)
    lane = lax.broadcasted_iota(jnp.int32, (CY, CZ), 1)
    half = 0.5 * DT_STEP
    visc = DT_STEP * NU_VISC
    not_last_y, not_first_y = row < CY - 1, row > 0
    not_last_z, not_first_z = lane < CZ - 1, lane > 0

    def step(k, carry):
        x = start + k
        up = jnp.minimum(x + 1, CX - 1)
        down = jnp.maximum(x - 1, 0)
        v0, v1, v2 = v_ref[0, x], v_ref[1, x], v_ref[2, x]
        a_x = jnp.where(x < CX - 1, visc - half * v0, 0.0)
        b_x = jnp.where(x > 0, visc + half * v0, 0.0)
        a_y = jnp.where(not_last_y, visc - half * v1, 0.0)
        b_y = jnp.where(not_first_y, visc + half * v1, 0.0)
        a_z = jnp.where(not_last_z, visc - half * v2, 0.0)
        b_z = jnp.where(not_first_z, visc + half * v2, 0.0)
        for c in range(3):
            mid = (v0, v1, v2)[c]
            along_x = a_x * v_ref[c, up] + b_x * v_ref[c, down]
            along_y = a_y * pltpu.roll(mid, CY - 1, 0) + b_y * pltpu.roll(mid, 1, 0)
            along_z = a_z * pltpu.roll(mid, CZ - 1, 1) + b_z * pltpu.roll(mid, 1, 1)
            out_ref[c, k] = (1.0 - 6.0 * visc) * mid + along_x + (along_y + along_z)
        return carry

    lax.fori_loop(0, CX // 2, step, 0, unroll=2)


def weight(coord, base, frac):
    return jnp.where(coord == base, 1.0 - frac, jnp.where(coord == base + 1, frac, 0.0))


def sample_part(start, v_ref, table, out_ref):
    x_col, y_col, z_col = [table[:, k : k + 1].astype(jnp.int32) for k in range(3)]
    fx, fy, fz = [table[:, k : k + 1] for k in range(3, 6)]
    lane = lax.broadcasted_iota(jnp.int32, (HOST, CZ), 1)
    wy = weight(lane % CY, y_col, fy)
    x_lane = lane // CY + start - x_col
    acc = None
    per = 4
    nx = CZ * per // CY
    for j in range(CX // 2 // nx):
        parts = []
        for i in range(per):
            shift = (CZ // CY) * (j * per + i)
            wx = jnp.where(x_lane == -shift, 1.0 - fx, jnp.where(x_lane == 1 - shift, fx, 0.0))
            parts.append(wx * wy)
        w_high, w_low = split(jnp.concatenate(parts, axis=1))
        first = start + j * nx
        field = [v_ref[c, first : first + nx].reshape(nx * CY, CZ) for c in range(3)]
        f_high, f_low = split(jnp.concatenate(field, axis=1))
        part = dot3(w_high, w_low, f_high, f_low)
        acc = part if acc is None else acc + part
    wz = weight(lane, z_col, fz)
    out = table
    for c in range(3):
        value = jnp.sum(acc[:, c * CZ : (c + 1) * CZ] * wz, axis=1, keepdims=True)
        out = out + jnp.where(lane == 6 + c, value, 0.0)
    out_ref[...] = out


def sample_low_body(v_ref, cell_ref, frac_ref, tab_ref, x_ref, y_ref):
    for c in range(3):
        x_ref[c] = v_ref[c, 0]
        x_ref[c + 3] = v_ref[c, CX - 1]
    y_ref[0] = v_ref[1, :, 0, :]
    y_ref[1] = v_ref[1, :, CY - 1, :]
    rows = jnp.concatenate([cell_ref[...].astype(F32), frac_ref[...], jnp.zeros((CZ - 6, HOST), F32)], axis=0)
    sample_part(0, v_ref, rows.T, tab_ref)


def sample_high_body(v_ref, low_ref, tab_ref):
    sample_part(CX // 2, v_ref, low_ref[...], tab_ref)


def split_blocks(sources):
    return [
        ref[first + k * ROWS : first + (k + 1) * ROWS]
        for ref, first in sources
        for k in range((ref.shape[0] - first) // ROWS)
    ]


def pick_pair(values, b0, ny):
    keys = [value[12:13, 0:1] for value in values]
    members = []
    for key in keys:
        home = jnp.floor(key * (1.0 / HOST)).astype(jnp.int32)
        members.append((home == b0) | (home == b0 + ny))
    low_key = reduce_list([jnp.where(m, k, 1e9) for k, m in zip(keys, members)], jnp.minimum)
    high_key = reduce_list([jnp.where(m, k, -9.0) for k, m in zip(keys, members)], jnp.maximum)
    low = jnp.full((ROWS, CZ), -1.0, F32)
    high = low
    for key, value in zip(keys, values):
        low = jnp.where(key == low_key, value, low)
        high = jnp.where(key == high_key, value, high)
    return low, high


def xpack_body(n_blk, x_ref, rec_c, rec_d, *rest):
    pieces, (pay_a, pay_b, own_ref, *others) = rest[:n_blk], rest[n_blk:]
    even_x, even_y, inner, _, b0, ny = place()
    for c in range(3):
        at = c * CX
        y_high = jnp.where(even_y, rec_c[at : at + 1], jnp.where(odd_side(), rec_d[at : at + 1], 0.0))
        tail = jnp.concatenate([y_high, jnp.zeros((XROWS - CY - 1, CZ), F32)], axis=0)
        low, high = x_ref[c], x_ref[c + 3]
        at = c * XROWS
        pay_a[at : at + CY] = jnp.where(even_x, high, low)
        pay_b[at : at + CY] = jnp.where(even_x, low, high)
        pay_a[at + CY : at + XROWS] = tail
        pay_b[at + CY : at + XROWS] = tail
    if not others:
        own_ref[...] = jnp.concatenate([p[...] for p in pieces], axis=0)
        return
    values = split_blocks([(p, 0) for p in pieces])
    chips = ny * 2
    side = jnp.where(even_x, -chips, chips)
    total = lax.axis_size("gx") * ny
    own_ref[...] = jnp.concatenate(pick_pair(values, b0, ny), axis=0)
    beside = jnp.concatenate(pick_pair(values, lax.rem(b0 + side + total, total), ny), axis=0)
    pay_b[FACE_X:] = beside
    others[1][...] = beside
    others[0][...] = jnp.concatenate(pick_pair(values, lax.rem(b0 + 2 * chips, total), ny), axis=0)


def select_body(n_blk, tab_ref, face_a, face_b, rec_c, rec_d, blk_ref, *rest):
    others, (samp_ref, sel_ref, pts_ref) = rest[:n_blk], rest[n_blk:]
    even_x, even_y, inner, brick, b0, ny = place()
    sources = [(blk_ref, 0), (face_b, FACE_X)] + [(o, 0) for o in others]
    turbine_a, turbine_b = pick_pair(split_blocks(sources), b0, ny)
    sel = jnp.concatenate([turbine_a, turbine_b], axis=0)
    sel_ref[...] = sel
    turned = jnp.concatenate([sel, jnp.zeros((CZ - 2 * ROWS, CZ), F32)], axis=0).T

    def column(k):
        picks = (2 * k, 2 * k + 1, ROWS + 2 * k, ROWS + 2 * k + 1)
        return jnp.concatenate([turned[:, j : j + 1] for j in picks], axis=0)

    table = tab_ref[...]
    lane = lax.broadcasted_iota(jnp.int32, (PTS, CZ), 1)
    x_col, y_col, z_col = [table[:, k : k + 1].astype(jnp.int32) for k in range(3)]
    fx, fy, fz = [table[:, k : k + 1] for k in range(3, 6)]
    on_line = lane >= CX
    edge_x = jnp.where(on_line, lane - CX, CX)
    edge_y = jnp.where(on_line, CY, lane)
    edge_w = jnp.where(on_line | (lane <= CY), weight(edge_x, x_col, fx) * weight(edge_y, y_col, fy), 0.0)
    field = []
    for c in range(3):
        at = c * XROWS
        past = jnp.where(inner, face_b[at : at + XROWS], 0.0)
        plane = jnp.where(even_x, face_a[at : at + XROWS], past)
        at = c * CX
        line = jnp.where(even_y, rec_c[at : at + CX], jnp.where(odd_side(), rec_d[at : at + CX], 0.0))
        field.append(jnp.concatenate([plane, jnp.zeros((CX - XROWS, CZ), F32), line], axis=0))
    w_high, w_low = split(edge_w)
    f_high, f_low = split(jnp.concatenate(field, axis=1))
    acc = dot3(w_high, w_low, f_high, f_low)
    wz = weight(lane, z_col, fz)
    for c in range(3):
        value = jnp.sum(acc[:, c * CZ : (c + 1) * CZ] * wz, axis=1, keepdims=True)
        table = table + jnp.where(lane == 6 + c, value, 0.0)
    slot = column(6).astype(jnp.int32)
    mine = (slot // HOST) == brick
    local = jnp.where(mine, slot % HOST, -1)
    hit = (lax.broadcasted_iota(jnp.int32, (PTS, HOST), 1) == local).astype(F32).astype(BF16)
    first, second = split(table)
    third = (table - first.astype(F32) - second.astype(F32)).astype(BF16)
    pulled = [jnp.dot(hit, part, preferred_element_type=F32) for part in (first, second, third)]
    points = pulled[0] + pulled[1] + pulled[2]
    points = jnp.where(lane == 9, column(0), points)
    pts_ref[...] = jnp.where((lane == 0) & jnp.logical_not(mine), -100.0, points)
    samp_ref[...] = points.T[6:14]


def offsets(frac):
    raw = [jnp.exp(-((o - frac) ** 2) / EPS_SQ) for o in (-1.0, 0.0, 1.0, 2.0)]
    total = (raw[0] + raw[1]) + (raw[2] + raw[3])
    return [value / total for value in raw]


def profile(rows, inner, base, frac):
    index = lax.broadcasted_iota(jnp.int32, (rows, PTS), 0)
    late = index - inner
    index = jnp.where(index < inner, index, jnp.where(late < 2, late - 2, late - 2 + inner))
    rel = index - base.astype(jnp.int32)
    result = jnp.zeros((rows, PTS), F32)
    for k, w in enumerate(offsets(frac)):
        result = jnp.where(rel == k - 1, w, result)
    return result


def line_profile(base, frac, extra):
    stack = jnp.concatenate(offsets(frac) + [base] + extra + [jnp.zeros((CZ - 5 - len(extra), PTS), F32)], axis=0).T
    rel = lax.broadcasted_iota(jnp.int32, (PTS, CZ), 1) - stack[:, 4:5].astype(jnp.int32)
    result = jnp.zeros((PTS, CZ), F32)
    for k in range(4):
        result = jnp.where(rel == k - 1, stack[:, k : k + 1], result)
    return result, [stack[:, 5 + k : 6 + k] for k in range(len(extra))]


def weights_body(pts_ref, gx_ref, gy_ref, pz_ref, pos_ref):
    table = pts_ref[...].T
    gx_ref[...] = profile(YROWS, CX, table[0:1], table[3:4])
    gy_ref[...] = profile(CY, CY, table[1:2], table[4:5])
    pz_ref[...] = line_profile(table[2:3], table[5:6], [])[0]
    pos_ref[...] = jnp.concatenate([table[q : q + 1, k * CZ : (k + 1) * CZ] for q in range(6) for k in range(4)], axis=0)


def attack(axial_flow, tangent, cos_twist, sin_twist):
    rel_speed = jnp.sqrt(axial_flow * axial_flow + tangent * tangent + 1.0)
    cos_phi = tangent / rel_speed
    sin_phi = axial_flow / rel_speed
    sin_alpha = sin_phi * cos_twist - cos_phi * sin_twist
    cos_alpha = cos_phi * cos_twist + sin_phi * sin_twist
    lift_coef = 2.0 * jnp.pi * sin_alpha * cos_alpha / (1.0 + 4.0 * sin_alpha * sin_alpha)
    drag_coef = 0.02 + 0.8 * sin_alpha * sin_alpha
    return rel_speed, cos_phi, sin_phi, lift_coef, drag_coef


def loads_body(samp_ref, other_ref, sel_ref, pts_ref, gx_ref, gy_ref, pz_ref, pos_ref, lh_ref, pay_ref, xrim_ref):
    def row(k):
        picks = (2 * k, 2 * k + 1, ROWS + 2 * k, ROWS + 2 * k + 1)
        return jnp.concatenate([sel_ref[j : j + 1] for j in picks], axis=1)

    radius, chord, cos_t, sin_t, cos_a, sin_a = [row(k) for k in range(6)]
    spin = radius * jnp.concatenate([sel_ref[j : j + 1] for j in (14, 14, ROWS + 14, ROWS + 14)], axis=1)
    flow = samp_ref[...] + other_ref[...]
    axial = flow[0:1]
    tangent = spin - (cos_a * flow[2:3] - sin_a * flow[1:2])
    rel_speed, cos_phi, sin_phi, lift_coef, drag_coef = attack(axial, tangent, cos_t, sin_t)
    circ = 0.5 * chord * rel_speed * lift_coef
    parts = []
    for t in range(2):
        seg = slice(t * P_SIZE, (t + 1) * P_SIZE)
        spacing = radius[:, seg] - pts_ref[seg, 9:10]
        kernel = spacing / (spacing * spacing + CORE_SQ)
        lhs = jnp.concatenate([cos_a[:, seg] * circ[:, seg], sin_a[:, seg] * circ[:, seg], jnp.zeros((6, P_SIZE), F32)], axis=0)
        both = jnp.dot(lhs, kernel, preferred_element_type=F32, precision=lax.Precision.HIGHEST)
        parts.append((cos_a[:, seg] * both[0:1] + sin_a[:, seg] * both[1:2]) / (4.0 * math.pi))
    induced = jnp.concatenate(parts, axis=1)
    rel_speed, cos_phi, sin_phi, lift_coef, drag_coef = attack(axial + induced, tangent, cos_t, sin_t)
    dynamic = 0.5 * chord * rel_speed * rel_speed
    lift = dynamic * lift_coef
    drag = dynamic * drag_coef
    thrust = lift * cos_phi + drag * sin_phi
    torque = lift * sin_phi - drag * cos_phi
    force = [-thrust, torque * sin_a, -torque * cos_a]
    pieces = []
    for t in range(2):
        for c in range(3):
            for h in range(2):
                at = t * P_SIZE + h * CZ
                pieces.append(force[c][:, at : at + CZ])
        pieces += [sel_ref[t * ROWS + 15 : t * ROWS + 16]] * 2
    blocks = jnp.concatenate(pieces, axis=0)
    pay_ref[0 : 2 * BACK] = blocks
    pay_ref[2 * BACK :] = pos_ref[...]
    cols = jnp.concatenate(force + [jnp.zeros((CZ - 3, PTS), F32)], axis=0).T
    pz = pz_ref[...] * DT_STEP
    lines = jnp.concatenate([cols[:, c : c + 1] * pz for c in range(3)], axis=1)
    l_high, l_low = split(lines)
    lh_ref[...] = lines
    gx = gx_ref[...]
    gy = gy_ref[...]
    planes = [gx[CX + k : CX + k + 1] * gy for k in range(4)]
    w_high, w_low = split(jnp.concatenate(planes, axis=0))
    rim = dot3(w_high, w_low, l_high, l_low)
    for k in range(4):
        for c in range(3):
            at = (k * 3 + c) * CY
            xrim_ref[at : at + CY] = rim[k * CY : (k + 1) * CY, c * CZ : (c + 1) * CZ]


def near_body(rec_c, rec_d, low_ref, high_ref):
    _, even_y, _, _, _, _ = place()
    c_all, d_all = rec_c[...], jnp.where(odd_side(), rec_d[...], 0.0)
    for side, out_ref in ((0, low_ref), (1, high_ref)):
        got = jnp.where(even_y, d_all, c_all) if side == 0 else jnp.where(even_y, c_all, d_all)

        def wide(first, picks):
            return jnp.concatenate([got[first + j : first + j + 1] for j in picks], axis=1)

        x, y, z, fx, fy, fz = [wide(2 * BACK + 4 * q, range(4)) for q in range(6)]
        force = [wide(2 * c, (0, 1, BACK, BACK + 1)) * DT_STEP for c in range(3)]
        pz, columns = line_profile(z, fz, force)
        l_high, l_low = split(jnp.concatenate([col * pz for col in columns], axis=1))
        gx = profile(YROWS, CX, x, fx)
        wy = offsets(fy)
        planes = []
        for i in range(2):
            rel = (CY + i if side == 0 else i - 2) - y.astype(jnp.int32)
            gy = jnp.zeros((1, PTS), F32)
            for k in range(4):
                gy = jnp.where(rel == k - 1, wy[k], gy)
            planes.append(gx * gy)
        w_high, w_low = split(jnp.concatenate(planes, axis=0))
        rim = dot3(w_high, w_low, l_high, l_low)
        for i in range(2):
            for c in range(3):
                at = (i * 3 + c) * YROWS
                out_ref[at : at + YROWS] = rim[i * YROWS : (i + 1) * YROWS, c * CZ : (c + 1) * CZ]


SPREAD_X = 8


def spread_body(start, lines_ref, gx_ref, gy_ref, base_ref, out_ref):
    l_high, l_low = split(lines_ref[...])
    gy = gy_ref[0:CY]
    for k in range(out_ref.shape[1] // SPREAD_X):
        at = k * SPREAD_X
        first = start + at
        planes = jnp.concatenate([gx_ref[first + i : first + i + 1] * gy for i in range(SPREAD_X)], axis=0)
        w_high, w_low = split(planes)
        value = dot3(w_high, w_low, l_high, l_low)
        for c in range(3):
            part = value[:, c * CZ : (c + 1) * CZ].reshape(SPREAD_X, CY, CZ)
            out_ref[c, at : at + SPREAD_X] = base_ref[c, at : at + SPREAD_X] + part


def rimpack_body(n_blk, xrim_ref, low_ref, high_ref, *rest):
    pieces, (pay_a, pay_b, back_ref, *others) = rest[:n_blk], rest[n_blk:]
    even_x, even_y, inner, _, b0, ny = place()
    zero = jnp.zeros((CY - 4, CZ), F32)
    for k in range(2):
        for c in range(3):
            sides = []
            for s in range(2):
                near, far = [], []
                for y in range(2):
                    at = (y * 3 + c) * YROWS + CX + 2 * s + k
                    near.append(low_ref[at : at + 1])
                    far.append(high_ref[at : at + 1])
                at = ((2 * s + k) * 3 + c) * CY
                sides.append(xrim_ref[at : at + CY] + jnp.concatenate(near + [zero] + far, axis=0))
            at = (k * 3 + c) * CY
            pay_a[at : at + CY] = jnp.where(even_x, sides[1], sides[0])
            pay_b[at : at + CY] = jnp.where(even_x, sides[0], sides[1])
    back = jnp.concatenate([p[...] for p in pieces], axis=0)
    back_ref[...] = back
    if others:
        chips = ny * 2
        side = jnp.where(even_x, -chips, chips)
        total = lax.axis_size("gx") * ny
        for ref, at, target in (
            (pay_b, RIM_X, lax.rem(b0 + side + total, total)),
            (others[0], 0, lax.rem(b0 + 2 * chips, total)),
        ):
            for core in range(2):
                wanted = (target + core * ny).astype(F32)
                found = jnp.full((BACK, CZ), -1.0, F32)
                for k in range(back.shape[0] // BACK):
                    value = back[k * BACK : (k + 1) * BACK]
                    found = jnp.where(value[6:7, 0:1] == wanted, value, found)
                ref[at + core * BACK : at + (core + 1) * BACK] = found


def face_terms(buf, at, first, main_low, main_high, y_ref, rec_c, rec_d, rim_low, rim_high, even_y):
    half = 0.5 * DT_STEP
    visc = DT_STEP * NU_VISC
    part = slice(first, first + CHUNK)
    here = slice(at, at + CHUNK)
    half_of = main_low if first < CX // 2 else main_high
    inner = first % (CX // 2)
    for c in range(3):
        buf[c, here] = half_of[c, inner : inner + CHUNK]
        rows = slice(c * CX + first, c * CX + first + CHUNK)
        a, b = rec_c[rows], jnp.where(odd_side(), rec_d[rows], 0.0)
        low = [jnp.where(even_y, b, a) * (visc + half * y_ref[0, part]), 0.0]
        high = [0.0, jnp.where(even_y, a, b) * (visc - half * y_ref[1, part])]
        for i in range(2):
            row = (i * 3 + c) * YROWS + first
            buf[c, here, i, :] += rim_low[row : row + CHUNK] + low[i]
            buf[c, here, CY - 2 + i, :] += rim_high[row : row + CHUNK] + high[i]


def chunk_copy(buf, at, out_ref, first, sem):
    return pltpu.make_async_copy(buf.at[:, pl.ds(at, CHUNK)], out_ref.at[:, pl.ds(first, CHUNK)], sem)


def inside_body(main_low, main_high, y_ref, rec_c, rec_d, rim_low, rim_high, out_ref, buf, sems):
    _, even_y, _, _, _, _ = place()
    copies = []
    for k in range(N_CHUNK - 2):
        first = (k + 1) * CHUNK
        face_terms(buf, k * CHUNK, first, main_low, main_high, y_ref, rec_c, rec_d, rim_low, rim_high, even_y)
        copies.append(chunk_copy(buf, k * CHUNK, out_ref, first, sems.at[k]))
        copies[-1].start()
    for copy in copies:
        copy.wait()


def final_body(n_ret, _, main_low, main_high, x_ref, y_ref, face_a, face_b, rec_c, rec_d, rim_a, rim_b, rim_low, rim_high, back_ref, *rest):
    rets, (out_ref, pf_ref, buf, sems) = rest[:n_ret], rest[n_ret:]
    even_x, even_y, inner, brick, _, _ = place()
    half = 0.5 * DT_STEP
    visc = DT_STEP * NU_VISC
    copies = []
    for k in range(2):
        first, at = k * (CX - CHUNK), k * CHUNK
        face_terms(buf, at, first, main_low, main_high, y_ref, rec_c, rec_d, rim_low, rim_high, even_y)
        for c in range(3):
            a = face_a[c * XROWS : c * XROWS + CY]
            b = jnp.where(inner, face_b[c * XROWS : c * XROWS + CY], 0.0)
            if k == 0:
                buf[c, 0] += jnp.where(even_x, b, a) * (visc + half * x_ref[0])
            else:
                buf[c, 2 * CHUNK - 1] += jnp.where(even_x, a, b) * (visc - half * x_ref[3])
            for i in range(2):
                rows = slice((i * 3 + c) * CY, (i * 3 + c + 1) * CY)
                a, b = rim_a[rows], jnp.where(inner, rim_b[rows], 0.0)
                if k == 0:
                    buf[c, i] += jnp.where(even_x, b, a)
                else:
                    buf[c, 2 * CHUNK - 2 + i] += jnp.where(even_x, a, b)
        copies.append(chunk_copy(buf, at, out_ref, first, sems.at[k]))
        copies[-1].start()
    mine = brick.astype(F32)
    found = jnp.zeros((BACK, CZ), F32)
    for ref, first in [(back_ref, 0), (rim_b, RIM_X)] + [(r, 0) for r in rets]:
        for k in range((ref.shape[0] - first) // BACK):
            value = ref[first + BACK * k : first + BACK * k + BACK]
            found = jnp.where(value[6:7, 0:1] == mine, value, found)
    for c in range(3):
        pf_ref[c : c + 1] = jnp.concatenate([found[2 * c : 2 * c + 1], found[2 * c + 1 : 2 * c + 2]], axis=1)
    for copy in copies:
        copy.wait()


def per_device(
    velocity,
    host_cell,
    host_frac,
    host_dst,
    owner_src,
    rotor_speed,
    blade_radius,
    blade_chord,
    blade_twist,
    blade_angle,
):
    nx, ny = lax.axis_size("gx"), lax.axis_size("gy")
    ring, short = nx == 8, ny == 4

    def flip(n, bits):
        return [(i, i ^ bits) for i in range(n)]

    def odd_pairs(n, closed=False):
        up = [(i, (i + 1) % n) for i in range(1, n if closed else n - 1, 2)]
        return up + [(t, s) for s, t in up]

    def same_side(n):
        return [(i, (i + (2 if i % 2 else n - 2)) % n) for i in range(n)]

    def across_x(blocks):
        return [lax.ppermute(b, "gx", p) for b, p in zip(blocks, (flip(nx, 4), same_side(nx)))]

    def swap(block):
        return lax.ppermute(block, "gx", flip(nx, 1))

    def join(pieces):
        return pieces[0] if len(pieces) == 1 else jnp.concatenate(pieces, axis=0)

    def after(values, other):
        return lax.optimization_barrier((values, other))

    def gather_y(first):
        pieces = [first]
        for bit in [b for b in (2, 4, 8) if b < ny]:
            pieces.append(lax.ppermute(join(pieces), "gy", flip(ny, bit)))
        return pieces

    def exchange_y(to_c, to_d, block):
        from_c = lax.ppermute(to_c, "gy", flip(ny, 1))
        from_d = lax.ppermute(to_d, "gy", flip(ny, 3) if short else odd_pairs(ny))
        return from_c, from_d, [lax.ppermute(block, "gy", flip(ny, 2))] if short else []

    def blocks_y(block, from_c, from_d, far, size, at):
        got = join([block, from_c[at : at + size]])
        if short:
            return [join([got, from_d[at : at + size]] + far)]
        return gather_y(got)

    def gather_x(blocks):
        pieces = []
        for bit in [b for b in (2, 4, 8, 16) if b < nx]:
            pieces.append(lax.ppermute(join([blocks] + pieces), "gx", flip(nx, bit)))
        return pieces

    dma = pltpu.SemaphoreType.DMA
    pay_c, pay_d, block = call(
        pack_body,
        [(FACE_Y + ROWS, CZ)] * 2 + [(ROWS, CZ)],
        7,
        "pack",
        scratch=[pltpu.VMEM((4, 2, CZ), F32), pltpu.VMEM((2, CZ), jnp.int32), pltpu.SMEM((1,), F32), dma((12,))],
        in_specs=[HB] * 7,
        vmem=56,
    )(velocity, rotor_speed, *[a.reshape(2, CZ) for a in (blade_radius, blade_chord, blade_twist, blade_angle, owner_src)])
    rec_c, rec_d, far = exchange_y(pay_c, pay_d, block)

    def stencil(start):
        return call(lambda *refs: stencil_body(start, *refs), [(3, CX // 2, CY, CZ)], 1, "stencil")(velocity)[0]

    base_low = stencil(0)
    table, x_faces, y_faces = call(
        sample_low_body, [(HOST, CZ), (6, CY, CZ), (2, CX, CZ)], 3, "sample_low", vmem=24
    )(velocity, host_cell, host_frac)
    (rec_c, rec_d, far), (base_low, table) = after((rec_c, rec_d, far), (base_low, table))
    pieces = blocks_y(block, rec_c, rec_d, far, ROWS, FACE_Y)
    beside = [swap(p) for p in pieces]
    beside, base_high = after(beside, stencil(CX // 2))
    pieces = pieces + beside
    n_rows = 2 * ny * ROWS
    pair = (2 * ROWS, CZ)
    pay_a, pay_b, blocks, *across = call(
        lambda *refs: xpack_body(len(pieces), *refs),
        [(FACE_X, CZ), (FACE_X + 2 * ROWS, CZ), pair, pair, pair] if ring else [(FACE_X, CZ), (FACE_X, CZ), (n_rows, CZ)],
        3 + len(pieces),
        "xpack",
    )(x_faces, rec_c, rec_d, *pieces)
    face_b = lax.ppermute(pay_b, "gx", odd_pairs(nx, ring))
    from_x = across_x(across) if ring else gather_x(blocks)
    face_a = swap(pay_a)
    table = call(sample_high_body, [(HOST, CZ)], 2, "sample_high", vmem=24)(velocity, table)[0]
    (face_a, face_b, from_x), table = after((face_a, face_b, from_x), table)
    samp, sel, pts = call(
        lambda *refs: select_body(len(from_x), *refs),
        [(8, PTS), (2 * ROWS, CZ), (PTS, CZ)],
        6 + len(from_x),
        "select",
    )(table, face_a, face_b, rec_c, rec_d, blocks, *from_x)
    other = swap(samp)
    gx, gy, pz, pos = call(weights_body, [(YROWS, PTS), (CY, PTS), (PTS, CZ), (24, CZ)], 1, "weights")(pts)
    lines, points, xrim = call(
        loads_body,
        [(PTS, 3 * CZ), (2 * BACK + 24, CZ), (2 * RIM_X, CZ)],
        8,
        "loads",
    )(samp, other, sel, pts, gx, gy, pz, pos)
    ret = points[: 2 * BACK]
    near_c, near_d, far = exchange_y(points, points, ret)

    def spread(start, base):
        return call(
            lambda *refs: spread_body(start, *refs), [(3, CX // 2, CY, CZ)], 4, "spread"
        )(lines, gx, gy, base)[0]

    (near_c, near_d, far), main_low = after((near_c, near_d, far), spread(0, base_low))
    rim_low, rim_high = call(near_body, [(RIM_Y, CZ)] * 2, 2, "near")(near_c, near_d)
    pieces = blocks_y(ret, near_c, near_d, far, 2 * BACK, 0)
    n_rows = 2 * ny * BACK
    pair = (2 * BACK, CZ)
    pay_a, pay_b, back, *across = call(
        lambda *refs: rimpack_body(len(pieces), *refs),
        [(RIM_X, CZ), (RIM_X + 2 * BACK, CZ), (n_rows, CZ), pair] if ring else [(RIM_X, CZ), (RIM_X, CZ), (n_rows, CZ)],
        3 + len(pieces),
        "rimpack",
    )(xrim, rim_low, rim_high, *pieces)
    rim_b = lax.ppermute(pay_b, "gx", odd_pairs(nx, ring))
    rets = [lax.ppermute(across[0], "gx", flip(nx, 4))] if ring else gather_x(back)
    rim_a = swap(pay_a)
    main_high = spread(CX // 2, base_high)
    (rim_a, rim_b), (main_low, main_high) = after((rim_a, rim_b), (main_low, main_high))
    if ring:
        rets.append(swap(rim_b[RIM_X:]))
    inside = call(
        inside_body,
        [velocity.shape],
        7,
        "inside",
        scratch=[pltpu.VMEM((3, CX - 2 * CHUNK, CY, CZ), F32), dma((N_CHUNK - 2,))],
        out_specs=[HB],
        vmem=16,
    )(main_low, main_high, y_faces, rec_c, rec_d, rim_low, rim_high)[0]
    rets, inside = after(rets, inside)
    return tuple(
        call(
            lambda *refs: final_body(len(rets), *refs),
            [velocity.shape, (3, P_SIZE)],
            14 + len(rets),
            "final",
            scratch=[pltpu.VMEM((3, 2 * CHUNK, CY, CZ), F32), dma((2,))],
            first=HB,
            out_specs=[HB, VM],
            aliases={0: 0},
        )(inside, main_low, main_high, x_faces, y_faces, face_a, face_b, rec_c, rec_d, rim_a, rim_b, rim_low, rim_high, back, *rets)
    )


def solution(mesh):
    return jax.shard_map(
        per_device,
        mesh=mesh,
        in_specs=(
            P(None, "gx", "gy", None),
            P(None, ("gx", "gy")),
            P(None, ("gx", "gy")),
            P(("gx", "gy")),
            P(("gx", "gy")),
            P(("gx", "gy")),
            P(("gx", "gy")),
            P(("gx", "gy")),
            P(("gx", "gy")),
            P(("gx", "gy")),
        ),
        out_specs=(P(None, "gx", "gy", None), P(None, ("gx", "gy"))),
        check_vma=False,
    )
```

```python
import math

import jax
import jax.numpy as jnp
from jax import lax
from jax.experimental import pallas as pl
from jax.experimental.pallas import tpu as pltpu
from jax.sharding import PartitionSpec as P

CX = 64
CY = 32
CZ = 128
P_SIZE = 256
HOST = 512
PTS = 2 * P_SIZE

DT_STEP = 0.2
NU_VISC = 0.5
EPS_SQ = 1.44
CORE_SQ = 0.01

ROWS = 16
BACK = 8
YROWS = 72
XROWS = 40
FACE_Y = 3 * CX
FACE_X = 3 * XROWS
RIM_Y = 2 * 3 * YROWS
RIM_X = 2 * 3 * CY
CHUNK = 8
N_CHUNK = CX // CHUNK

F32 = jnp.float32
BF16 = jnp.bfloat16
VM = pl.BlockSpec(memory_space=pltpu.MemorySpace.VMEM)
SM = pl.BlockSpec(memory_space=pltpu.MemorySpace.SMEM)
HB = pl.BlockSpec(memory_space=pltpu.MemorySpace.HBM)
MIB = 1024 * 1024


def call(body, outs, n_in, name, scratch=(), first=VM, second=VM, out_specs=None, in_specs=None, vmem=12, aliases=None):
    return pl.pallas_call(
        body,
        out_shape=[jax.ShapeDtypeStruct(s, F32) for s in outs],
        in_specs=in_specs or ([first, second] + [VM] * n_in)[:n_in],
        out_specs=out_specs or [VM] * len(outs),
        scratch_shapes=list(scratch),
        input_output_aliases=aliases or {},
        compiler_params=pltpu.CompilerParams(vmem_limit_bytes=vmem * MIB),
        name=name,
    )


def place():
    nx, ny = lax.axis_size("gx"), lax.axis_size("gy")
    ix, iy = lax.axis_index("gx"), lax.axis_index("gy")
    px, py = lax.rem(ix, 2), lax.rem(iy, 2)
    inner = (ix + px > 0) & (ix + px < nx)
    return px == 0, py == 0, inner, ix * ny + iy, (ix - px) * ny + iy, ny


def odd_side():
    ny, iy = lax.axis_size("gy"), lax.axis_index("gy")
    py = lax.rem(iy, 2)
    return (iy + py > 0) & (iy + py < ny)


def split(value):
    high = value.astype(BF16)
    low = (value - high.astype(F32)).astype(BF16)
    return high, low


def dot3(a_high, a_low, b_high, b_low):
    def one(a, b):
        return jnp.dot(a, b, preferred_element_type=F32)

    return one(a_high, b_high) + (one(a_high, b_low) + one(a_low, b_high))


def reduce_list(items, op):
    result = items[0]
    for item in items[1:]:
        result = op(result, item)
    return result


def pack_body(v_ref, spin_hbm, *rest):
    params, (pay_c, pay_d, blk_ref, held, held_int, made, spin_ref, sems) = rest[:5], rest[5:]
    _, even_y, _, brick, _, _ = place()

    def faces(first, second):
        copies = []
        for k, (ref, y) in enumerate(((pay_c, first), (pay_d, second))):
            for c in range(3):
                copies.append(pltpu.make_async_copy(v_ref.at[c, :, y], ref.at[pl.ds(c * CX, CX)], sems.at[3 * k + c]))
        return copies

    @pl.when(even_y)
    def _():
        for copy in faces(CY - 1, 0):
            copy.start()

    @pl.when(jnp.logical_not(even_y))
    def _():
        for copy in faces(0, CY - 1):
            copy.start()

    small = [pltpu.make_async_copy(spin_hbm, spin_ref, sems.at[6])]
    small += [pltpu.make_async_copy(p, held.at[k], sems.at[7 + k]) for k, p in enumerate(params[:4])]
    small.append(pltpu.make_async_copy(params[4], held_int, sems.at[11]))
    for copy in small:
        copy.start()
    for copy in small:
        copy.wait()
    radius, chord, twist, angle = [held[k] for k in range(4)]
    parts = [
        radius,
        chord,
        jnp.cos(twist),
        jnp.sin(twist),
        jnp.cos(angle),
        jnp.sin(angle),
        held_int[...].astype(F32),
        jnp.full((1, CZ), spin_ref[0], F32),
        jnp.full((1, CZ), brick.astype(F32), F32),
    ]
    made[...] = jnp.concatenate(parts, axis=0)
    targets = (pay_c.at[pl.ds(FACE_Y, ROWS)], pay_d.at[pl.ds(FACE_Y, ROWS)], blk_ref)
    outward = [pltpu.make_async_copy(made, ref, sems.at[12 + k]) for k, ref in enumerate(targets)]
    for copy in outward:
        copy.start()
    for copy in faces(0, 0) + outward:
        copy.wait()


def stencil_body(start, v_ref, out_ref):
    row = lax.broadcasted_iota(jnp.int32, (CY, CZ), 0)
    lane = lax.broadcasted_iota(jnp.int32, (CY, CZ), 1)
    half = 0.5 * DT_STEP
    visc = DT_STEP * NU_VISC
    not_last_y, not_first_y = row < CY - 1, row > 0
    not_last_z, not_first_z = lane < CZ - 1, lane > 0

    def plane(x, down, up):
        at = x * CY if isinstance(x, int) else pl.multiple_of(x * CY, CY)
        v0, v1, v2 = [v_ref[c, pl.ds(at, CY)] for c in range(3)]
        a_x, b_x = visc - half * v0, visc + half * v0
        a_y = jnp.where(not_last_y, visc - half * v1, 0.0)
        b_y = jnp.where(not_first_y, visc + half * v1, 0.0)
        a_z = jnp.where(not_last_z, visc - half * v2, 0.0)
        b_z = jnp.where(not_first_z, visc + half * v2, 0.0)
        for c in range(3):
            mid = (v0, v1, v2)[c]
            total = (1.0 - 6.0 * visc) * mid
            total += a_z * pltpu.roll(mid, CZ - 1, 1) + b_z * pltpu.roll(mid, 1, 1)
            if up is None:
                y_up = pltpu.roll(mid, CY - 1, 0)
            else:
                y_up = v_ref[c, pl.ds(at + 1, CY)]
                total += a_x * v_ref[c, pl.ds(at + CY, CY)]
            if down is None:
                y_down = pltpu.roll(mid, 1, 0)
            else:
                y_down = v_ref[c, pl.ds(at - 1, CY)]
                total += b_x * v_ref[c, pl.ds(at - CY, CY)]
            out_ref[c, x - start] = total + (a_y * y_up + b_y * y_down)

    first, last = start, start + CX // 2
    if start == 0:
        plane(0, None, True)
        first = 1
    if last == CX:
        last = CX - 1
        plane(last, True, None)

    def step(x, carry):
        plane(x, True, True)
        return carry

    lax.fori_loop(first, last, step, 0, unroll=2)


def weight(coord, base, frac):
    return jnp.where(coord == base, 1.0 - frac, jnp.where(coord == base + 1, frac, 0.0))


def sample_part(start, v_ref, table, acc):
    x_col, y_col = [table[:, k : k + 1].astype(jnp.int32) for k in range(2)]
    fx, fy = [table[:, k : k + 1] for k in range(3, 5)]
    lane = lax.broadcasted_iota(jnp.int32, (HOST, CZ), 1)
    wy = weight(lane % CY, y_col, fy)
    x_lane = lane // CY + start - x_col
    per = 4
    nx = CZ * per // CY
    for j in range(CX // 2 // nx):
        parts = []
        for i in range(per):
            shift = (CZ // CY) * (j * per + i)
            wx = jnp.where(x_lane == -shift, 1.0 - fx, jnp.where(x_lane == 1 - shift, fx, 0.0))
            parts.append(wx * wy)
        w_high, w_low = split(jnp.concatenate(parts, axis=1))
        first = start + j * nx
        field = [v_ref[c, first : first + nx].reshape(nx * CY, CZ) for c in range(3)]
        f_high, f_low = split(jnp.concatenate(field, axis=1))
        part = dot3(w_high, w_low, f_high, f_low)
        acc = part if acc is None else acc + part
    return acc


def sample_low_body(v_ref, cell_ref, frac_ref, tab_ref, acc_ref, x_ref, y_ref):
    for c in range(3):
        x_ref[c] = v_ref[c, 0]
        x_ref[c + 3] = v_ref[c, CX - 1]
    y_ref[0] = v_ref[1, :, 0, :]
    y_ref[1] = v_ref[1, :, CY - 1, :]
    rows = jnp.concatenate([cell_ref[...].astype(F32), frac_ref[...], jnp.zeros((CZ - 6, HOST), F32)], axis=0)
    table = rows.T
    tab_ref[...] = table
    acc_ref[...] = sample_part(0, v_ref, table, None)


def sample_high_body(v_ref, tab_ref, low_ref, acc_ref):
    acc_ref[...] = sample_part(CX // 2, v_ref, tab_ref[...], low_ref[...])


def split_blocks(sources):
    return [
        ref[first + k * ROWS : first + (k + 1) * ROWS]
        for ref, first in sources
        for k in range((ref.shape[0] - first) // ROWS)
    ]


def pick_pair(values, b0, ny):
    keys = [value[12:13, 0:1] for value in values]
    members = []
    for key in keys:
        home = jnp.floor(key * (1.0 / HOST)).astype(jnp.int32)
        members.append((home == b0) | (home == b0 + ny))
    low_key = reduce_list([jnp.where(m, k, 1e9) for k, m in zip(keys, members)], jnp.minimum)
    high_key = reduce_list([jnp.where(m, k, -9.0) for k, m in zip(keys, members)], jnp.maximum)
    low = jnp.full((ROWS, CZ), -1.0, F32)
    high = low
    for key, value in zip(keys, values):
        low = jnp.where(key == low_key, value, low)
        high = jnp.where(key == high_key, value, high)
    return low, high


def xpack_body(n_blk, x_ref, rec_c, rec_d, *rest):
    pieces, (pay_a, pay_b, own_ref, *others) = rest[:n_blk], rest[n_blk:]
    even_x, even_y, inner, _, b0, ny = place()
    for c in range(3):
        at = c * CX
        y_high = jnp.where(even_y, rec_c[at : at + 1], jnp.where(odd_side(), rec_d[at : at + 1], 0.0))
        tail = jnp.concatenate([y_high, jnp.zeros((XROWS - CY - 1, CZ), F32)], axis=0)
        low, high = x_ref[c], x_ref[c + 3]
        at = c * XROWS
        pay_a[at : at + CY] = jnp.where(even_x, high, low)
        pay_b[at : at + CY] = jnp.where(even_x, low, high)
        pay_a[at + CY : at + XROWS] = tail
        pay_b[at + CY : at + XROWS] = tail
    if not others:
        own_ref[...] = jnp.concatenate([p[...] for p in pieces], axis=0)
        return
    values = split_blocks([(p, 0) for p in pieces])
    chips = ny * 2
    side = jnp.where(even_x, -chips, chips)
    total = lax.axis_size("gx") * ny
    own_ref[...] = jnp.concatenate(pick_pair(values, b0, ny), axis=0)
    beside = jnp.concatenate(pick_pair(values, lax.rem(b0 + side + total, total), ny), axis=0)
    pay_b[FACE_X:] = beside
    others[1][...] = beside
    others[0][...] = jnp.concatenate(pick_pair(values, lax.rem(b0 + 2 * chips, total), ny), axis=0)


def select_body(n_blk, tab_ref, acc_ref, face_a, face_b, rec_c, rec_d, blk_ref, *rest):
    others, (samp_ref, sel_ref, pts_ref) = rest[:n_blk], rest[n_blk:]
    even_x, even_y, inner, brick, b0, ny = place()
    sources = [(blk_ref, 0), (face_b, FACE_X)] + [(o, 0) for o in others]
    turbine_a, turbine_b = pick_pair(split_blocks(sources), b0, ny)
    sel = jnp.concatenate([turbine_a, turbine_b], axis=0)
    sel_ref[...] = sel
    turned = jnp.concatenate([sel, jnp.zeros((CZ - 2 * ROWS, CZ), F32)], axis=0).T

    def column(k):
        picks = (2 * k, 2 * k + 1, ROWS + 2 * k, ROWS + 2 * k + 1)
        return jnp.concatenate([turned[:, j : j + 1] for j in picks], axis=0)

    table = tab_ref[...]
    lane = lax.broadcasted_iota(jnp.int32, (PTS, CZ), 1)
    x_col, y_col, z_col = [table[:, k : k + 1].astype(jnp.int32) for k in range(3)]
    fx, fy, fz = [table[:, k : k + 1] for k in range(3, 6)]
    on_line = lane >= CX
    edge_x = jnp.where(on_line, lane - CX, CX)
    edge_y = jnp.where(on_line, CY, lane)
    edge_w = jnp.where(on_line | (lane <= CY), weight(edge_x, x_col, fx) * weight(edge_y, y_col, fy), 0.0)
    field = []
    for c in range(3):
        at = c * XROWS
        past = jnp.where(inner, face_b[at : at + XROWS], 0.0)
        plane = jnp.where(even_x, face_a[at : at + XROWS], past)
        at = c * CX
        line = jnp.where(even_y, rec_c[at : at + CX], jnp.where(odd_side(), rec_d[at : at + CX], 0.0))
        field.append(jnp.concatenate([plane, jnp.zeros((CX - XROWS, CZ), F32), line], axis=0))
    w_high, w_low = split(edge_w)
    f_high, f_low = split(jnp.concatenate(field, axis=1))
    acc = acc_ref[...] + dot3(w_high, w_low, f_high, f_low)
    wz = weight(lane, z_col, fz)
    for c in range(3):
        value = jnp.sum(acc[:, c * CZ : (c + 1) * CZ] * wz, axis=1, keepdims=True)
        table = table + jnp.where(lane == 6 + c, value, 0.0)
    slot = column(6).astype(jnp.int32)
    mine = (slot // HOST) == brick
    local = jnp.where(mine, slot % HOST, -1)
    hit = (lax.broadcasted_iota(jnp.int32, (PTS, HOST), 1) == local).astype(F32).astype(BF16)
    first, second = split(table)
    third = (table - first.astype(F32) - second.astype(F32)).astype(BF16)
    pulled = [jnp.dot(hit, part, preferred_element_type=F32) for part in (first, second, third)]
    points = pulled[0] + pulled[1] + pulled[2]
    points = jnp.where(lane == 9, column(0), points)
    pts_ref[...] = jnp.where((lane == 0) & jnp.logical_not(mine), -100.0, points)
    samp_ref[...] = points.T[6:14]


def offsets(frac):
    raw = [jnp.exp(-((o - frac) ** 2) / EPS_SQ) for o in (-1.0, 0.0, 1.0, 2.0)]
    total = (raw[0] + raw[1]) + (raw[2] + raw[3])
    return [value / total for value in raw]


def profile(rows, inner, base, frac):
    index = lax.broadcasted_iota(jnp.int32, (rows, PTS), 0)
    late = index - inner
    index = jnp.where(index < inner, index, jnp.where(late < 2, late - 2, late - 2 + inner))
    rel = index - base.astype(jnp.int32)
    result = jnp.zeros((rows, PTS), F32)
    for k, w in enumerate(offsets(frac)):
        result = jnp.where(rel == k - 1, w, result)
    return result


def line_profile(base, frac, extra):
    stack = jnp.concatenate(offsets(frac) + [base] + extra + [jnp.zeros((CZ - 5 - len(extra), PTS), F32)], axis=0).T
    rel = lax.broadcasted_iota(jnp.int32, (PTS, CZ), 1) - stack[:, 4:5].astype(jnp.int32)
    result = jnp.zeros((PTS, CZ), F32)
    for k in range(4):
        result = jnp.where(rel == k - 1, stack[:, k : k + 1], result)
    return result, [stack[:, 5 + k : 6 + k] for k in range(len(extra))]


def weights_body(pts_ref, sel_ref, gx_ref, gy_ref, pz_ref, pos_ref, pair_ref, edge_ref):
    table = pts_ref[...].T
    gx = profile(YROWS, CX, table[0:1], table[3:4])
    gy = profile(CY, CY, table[1:2], table[4:5])
    gx_ref[...] = gx
    gy_ref[...] = gy
    pz_ref[...] = line_profile(table[2:3], table[5:6], [])[0] * DT_STEP
    pos_ref[...] = jnp.concatenate([table[q : q + 1, k * CZ : (k + 1) * CZ] for q in range(6) for k in range(4)], axis=0)
    for t in range(2):
        at = t * ROWS
        radius = jnp.concatenate([sel_ref[at : at + 1], sel_ref[at + 1 : at + 2]], axis=1)
        spacing = radius - pts_ref[t * P_SIZE : (t + 1) * P_SIZE, 9:10]
        pair_ref[t] = spacing / (spacing * spacing + CORE_SQ)
    for k in range(4):
        edge_ref[k * CY : (k + 1) * CY] = gx[CX + k : CX + k + 1] * gy


def attack(axial_flow, tangent, cos_twist, sin_twist):
    rel_speed = jnp.sqrt(axial_flow * axial_flow + tangent * tangent + 1.0)
    cos_phi = tangent / rel_speed
    sin_phi = axial_flow / rel_speed
    sin_alpha = sin_phi * cos_twist - cos_phi * sin_twist
    cos_alpha = cos_phi * cos_twist + sin_phi * sin_twist
    lift_coef = 2.0 * jnp.pi * sin_alpha * cos_alpha / (1.0 + 4.0 * sin_alpha * sin_alpha)
    drag_coef = 0.02 + 0.8 * sin_alpha * sin_alpha
    return rel_speed, cos_phi, sin_phi, lift_coef, drag_coef


def loads_body(samp_ref, other_ref, sel_ref, pz_ref, pos_ref, pair_ref, edge_ref, lh_ref, pay_ref, xrim_ref):
    def row(k):
        picks = (2 * k, 2 * k + 1, ROWS + 2 * k, ROWS + 2 * k + 1)
        return jnp.concatenate([sel_ref[j : j + 1] for j in picks], axis=1)

    radius, chord, cos_t, sin_t, cos_a, sin_a = [row(k) for k in range(6)]
    spin = radius * jnp.concatenate([sel_ref[j : j + 1] for j in (14, 14, ROWS + 14, ROWS + 14)], axis=1)
    flow = samp_ref[...] + other_ref[...]
    axial = flow[0:1]
    tangent = spin - (cos_a * flow[2:3] - sin_a * flow[1:2])
    rel_speed, cos_phi, sin_phi, lift_coef, drag_coef = attack(axial, tangent, cos_t, sin_t)
    circ = 0.5 * chord * rel_speed * lift_coef
    parts = []
    for t in range(2):
        seg = slice(t * P_SIZE, (t + 1) * P_SIZE)
        lhs = jnp.concatenate([cos_a[:, seg] * circ[:, seg], sin_a[:, seg] * circ[:, seg], jnp.zeros((6, P_SIZE), F32)], axis=0)
        both = jnp.dot(lhs, pair_ref[t], preferred_element_type=F32, precision=lax.Precision.HIGHEST)
        parts.append((cos_a[:, seg] * both[0:1] + sin_a[:, seg] * both[1:2]) / (4.0 * math.pi))
    induced = jnp.concatenate(parts, axis=1)
    rel_speed, cos_phi, sin_phi, lift_coef, drag_coef = attack(axial + induced, tangent, cos_t, sin_t)
    dynamic = 0.5 * chord * rel_speed * rel_speed
    lift = dynamic * lift_coef
    drag = dynamic * drag_coef
    thrust = lift * cos_phi + drag * sin_phi
    torque = lift * sin_phi - drag * cos_phi
    force = [-thrust, torque * sin_a, -torque * cos_a]
    pieces = []
    for t in range(2):
        for c in range(3):
            for h in range(2):
                at = t * P_SIZE + h * CZ
                pieces.append(force[c][:, at : at + CZ])
        pieces += [sel_ref[t * ROWS + 15 : t * ROWS + 16]] * 2
    blocks = jnp.concatenate(pieces, axis=0)
    pay_ref[0 : 2 * BACK] = blocks
    pay_ref[2 * BACK :] = pos_ref[...]
    cols = jnp.concatenate(force + [jnp.zeros((CZ - 3, PTS), F32)], axis=0).T
    pz = pz_ref[...]
    lines = jnp.concatenate([cols[:, c : c + 1] * pz for c in range(3)], axis=1)
    l_high, l_low = split(lines)
    lh_ref[...] = lines
    w_high, w_low = split(edge_ref[...])
    rim = dot3(w_high, w_low, l_high, l_low)
    for k in range(4):
        for c in range(3):
            at = (k * 3 + c) * CY
            xrim_ref[at : at + CY] = rim[k * CY : (k + 1) * CY, c * CZ : (c + 1) * CZ]


def near_body(rec_c, rec_d, low_ref, high_ref):
    _, even_y, _, _, _, _ = place()
    c_all, d_all = rec_c[...], jnp.where(odd_side(), rec_d[...], 0.0)
    for side, out_ref in ((0, low_ref), (1, high_ref)):
        got = jnp.where(even_y, d_all, c_all) if side == 0 else jnp.where(even_y, c_all, d_all)

        def wide(first, picks):
            return jnp.concatenate([got[first + j : first + j + 1] for j in picks], axis=1)

        x, y, z, fx, fy, fz = [wide(2 * BACK + 4 * q, range(4)) for q in range(6)]
        force = [wide(2 * c, (0, 1, BACK, BACK + 1)) * DT_STEP for c in range(3)]
        pz, columns = line_profile(z, fz, force)
        l_high, l_low = split(jnp.concatenate([col * pz for col in columns], axis=1))
        gx = profile(YROWS, CX, x, fx)
        wy = offsets(fy)
        planes = []
        for i in range(2):
            rel = (CY + i if side == 0 else i - 2) - y.astype(jnp.int32)
            gy = jnp.zeros((1, PTS), F32)
            for k in range(4):
                gy = jnp.where(rel == k - 1, wy[k], gy)
            planes.append(gx * gy)
        w_high, w_low = split(jnp.concatenate(planes, axis=0))
        rim = dot3(w_high, w_low, l_high, l_low)
        for i in range(2):
            for c in range(3):
                at = (i * 3 + c) * YROWS
                out_ref[at : at + YROWS] = rim[i * YROWS : (i + 1) * YROWS, c * CZ : (c + 1) * CZ]


SPREAD_X = 8


def spread_body(start, lines_ref, gx_ref, gy_ref, base_ref, out_ref):
    l_high, l_low = split(lines_ref[...])
    gy = gy_ref[0:CY]
    for k in range(out_ref.shape[1] // SPREAD_X):
        at = k * SPREAD_X
        first = start + at
        planes = jnp.concatenate([gx_ref[first + i : first + i + 1] * gy for i in range(SPREAD_X)], axis=0)
        w_high, w_low = split(planes)
        value = dot3(w_high, w_low, l_high, l_low)
        for c in range(3):
            part = value[:, c * CZ : (c + 1) * CZ].reshape(SPREAD_X, CY, CZ)
            out_ref[c, at : at + SPREAD_X] = base_ref[c, at : at + SPREAD_X] + part


def rimpack_body(n_blk, xrim_ref, low_ref, high_ref, *rest):
    pieces, (pay_a, pay_b, back_ref, *others) = rest[:n_blk], rest[n_blk:]
    even_x, even_y, inner, _, b0, ny = place()
    zero = jnp.zeros((CY - 4, CZ), F32)
    for k in range(2):
        for c in range(3):
            sides = []
            for s in range(2):
                near, far = [], []
                for y in range(2):
                    at = (y * 3 + c) * YROWS + CX + 2 * s + k
                    near.append(low_ref[at : at + 1])
                    far.append(high_ref[at : at + 1])
                at = ((2 * s + k) * 3 + c) * CY
                sides.append(xrim_ref[at : at + CY] + jnp.concatenate(near + [zero] + far, axis=0))
            at = (k * 3 + c) * CY
            pay_a[at : at + CY] = jnp.where(even_x, sides[1], sides[0])
            pay_b[at : at + CY] = jnp.where(even_x, sides[0], sides[1])
    back = jnp.concatenate([p[...] for p in pieces], axis=0)
    back_ref[...] = back
    if others:
        chips = ny * 2
        side = jnp.where(even_x, -chips, chips)
        total = lax.axis_size("gx") * ny
        for ref, at, target in (
            (pay_b, RIM_X, lax.rem(b0 + side + total, total)),
            (others[0], 0, lax.rem(b0 + 2 * chips, total)),
        ):
            for core in range(2):
                wanted = (target + core * ny).astype(F32)
                found = jnp.full((BACK, CZ), -1.0, F32)
                for k in range(back.shape[0] // BACK):
                    value = back[k * BACK : (k + 1) * BACK]
                    found = jnp.where(value[6:7, 0:1] == wanted, value, found)
                ref[at + core * BACK : at + (core + 1) * BACK] = found


def face_terms(buf, at, first, size, main_low, main_high, y_ref, rec_c, rec_d, rim_low, rim_high, even_y):
    half = 0.5 * DT_STEP
    visc = DT_STEP * NU_VISC
    part = slice(first, first + size)
    here = slice(at, at + size)
    half_of = main_low if first < CX // 2 else main_high
    inner = first % (CX // 2)
    for c in range(3):
        buf[c, here] = half_of[c, inner : inner + size]
        rows = slice(c * CX + first, c * CX + first + size)
        a, b = rec_c[rows], jnp.where(odd_side(), rec_d[rows], 0.0)
        low = [jnp.where(even_y, b, a) * (visc + half * y_ref[0, part]), 0.0]
        high = [0.0, jnp.where(even_y, a, b) * (visc - half * y_ref[1, part])]
        for i in range(2):
            row = (i * 3 + c) * YROWS + first
            buf[c, here, i, :] += rim_low[row : row + size] + low[i]
            buf[c, here, CY - 2 + i, :] += rim_high[row : row + size] + high[i]


INNER = [(2, CHUNK - 2)] + [(k * CHUNK, CHUNK) for k in range(1, N_CHUNK - 1)] + [(CX - CHUNK, CHUNK - 2)]


def chunk_copy(buf, at, out_ref, first, size, sem):
    return pltpu.make_async_copy(buf.at[:, pl.ds(at, size)], out_ref.at[:, pl.ds(first, size)], sem)


def inside_body(main_low, main_high, y_ref, rec_c, rec_d, rim_low, rim_high, out_ref, buf, sems):
    _, even_y, _, _, _, _ = place()
    copies = []
    for k, (first, size) in enumerate(INNER):
        face_terms(buf, first - 2, first, size, main_low, main_high, y_ref, rec_c, rec_d, rim_low, rim_high, even_y)
        copies.append(chunk_copy(buf, first - 2, out_ref, first, size, sems.at[k]))
        copies[-1].start()
    for copy in copies:
        copy.wait()


def final_body(n_ret, _, main_low, main_high, x_ref, y_ref, face_a, face_b, rec_c, rec_d, rim_a, rim_b, rim_low, rim_high, back_ref, *rest):
    rets, (out_ref, pf_ref, buf, sems) = rest[:n_ret], rest[n_ret:]
    even_x, even_y, inner, brick, _, _ = place()
    half = 0.5 * DT_STEP
    visc = DT_STEP * NU_VISC
    copies = []
    for k in range(2):
        first, at = k * (CX - 2), k * 2
        face_terms(buf, at, first, 2, main_low, main_high, y_ref, rec_c, rec_d, rim_low, rim_high, even_y)
        for c in range(3):
            a = face_a[c * XROWS : c * XROWS + CY]
            b = jnp.where(inner, face_b[c * XROWS : c * XROWS + CY], 0.0)
            if k == 0:
                buf[c, 0] += jnp.where(even_x, b, a) * (visc + half * x_ref[0])
            else:
                buf[c, 3] += jnp.where(even_x, a, b) * (visc - half * x_ref[3])
            for i in range(2):
                rows = slice((i * 3 + c) * CY, (i * 3 + c + 1) * CY)
                a, b = rim_a[rows], jnp.where(inner, rim_b[rows], 0.0)
                if k == 0:
                    buf[c, i] += jnp.where(even_x, b, a)
                else:
                    buf[c, 2 + i] += jnp.where(even_x, a, b)
        copies.append(chunk_copy(buf, at, out_ref, first, 2, sems.at[k]))
        copies[-1].start()
    mine = brick.astype(F32)
    found = jnp.zeros((BACK, CZ), F32)
    for ref, first in [(back_ref, 0), (rim_b, RIM_X)] + [(r, 0) for r in rets]:
        for k in range((ref.shape[0] - first) // BACK):
            value = ref[first + BACK * k : first + BACK * k + BACK]
            found = jnp.where(value[6:7, 0:1] == mine, value, found)
    for c in range(3):
        pf_ref[c : c + 1] = jnp.concatenate([found[2 * c : 2 * c + 1], found[2 * c + 1 : 2 * c + 2]], axis=1)
    for copy in copies:
        copy.wait()


def per_device(
    velocity,
    host_cell,
    host_frac,
    host_dst,
    owner_src,
    rotor_speed,
    blade_radius,
    blade_chord,
    blade_twist,
    blade_angle,
):
    nx, ny = lax.axis_size("gx"), lax.axis_size("gy")
    ring, short = nx == 8, ny == 4

    def flip(n, bits):
        return [(i, i ^ bits) for i in range(n)]

    def odd_pairs(n, closed=False):
        up = [(i, (i + 1) % n) for i in range(1, n if closed else n - 1, 2)]
        return up + [(t, s) for s, t in up]

    def same_side(n):
        return [(i, (i + (2 if i % 2 else n - 2)) % n) for i in range(n)]

    def across_x(blocks):
        return [lax.ppermute(b, "gx", p) for b, p in zip(blocks, (flip(nx, 4), same_side(nx)))]

    def swap(block):
        return lax.ppermute(block, "gx", flip(nx, 1))

    def join(pieces):
        return pieces[0] if len(pieces) == 1 else jnp.concatenate(pieces, axis=0)

    def after(values, other):
        return lax.optimization_barrier((values, other))

    def gather_y(first):
        pieces = [first]
        for bit in [b for b in (2, 4, 8) if b < ny]:
            pieces.append(lax.ppermute(join(pieces), "gy", flip(ny, bit)))
        return pieces

    def exchange_y(to_c, to_d, block):
        from_c = lax.ppermute(to_c, "gy", flip(ny, 1))
        from_d = lax.ppermute(to_d, "gy", flip(ny, 3) if short else odd_pairs(ny))
        return from_c, from_d, [lax.ppermute(block, "gy", flip(ny, 2))] if short else []

    def blocks_y(block, from_c, from_d, far, size, at):
        got = join([block, from_c[at : at + size]])
        if short:
            return [join([got, from_d[at : at + size]] + far)]
        return gather_y(got)

    def gather_x(blocks):
        pieces = []
        for bit in [b for b in (2, 4, 8, 16) if b < nx]:
            pieces.append(lax.ppermute(join([blocks] + pieces), "gx", flip(nx, bit)))
        return pieces

    dma = pltpu.SemaphoreType.DMA
    pay_c, pay_d, block = call(
        pack_body,
        [(FACE_Y + ROWS, CZ)] * 2 + [(ROWS, CZ)],
        7,
        "pack",
        scratch=[pltpu.VMEM((4, 2, CZ), F32), pltpu.VMEM((2, CZ), jnp.int32), pltpu.VMEM((ROWS, CZ), F32), pltpu.SMEM((1,), F32), dma((15,))],
        in_specs=[HB] * 7,
        out_specs=[HB] * 3,
        vmem=56,
    )(velocity, rotor_speed, *[a.reshape(2, CZ) for a in (blade_radius, blade_chord, blade_twist, blade_angle, owner_src)])
    rec_c, rec_d, far = exchange_y(pay_c, pay_d, block)

    def stencil(start):
        return call(lambda *refs: stencil_body(start, *refs), [(3, CX // 2, CY, CZ)], 1, "stencil")(
            velocity.reshape(3, CX * CY, CZ)
        )[0]

    base_low = stencil(0)
    table, sums, x_faces, y_faces = call(
        sample_low_body, [(HOST, CZ), (HOST, 3 * CZ), (6, CY, CZ), (2, CX, CZ)], 3, "sample_low", vmem=24
    )(velocity, host_cell, host_frac)
    (rec_c, rec_d, far), (base_low, sums) = after((rec_c, rec_d, far), (base_low, sums))
    pieces = blocks_y(block, rec_c, rec_d, far, ROWS, FACE_Y)
    beside = [swap(p) for p in pieces]
    beside, base_high = after(beside, stencil(CX // 2))
    pieces = pieces + beside
    n_rows = 2 * ny * ROWS
    pair = (2 * ROWS, CZ)
    pay_a, pay_b, blocks, *across = call(
        lambda *refs: xpack_body(len(pieces), *refs),
        [(FACE_X, CZ), (FACE_X + 2 * ROWS, CZ), pair, pair, pair] if ring else [(FACE_X, CZ), (FACE_X, CZ), (n_rows, CZ)],
        3 + len(pieces),
        "xpack",
    )(x_faces, rec_c, rec_d, *pieces)
    face_b = lax.ppermute(pay_b, "gx", odd_pairs(nx, ring))
    from_x = across_x(across) if ring else gather_x(blocks)
    face_a = swap(pay_a)
    sums = call(sample_high_body, [(HOST, 3 * CZ)], 3, "sample_high", vmem=24)(velocity, table, sums)[0]
    (face_a, face_b, from_x), sums = after((face_a, face_b, from_x), sums)
    samp, sel, pts = call(
        lambda *refs: select_body(len(from_x), *refs),
        [(8, PTS), (2 * ROWS, CZ), (PTS, CZ)],
        7 + len(from_x),
        "select",
    )(table, sums, face_a, face_b, rec_c, rec_d, blocks, *from_x)
    other = swap(samp)
    gx, gy, pz, pos, pair_kernel, edge = call(
        weights_body,
        [(YROWS, PTS), (CY, PTS), (PTS, CZ), (24, CZ), (2, P_SIZE, P_SIZE), (4 * CY, PTS)],
        2,
        "weights",
    )(pts, sel)
    lines, points, xrim = call(
        loads_body,
        [(PTS, 3 * CZ), (2 * BACK + 24, CZ), (2 * RIM_X, CZ)],
        7,
        "loads",
    )(samp, other, sel, pz, pos, pair_kernel, edge)
    ret = points[: 2 * BACK]
    near_c, near_d, far = exchange_y(points, points, ret)

    def spread(start, base):
        return call(
            lambda *refs: spread_body(start, *refs), [(3, CX // 2, CY, CZ)], 4, "spread"
        )(lines, gx, gy, base)[0]

    (near_c, near_d), main_low = after((near_c, near_d), spread(0, base_low))
    rim_low, rim_high = call(near_body, [(RIM_Y, CZ)] * 2, 2, "near")(near_c, near_d)
    far, rim_low = after(far, rim_low)
    pieces = blocks_y(ret, near_c, near_d, far, 2 * BACK, 0)
    n_rows = 2 * ny * BACK
    pair = (2 * BACK, CZ)
    pay_a, pay_b, back, *across = call(
        lambda *refs: rimpack_body(len(pieces), *refs),
        [(RIM_X, CZ), (RIM_X + 2 * BACK, CZ), (n_rows, CZ), pair] if ring else [(RIM_X, CZ), (RIM_X, CZ), (n_rows, CZ)],
        3 + len(pieces),
        "rimpack",
    )(xrim, rim_low, rim_high, *pieces)
    rim_b = lax.ppermute(pay_b, "gx", odd_pairs(nx, ring))
    rets = [lax.ppermute(across[0], "gx", flip(nx, 4))] if ring else gather_x(back)
    rim_a = swap(pay_a)
    main_high = spread(CX // 2, base_high)
    (rim_a, rim_b), (main_low, main_high) = after((rim_a, rim_b), (main_low, main_high))
    if ring:
        rets.append(swap(rim_b[RIM_X:]))
    inside = call(
        inside_body,
        [velocity.shape],
        7,
        "inside",
        scratch=[pltpu.VMEM((3, CX - 4, CY, CZ), F32), dma((N_CHUNK,))],
        out_specs=[HB],
        vmem=16,
    )(main_low, main_high, y_faces, rec_c, rec_d, rim_low, rim_high)[0]
    rets, inside = after(rets, inside)
    return tuple(
        call(
            lambda *refs: final_body(len(rets), *refs),
            [velocity.shape, (3, P_SIZE)],
            14 + len(rets),
            "final",
            scratch=[pltpu.VMEM((3, 4, CY, CZ), F32), dma((2,))],
            first=HB,
            out_specs=[HB, VM],
            aliases={0: 0},
        )(inside, main_low, main_high, x_faces, y_faces, face_a, face_b, rec_c, rec_d, rim_a, rim_b, rim_low, rim_high, back, *rets)
    )


def solution(mesh):
    return jax.shard_map(
        per_device,
        mesh=mesh,
        in_specs=(
            P(None, "gx", "gy", None),
            P(None, ("gx", "gy")),
            P(None, ("gx", "gy")),
            P(("gx", "gy")),
            P(("gx", "gy")),
            P(("gx", "gy")),
            P(("gx", "gy")),
            P(("gx", "gy")),
            P(("gx", "gy")),
            P(("gx", "gy")),
        ),
        out_specs=(P(None, "gx", "gy", None), P(None, ("gx", "gy"))),
        check_vma=False,
    )
```

```python
import math

import jax
import jax.numpy as jnp
from jax import lax
from jax.experimental import pallas as pl
from jax.experimental.pallas import tpu as pltpu
from jax.sharding import PartitionSpec as P

CX = 64
CY = 32
CZ = 128
P_SIZE = 256
HOST = 512
PTS = 2 * P_SIZE

DT_STEP = 0.2
NU_VISC = 0.5
EPS_SQ = 1.44
CORE_SQ = 0.01

ROWS = 16
BACK = 8
YROWS = 72
XROWS = 40
FACE_Y = 3 * CX
FACE_X = 3 * XROWS
RIM_Y = 2 * 3 * YROWS
RIM_X = 2 * 3 * CY
CHUNK = 8
N_CHUNK = CX // CHUNK

F32 = jnp.float32
BF16 = jnp.bfloat16
VM = pl.BlockSpec(memory_space=pltpu.MemorySpace.VMEM)
SM = pl.BlockSpec(memory_space=pltpu.MemorySpace.SMEM)
HB = pl.BlockSpec(memory_space=pltpu.MemorySpace.HBM)
MIB = 1024 * 1024


def call(body, outs, n_in, name, scratch=(), first=VM, second=VM, out_specs=None, in_specs=None, vmem=12, aliases=None):
    return pl.pallas_call(
        body,
        out_shape=[jax.ShapeDtypeStruct(s, F32) for s in outs],
        in_specs=in_specs or ([first, second] + [VM] * n_in)[:n_in],
        out_specs=out_specs or [VM] * len(outs),
        scratch_shapes=list(scratch),
        input_output_aliases=aliases or {},
        compiler_params=pltpu.CompilerParams(vmem_limit_bytes=vmem * MIB),
        name=name,
    )


def place():
    nx, ny = lax.axis_size("gx"), lax.axis_size("gy")
    ix, iy = lax.axis_index("gx"), lax.axis_index("gy")
    px, py = lax.rem(ix, 2), lax.rem(iy, 2)
    inner = (ix + px > 0) & (ix + px < nx)
    return px == 0, py == 0, inner, ix * ny + iy, (ix - px) * ny + iy, ny


def odd_side():
    ny, iy = lax.axis_size("gy"), lax.axis_index("gy")
    py = lax.rem(iy, 2)
    return (iy + py > 0) & (iy + py < ny)


def split(value):
    high = value.astype(BF16)
    low = (value - high.astype(F32)).astype(BF16)
    return high, low


def dot3(a_high, a_low, b_high, b_low):
    def one(a, b):
        return jnp.dot(a, b, preferred_element_type=F32)

    return one(a_high, b_high) + (one(a_high, b_low) + one(a_low, b_high))


def reduce_list(items, op):
    result = items[0]
    for item in items[1:]:
        result = op(result, item)
    return result


def pack_body(v_ref, spin_hbm, *rest):
    params, (pay_c, pay_d, blk_ref, held, held_int, spin_ref, sems) = rest[:5], rest[5:]
    _, even_y, _, brick, _, _ = place()

    def faces(first, second):
        made = []
        for k, (ref, y) in enumerate(((pay_c, first), (pay_d, second))):
            for c in range(3):
                made.append(pltpu.make_async_copy(v_ref.at[c, :, y], ref.at[pl.ds(c * CX, CX)], sems.at[3 * k + c]))
        return made

    @pl.when(even_y)
    def _():
        for copy in faces(CY - 1, 0):
            copy.start()

    @pl.when(jnp.logical_not(even_y))
    def _():
        for copy in faces(0, CY - 1):
            copy.start()

    small = [pltpu.make_async_copy(spin_hbm, spin_ref, sems.at[6])]
    small += [pltpu.make_async_copy(p, held.at[k], sems.at[7 + k]) for k, p in enumerate(params[:4])]
    small.append(pltpu.make_async_copy(params[4], held_int, sems.at[11]))
    for copy in small:
        copy.start()
    for copy in small:
        copy.wait()
    radius, chord, twist, angle = [held[k] for k in range(4)]
    parts = [
        radius,
        chord,
        jnp.cos(twist),
        jnp.sin(twist),
        jnp.cos(angle),
        jnp.sin(angle),
        held_int[...].astype(F32),
        jnp.full((1, CZ), spin_ref[0], F32),
        jnp.full((1, CZ), brick.astype(F32), F32),
    ]
    block = jnp.concatenate(parts, axis=0)
    blk_ref[...] = block
    pay_c[FACE_Y:] = block
    pay_d[FACE_Y:] = block
    for copy in faces(0, 0):
        copy.wait()


def stencil_body(start, v_ref, out_ref):
    row = lax.broadcasted_iota(jnp.int32, (CY, CZ), 0)
    lane = lax.broadcasted_iota(jnp.int32, (CY, CZ), 1)
    half = 0.5 * DT_STEP
    visc = DT_STEP * NU_VISC
    not_last_y, not_first_y = row < CY - 1, row > 0
    not_last_z, not_first_z = lane < CZ - 1, lane > 0

    def step(k, carry):
        x = start + k
        up = jnp.minimum(x + 1, CX - 1)
        down = jnp.maximum(x - 1, 0)
        v0, v1, v2 = v_ref[0, x], v_ref[1, x], v_ref[2, x]
        a_x = jnp.where(x < CX - 1, visc - half * v0, 0.0)
        b_x = jnp.where(x > 0, visc + half * v0, 0.0)
        a_y = jnp.where(not_last_y, visc - half * v1, 0.0)
        b_y = jnp.where(not_first_y, visc + half * v1, 0.0)
        a_z = jnp.where(not_last_z, visc - half * v2, 0.0)
        b_z = jnp.where(not_first_z, visc + half * v2, 0.0)
        for c in range(3):
            mid = (v0, v1, v2)[c]
            along_x = a_x * v_ref[c, up] + b_x * v_ref[c, down]
            along_y = a_y * pltpu.roll(mid, CY - 1, 0) + b_y * pltpu.roll(mid, 1, 0)
            along_z = a_z * pltpu.roll(mid, CZ - 1, 1) + b_z * pltpu.roll(mid, 1, 1)
            out_ref[c, k] = (1.0 - 6.0 * visc) * mid + along_x + (along_y + along_z)
        return carry

    lax.fori_loop(0, CX // 2, step, 0, unroll=2)


def weight(coord, base, frac):
    return jnp.where(coord == base, 1.0 - frac, jnp.where(coord == base + 1, frac, 0.0))


def sample_part(start, v_ref, table, acc):
    x_col, y_col = [table[:, k : k + 1].astype(jnp.int32) for k in range(2)]
    fx, fy = [table[:, k : k + 1] for k in range(3, 5)]
    lane = lax.broadcasted_iota(jnp.int32, (HOST, CZ), 1)
    wy = weight(lane % CY, y_col, fy)
    x_lane = (lane // CY + start - x_col).astype(F32).astype(BF16)
    near, far = split((1.0 - fx) * wy), split(fx * wy)
    zero = jnp.zeros((HOST, CZ), BF16)
    per = 4
    nx = CZ * per // CY
    for j in range(CX // 2 // nx):
        highs, lows = [], []
        for i in range(per):
            shift = (CZ // CY) * (j * per + i)
            at_base, at_next = x_lane == jnp.bfloat16(-shift), x_lane == jnp.bfloat16(1 - shift)
            highs.append(jnp.where(at_base, near[0], jnp.where(at_next, far[0], zero)))
            lows.append(jnp.where(at_base, near[1], jnp.where(at_next, far[1], zero)))
        w_high, w_low = jnp.concatenate(highs, axis=1), jnp.concatenate(lows, axis=1)
        first = start + j * nx
        field = [v_ref[c, first : first + nx].reshape(nx * CY, CZ) for c in range(3)]
        f_high, f_low = split(jnp.concatenate(field, axis=1))
        part = dot3(w_high, w_low, f_high, f_low)
        acc = part if acc is None else acc + part
    return acc


def sample_low_body(v_ref, cell_ref, frac_ref, tab_ref, acc_ref, x_ref, y_ref):
    for c in range(3):
        x_ref[c] = v_ref[c, 0]
        x_ref[c + 3] = v_ref[c, CX - 1]
    y_ref[0] = v_ref[1, :, 0, :]
    y_ref[1] = v_ref[1, :, CY - 1, :]
    rows = jnp.concatenate([cell_ref[...].astype(F32), frac_ref[...], jnp.zeros((CZ - 6, HOST), F32)], axis=0)
    table = rows.T
    tab_ref[...] = table
    acc_ref[...] = sample_part(0, v_ref, table, None)


def sample_high_body(v_ref, tab_ref, low_ref, acc_ref):
    acc_ref[...] = sample_part(CX // 2, v_ref, tab_ref[...], low_ref[...])


def split_blocks(sources):
    return [
        ref[first + k * ROWS : first + (k + 1) * ROWS]
        for ref, first in sources
        for k in range((ref.shape[0] - first) // ROWS)
    ]


def pick_pair(values, b0, ny):
    keys = [value[12:13, 0:1] for value in values]
    members = []
    for key in keys:
        home = jnp.floor(key * (1.0 / HOST)).astype(jnp.int32)
        members.append((home == b0) | (home == b0 + ny))
    low_key = reduce_list([jnp.where(m, k, 1e9) for k, m in zip(keys, members)], jnp.minimum)
    high_key = reduce_list([jnp.where(m, k, -9.0) for k, m in zip(keys, members)], jnp.maximum)
    low = jnp.full((ROWS, CZ), -1.0, F32)
    high = low
    for key, value in zip(keys, values):
        low = jnp.where(key == low_key, value, low)
        high = jnp.where(key == high_key, value, high)
    return low, high


def xpack_body(n_blk, x_ref, rec_c, rec_d, *rest):
    pieces, (pay_a, pay_b, own_ref, *others) = rest[:n_blk], rest[n_blk:]
    even_x, even_y, inner, _, b0, ny = place()
    for c in range(3):
        at = c * CX
        y_high = jnp.where(even_y, rec_c[at : at + 1], jnp.where(odd_side(), rec_d[at : at + 1], 0.0))
        tail = jnp.concatenate([y_high, jnp.zeros((XROWS - CY - 1, CZ), F32)], axis=0)
        low, high = x_ref[c], x_ref[c + 3]
        at = c * XROWS
        pay_a[at : at + CY] = jnp.where(even_x, high, low)
        pay_b[at : at + CY] = jnp.where(even_x, low, high)
        pay_a[at + CY : at + XROWS] = tail
        pay_b[at + CY : at + XROWS] = tail
    if not others:
        own_ref[...] = jnp.concatenate([p[...] for p in pieces], axis=0)
        return
    values = split_blocks([(p, 0) for p in pieces])
    chips = ny * 2
    side = jnp.where(even_x, -chips, chips)
    total = lax.axis_size("gx") * ny
    own_ref[...] = jnp.concatenate(pick_pair(values, b0, ny), axis=0)
    beside = jnp.concatenate(pick_pair(values, lax.rem(b0 + side + total, total), ny), axis=0)
    pay_b[FACE_X:] = beside
    others[1][...] = beside
    others[0][...] = jnp.concatenate(pick_pair(values, lax.rem(b0 + 2 * chips, total), ny), axis=0)


def select_body(n_blk, tab_ref, acc_ref, face_a, face_b, rec_c, rec_d, blk_ref, *rest):
    others, (samp_ref, sel_ref, pts_ref) = rest[:n_blk], rest[n_blk:]
    even_x, even_y, inner, brick, b0, ny = place()
    sources = [(blk_ref, 0), (face_b, FACE_X)] + [(o, 0) for o in others]
    turbine_a, turbine_b = pick_pair(split_blocks(sources), b0, ny)
    sel = jnp.concatenate([turbine_a, turbine_b], axis=0)
    sel_ref[...] = sel
    turned = jnp.concatenate([sel, jnp.zeros((CZ - 2 * ROWS, CZ), F32)], axis=0).T

    def column(k):
        picks = (2 * k, 2 * k + 1, ROWS + 2 * k, ROWS + 2 * k + 1)
        return jnp.concatenate([turned[:, j : j + 1] for j in picks], axis=0)

    table = tab_ref[...]
    lane = lax.broadcasted_iota(jnp.int32, (PTS, CZ), 1)
    x_col, y_col, z_col = [table[:, k : k + 1].astype(jnp.int32) for k in range(3)]
    fx, fy, fz = [table[:, k : k + 1] for k in range(3, 6)]
    on_line = lane >= CX
    edge_x = jnp.where(on_line, lane - CX, CX)
    edge_y = jnp.where(on_line, CY, lane)
    edge_w = jnp.where(on_line | (lane <= CY), weight(edge_x, x_col, fx) * weight(edge_y, y_col, fy), 0.0)
    field = []
    for c in range(3):
        at = c * XROWS
        past = jnp.where(inner, face_b[at : at + XROWS], 0.0)
        plane = jnp.where(even_x, face_a[at : at + XROWS], past)
        at = c * CX
        line = jnp.where(even_y, rec_c[at : at + CX], jnp.where(odd_side(), rec_d[at : at + CX], 0.0))
        field.append(jnp.concatenate([plane, jnp.zeros((CX - XROWS, CZ), F32), line], axis=0))
    w_high, w_low = split(edge_w)
    f_high, f_low = split(jnp.concatenate(field, axis=1))
    acc = acc_ref[...] + dot3(w_high, w_low, f_high, f_low)
    wz = weight(lane, z_col, fz)
    for c in range(3):
        value = jnp.sum(acc[:, c * CZ : (c + 1) * CZ] * wz, axis=1, keepdims=True)
        table = table + jnp.where(lane == 6 + c, value, 0.0)
    slot = column(6).astype(jnp.int32)
    mine = (slot // HOST) == brick
    local = jnp.where(mine, slot % HOST, -1)
    hit = (lax.broadcasted_iota(jnp.int32, (PTS, HOST), 1) == local).astype(F32).astype(BF16)
    first, second = split(table)
    third = (table - first.astype(F32) - second.astype(F32)).astype(BF16)
    pulled = [jnp.dot(hit, part, preferred_element_type=F32) for part in (first, second, third)]
    points = pulled[0] + pulled[1] + pulled[2]
    points = jnp.where(lane == 9, column(0), points)
    pts_ref[...] = jnp.where((lane == 0) & jnp.logical_not(mine), -100.0, points)
    samp_ref[...] = points.T[6:14]


def offsets(frac):
    raw = [jnp.exp(-((o - frac) ** 2) / EPS_SQ) for o in (-1.0, 0.0, 1.0, 2.0)]
    total = (raw[0] + raw[1]) + (raw[2] + raw[3])
    return [value / total for value in raw]


def profile(rows, inner, base, frac):
    index = lax.broadcasted_iota(jnp.int32, (rows, PTS), 0)
    late = index - inner
    index = jnp.where(index < inner, index, jnp.where(late < 2, late - 2, late - 2 + inner))
    rel = index - base.astype(jnp.int32)
    result = jnp.zeros((rows, PTS), F32)
    for k, w in enumerate(offsets(frac)):
        result = jnp.where(rel == k - 1, w, result)
    return result


def line_profile(base, frac, extra):
    stack = jnp.concatenate(offsets(frac) + [base] + extra + [jnp.zeros((CZ - 5 - len(extra), PTS), F32)], axis=0).T
    rel = lax.broadcasted_iota(jnp.int32, (PTS, CZ), 1) - stack[:, 4:5].astype(jnp.int32)
    result = jnp.zeros((PTS, CZ), F32)
    for k in range(4):
        result = jnp.where(rel == k - 1, stack[:, k : k + 1], result)
    return result, [stack[:, 5 + k : 6 + k] for k in range(len(extra))]


def weights_body(pts_ref, sel_ref, gx_ref, gy_ref, pz_ref, pos_ref, pair_ref, edge_ref):
    table = pts_ref[...].T
    gx = profile(YROWS, CX, table[0:1], table[3:4])
    gy = profile(CY, CY, table[1:2], table[4:5])
    gx_ref[...] = gx
    gy_ref[...] = gy
    pz_ref[...] = line_profile(table[2:3], table[5:6], [])[0] * DT_STEP
    pos_ref[...] = jnp.concatenate([table[q : q + 1, k * CZ : (k + 1) * CZ] for q in range(6) for k in range(4)], axis=0)
    for t in range(2):
        at = t * ROWS
        radius = jnp.concatenate([sel_ref[at : at + 1], sel_ref[at + 1 : at + 2]], axis=1)
        spacing = radius - pts_ref[t * P_SIZE : (t + 1) * P_SIZE, 9:10]
        pair_ref[t] = spacing / (spacing * spacing + CORE_SQ)
    for k in range(4):
        edge_ref[k * CY : (k + 1) * CY] = gx[CX + k : CX + k + 1] * gy


def attack(axial_flow, tangent, cos_twist, sin_twist):
    rel_speed = jnp.sqrt(axial_flow * axial_flow + tangent * tangent + 1.0)
    cos_phi = tangent / rel_speed
    sin_phi = axial_flow / rel_speed
    sin_alpha = sin_phi * cos_twist - cos_phi * sin_twist
    cos_alpha = cos_phi * cos_twist + sin_phi * sin_twist
    lift_coef = 2.0 * jnp.pi * sin_alpha * cos_alpha / (1.0 + 4.0 * sin_alpha * sin_alpha)
    drag_coef = 0.02 + 0.8 * sin_alpha * sin_alpha
    return rel_speed, cos_phi, sin_phi, lift_coef, drag_coef


def loads_body(samp_ref, other_ref, sel_ref, pz_ref, pos_ref, pair_ref, edge_ref, lh_ref, pay_ref, xrim_ref):
    def row(k):
        picks = (2 * k, 2 * k + 1, ROWS + 2 * k, ROWS + 2 * k + 1)
        return jnp.concatenate([sel_ref[j : j + 1] for j in picks], axis=1)

    radius, chord, cos_t, sin_t, cos_a, sin_a = [row(k) for k in range(6)]
    spin = radius * jnp.concatenate([sel_ref[j : j + 1] for j in (14, 14, ROWS + 14, ROWS + 14)], axis=1)
    flow = samp_ref[...] + other_ref[...]
    axial = flow[0:1]
    tangent = spin - (cos_a * flow[2:3] - sin_a * flow[1:2])
    rel_speed, cos_phi, sin_phi, lift_coef, drag_coef = attack(axial, tangent, cos_t, sin_t)
    circ = 0.5 * chord * rel_speed * lift_coef
    parts = []
    for t in range(2):
        seg = slice(t * P_SIZE, (t + 1) * P_SIZE)
        lhs = jnp.concatenate([cos_a[:, seg] * circ[:, seg], sin_a[:, seg] * circ[:, seg], jnp.zeros((6, P_SIZE), F32)], axis=0)
        both = jnp.dot(lhs, pair_ref[t], preferred_element_type=F32, precision=lax.Precision.HIGHEST)
        parts.append((cos_a[:, seg] * both[0:1] + sin_a[:, seg] * both[1:2]) / (4.0 * math.pi))
    induced = jnp.concatenate(parts, axis=1)
    rel_speed, cos_phi, sin_phi, lift_coef, drag_coef = attack(axial + induced, tangent, cos_t, sin_t)
    dynamic = 0.5 * chord * rel_speed * rel_speed
    lift = dynamic * lift_coef
    drag = dynamic * drag_coef
    thrust = lift * cos_phi + drag * sin_phi
    torque = lift * sin_phi - drag * cos_phi
    force = [-thrust, torque * sin_a, -torque * cos_a]
    pieces = []
    for t in range(2):
        for c in range(3):
            for h in range(2):
                at = t * P_SIZE + h * CZ
                pieces.append(force[c][:, at : at + CZ])
        pieces += [sel_ref[t * ROWS + 15 : t * ROWS + 16] + 1.0] * 2
    blocks = jnp.concatenate(pieces, axis=0)
    pay_ref[0 : 2 * BACK] = blocks
    pay_ref[2 * BACK :] = pos_ref[...]
    cols = jnp.concatenate(force + [jnp.zeros((CZ - 3, PTS), F32)], axis=0).T
    pz = pz_ref[...]
    lines = jnp.concatenate([cols[:, c : c + 1] * pz for c in range(3)], axis=1)
    l_high, l_low = split(lines)
    lh_ref[...] = lines
    w_high, w_low = split(edge_ref[...])
    rim = dot3(w_high, w_low, l_high, l_low)
    for k in range(4):
        for c in range(3):
            at = (k * 3 + c) * CY
            xrim_ref[at : at + CY] = rim[k * CY : (k + 1) * CY, c * CZ : (c + 1) * CZ]


def near_body(rec_c, rec_d, low_ref, high_ref):
    _, even_y, _, _, _, _ = place()
    c_all, d_all = rec_c[...], jnp.where(odd_side(), rec_d[...], 0.0)
    for side, out_ref in ((0, low_ref), (1, high_ref)):
        got = jnp.where(even_y, d_all, c_all) if side == 0 else jnp.where(even_y, c_all, d_all)

        def wide(first, picks):
            return jnp.concatenate([got[first + j : first + j + 1] for j in picks], axis=1)

        x, y, z, fx, fy, fz = [wide(2 * BACK + 4 * q, range(4)) for q in range(6)]
        force = [wide(2 * c, (0, 1, BACK, BACK + 1)) * DT_STEP for c in range(3)]
        pz, columns = line_profile(z, fz, force)
        l_high, l_low = split(jnp.concatenate([col * pz for col in columns], axis=1))
        gx = profile(YROWS, CX, x, fx)
        wy = offsets(fy)
        planes = []
        for i in range(2):
            rel = (CY + i if side == 0 else i - 2) - y.astype(jnp.int32)
            gy = jnp.zeros((1, PTS), F32)
            for k in range(4):
                gy = jnp.where(rel == k - 1, wy[k], gy)
            planes.append(gx * gy)
        w_high, w_low = split(jnp.concatenate(planes, axis=0))
        rim = dot3(w_high, w_low, l_high, l_low)
        for i in range(2):
            for c in range(3):
                at = (i * 3 + c) * YROWS
                out_ref[at : at + YROWS] = rim[i * YROWS : (i + 1) * YROWS, c * CZ : (c + 1) * CZ]


SPREAD_X = 8


def spread_body(start, lines_ref, gx_ref, gy_ref, base_ref, out_ref):
    l_high, l_low = split(lines_ref[...])
    gy = gy_ref[0:CY]
    for k in range(out_ref.shape[1] // SPREAD_X):
        at = k * SPREAD_X
        first = start + at
        planes = jnp.concatenate([gx_ref[first + i : first + i + 1] * gy for i in range(SPREAD_X)], axis=0)
        w_high, w_low = split(planes)
        value = dot3(w_high, w_low, l_high, l_low)
        for c in range(3):
            part = value[:, c * CZ : (c + 1) * CZ].reshape(SPREAD_X, CY, CZ)
            out_ref[c, at : at + SPREAD_X] = base_ref[c, at : at + SPREAD_X] + part


def rimpack_body(n_blk, xrim_ref, low_ref, high_ref, *rest):
    pieces, (pay_a, pay_b, back_ref, *others) = rest[:n_blk], rest[n_blk:]
    even_x, even_y, inner, _, b0, ny = place()
    zero = jnp.zeros((CY - 4, CZ), F32)
    for k in range(2):
        for c in range(3):
            sides = []
            for s in range(2):
                near, far = [], []
                for y in range(2):
                    at = (y * 3 + c) * YROWS + CX + 2 * s + k
                    near.append(low_ref[at : at + 1])
                    far.append(high_ref[at : at + 1])
                at = ((2 * s + k) * 3 + c) * CY
                sides.append(xrim_ref[at : at + CY] + jnp.concatenate(near + [zero] + far, axis=0))
            at = (k * 3 + c) * CY
            pay_a[at : at + CY] = jnp.where(even_x, sides[1], sides[0])
            pay_b[at : at + CY] = jnp.where(even_x, sides[0], sides[1])
    back = jnp.concatenate([p[...] for p in pieces], axis=0)
    back_ref[...] = back
    if others:
        chips = ny * 2
        side = jnp.where(even_x, -chips, chips)
        total = lax.axis_size("gx") * ny
        closing = jnp.where(b0 < chips, total - chips, chips)
        for ref, at, target in (
            (pay_b, RIM_X, lax.rem(b0 + side + total, total)),
            (others[0], 0, lax.rem(b0 + jnp.where(even_x, 2 * chips, closing), total)),
        ):
            for core in range(2):
                wanted = (target + core * ny + 1).astype(F32)
                found = jnp.full((BACK, CZ), -1.0, F32)
                for k in range(back.shape[0] // BACK):
                    value = back[k * BACK : (k + 1) * BACK]
                    found = jnp.where(value[6:7, 0:1] == wanted, value, found)
                ref[at + core * BACK : at + (core + 1) * BACK] = found


def face_terms(buf, at, first, size, main_low, main_high, y_ref, rec_c, rec_d, rim_low, rim_high, even_y):
    half = 0.5 * DT_STEP
    visc = DT_STEP * NU_VISC
    part = slice(first, first + size)
    here = slice(at, at + size)
    half_of = main_low if first < CX // 2 else main_high
    inner = first % (CX // 2)
    for c in range(3):
        buf[c, here] = half_of[c, inner : inner + size]
        rows = slice(c * CX + first, c * CX + first + size)
        a, b = rec_c[rows], jnp.where(odd_side(), rec_d[rows], 0.0)
        low = [jnp.where(even_y, b, a) * (visc + half * y_ref[0, part]), 0.0]
        high = [0.0, jnp.where(even_y, a, b) * (visc - half * y_ref[1, part])]
        for i in range(2):
            row = (i * 3 + c) * YROWS + first
            buf[c, here, i, :] += rim_low[row : row + size] + low[i]
            buf[c, here, CY - 2 + i, :] += rim_high[row : row + size] + high[i]


INNER = [(2, CHUNK - 2)] + [(k * CHUNK, CHUNK) for k in range(1, N_CHUNK - 1)] + [(CX - CHUNK, CHUNK - 2)]


def chunk_copy(buf, at, out_ref, first, size, sem):
    return pltpu.make_async_copy(buf.at[:, pl.ds(at, size)], out_ref.at[:, pl.ds(first, size)], sem)


def low_body(lines_ref, gx_ref, gy_ref, base_ref, main_low, y_ref, rec_c, rec_d, rim_low, rim_high, main_ref, out_ref, buf, sems):
    _, even_y, _, _, _, _ = place()
    copies = []
    for k, (first, size) in enumerate(INNER[: N_CHUNK // 2]):
        face_terms(buf, first - 2, first, size, main_low, None, y_ref, rec_c, rec_d, rim_low, rim_high, even_y)
        copies.append(chunk_copy(buf, first - 2, out_ref, first, size, sems.at[k]))
        copies[-1].start()
    spread_body(CX // 2, lines_ref, gx_ref, gy_ref, base_ref, main_ref)
    for copy in copies:
        copy.wait()


def high_body(_, main_high, y_ref, rec_c, rec_d, rim_low, rim_high, out_ref, buf, sems):
    _, even_y, _, _, _, _ = place()
    copies = []
    for k, (first, size) in enumerate(INNER[N_CHUNK // 2 :]):
        at = first - CX // 2
        face_terms(buf, at, first, size, None, main_high, y_ref, rec_c, rec_d, rim_low, rim_high, even_y)
        copies.append(chunk_copy(buf, at, out_ref, first, size, sems.at[k]))
        copies[-1].start()
    for copy in copies:
        copy.wait()


def final_body(n_ret, _, main_low, main_high, x_ref, y_ref, face_a, face_b, rec_c, rec_d, rim_a, rim_b, rim_low, rim_high, back_ref, *rest):
    rets, (out_ref, pf_ref, buf, sems) = rest[:n_ret], rest[n_ret:]
    even_x, even_y, inner, brick, _, _ = place()
    half = 0.5 * DT_STEP
    visc = DT_STEP * NU_VISC
    copies = []
    for k in range(2):
        first, at = k * (CX - 2), k * 2
        face_terms(buf, at, first, 2, main_low, main_high, y_ref, rec_c, rec_d, rim_low, rim_high, even_y)
        for c in range(3):
            a = face_a[c * XROWS : c * XROWS + CY]
            b = jnp.where(inner, face_b[c * XROWS : c * XROWS + CY], 0.0)
            if k == 0:
                buf[c, 0] += jnp.where(even_x, b, a) * (visc + half * x_ref[0])
            else:
                buf[c, 3] += jnp.where(even_x, a, b) * (visc - half * x_ref[3])
            for i in range(2):
                rows = slice((i * 3 + c) * CY, (i * 3 + c + 1) * CY)
                a, b = rim_a[rows], jnp.where(inner, rim_b[rows], 0.0)
                if k == 0:
                    buf[c, i] += jnp.where(even_x, b, a)
                else:
                    buf[c, 2 + i] += jnp.where(even_x, a, b)
        copies.append(chunk_copy(buf, at, out_ref, first, 2, sems.at[k]))
        copies[-1].start()
    mine = (brick + 1).astype(F32)
    found = jnp.zeros((BACK, CZ), F32)
    for ref, first in [(back_ref, 0), (rim_b, RIM_X)] + [(r, 0) for r in rets]:
        for k in range((ref.shape[0] - first) // BACK):
            value = ref[first + BACK * k : first + BACK * k + BACK]
            found = jnp.where(value[6:7, 0:1] == mine, value, found)
    for c in range(3):
        pf_ref[c : c + 1] = jnp.concatenate([found[2 * c : 2 * c + 1], found[2 * c + 1 : 2 * c + 2]], axis=1)
    for copy in copies:
        copy.wait()


def per_device(
    velocity,
    host_cell,
    host_frac,
    host_dst,
    owner_src,
    rotor_speed,
    blade_radius,
    blade_chord,
    blade_twist,
    blade_angle,
):
    nx, ny = lax.axis_size("gx"), lax.axis_size("gy")
    ring, short = nx == 8, ny == 4

    def flip(n, bits):
        return [(i, i ^ bits) for i in range(n)]

    def odd_pairs(n, closed=False):
        up = [(i, (i + 1) % n) for i in range(1, n if closed else n - 1, 2)]
        return up + [(t, s) for s, t in up]

    def same_side(n):
        return [(i, (i + (2 if i % 2 else n - 2)) % n) for i in range(n)]

    def opposite(n):
        return [(i, (i + n // 2) % n) for i in range(0, n, 2)] + [(1, n - 1), (n - 1, 1)]

    def across_x(blocks):
        return [lax.ppermute(b, "gx", p) for b, p in zip(blocks, (flip(nx, 4), same_side(nx)))]

    def swap(block):
        return lax.ppermute(block, "gx", flip(nx, 1))

    def join(pieces):
        return pieces[0] if len(pieces) == 1 else jnp.concatenate(pieces, axis=0)

    def after(values, other):
        return lax.optimization_barrier((values, other))

    def gather_y(first):
        pieces = [first]
        for bit in [b for b in (2, 4, 8) if b < ny]:
            pieces.append(lax.ppermute(join(pieces), "gy", flip(ny, bit)))
        return pieces

    def exchange_y(to_c, to_d, block):
        from_c = lax.ppermute(to_c, "gy", flip(ny, 1))
        from_d = lax.ppermute(to_d, "gy", flip(ny, 3) if short else odd_pairs(ny))
        return from_c, from_d, [lax.ppermute(block, "gy", flip(ny, 2))] if short else []

    def blocks_y(block, from_c, from_d, far, size, at):
        got = join([block, from_c[at : at + size]])
        if short:
            return [join([got, from_d[at : at + size]] + far)]
        return gather_y(got)

    def gather_x(blocks):
        pieces = []
        for bit in [b for b in (2, 4, 8, 16) if b < nx]:
            pieces.append(lax.ppermute(join([blocks] + pieces), "gx", flip(nx, bit)))
        return pieces

    dma = pltpu.SemaphoreType.DMA
    pay_c, pay_d, block = call(
        pack_body,
        [(FACE_Y + ROWS, CZ)] * 2 + [(ROWS, CZ)],
        7,
        "pack",
        scratch=[pltpu.VMEM((4, 2, CZ), F32), pltpu.VMEM((2, CZ), jnp.int32), pltpu.SMEM((1,), F32), dma((12,))],
        in_specs=[HB] * 7,
        vmem=56,
    )(velocity, rotor_speed, *[a.reshape(2, CZ) for a in (blade_radius, blade_chord, blade_twist, blade_angle, owner_src)])
    rec_c, rec_d, far = exchange_y(pay_c, pay_d, block)

    def stencil(start):
        return call(lambda *refs: stencil_body(start, *refs), [(3, CX // 2, CY, CZ)], 1, "stencil")(velocity)[0]

    base_low = stencil(0)
    table, sums, x_faces, y_faces = call(
        sample_low_body, [(HOST, CZ), (HOST, 3 * CZ), (6, CY, CZ), (2, CX, CZ)], 3, "sample_low", vmem=24
    )(velocity, host_cell, host_frac)
    (rec_c, rec_d, far), (base_low, sums) = after((rec_c, rec_d, far), (base_low, sums))
    pieces = blocks_y(block, rec_c, rec_d, far, ROWS, FACE_Y)
    beside = [swap(p) for p in pieces]
    beside, base_high = after(beside, stencil(CX // 2))
    pieces = pieces + beside
    n_rows = 2 * ny * ROWS
    pair = (2 * ROWS, CZ)
    pay_a, pay_b, blocks, *across = call(
        lambda *refs: xpack_body(len(pieces), *refs),
        [(FACE_X, CZ), (FACE_X + 2 * ROWS, CZ), pair, pair, pair] if ring else [(FACE_X, CZ), (FACE_X, CZ), (n_rows, CZ)],
        3 + len(pieces),
        "xpack",
    )(x_faces, rec_c, rec_d, *pieces)
    face_b = lax.ppermute(pay_b, "gx", odd_pairs(nx, ring))
    from_x = across_x(across) if ring else gather_x(blocks)
    face_a = swap(pay_a)
    sums = call(sample_high_body, [(HOST, 3 * CZ)], 3, "sample_high", vmem=24)(velocity, table, sums)[0]
    (face_a, face_b, from_x), sums = after((face_a, face_b, from_x), sums)
    samp, sel, pts = call(
        lambda *refs: select_body(len(from_x), *refs),
        [(8, PTS), (2 * ROWS, CZ), (PTS, CZ)],
        7 + len(from_x),
        "select",
    )(table, sums, face_a, face_b, rec_c, rec_d, blocks, *from_x)
    other = swap(samp)
    gx, gy, pz, pos, pair_kernel, edge = call(
        weights_body,
        [(YROWS, PTS), (CY, PTS), (PTS, CZ), (24, CZ), (2, P_SIZE, P_SIZE), (4 * CY, PTS)],
        2,
        "weights",
    )(pts, sel)
    lines, points, xrim = call(
        loads_body,
        [(PTS, 3 * CZ), (2 * BACK + 24, CZ), (2 * RIM_X, CZ)],
        7,
        "loads",
    )(samp, other, sel, pz, pos, pair_kernel, edge)
    ret = points[: 2 * BACK]
    near_c, near_d, far = exchange_y(points, points, ret)

    def spread(start, base):
        return call(
            lambda *refs: spread_body(start, *refs), [(3, CX // 2, CY, CZ)], 4, "spread"
        )(lines, gx, gy, base)[0]

    (near_c, near_d), main_low = after((near_c, near_d), spread(0, base_low))
    rim_low, rim_high = call(near_body, [(RIM_Y, CZ)] * 2, 2, "near")(near_c, near_d)
    far, rim_low = after(far, rim_low)
    pieces = blocks_y(ret, near_c, near_d, far, 2 * BACK, 0)
    n_rows = 2 * ny * BACK
    pair = (2 * BACK, CZ)
    pay_a, pay_b, back, *across = call(
        lambda *refs: rimpack_body(len(pieces), *refs),
        [(RIM_X, CZ), (RIM_X + 2 * BACK, CZ), (n_rows, CZ), pair] if ring else [(RIM_X, CZ), (RIM_X, CZ), (n_rows, CZ)],
        3 + len(pieces),
        "rimpack",
    )(xrim, rim_low, rim_high, *pieces)
    rim_b = lax.ppermute(pay_b, "gx", odd_pairs(nx))
    rets = [lax.ppermute(across[0], "gx", opposite(nx))] if ring else gather_x(back)
    rim_a = swap(pay_a)
    faces = (y_faces, rec_c, rec_d, rim_low, rim_high)
    half_buf = pltpu.VMEM((3, CX // 2 - 2, CY, CZ), F32)
    main_high, inside = call(
        low_body,
        [(3, CX // 2, CY, CZ), velocity.shape],
        10,
        "low",
        scratch=[half_buf, dma((N_CHUNK // 2,))],
        out_specs=[VM, HB],
    )(lines, gx, gy, base_high, main_low, *faces)
    (rim_a, rim_b, rets), inside = after((rim_a, rim_b, rets), inside)
    if ring:
        rets.append(swap(join([rim_b[RIM_X:]] + rets)))
    inside = call(
        high_body,
        [velocity.shape],
        7,
        "high",
        scratch=[half_buf, dma((N_CHUNK // 2,))],
        first=HB,
        out_specs=[HB],
        aliases={0: 0},
    )(inside, main_high, *faces)[0]
    rets, inside = after(rets, inside)
    return tuple(
        call(
            lambda *refs: final_body(len(rets), *refs),
            [velocity.shape, (3, P_SIZE)],
            14 + len(rets),
            "final",
            scratch=[pltpu.VMEM((3, 4, CY, CZ), F32), dma((2,))],
            first=HB,
            out_specs=[HB, VM],
            aliases={0: 0},
        )(inside, main_low, main_high, x_faces, y_faces, face_a, face_b, rec_c, rec_d, rim_a, rim_b, rim_low, rim_high, back, *rets)
    )


def solution(mesh):
    return jax.shard_map(
        per_device,
        mesh=mesh,
        in_specs=(
            P(None, "gx", "gy", None),
            P(None, ("gx", "gy")),
            P(None, ("gx", "gy")),
            P(("gx", "gy")),
            P(("gx", "gy")),
            P(("gx", "gy")),
            P(("gx", "gy")),
            P(("gx", "gy")),
            P(("gx", "gy")),
            P(("gx", "gy")),
        ),
        out_specs=(P(None, "gx", "gy", None), P(None, ("gx", "gy"))),
        check_vma=False,
    )
```

```python
import math

import jax
import jax.numpy as jnp
from jax import lax
from jax.experimental import pallas as pl
from jax.experimental.pallas import tpu as pltpu
from jax.sharding import PartitionSpec as P

CX = 64
CY = 32
CZ = 128
P_SIZE = 256
HOST = 512
PTS = 2 * P_SIZE

DT_STEP = 0.2
NU_VISC = 0.5
EPS_SQ = 1.44
CORE_SQ = 0.01

ROWS = 16
BACK = 8
YROWS = 72
XROWS = 40
FACE_Y = 3 * CX
FACE_X = 3 * XROWS
RIM_Y = 2 * 3 * YROWS
RIM_X = 2 * 3 * CY
CHUNK = 8
N_CHUNK = CX // CHUNK

F32 = jnp.float32
BF16 = jnp.bfloat16
VM = pl.BlockSpec(memory_space=pltpu.MemorySpace.VMEM)
SM = pl.BlockSpec(memory_space=pltpu.MemorySpace.SMEM)
HB = pl.BlockSpec(memory_space=pltpu.MemorySpace.HBM)
MIB = 1024 * 1024


def call(body, outs, n_in, name, scratch=(), first=VM, second=VM, out_specs=None, in_specs=None, vmem=12, aliases=None):
    return pl.pallas_call(
        body,
        out_shape=[jax.ShapeDtypeStruct(s, F32) for s in outs],
        in_specs=in_specs or ([first, second] + [VM] * n_in)[:n_in],
        out_specs=out_specs or [VM] * len(outs),
        scratch_shapes=list(scratch),
        input_output_aliases=aliases or {},
        compiler_params=pltpu.CompilerParams(vmem_limit_bytes=vmem * MIB),
        name=name,
    )


def place():
    nx, ny = lax.axis_size("gx"), lax.axis_size("gy")
    ix, iy = lax.axis_index("gx"), lax.axis_index("gy")
    px, py = lax.rem(ix, 2), lax.rem(iy, 2)
    inner = (ix + px > 0) & (ix + px < nx)
    return px == 0, py == 0, inner, ix * ny + iy, (ix - px) * ny + iy, ny


def odd_side():
    ny, iy = lax.axis_size("gy"), lax.axis_index("gy")
    py = lax.rem(iy, 2)
    return (iy + py > 0) & (iy + py < ny)


def split(value):
    high = value.astype(BF16)
    low = (value - high.astype(F32)).astype(BF16)
    return high, low


def dot3(a_high, a_low, b_high, b_low):
    def one(a, b):
        return jnp.dot(a, b, preferred_element_type=F32)

    return one(a_high, b_high) + (one(a_high, b_low) + one(a_low, b_high))


def reduce_list(items, op):
    result = items[0]
    for item in items[1:]:
        result = op(result, item)
    return result


def pack_body(v_ref, spin_hbm, *rest):
    params, (pay_c, pay_d, blk_ref, held, held_int, spin_ref, sems) = rest[:5], rest[5:]
    _, even_y, _, brick, _, _ = place()

    def faces(first, second):
        made = []
        for k, (ref, y) in enumerate(((pay_c, first), (pay_d, second))):
            for c in range(3):
                made.append(pltpu.make_async_copy(v_ref.at[c, :, y], ref.at[pl.ds(c * CX, CX)], sems.at[3 * k + c]))
        return made

    @pl.when(even_y)
    def _():
        for copy in faces(CY - 1, 0):
            copy.start()

    @pl.when(jnp.logical_not(even_y))
    def _():
        for copy in faces(0, CY - 1):
            copy.start()

    small = [pltpu.make_async_copy(spin_hbm, spin_ref, sems.at[6])]
    small += [pltpu.make_async_copy(p, held.at[k], sems.at[7 + k]) for k, p in enumerate(params[:4])]
    small.append(pltpu.make_async_copy(params[4], held_int, sems.at[11]))
    for copy in small:
        copy.start()
    for copy in small:
        copy.wait()
    radius, chord, twist, angle = [held[k] for k in range(4)]
    parts = [
        radius,
        chord,
        jnp.cos(twist),
        jnp.sin(twist),
        jnp.cos(angle),
        jnp.sin(angle),
        held_int[...].astype(F32),
        jnp.broadcast_to(spin_ref[...], (1, CZ)),
        jnp.full((1, CZ), brick.astype(F32), F32),
    ]
    block = jnp.concatenate(parts, axis=0)
    blk_ref[...] = block
    pay_c[FACE_Y:] = block
    pay_d[FACE_Y:] = block
    for copy in faces(0, 0):
        copy.wait()


def stencil_body(start, v_ref, out_ref):
    row = lax.broadcasted_iota(jnp.int32, (CY, CZ), 0)
    lane = lax.broadcasted_iota(jnp.int32, (CY, CZ), 1)
    half = 0.5 * DT_STEP
    visc = DT_STEP * NU_VISC
    not_last_y, not_first_y = row < CY - 1, row > 0
    not_last_z, not_first_z = lane < CZ - 1, lane > 0

    def step(k, carry):
        x = start + k
        up = jnp.minimum(x + 1, CX - 1)
        down = jnp.maximum(x - 1, 0)
        v0, v1, v2 = v_ref[0, x], v_ref[1, x], v_ref[2, x]
        a_x = jnp.where(x < CX - 1, visc - half * v0, 0.0)
        b_x = jnp.where(x > 0, visc + half * v0, 0.0)
        a_y = jnp.where(not_last_y, visc - half * v1, 0.0)
        b_y = jnp.where(not_first_y, visc + half * v1, 0.0)
        a_z = jnp.where(not_last_z, visc - half * v2, 0.0)
        b_z = jnp.where(not_first_z, visc + half * v2, 0.0)
        for c in range(3):
            mid = (v0, v1, v2)[c]
            along_x = a_x * v_ref[c, up] + b_x * v_ref[c, down]
            along_y = a_y * pltpu.roll(mid, CY - 1, 0) + b_y * pltpu.roll(mid, 1, 0)
            along_z = a_z * pltpu.roll(mid, CZ - 1, 1) + b_z * pltpu.roll(mid, 1, 1)
            out_ref[c, k] = (1.0 - 6.0 * visc) * mid + along_x + (along_y + along_z)
        return carry

    lax.fori_loop(0, CX // 2, step, 0, unroll=2)


def weight(coord, base, frac):
    return jnp.where(coord == base, 1.0 - frac, jnp.where(coord == base + 1, frac, 0.0))


def sample_part(start, v_ref, table, acc):
    x_col, y_col = [table[:, k : k + 1].astype(jnp.int32) for k in range(2)]
    fx, fy = [table[:, k : k + 1] for k in range(3, 5)]
    lane = lax.broadcasted_iota(jnp.int32, (HOST, CZ), 1)
    wy = weight(lane % CY, y_col, fy)
    x_lane = (lane // CY + start - x_col).astype(F32).astype(BF16)
    near, far = split((1.0 - fx) * wy), split(fx * wy)
    zero = jnp.zeros((HOST, CZ), BF16)
    per = 4
    nx = CZ * per // CY
    for j in range(CX // 2 // nx):
        highs, lows = [], []
        for i in range(per):
            shift = (CZ // CY) * (j * per + i)
            at_base, at_next = x_lane == jnp.bfloat16(-shift), x_lane == jnp.bfloat16(1 - shift)
            highs.append(jnp.where(at_base, near[0], jnp.where(at_next, far[0], zero)))
            lows.append(jnp.where(at_base, near[1], jnp.where(at_next, far[1], zero)))
        w_high, w_low = jnp.concatenate(highs, axis=1), jnp.concatenate(lows, axis=1)
        first = start + j * nx
        field = [v_ref[c, first : first + nx].reshape(nx * CY, CZ) for c in range(3)]
        f_high, f_low = split(jnp.concatenate(field, axis=1))
        part = dot3(w_high, w_low, f_high, f_low)
        acc = part if acc is None else acc + part
    return acc


def sample_low_body(v_ref, cell_ref, frac_ref, tab_ref, acc_ref, x_ref, y_ref):
    for c in range(3):
        x_ref[c] = v_ref[c, 0]
        x_ref[c + 3] = v_ref[c, CX - 1]
    y_ref[0] = v_ref[1, :, 0, :]
    y_ref[1] = v_ref[1, :, CY - 1, :]
    rows = jnp.concatenate([cell_ref[...].astype(F32), frac_ref[...], jnp.zeros((CZ - 6, HOST), F32)], axis=0)
    table = rows.T
    tab_ref[...] = table
    acc_ref[...] = sample_part(0, v_ref, table, None)


def sample_high_body(v_ref, tab_ref, low_ref, acc_ref):
    acc_ref[...] = sample_part(CX // 2, v_ref, tab_ref[...], low_ref[...])


def split_blocks(sources):
    return [
        ref[first + k * ROWS : first + (k + 1) * ROWS]
        for ref, first in sources
        for k in range((ref.shape[0] - first) // ROWS)
    ]


def pick_pair(values, b0, ny):
    keys = [value[12:13, 0:1] for value in values]
    members = []
    for key in keys:
        home = jnp.floor(key * (1.0 / HOST)).astype(jnp.int32)
        members.append((home == b0) | (home == b0 + ny))
    low_key = reduce_list([jnp.where(m, k, 1e9) for k, m in zip(keys, members)], jnp.minimum)
    high_key = reduce_list([jnp.where(m, k, -9.0) for k, m in zip(keys, members)], jnp.maximum)
    low = jnp.full((ROWS, CZ), -1.0, F32)
    high = low
    for key, value in zip(keys, values):
        low = jnp.where(key == low_key, value, low)
        high = jnp.where(key == high_key, value, high)
    return low, high


def xpack_body(n_blk, x_ref, rec_c, rec_d, *rest):
    pieces, (pay_a, pay_b, own_ref, *others) = rest[:n_blk], rest[n_blk:]
    even_x, even_y, inner, _, b0, ny = place()
    for c in range(3):
        at = c * CX
        y_high = jnp.where(even_y, rec_c[at : at + 1], jnp.where(odd_side(), rec_d[at : at + 1], 0.0))
        tail = jnp.concatenate([y_high, jnp.zeros((XROWS - CY - 1, CZ), F32)], axis=0)
        low, high = x_ref[c], x_ref[c + 3]
        at = c * XROWS
        pay_a[at : at + CY] = jnp.where(even_x, high, low)
        pay_b[at : at + CY] = jnp.where(even_x, low, high)
        pay_a[at + CY : at + XROWS] = tail
        pay_b[at + CY : at + XROWS] = tail
    if not others:
        own_ref[...] = jnp.concatenate([p[...] for p in pieces], axis=0)
        return
    values = split_blocks([(p, 0) for p in pieces])
    chips = ny * 2
    side = jnp.where(even_x, -chips, chips)
    total = lax.axis_size("gx") * ny
    own_ref[...] = jnp.concatenate(pick_pair(values, b0, ny), axis=0)
    beside = jnp.concatenate(pick_pair(values, lax.rem(b0 + side + total, total), ny), axis=0)
    pay_b[FACE_X:] = beside
    others[1][...] = beside
    others[0][...] = jnp.concatenate(pick_pair(values, lax.rem(b0 + 2 * chips, total), ny), axis=0)


def select_body(n_blk, tab_ref, acc_ref, face_a, face_b, rec_c, rec_d, blk_ref, *rest):
    others, (samp_ref, sel_ref, pts_ref) = rest[:n_blk], rest[n_blk:]
    even_x, even_y, inner, brick, b0, ny = place()
    sources = [(blk_ref, 0), (face_b, FACE_X)] + [(o, 0) for o in others]
    turbine_a, turbine_b = pick_pair(split_blocks(sources), b0, ny)
    sel = jnp.concatenate([turbine_a, turbine_b], axis=0)
    sel_ref[...] = sel
    turned = jnp.concatenate([sel, jnp.zeros((CZ - 2 * ROWS, CZ), F32)], axis=0).T

    def column(k):
        picks = (2 * k, 2 * k + 1, ROWS + 2 * k, ROWS + 2 * k + 1)
        return jnp.concatenate([turned[:, j : j + 1] for j in picks], axis=0)

    table = tab_ref[...]
    lane = lax.broadcasted_iota(jnp.int32, (PTS, CZ), 1)
    x_col, y_col, z_col = [table[:, k : k + 1].astype(jnp.int32) for k in range(3)]
    fx, fy, fz = [table[:, k : k + 1] for k in range(3, 6)]
    on_line = lane >= CX
    edge_x = jnp.where(on_line, lane - CX, CX)
    edge_y = jnp.where(on_line, CY, lane)
    edge_w = jnp.where(on_line | (lane <= CY), weight(edge_x, x_col, fx) * weight(edge_y, y_col, fy), 0.0)
    field = []
    for c in range(3):
        at = c * XROWS
        past = jnp.where(inner, face_b[at : at + XROWS], 0.0)
        plane = jnp.where(even_x, face_a[at : at + XROWS], past)
        at = c * CX
        line = jnp.where(even_y, rec_c[at : at + CX], jnp.where(odd_side(), rec_d[at : at + CX], 0.0))
        field.append(jnp.concatenate([plane, jnp.zeros((CX - XROWS, CZ), F32), line], axis=0))
    w_high, w_low = split(edge_w)
    f_high, f_low = split(jnp.concatenate(field, axis=1))
    acc = acc_ref[...] + dot3(w_high, w_low, f_high, f_low)
    wz = weight(lane, z_col, fz)
    for c in range(3):
        value = jnp.sum(acc[:, c * CZ : (c + 1) * CZ] * wz, axis=1, keepdims=True)
        table = table + jnp.where(lane == 6 + c, value, 0.0)
    slot = column(6).astype(jnp.int32)
    mine = (slot // HOST) == brick
    local = jnp.where(mine, slot % HOST, -1)
    hit = (lax.broadcasted_iota(jnp.int32, (PTS, HOST), 1) == local).astype(F32).astype(BF16)
    first, second = split(table)
    third = (table - first.astype(F32) - second.astype(F32)).astype(BF16)
    pulled = [jnp.dot(hit, part, preferred_element_type=F32) for part in (first, second, third)]
    points = pulled[0] + pulled[1] + pulled[2]
    points = jnp.where(lane == 9, column(0), points)
    pts_ref[...] = jnp.where((lane == 0) & jnp.logical_not(mine), -100.0, points)
    samp_ref[...] = points.T[6:14]


def offsets(frac):
    raw = [jnp.exp(-((o - frac) ** 2) / EPS_SQ) for o in (-1.0, 0.0, 1.0, 2.0)]
    total = (raw[0] + raw[1]) + (raw[2] + raw[3])
    return [value / total for value in raw]


def profile(rows, inner, base, frac):
    index = lax.broadcasted_iota(jnp.int32, (rows, PTS), 0)
    late = index - inner
    index = jnp.where(index < inner, index, jnp.where(late < 2, late - 2, late - 2 + inner))
    rel = index - base.astype(jnp.int32)
    result = jnp.zeros((rows, PTS), F32)
    for k, w in enumerate(offsets(frac)):
        result = jnp.where(rel == k - 1, w, result)
    return result


def line_profile(base, frac, extra):
    stack = jnp.concatenate(offsets(frac) + [base] + extra + [jnp.zeros((CZ - 5 - len(extra), PTS), F32)], axis=0).T
    rel = lax.broadcasted_iota(jnp.int32, (PTS, CZ), 1) - stack[:, 4:5].astype(jnp.int32)
    result = jnp.zeros((PTS, CZ), F32)
    for k in range(4):
        result = jnp.where(rel == k - 1, stack[:, k : k + 1], result)
    return result, [stack[:, 5 + k : 6 + k] for k in range(len(extra))]


def weights_body(pts_ref, sel_ref, gx_ref, gy_ref, pz_ref, pos_ref, pair_ref, edge_ref):
    table = pts_ref[...].T
    gx = profile(YROWS, CX, table[0:1], table[3:4])
    gy = profile(CY, CY, table[1:2], table[4:5])
    gx_ref[...] = gx
    gy_ref[...] = gy
    pz_ref[...] = line_profile(table[2:3], table[5:6], [])[0] * DT_STEP
    pos_ref[...] = jnp.concatenate([table[q : q + 1, k * CZ : (k + 1) * CZ] for q in range(6) for k in range(4)], axis=0)
    for t in range(2):
        at = t * ROWS
        radius = jnp.concatenate([sel_ref[at : at + 1], sel_ref[at + 1 : at + 2]], axis=1)
        spacing = radius - pts_ref[t * P_SIZE : (t + 1) * P_SIZE, 9:10]
        pair_ref[t] = spacing / (spacing * spacing + CORE_SQ)
    for k in range(4):
        edge_ref[k * CY : (k + 1) * CY] = gx[CX + k : CX + k + 1] * gy


def attack(axial_flow, tangent, cos_twist, sin_twist):
    rel_speed = jnp.sqrt(axial_flow * axial_flow + tangent * tangent + 1.0)
    cos_phi = tangent / rel_speed
    sin_phi = axial_flow / rel_speed
    sin_alpha = sin_phi * cos_twist - cos_phi * sin_twist
    cos_alpha = cos_phi * cos_twist + sin_phi * sin_twist
    lift_coef = 2.0 * jnp.pi * sin_alpha * cos_alpha / (1.0 + 4.0 * sin_alpha * sin_alpha)
    drag_coef = 0.02 + 0.8 * sin_alpha * sin_alpha
    return rel_speed, cos_phi, sin_phi, lift_coef, drag_coef


def loads_body(samp_ref, other_ref, sel_ref, pz_ref, pos_ref, pair_ref, edge_ref, lh_ref, pay_ref, xrim_ref):
    def row(k):
        picks = (2 * k, 2 * k + 1, ROWS + 2 * k, ROWS + 2 * k + 1)
        return jnp.concatenate([sel_ref[j : j + 1] for j in picks], axis=1)

    radius, chord, cos_t, sin_t, cos_a, sin_a = [row(k) for k in range(6)]
    spin = radius * jnp.concatenate([sel_ref[j : j + 1] for j in (14, 14, ROWS + 14, ROWS + 14)], axis=1)
    flow = samp_ref[...] + other_ref[...]
    axial = flow[0:1]
    tangent = spin - (cos_a * flow[2:3] - sin_a * flow[1:2])
    rel_speed, cos_phi, sin_phi, lift_coef, drag_coef = attack(axial, tangent, cos_t, sin_t)
    circ = 0.5 * chord * rel_speed * lift_coef
    parts = []
    for t in range(2):
        seg = slice(t * P_SIZE, (t + 1) * P_SIZE)
        lhs = jnp.concatenate([cos_a[:, seg] * circ[:, seg], sin_a[:, seg] * circ[:, seg], jnp.zeros((6, P_SIZE), F32)], axis=0)
        both = jnp.dot(lhs, pair_ref[t], preferred_element_type=F32, precision=lax.Precision.HIGHEST)
        parts.append((cos_a[:, seg] * both[0:1] + sin_a[:, seg] * both[1:2]) / (4.0 * math.pi))
    induced = jnp.concatenate(parts, axis=1)
    rel_speed, cos_phi, sin_phi, lift_coef, drag_coef = attack(axial + induced, tangent, cos_t, sin_t)
    dynamic = 0.5 * chord * rel_speed * rel_speed
    lift = dynamic * lift_coef
    drag = dynamic * drag_coef
    thrust = lift * cos_phi + drag * sin_phi
    torque = lift * sin_phi - drag * cos_phi
    force = [-thrust, torque * sin_a, -torque * cos_a]
    pieces = []
    for t in range(2):
        for c in range(3):
            for h in range(2):
                at = t * P_SIZE + h * CZ
                pieces.append(force[c][:, at : at + CZ])
        pieces += [sel_ref[t * ROWS + 15 : t * ROWS + 16]] * 2
    blocks = jnp.concatenate(pieces, axis=0)
    pay_ref[0 : 2 * BACK] = blocks
    pay_ref[2 * BACK :] = pos_ref[...]
    cols = jnp.concatenate(force + [jnp.zeros((CZ - 3, PTS), F32)], axis=0).T
    pz = pz_ref[...]
    lines = jnp.concatenate([cols[:, c : c + 1] * pz for c in range(3)], axis=1)
    l_high, l_low = split(lines)
    lh_ref[...] = lines
    w_high, w_low = split(edge_ref[...])
    rim = dot3(w_high, w_low, l_high, l_low)
    for k in range(4):
        for c in range(3):
            at = (k * 3 + c) * CY
            xrim_ref[at : at + CY] = rim[k * CY : (k + 1) * CY, c * CZ : (c + 1) * CZ]


def near_body(rec_c, rec_d, low_ref, high_ref):
    _, even_y, _, _, _, _ = place()
    c_all, d_all = rec_c[...], jnp.where(odd_side(), rec_d[...], 0.0)
    for side, out_ref in ((0, low_ref), (1, high_ref)):
        got = jnp.where(even_y, d_all, c_all) if side == 0 else jnp.where(even_y, c_all, d_all)

        def wide(first, picks):
            return jnp.concatenate([got[first + j : first + j + 1] for j in picks], axis=1)

        x, y, z, fx, fy, fz = [wide(2 * BACK + 4 * q, range(4)) for q in range(6)]
        force = [wide(2 * c, (0, 1, BACK, BACK + 1)) * DT_STEP for c in range(3)]
        pz, columns = line_profile(z, fz, force)
        l_high, l_low = split(jnp.concatenate([col * pz for col in columns], axis=1))
        gx = profile(YROWS, CX, x, fx)
        wy = offsets(fy)
        planes = []
        for i in range(2):
            rel = (CY + i if side == 0 else i - 2) - y.astype(jnp.int32)
            gy = jnp.zeros((1, PTS), F32)
            for k in range(4):
                gy = jnp.where(rel == k - 1, wy[k], gy)
            planes.append(gx * gy)
        w_high, w_low = split(jnp.concatenate(planes, axis=0))
        rim = dot3(w_high, w_low, l_high, l_low)
        for i in range(2):
            for c in range(3):
                at = (i * 3 + c) * YROWS
                out_ref[at : at + YROWS] = rim[i * YROWS : (i + 1) * YROWS, c * CZ : (c + 1) * CZ]


SPREAD_X = 8


def spread_body(start, lines_ref, gx_ref, gy_ref, base_ref, out_ref):
    l_high, l_low = split(lines_ref[...])
    gy = gy_ref[0:CY]
    for k in range(out_ref.shape[1] // SPREAD_X):
        at = k * SPREAD_X
        first = start + at
        planes = jnp.concatenate([gx_ref[first + i : first + i + 1] * gy for i in range(SPREAD_X)], axis=0)
        w_high, w_low = split(planes)
        value = dot3(w_high, w_low, l_high, l_low)
        for c in range(3):
            part = value[:, c * CZ : (c + 1) * CZ].reshape(SPREAD_X, CY, CZ)
            out_ref[c, at : at + SPREAD_X] = base_ref[c, at : at + SPREAD_X] + part


def rimpack_body(n_blk, xrim_ref, low_ref, high_ref, *rest):
    pieces, (pay_a, pay_b, back_ref, *others) = rest[:n_blk], rest[n_blk:]
    even_x, even_y, inner, _, b0, ny = place()
    zero = jnp.zeros((CY - 4, CZ), F32)
    for k in range(2):
        for c in range(3):
            sides = []
            for s in range(2):
                near, far = [], []
                for y in range(2):
                    at = (y * 3 + c) * YROWS + CX + 2 * s + k
                    near.append(low_ref[at : at + 1])
                    far.append(high_ref[at : at + 1])
                at = ((2 * s + k) * 3 + c) * CY
                sides.append(xrim_ref[at : at + CY] + jnp.concatenate(near + [zero] + far, axis=0))
            at = (k * 3 + c) * CY
            pay_a[at : at + CY] = jnp.where(even_x, sides[1], sides[0])
            pay_b[at : at + CY] = jnp.where(even_x, sides[0], sides[1])
    back = jnp.concatenate([p[...] for p in pieces], axis=0)
    back_ref[...] = back
    if others:
        chips = ny * 2
        side = jnp.where(even_x, -chips, chips)
        total = lax.axis_size("gx") * ny
        for ref, at, target in (
            (pay_b, RIM_X, lax.rem(b0 + side + total, total)),
            (others[0], 0, lax.rem(b0 + 2 * chips, total)),
        ):
            for core in range(2):
                wanted = (target + core * ny).astype(F32)
                found = jnp.full((BACK, CZ), -1.0, F32)
                for k in range(back.shape[0] // BACK):
                    value = back[k * BACK : (k + 1) * BACK]
                    found = jnp.where(value[6:7, 0:1] == wanted, value, found)
                ref[at + core * BACK : at + (core + 1) * BACK] = found


def face_terms(buf, at, first, size, main_low, main_high, y_ref, rec_c, rec_d, rim_low, rim_high, even_y):
    half = 0.5 * DT_STEP
    visc = DT_STEP * NU_VISC
    part = slice(first, first + size)
    here = slice(at, at + size)
    half_of = main_low if first < CX // 2 else main_high
    inner = first % (CX // 2)
    for c in range(3):
        buf[c, here] = half_of[c, inner : inner + size]
        rows = slice(c * CX + first, c * CX + first + size)
        a, b = rec_c[rows], jnp.where(odd_side(), rec_d[rows], 0.0)
        low = [jnp.where(even_y, b, a) * (visc + half * y_ref[0, part]), 0.0]
        high = [0.0, jnp.where(even_y, a, b) * (visc - half * y_ref[1, part])]
        for i in range(2):
            row = (i * 3 + c) * YROWS + first
            buf[c, here, i, :] += rim_low[row : row + size] + low[i]
            buf[c, here, CY - 2 + i, :] += rim_high[row : row + size] + high[i]


INNER = [(2, CHUNK - 2)] + [(k * CHUNK, CHUNK) for k in range(1, N_CHUNK - 1)] + [(CX - CHUNK, CHUNK - 2)]


def chunk_copy(buf, at, out_ref, first, size, sem):
    return pltpu.make_async_copy(buf.at[:, pl.ds(at, size)], out_ref.at[:, pl.ds(first, size)], sem)


def inside_body(main_low, main_high, y_ref, rec_c, rec_d, rim_low, rim_high, out_ref, buf, sems):
    _, even_y, _, _, _, _ = place()
    copies = []
    for k, (first, size) in enumerate(INNER):
        face_terms(buf, first - 2, first, size, main_low, main_high, y_ref, rec_c, rec_d, rim_low, rim_high, even_y)
        copies.append(chunk_copy(buf, first - 2, out_ref, first, size, sems.at[k]))
        copies[-1].start()
    for copy in copies:
        copy.wait()


def final_body(n_ret, _, main_low, main_high, x_ref, y_ref, face_a, face_b, rec_c, rec_d, rim_a, rim_b, rim_low, rim_high, back_ref, *rest):
    rets, (out_ref, pf_ref, buf, sems) = rest[:n_ret], rest[n_ret:]
    even_x, even_y, inner, brick, _, _ = place()
    half = 0.5 * DT_STEP
    visc = DT_STEP * NU_VISC
    copies = []
    for k in range(2):
        first, at = k * (CX - 2), k * 2
        face_terms(buf, at, first, 2, main_low, main_high, y_ref, rec_c, rec_d, rim_low, rim_high, even_y)
        for c in range(3):
            a = face_a[c * XROWS : c * XROWS + CY]
            b = jnp.where(inner, face_b[c * XROWS : c * XROWS + CY], 0.0)
            if k == 0:
                buf[c, 0] += jnp.where(even_x, b, a) * (visc + half * x_ref[0])
            else:
                buf[c, 3] += jnp.where(even_x, a, b) * (visc - half * x_ref[3])
            for i in range(2):
                rows = slice((i * 3 + c) * CY, (i * 3 + c + 1) * CY)
                a, b = rim_a[rows], jnp.where(inner, rim_b[rows], 0.0)
                if k == 0:
                    buf[c, i] += jnp.where(even_x, b, a)
                else:
                    buf[c, 2 + i] += jnp.where(even_x, a, b)
        copies.append(chunk_copy(buf, at, out_ref, first, 2, sems.at[k]))
        copies[-1].start()
    mine = brick.astype(F32)
    found = jnp.zeros((BACK, CZ), F32)
    for ref, first in [(back_ref, 0), (rim_b, RIM_X)] + [(r, 0) for r in rets]:
        for k in range((ref.shape[0] - first) // BACK):
            value = ref[first + BACK * k : first + BACK * k + BACK]
            found = jnp.where(value[6:7, 0:1] == mine, value, found)
    for c in range(3):
        pf_ref[c : c + 1] = jnp.concatenate([found[2 * c : 2 * c + 1], found[2 * c + 1 : 2 * c + 2]], axis=1)
    for copy in copies:
        copy.wait()


def per_device(
    velocity,
    host_cell,
    host_frac,
    host_dst,
    owner_src,
    rotor_speed,
    blade_radius,
    blade_chord,
    blade_twist,
    blade_angle,
):
    nx, ny = lax.axis_size("gx"), lax.axis_size("gy")
    ring, short = nx == 8, ny == 4

    def flip(n, bits):
        return [(i, i ^ bits) for i in range(n)]

    def odd_pairs(n, closed=False):
        up = [(i, (i + 1) % n) for i in range(1, n if closed else n - 1, 2)]
        return up + [(t, s) for s, t in up]

    def same_side(n):
        return [(i, (i + (2 if i % 2 else n - 2)) % n) for i in range(n)]

    def across_x(blocks):
        return [lax.ppermute(b, "gx", p) for b, p in zip(blocks, (flip(nx, 4), same_side(nx)))]

    def swap(block):
        return lax.ppermute(block, "gx", flip(nx, 1))

    def join(pieces):
        return pieces[0] if len(pieces) == 1 else jnp.concatenate(pieces, axis=0)

    def after(values, other):
        return lax.optimization_barrier((values, other))

    def gather_y(first):
        pieces = [first]
        for bit in [b for b in (2, 4, 8) if b < ny]:
            pieces.append(lax.ppermute(join(pieces), "gy", flip(ny, bit)))
        return pieces

    def exchange_y(to_c, to_d, block):
        from_c = lax.ppermute(to_c, "gy", flip(ny, 1))
        from_d = lax.ppermute(to_d, "gy", flip(ny, 3) if short else odd_pairs(ny))
        return from_c, from_d, [lax.ppermute(block, "gy", flip(ny, 2))] if short else []

    def blocks_y(block, from_c, from_d, far, size, at):
        got = join([block, from_c[at : at + size]])
        if short:
            return [join([got, from_d[at : at + size]] + far)]
        return gather_y(got)

    def gather_x(blocks):
        pieces = []
        for bit in [b for b in (2, 4, 8, 16) if b < nx]:
            pieces.append(lax.ppermute(join([blocks] + pieces), "gx", flip(nx, bit)))
        return pieces

    dma = pltpu.SemaphoreType.DMA
    pay_c, pay_d, block = call(
        pack_body,
        [(FACE_Y + ROWS, CZ)] * 2 + [(ROWS, CZ)],
        7,
        "pack",
        scratch=[pltpu.VMEM((4, 2, CZ), F32), pltpu.VMEM((2, CZ), jnp.int32), pltpu.VMEM((1, 1), F32), dma((12,))],
        in_specs=[HB] * 7,
        vmem=56,
    )(velocity, rotor_speed.reshape(1, 1), *[a.reshape(2, CZ) for a in (blade_radius, blade_chord, blade_twist, blade_angle, owner_src)])
    rec_c, rec_d, far = exchange_y(pay_c, pay_d, block)

    def stencil(start):
        return call(lambda *refs: stencil_body(start, *refs), [(3, CX // 2, CY, CZ)], 1, "stencil")(velocity)[0]

    base_low = stencil(0)
    table, sums, x_faces, y_faces = call(
        sample_low_body, [(HOST, CZ), (HOST, 3 * CZ), (6, CY, CZ), (2, CX, CZ)], 3, "sample_low", vmem=24
    )(velocity, host_cell, host_frac)
    (rec_c, rec_d, far), (base_low, sums) = after((rec_c, rec_d, far), (base_low, sums))
    pieces = blocks_y(block, rec_c, rec_d, far, ROWS, FACE_Y)
    beside = [swap(p) for p in pieces]
    beside, base_high = after(beside, stencil(CX // 2))
    pieces = pieces + beside
    n_rows = 2 * ny * ROWS
    pair = (2 * ROWS, CZ)
    pay_a, pay_b, blocks, *across = call(
        lambda *refs: xpack_body(len(pieces), *refs),
        [(FACE_X, CZ), (FACE_X + 2 * ROWS, CZ), pair, pair, pair] if ring else [(FACE_X, CZ), (FACE_X, CZ), (n_rows, CZ)],
        3 + len(pieces),
        "xpack",
    )(x_faces, rec_c, rec_d, *pieces)
    face_b = lax.ppermute(pay_b, "gx", odd_pairs(nx, ring))
    from_x = across_x(across) if ring else gather_x(blocks)
    face_a = swap(pay_a)
    sums = call(sample_high_body, [(HOST, 3 * CZ)], 3, "sample_high", vmem=24)(velocity, table, sums)[0]
    (face_a, face_b, from_x), sums = after((face_a, face_b, from_x), sums)
    samp, sel, pts = call(
        lambda *refs: select_body(len(from_x), *refs),
        [(8, PTS), (2 * ROWS, CZ), (PTS, CZ)],
        7 + len(from_x),
        "select",
    )(table, sums, face_a, face_b, rec_c, rec_d, blocks, *from_x)
    other = swap(samp)
    gx, gy, pz, pos, pair_kernel, edge = call(
        weights_body,
        [(YROWS, PTS), (CY, PTS), (PTS, CZ), (24, CZ), (2, P_SIZE, P_SIZE), (4 * CY, PTS)],
        2,
        "weights",
    )(pts, sel)
    lines, points, xrim = call(
        loads_body,
        [(PTS, 3 * CZ), (2 * BACK + 24, CZ), (2 * RIM_X, CZ)],
        7,
        "loads",
    )(samp, other, sel, pz, pos, pair_kernel, edge)
    ret = points[: 2 * BACK]
    near_c, near_d, far = exchange_y(points, points, ret)

    def spread(start, base):
        return call(
            lambda *refs: spread_body(start, *refs), [(3, CX // 2, CY, CZ)], 4, "spread"
        )(lines, gx, gy, base)[0]

    (near_c, near_d), main_low = after((near_c, near_d), spread(0, base_low))
    rim_low, rim_high = call(near_body, [(RIM_Y, CZ)] * 2, 2, "near")(near_c, near_d)
    far, rim_low = after(far, rim_low)
    pieces = blocks_y(ret, near_c, near_d, far, 2 * BACK, 0)
    n_rows = 2 * ny * BACK
    pair = (2 * BACK, CZ)
    pay_a, pay_b, back, *across = call(
        lambda *refs: rimpack_body(len(pieces), *refs),
        [(RIM_X, CZ), (RIM_X + 2 * BACK, CZ), (n_rows, CZ), pair] if ring else [(RIM_X, CZ), (RIM_X, CZ), (n_rows, CZ)],
        3 + len(pieces),
        "rimpack",
    )(xrim, rim_low, rim_high, *pieces)
    rim_b = lax.ppermute(pay_b, "gx", odd_pairs(nx, ring))
    rets = [lax.ppermute(across[0], "gx", flip(nx, 4))] if ring else gather_x(back)
    rim_a = swap(pay_a)
    main_high = spread(CX // 2, base_high)
    (rim_a, rim_b), (main_low, main_high) = after((rim_a, rim_b), (main_low, main_high))
    if ring:
        rets.append(swap(rim_b[RIM_X:]))
    inside = call(
        inside_body,
        [velocity.shape],
        7,
        "inside",
        scratch=[pltpu.VMEM((3, CX - 4, CY, CZ), F32), dma((N_CHUNK,))],
        out_specs=[HB],
        vmem=16,
    )(main_low, main_high, y_faces, rec_c, rec_d, rim_low, rim_high)[0]
    rets, inside = after(rets, inside)
    return tuple(
        call(
            lambda *refs: final_body(len(rets), *refs),
            [velocity.shape, (3, P_SIZE)],
            14 + len(rets),
            "final",
            scratch=[pltpu.VMEM((3, 4, CY, CZ), F32), dma((2,))],
            first=HB,
            out_specs=[HB, VM],
            aliases={0: 0},
        )(inside, main_low, main_high, x_faces, y_faces, face_a, face_b, rec_c, rec_d, rim_a, rim_b, rim_low, rim_high, back, *rets)
    )


def solution(mesh):
    return jax.shard_map(
        per_device,
        mesh=mesh,
        in_specs=(
            P(None, "gx", "gy", None),
            P(None, ("gx", "gy")),
            P(None, ("gx", "gy")),
            P(("gx", "gy")),
            P(("gx", "gy")),
            P(("gx", "gy")),
            P(("gx", "gy")),
            P(("gx", "gy")),
            P(("gx", "gy")),
            P(("gx", "gy")),
        ),
        out_specs=(P(None, "gx", "gy", None), P(None, ("gx", "gy"))),
        check_vma=False,
    )
```

```python
import math

import jax
import jax.numpy as jnp
from jax import lax
from jax.experimental import pallas as pl
from jax.experimental.pallas import tpu as pltpu
from jax.sharding import PartitionSpec as P

CX = 64
CY = 32
CZ = 128
P_SIZE = 256
HOST = 512
PTS = 2 * P_SIZE

DT_STEP = 0.2
NU_VISC = 0.5
EPS_SQ = 1.44
CORE_SQ = 0.01

ROWS = 16
BACK = 8
YROWS = 72
XROWS = 40
FACE_Y = 3 * CX
FACE_X = 3 * XROWS
RIM_Y = 2 * 3 * YROWS
RIM_X = 2 * 3 * CY
CHUNK = 8
N_CHUNK = CX // CHUNK

F32 = jnp.float32
BF16 = jnp.bfloat16
VM = pl.BlockSpec(memory_space=pltpu.MemorySpace.VMEM)
SM = pl.BlockSpec(memory_space=pltpu.MemorySpace.SMEM)
HB = pl.BlockSpec(memory_space=pltpu.MemorySpace.HBM)
MIB = 1024 * 1024


def call(body, outs, n_in, name, scratch=(), first=VM, second=VM, out_specs=None, in_specs=None, vmem=12, aliases=None):
    return pl.pallas_call(
        body,
        out_shape=[jax.ShapeDtypeStruct(s, F32) for s in outs],
        in_specs=in_specs or ([first, second] + [VM] * n_in)[:n_in],
        out_specs=out_specs or [VM] * len(outs),
        scratch_shapes=list(scratch),
        input_output_aliases=aliases or {},
        compiler_params=pltpu.CompilerParams(vmem_limit_bytes=vmem * MIB),
        name=name,
    )


def place():
    nx, ny = lax.axis_size("gx"), lax.axis_size("gy")
    ix, iy = lax.axis_index("gx"), lax.axis_index("gy")
    px, py = lax.rem(ix, 2), lax.rem(iy, 2)
    inner = (ix + px > 0) & (ix + px < nx)
    return px == 0, py == 0, inner, ix * ny + iy, (ix - px) * ny + iy, ny


def odd_side():
    ny, iy = lax.axis_size("gy"), lax.axis_index("gy")
    py = lax.rem(iy, 2)
    return (iy + py > 0) & (iy + py < ny)


def split(value):
    high = value.astype(BF16)
    low = (value - high.astype(F32)).astype(BF16)
    return high, low


def dot3(a_high, a_low, b_high, b_low):
    def one(a, b):
        return jnp.dot(a, b, preferred_element_type=F32)

    return one(a_high, b_high) + (one(a_high, b_low) + one(a_low, b_high))


def dot3_last(a_high, a_low, b_high, b_low):
    def one(a, b):
        return lax.dot_general(a, b, (((1,), (1,)), ((), ())), preferred_element_type=F32)

    return one(a_high, b_high) + (one(a_high, b_low) + one(a_low, b_high))


def reduce_list(items, op):
    result = items[0]
    for item in items[1:]:
        result = op(result, item)
    return result


def pack_body(v_ref, spin_hbm, *rest):
    params, (pay_c, pay_d, blk_ref, held, held_int, spin_ref, sems) = rest[:5], rest[5:]
    _, even_y, _, brick, _, _ = place()

    def faces(first, second):
        made = []
        for k, (ref, y) in enumerate(((pay_c, first), (pay_d, second))):
            for c in range(3):
                made.append(pltpu.make_async_copy(v_ref.at[c, :, y], ref.at[pl.ds(c * CX, CX)], sems.at[3 * k + c]))
        return made

    @pl.when(even_y)
    def _():
        for copy in faces(CY - 1, 0):
            copy.start()

    @pl.when(jnp.logical_not(even_y))
    def _():
        for copy in faces(0, CY - 1):
            copy.start()

    small = [pltpu.make_async_copy(spin_hbm, spin_ref, sems.at[6])]
    small += [pltpu.make_async_copy(p, held.at[k], sems.at[7 + k]) for k, p in enumerate(params[:4])]
    small.append(pltpu.make_async_copy(params[4], held_int, sems.at[11]))
    for copy in small:
        copy.start()
    for copy in small:
        copy.wait()
    radius, chord, twist, angle = [held[k] for k in range(4)]
    parts = [
        radius,
        chord,
        jnp.cos(twist),
        jnp.sin(twist),
        jnp.cos(angle),
        jnp.sin(angle),
        held_int[...].astype(F32),
        jnp.broadcast_to(spin_ref[...], (1, CZ)),
        jnp.full((1, CZ), brick.astype(F32), F32),
    ]
    block = jnp.concatenate(parts, axis=0)
    blk_ref[...] = block
    pay_c[FACE_Y:] = block
    pay_d[FACE_Y:] = block
    for copy in faces(0, 0):
        copy.wait()


def stencil_body(start, v_ref, out_ref):
    row = lax.broadcasted_iota(jnp.int32, (CY, CZ), 0)
    lane = lax.broadcasted_iota(jnp.int32, (CY, CZ), 1)
    half = 0.5 * DT_STEP
    visc = DT_STEP * NU_VISC
    not_last_y, not_first_y = row < CY - 1, row > 0
    not_last_z, not_first_z = lane < CZ - 1, lane > 0

    def step(k, carry):
        x = start + k
        up = jnp.minimum(x + 1, CX - 1)
        down = jnp.maximum(x - 1, 0)
        v0, v1, v2 = v_ref[0, x], v_ref[1, x], v_ref[2, x]
        a_x = jnp.where(x < CX - 1, visc - half * v0, 0.0)
        b_x = jnp.where(x > 0, visc + half * v0, 0.0)
        a_y = jnp.where(not_last_y, visc - half * v1, 0.0)
        b_y = jnp.where(not_first_y, visc + half * v1, 0.0)
        a_z = jnp.where(not_last_z, visc - half * v2, 0.0)
        b_z = jnp.where(not_first_z, visc + half * v2, 0.0)
        for c in range(3):
            mid = (v0, v1, v2)[c]
            along_x = a_x * v_ref[c, up] + b_x * v_ref[c, down]
            along_y = a_y * pltpu.roll(mid, CY - 1, 0) + b_y * pltpu.roll(mid, 1, 0)
            along_z = a_z * pltpu.roll(mid, CZ - 1, 1) + b_z * pltpu.roll(mid, 1, 1)
            out_ref[c, k] = (1.0 - 6.0 * visc) * mid + along_x + (along_y + along_z)
        return carry

    lax.fori_loop(0, out_ref.shape[1], step, 0, unroll=2)


def weight(coord, base, frac):
    return jnp.where(coord == base, 1.0 - frac, jnp.where(coord == base + 1, frac, 0.0))


def sample_part(start, v_ref, table, acc):
    x_col, y_col = [table[:, k : k + 1].astype(jnp.int32) for k in range(2)]
    fx, fy = [table[:, k : k + 1] for k in range(3, 5)]
    lane = lax.broadcasted_iota(jnp.int32, (HOST, CZ), 1)
    wy = weight(lane % CY, y_col, fy)
    x_lane = (lane // CY + start - x_col).astype(F32).astype(BF16)
    near, far = split((1.0 - fx) * wy), split(fx * wy)
    zero = jnp.zeros((HOST, CZ), BF16)
    per = 4
    nx = CZ * per // CY
    for j in range(CX // 2 // nx):
        highs, lows = [], []
        for i in range(per):
            shift = (CZ // CY) * (j * per + i)
            at_base, at_next = x_lane == jnp.bfloat16(-shift), x_lane == jnp.bfloat16(1 - shift)
            highs.append(jnp.where(at_base, near[0], jnp.where(at_next, far[0], zero)))
            lows.append(jnp.where(at_base, near[1], jnp.where(at_next, far[1], zero)))
        w_high, w_low = jnp.concatenate(highs, axis=1), jnp.concatenate(lows, axis=1)
        first = start + j * nx
        field = [v_ref[c, first : first + nx].reshape(nx * CY, CZ) for c in range(3)]
        f_high, f_low = split(jnp.concatenate(field, axis=1))
        part = dot3(w_high, w_low, f_high, f_low)
        acc = part if acc is None else acc + part
    return acc


def sample_low_body(v_ref, cell_ref, frac_ref, tab_ref, acc_ref, x_ref, y_ref):
    for c in range(3):
        x_ref[c] = v_ref[c, 0]
        x_ref[c + 3] = v_ref[c, CX - 1]
    y_ref[0] = v_ref[1, :, 0, :]
    y_ref[1] = v_ref[1, :, CY - 1, :]
    rows = jnp.concatenate([cell_ref[...].astype(F32), frac_ref[...], jnp.zeros((CZ - 6, HOST), F32)], axis=0)
    table = rows.T
    tab_ref[...] = table
    acc_ref[...] = sample_part(0, v_ref, table, None)


def sample_high_body(v_ref, tab_ref, low_ref, acc_ref):
    acc_ref[...] = sample_part(CX // 2, v_ref, tab_ref[...], low_ref[...])


def split_blocks(sources):
    return [
        ref[first + k * ROWS : first + (k + 1) * ROWS]
        for ref, first in sources
        for k in range((ref.shape[0] - first) // ROWS)
    ]


def pick_pair(values, b0, ny):
    keys = [value[12:13, 0:1] for value in values]
    members = []
    for key in keys:
        home = jnp.floor(key * (1.0 / HOST)).astype(jnp.int32)
        members.append((home == b0) | (home == b0 + ny))
    low_key = reduce_list([jnp.where(m, k, 1e9) for k, m in zip(keys, members)], jnp.minimum)
    high_key = reduce_list([jnp.where(m, k, -9.0) for k, m in zip(keys, members)], jnp.maximum)
    low = jnp.full((ROWS, CZ), -1.0, F32)
    high = low
    for key, value in zip(keys, values):
        low = jnp.where(key == low_key, value, low)
        high = jnp.where(key == high_key, value, high)
    return low, high


def xpack_body(n_blk, x_ref, rec_c, rec_d, *rest):
    pieces, (pay_a, pay_b, own_ref, *others) = rest[:n_blk], rest[n_blk:]
    even_x, even_y, inner, _, b0, ny = place()
    for c in range(3):
        at = c * CX
        y_high = jnp.where(even_y, rec_c[at : at + 1], jnp.where(odd_side(), rec_d[at : at + 1], 0.0))
        tail = jnp.concatenate([y_high, jnp.zeros((XROWS - CY - 1, CZ), F32)], axis=0)
        low, high = x_ref[c], x_ref[c + 3]
        at = c * XROWS
        pay_a[at : at + CY] = jnp.where(even_x, high, low)
        pay_b[at : at + CY] = jnp.where(even_x, low, high)
        pay_a[at + CY : at + XROWS] = tail
        pay_b[at + CY : at + XROWS] = tail
    if not others:
        own_ref[...] = jnp.concatenate([p[...] for p in pieces], axis=0)
        return
    values = split_blocks([(p, 0) for p in pieces])
    chips = ny * 2
    side = jnp.where(even_x, -chips, chips)
    total = lax.axis_size("gx") * ny
    own_ref[...] = jnp.concatenate(pick_pair(values, b0, ny), axis=0)
    beside = jnp.concatenate(pick_pair(values, lax.rem(b0 + side + total, total), ny), axis=0)
    pay_b[FACE_X:] = beside
    others[1][...] = beside
    others[0][...] = jnp.concatenate(pick_pair(values, lax.rem(b0 + 2 * chips, total), ny), axis=0)


def select_body(n_blk, tab_ref, acc_ref, face_a, face_b, rec_c, rec_d, blk_ref, *rest):
    others, (samp_ref, sel_ref, pts_ref) = rest[:n_blk], rest[n_blk:]
    even_x, even_y, inner, brick, b0, ny = place()
    sources = [(blk_ref, 0), (face_b, FACE_X)] + [(o, 0) for o in others]
    turbine_a, turbine_b = pick_pair(split_blocks(sources), b0, ny)
    sel = jnp.concatenate([turbine_a, turbine_b], axis=0)
    sel_ref[...] = sel
    turned = jnp.concatenate([sel, jnp.zeros((CZ - 2 * ROWS, CZ), F32)], axis=0).T

    def column(k):
        picks = (2 * k, 2 * k + 1, ROWS + 2 * k, ROWS + 2 * k + 1)
        return jnp.concatenate([turned[:, j : j + 1] for j in picks], axis=0)

    table = tab_ref[...]
    lane = lax.broadcasted_iota(jnp.int32, (PTS, CZ), 1)
    x_col, y_col, z_col = [table[:, k : k + 1].astype(jnp.int32) for k in range(3)]
    fx, fy, fz = [table[:, k : k + 1] for k in range(3, 6)]
    on_line = lane >= CX
    edge_x = jnp.where(on_line, lane - CX, CX)
    edge_y = jnp.where(on_line, CY, lane)
    edge_w = jnp.where(on_line | (lane <= CY), weight(edge_x, x_col, fx) * weight(edge_y, y_col, fy), 0.0)
    field = []
    for c in range(3):
        at = c * XROWS
        past = jnp.where(inner, face_b[at : at + XROWS], 0.0)
        plane = jnp.where(even_x, face_a[at : at + XROWS], past)
        at = c * CX
        line = jnp.where(even_y, rec_c[at : at + CX], jnp.where(odd_side(), rec_d[at : at + CX], 0.0))
        field.append(jnp.concatenate([plane, jnp.zeros((CX - XROWS, CZ), F32), line], axis=0))
    w_high, w_low = split(edge_w)
    f_high, f_low = split(jnp.concatenate(field, axis=1))
    acc = acc_ref[...] + dot3(w_high, w_low, f_high, f_low)
    wz = weight(lane, z_col, fz)
    for c in range(3):
        value = jnp.sum(acc[:, c * CZ : (c + 1) * CZ] * wz, axis=1, keepdims=True)
        table = table + jnp.where(lane == 6 + c, value, 0.0)
    slot = column(6).astype(jnp.int32)
    mine = (slot // HOST) == brick
    local = jnp.where(mine, slot % HOST, -1)
    hit = (lax.broadcasted_iota(jnp.int32, (PTS, HOST), 1) == local).astype(F32).astype(BF16)
    first, second = split(table)
    third = (table - first.astype(F32) - second.astype(F32)).astype(BF16)
    pulled = [jnp.dot(hit, part, preferred_element_type=F32) for part in (first, second, third)]
    points = pulled[0] + pulled[1] + pulled[2]
    points = jnp.where(lane == 9, column(0), points)
    pts_ref[...] = jnp.where((lane == 0) & jnp.logical_not(mine), -100.0, points)
    samp_ref[...] = points.T[6:14]


def offsets(frac):
    raw = [jnp.exp(-((o - frac) ** 2) / EPS_SQ) for o in (-1.0, 0.0, 1.0, 2.0)]
    total = (raw[0] + raw[1]) + (raw[2] + raw[3])
    return [value / total for value in raw]


def profile(rows, inner, base, frac):
    index = lax.broadcasted_iota(jnp.int32, (rows, PTS), 0)
    late = index - inner
    index = jnp.where(index < inner, index, jnp.where(late < 2, late - 2, late - 2 + inner))
    rel = index - base.astype(jnp.int32)
    result = jnp.zeros((rows, PTS), F32)
    for k, w in enumerate(offsets(frac)):
        result = jnp.where(rel == k - 1, w, result)
    return result


def weights_body(pts_ref, sel_ref, gx_ref, gy_ref, pz_ref, pos_ref, pair_ref, edge_ref):
    table = pts_ref[...].T
    gx = profile(YROWS, CX, table[0:1], table[3:4])
    gy = profile(CY, CY, table[1:2], table[4:5])
    gx_ref[...] = gx
    gy_ref[...] = gy
    pz_ref[...] = profile(CZ, CZ, table[2:3], table[5:6]) * DT_STEP
    pos_ref[...] = jnp.concatenate([table[q : q + 1, k * CZ : (k + 1) * CZ] for q in range(6) for k in range(4)], axis=0)
    for t in range(2):
        at = t * ROWS
        radius = jnp.concatenate([sel_ref[at : at + 1], sel_ref[at + 1 : at + 2]], axis=1)
        spacing = radius - pts_ref[t * P_SIZE : (t + 1) * P_SIZE, 9:10]
        pair_ref[t] = spacing / (spacing * spacing + CORE_SQ)
    for k in range(4):
        edge_ref[k * CY : (k + 1) * CY] = gx[CX + k : CX + k + 1] * gy


def attack(axial_flow, tangent, cos_twist, sin_twist):
    rel_speed = jnp.sqrt(axial_flow * axial_flow + tangent * tangent + 1.0)
    cos_phi = tangent / rel_speed
    sin_phi = axial_flow / rel_speed
    sin_alpha = sin_phi * cos_twist - cos_phi * sin_twist
    cos_alpha = cos_phi * cos_twist + sin_phi * sin_twist
    lift_coef = 2.0 * jnp.pi * sin_alpha * cos_alpha / (1.0 + 4.0 * sin_alpha * sin_alpha)
    drag_coef = 0.02 + 0.8 * sin_alpha * sin_alpha
    return rel_speed, cos_phi, sin_phi, lift_coef, drag_coef


def loads_body(samp_ref, other_ref, sel_ref, pz_ref, pos_ref, pair_ref, edge_ref, lh_ref, pay_ref, xrim_ref):
    def row(k):
        picks = (2 * k, 2 * k + 1, ROWS + 2 * k, ROWS + 2 * k + 1)
        return jnp.concatenate([sel_ref[j : j + 1] for j in picks], axis=1)

    radius, chord, cos_t, sin_t, cos_a, sin_a = [row(k) for k in range(6)]
    spin = radius * jnp.concatenate([sel_ref[j : j + 1] for j in (14, 14, ROWS + 14, ROWS + 14)], axis=1)
    flow = samp_ref[...] + other_ref[...]
    axial = flow[0:1]
    tangent = spin - (cos_a * flow[2:3] - sin_a * flow[1:2])
    rel_speed, cos_phi, sin_phi, lift_coef, drag_coef = attack(axial, tangent, cos_t, sin_t)
    circ = 0.5 * chord * rel_speed * lift_coef
    parts = []
    for t in range(2):
        seg = slice(t * P_SIZE, (t + 1) * P_SIZE)
        lhs = jnp.concatenate([cos_a[:, seg] * circ[:, seg], sin_a[:, seg] * circ[:, seg], jnp.zeros((6, P_SIZE), F32)], axis=0)
        both = jnp.dot(lhs, pair_ref[t], preferred_element_type=F32, precision=lax.Precision.HIGHEST)
        parts.append((cos_a[:, seg] * both[0:1] + sin_a[:, seg] * both[1:2]) / (4.0 * math.pi))
    induced = jnp.concatenate(parts, axis=1)
    rel_speed, cos_phi, sin_phi, lift_coef, drag_coef = attack(axial + induced, tangent, cos_t, sin_t)
    dynamic = 0.5 * chord * rel_speed * rel_speed
    lift = dynamic * lift_coef
    drag = dynamic * drag_coef
    thrust = lift * cos_phi + drag * sin_phi
    torque = lift * sin_phi - drag * cos_phi
    force = [-thrust, torque * sin_a, -torque * cos_a]
    pieces = []
    for t in range(2):
        for c in range(3):
            for h in range(2):
                at = t * P_SIZE + h * CZ
                pieces.append(force[c][:, at : at + CZ])
        pieces += [sel_ref[t * ROWS + 15 : t * ROWS + 16]] * 2
    blocks = jnp.concatenate(pieces, axis=0)
    pay_ref[0 : 2 * BACK] = blocks
    pay_ref[2 * BACK :] = pos_ref[...]
    pz = pz_ref[...]
    lines = jnp.concatenate([f * pz for f in force], axis=0)
    l_high, l_low = split(lines)
    lh_ref[...] = lines
    w_high, w_low = split(edge_ref[...])
    rim = dot3_last(w_high, w_low, l_high, l_low)
    for k in range(4):
        for c in range(3):
            at = (k * 3 + c) * CY
            xrim_ref[at : at + CY] = rim[k * CY : (k + 1) * CY, c * CZ : (c + 1) * CZ]


def near_body(rec_c, rec_d, low_ref, high_ref):
    _, even_y, _, _, _, _ = place()
    c_all, d_all = rec_c[...], jnp.where(odd_side(), rec_d[...], 0.0)
    for side, out_ref in ((0, low_ref), (1, high_ref)):
        got = jnp.where(even_y, d_all, c_all) if side == 0 else jnp.where(even_y, c_all, d_all)

        def wide(first, picks):
            return jnp.concatenate([got[first + j : first + j + 1] for j in picks], axis=1)

        x, y, z, fx, fy, fz = [wide(2 * BACK + 4 * q, range(4)) for q in range(6)]
        force = [wide(2 * c, (0, 1, BACK, BACK + 1)) * DT_STEP for c in range(3)]
        pz = profile(CZ, CZ, z, fz)
        l_high, l_low = split(jnp.concatenate([f * pz for f in force], axis=0))
        gx = profile(YROWS, CX, x, fx)
        wy = offsets(fy)
        planes = []
        for i in range(2):
            rel = (CY + i if side == 0 else i - 2) - y.astype(jnp.int32)
            gy = jnp.zeros((1, PTS), F32)
            for k in range(4):
                gy = jnp.where(rel == k - 1, wy[k], gy)
            planes.append(gx * gy)
        w_high, w_low = split(jnp.concatenate(planes, axis=0))
        rim = dot3_last(w_high, w_low, l_high, l_low)
        for i in range(2):
            for c in range(3):
                at = (i * 3 + c) * YROWS
                out_ref[at : at + YROWS] = rim[i * YROWS : (i + 1) * YROWS, c * CZ : (c + 1) * CZ]


SPREAD_X = 8


def spread_body(start, lines_ref, gx_ref, gy_ref, *rest):
    bases, out_ref = rest[:-1], rest[-1]
    l_high, l_low = split(lines_ref[...])
    gy = gy_ref[0:CY]
    held = bases[0].shape[1]
    for k in range(out_ref.shape[1] // SPREAD_X):
        at = k * SPREAD_X
        first = start + at
        planes = jnp.concatenate([gx_ref[first + i : first + i + 1] * gy for i in range(SPREAD_X)], axis=0)
        w_high, w_low = split(planes)
        value = dot3_last(w_high, w_low, l_high, l_low)
        base, inner = bases[at // held], at % held
        for c in range(3):
            part = value[:, c * CZ : (c + 1) * CZ].reshape(SPREAD_X, CY, CZ)
            out_ref[c, at : at + SPREAD_X] = base[c, inner : inner + SPREAD_X] + part


def rimpack_body(n_blk, xrim_ref, low_ref, high_ref, *rest):
    pieces, (pay_a, pay_b, back_ref, *others) = rest[:n_blk], rest[n_blk:]
    even_x, even_y, inner, _, b0, ny = place()
    zero = jnp.zeros((CY - 4, CZ), F32)
    for k in range(2):
        for c in range(3):
            sides = []
            for s in range(2):
                near, far = [], []
                for y in range(2):
                    at = (y * 3 + c) * YROWS + CX + 2 * s + k
                    near.append(low_ref[at : at + 1])
                    far.append(high_ref[at : at + 1])
                at = ((2 * s + k) * 3 + c) * CY
                sides.append(xrim_ref[at : at + CY] + jnp.concatenate(near + [zero] + far, axis=0))
            at = (k * 3 + c) * CY
            pay_a[at : at + CY] = jnp.where(even_x, sides[1], sides[0])
            pay_b[at : at + CY] = jnp.where(even_x, sides[0], sides[1])
    back = jnp.concatenate([p[...] for p in pieces], axis=0)
    back_ref[...] = back
    if others:
        chips = ny * 2
        side = jnp.where(even_x, -chips, chips)
        total = lax.axis_size("gx") * ny
        for ref, at, target in (
            (pay_b, RIM_X, lax.rem(b0 + side + total, total)),
            (others[0], 0, lax.rem(b0 + 2 * chips, total)),
        ):
            for core in range(2):
                wanted = (target + core * ny).astype(F32)
                found = jnp.full((BACK, CZ), -1.0, F32)
                for k in range(back.shape[0] // BACK):
                    value = back[k * BACK : (k + 1) * BACK]
                    found = jnp.where(value[6:7, 0:1] == wanted, value, found)
                ref[at + core * BACK : at + (core + 1) * BACK] = found


def face_terms(buf, at, first, size, main_low, main_high, y_ref, rec_c, rec_d, rim_low, rim_high, even_y):
    half = 0.5 * DT_STEP
    visc = DT_STEP * NU_VISC
    part = slice(first, first + size)
    here = slice(at, at + size)
    half_of = main_low if first < CX // 2 else main_high
    inner = first % (CX // 2)
    for c in range(3):
        buf[c, here] = half_of[c, inner : inner + size]
        rows = slice(c * CX + first, c * CX + first + size)
        a, b = rec_c[rows], jnp.where(odd_side(), rec_d[rows], 0.0)
        low = [jnp.where(even_y, b, a) * (visc + half * y_ref[0, part]), 0.0]
        high = [0.0, jnp.where(even_y, a, b) * (visc - half * y_ref[1, part])]
        for i in range(2):
            row = (i * 3 + c) * YROWS + first
            buf[c, here, i, :] += rim_low[row : row + size] + low[i]
            buf[c, here, CY - 2 + i, :] += rim_high[row : row + size] + high[i]


INNER = [(2, CHUNK - 2)] + [(k * CHUNK, CHUNK) for k in range(1, N_CHUNK - 1)] + [(CX - CHUNK, CHUNK - 2)]


def chunk_copy(buf, at, out_ref, first, size, sem):
    return pltpu.make_async_copy(buf.at[:, pl.ds(at, size)], out_ref.at[:, pl.ds(first, size)], sem)


def inside_body(main_low, main_high, y_ref, rec_c, rec_d, rim_low, rim_high, out_ref, buf, sems):
    _, even_y, _, _, _, _ = place()
    copies = []
    for k, (first, size) in enumerate(INNER):
        face_terms(buf, first - 2, first, size, main_low, main_high, y_ref, rec_c, rec_d, rim_low, rim_high, even_y)
        copies.append(chunk_copy(buf, first - 2, out_ref, first, size, sems.at[k]))
        copies[-1].start()
    for copy in copies:
        copy.wait()


def final_body(n_ret, _, main_low, main_high, x_ref, y_ref, face_a, face_b, rec_c, rec_d, rim_a, rim_b, rim_low, rim_high, back_ref, *rest):
    rets, (out_ref, pf_ref, buf, pf_buf, sems) = rest[:n_ret], rest[n_ret:]
    even_x, even_y, inner, brick, _, _ = place()
    half = 0.5 * DT_STEP
    visc = DT_STEP * NU_VISC
    mine = brick.astype(F32)
    found = jnp.zeros((BACK, CZ), F32)
    for ref, first in [(back_ref, 0), (rim_b, RIM_X)] + [(r, 0) for r in rets]:
        for k in range((ref.shape[0] - first) // BACK):
            value = ref[first + BACK * k : first + BACK * k + BACK]
            found = jnp.where(value[6:7, 0:1] == mine, value, found)
    for c in range(3):
        pf_buf[c : c + 1] = jnp.concatenate([found[2 * c : 2 * c + 1], found[2 * c + 1 : 2 * c + 2]], axis=1)
    copies = [pltpu.make_async_copy(pf_buf, pf_ref, sems.at[2])]
    copies[0].start()
    for k in range(2):
        first, at = k * (CX - 2), k * 2
        face_terms(buf, at, first, 2, main_low, main_high, y_ref, rec_c, rec_d, rim_low, rim_high, even_y)
        for c in range(3):
            a = face_a[c * XROWS : c * XROWS + CY]
            b = jnp.where(inner, face_b[c * XROWS : c * XROWS + CY], 0.0)
            if k == 0:
                buf[c, 0] += jnp.where(even_x, b, a) * (visc + half * x_ref[0])
            else:
                buf[c, 3] += jnp.where(even_x, a, b) * (visc - half * x_ref[3])
            for i in range(2):
                rows = slice((i * 3 + c) * CY, (i * 3 + c + 1) * CY)
                a, b = rim_a[rows], jnp.where(inner, rim_b[rows], 0.0)
                if k == 0:
                    buf[c, i] += jnp.where(even_x, b, a)
                else:
                    buf[c, 2 + i] += jnp.where(even_x, a, b)
        copies.append(chunk_copy(buf, at, out_ref, first, 2, sems.at[k]))
        copies[-1].start()
    for copy in copies:
        copy.wait()


def per_device(
    velocity,
    host_cell,
    host_frac,
    host_dst,
    owner_src,
    rotor_speed,
    blade_radius,
    blade_chord,
    blade_twist,
    blade_angle,
):
    nx, ny = lax.axis_size("gx"), lax.axis_size("gy")
    ring, short = nx == 8, ny == 4

    def flip(n, bits):
        return [(i, i ^ bits) for i in range(n)]

    def odd_pairs(n, closed=False):
        up = [(i, (i + 1) % n) for i in range(1, n if closed else n - 1, 2)]
        return up + [(t, s) for s, t in up]

    def same_side(n):
        return [(i, (i + (2 if i % 2 else n - 2)) % n) for i in range(n)]

    def across_x(blocks):
        return [lax.ppermute(b, "gx", p) for b, p in zip(blocks, (flip(nx, 4), same_side(nx)))]

    def swap(block):
        return lax.ppermute(block, "gx", flip(nx, 1))

    def join(pieces):
        return pieces[0] if len(pieces) == 1 else jnp.concatenate(pieces, axis=0)

    def after(values, other):
        return lax.optimization_barrier((values, other))

    def gather_y(first):
        pieces = [first]
        for bit in [b for b in (2, 4, 8) if b < ny]:
            pieces.append(lax.ppermute(join(pieces), "gy", flip(ny, bit)))
        return pieces

    def exchange_y(to_c, to_d, block):
        from_c = lax.ppermute(to_c, "gy", flip(ny, 1))
        from_d = lax.ppermute(to_d, "gy", flip(ny, 3) if short else odd_pairs(ny))
        return from_c, from_d, [lax.ppermute(block, "gy", flip(ny, 2))] if short else []

    def blocks_y(block, from_c, from_d, far, size, at):
        got = join([block, from_c[at : at + size]])
        if short:
            return [join([got, from_d[at : at + size]] + far)]
        return gather_y(got)

    def gather_x(blocks):
        pieces = []
        for bit in [b for b in (2, 4, 8, 16) if b < nx]:
            pieces.append(lax.ppermute(join([blocks] + pieces), "gx", flip(nx, bit)))
        return pieces

    dma = pltpu.SemaphoreType.DMA
    pay_c, pay_d, block = call(
        pack_body,
        [(FACE_Y + ROWS, CZ)] * 2 + [(ROWS, CZ)],
        7,
        "pack",
        scratch=[pltpu.VMEM((4, 2, CZ), F32), pltpu.VMEM((2, CZ), jnp.int32), pltpu.VMEM((1, 1), F32), dma((12,))],
        in_specs=[HB] * 7,
        vmem=56,
    )(velocity, rotor_speed.reshape(1, 1), *[a.reshape(2, CZ) for a in (blade_radius, blade_chord, blade_twist, blade_angle, owner_src)])
    rec_c, rec_d, far = exchange_y(pay_c, pay_d, block)

    def stencil(start, count):
        return call(lambda *refs: stencil_body(start, *refs), [(3, count, CY, CZ)], 1, "stencil")(velocity)[0]

    base_low = stencil(0, CX // 2)
    table, sums, x_faces, y_faces = call(
        sample_low_body, [(HOST, CZ), (HOST, 3 * CZ), (6, CY, CZ), (2, CX, CZ)], 3, "sample_low", vmem=24
    )(velocity, host_cell, host_frac)
    (rec_c, rec_d, far), (base_low, sums) = after((rec_c, rec_d, far), (base_low, sums))
    pieces = blocks_y(block, rec_c, rec_d, far, ROWS, FACE_Y)
    beside = [swap(p) for p in pieces]
    beside, base_third = after(beside, stencil(CX // 2, CX // 4))
    pieces = pieces + beside
    n_rows = 2 * ny * ROWS
    pair = (2 * ROWS, CZ)
    pay_a, pay_b, blocks, *across = call(
        lambda *refs: xpack_body(len(pieces), *refs),
        [(FACE_X, CZ), (FACE_X + 2 * ROWS, CZ), pair, pair, pair] if ring else [(FACE_X, CZ), (FACE_X, CZ), (n_rows, CZ)],
        3 + len(pieces),
        "xpack",
    )(x_faces, rec_c, rec_d, *pieces)
    face_b = lax.ppermute(pay_b, "gx", odd_pairs(nx, ring))
    from_x = across_x(across) if ring else gather_x(blocks)
    face_a = swap(pay_a)
    sums = call(sample_high_body, [(HOST, 3 * CZ)], 3, "sample_high", vmem=24)(velocity, table, sums)[0]
    base_last = stencil(3 * CX // 4, CX // 4)
    (face_a, face_b, from_x), (sums, base_last) = after((face_a, face_b, from_x), (sums, base_last))
    samp, sel, pts = call(
        lambda *refs: select_body(len(from_x), *refs),
        [(8, PTS), (2 * ROWS, CZ), (PTS, CZ)],
        7 + len(from_x),
        "select",
    )(table, sums, face_a, face_b, rec_c, rec_d, blocks, *from_x)
    other = swap(samp)
    gx, gy, pz, pos, pair_kernel, edge = call(
        weights_body,
        [(YROWS, PTS), (CY, PTS), (CZ, PTS), (24, CZ), (2, P_SIZE, P_SIZE), (4 * CY, PTS)],
        2,
        "weights",
    )(pts, sel)
    lines, points, xrim = call(
        loads_body,
        [(3 * CZ, PTS), (2 * BACK + 24, CZ), (2 * RIM_X, CZ)],
        7,
        "loads",
    )(samp, other, sel, pz, pos, pair_kernel, edge)
    ret = points[: 2 * BACK]
    near_c, near_d, far = exchange_y(points, points, ret)

    def spread(start, *bases):
        return call(
            lambda *refs: spread_body(start, *refs), [(3, CX // 2, CY, CZ)], 3 + len(bases), "spread"
        )(lines, gx, gy, *bases)[0]

    (near_c, near_d), main_low = after((near_c, near_d), spread(0, base_low))
    rim_low, rim_high = call(near_body, [(RIM_Y, CZ)] * 2, 2, "near")(near_c, near_d)
    far, rim_low = after(far, rim_low)
    pieces = blocks_y(ret, near_c, near_d, far, 2 * BACK, 0)
    n_rows = 2 * ny * BACK
    pair = (2 * BACK, CZ)
    pay_a, pay_b, back, *across = call(
        lambda *refs: rimpack_body(len(pieces), *refs),
        [(RIM_X, CZ), (RIM_X + 2 * BACK, CZ), (n_rows, CZ), pair] if ring else [(RIM_X, CZ), (RIM_X, CZ), (n_rows, CZ)],
        3 + len(pieces),
        "rimpack",
    )(xrim, rim_low, rim_high, *pieces)
    rim_b = lax.ppermute(pay_b, "gx", odd_pairs(nx, ring))
    rets = [lax.ppermute(across[0], "gx", flip(nx, 4))] if ring else gather_x(back)
    rim_a = swap(pay_a)
    main_high = spread(CX // 2, base_third, base_last)
    (rim_a, rim_b), (main_low, main_high) = after((rim_a, rim_b), (main_low, main_high))
    if ring:
        rets.append(swap(rim_b[RIM_X:]))
    inside = call(
        inside_body,
        [velocity.shape],
        7,
        "inside",
        scratch=[pltpu.VMEM((3, CX - 4, CY, CZ), F32), dma((N_CHUNK,))],
        out_specs=[HB],
        vmem=16,
    )(main_low, main_high, y_faces, rec_c, rec_d, rim_low, rim_high)[0]
    rets, inside = after(rets, inside)
    return tuple(
        call(
            lambda *refs: final_body(len(rets), *refs),
            [velocity.shape, (3, P_SIZE)],
            14 + len(rets),
            "final",
            scratch=[pltpu.VMEM((3, 4, CY, CZ), F32), pltpu.VMEM((3, P_SIZE), F32), dma((3,))],
            first=HB,
            out_specs=[HB, HB],
            aliases={0: 0},
        )(inside, main_low, main_high, x_faces, y_faces, face_a, face_b, rec_c, rec_d, rim_a, rim_b, rim_low, rim_high, back, *rets)
    )


def solution(mesh):
    return jax.shard_map(
        per_device,
        mesh=mesh,
        in_specs=(
            P(None, "gx", "gy", None),
            P(None, ("gx", "gy")),
            P(None, ("gx", "gy")),
            P(("gx", "gy")),
            P(("gx", "gy")),
            P(("gx", "gy")),
            P(("gx", "gy")),
            P(("gx", "gy")),
            P(("gx", "gy")),
            P(("gx", "gy")),
        ),
        out_specs=(P(None, "gx", "gy", None), P(None, ("gx", "gy"))),
        check_vma=False,
    )
```

```python
import math

import jax
import jax.numpy as jnp
from jax import lax
from jax.experimental import pallas as pl
from jax.experimental.pallas import tpu as pltpu
from jax.sharding import PartitionSpec as P

CX = 64
CY = 32
CZ = 128
P_SIZE = 256
HOST = 512
PTS = 2 * P_SIZE

DT_STEP = 0.2
NU_VISC = 0.5
EPS_SQ = 1.44
CORE_SQ = 0.01

ROWS = 16
BACK = 8
YROWS = 72
XROWS = 40
FACE_Y = 3 * CX
FACE_X = 3 * XROWS
RIM_Y = 2 * 3 * YROWS
RIM_X = 2 * 3 * CY
CHUNK = 8
N_CHUNK = CX // CHUNK

F32 = jnp.float32
BF16 = jnp.bfloat16
VM = pl.BlockSpec(memory_space=pltpu.MemorySpace.VMEM)
SM = pl.BlockSpec(memory_space=pltpu.MemorySpace.SMEM)
HB = pl.BlockSpec(memory_space=pltpu.MemorySpace.HBM)
MIB = 1024 * 1024


def call(body, outs, n_in, name, scratch=(), first=VM, second=VM, out_specs=None, in_specs=None, vmem=12, aliases=None):
    return pl.pallas_call(
        body,
        out_shape=[jax.ShapeDtypeStruct(s, F32) for s in outs],
        in_specs=in_specs or ([first, second] + [VM] * n_in)[:n_in],
        out_specs=out_specs or [VM] * len(outs),
        scratch_shapes=list(scratch),
        input_output_aliases=aliases or {},
        compiler_params=pltpu.CompilerParams(vmem_limit_bytes=vmem * MIB),
        name=name,
    )


def place():
    nx, ny = lax.axis_size("gx"), lax.axis_size("gy")
    ix, iy = lax.axis_index("gx"), lax.axis_index("gy")
    px, py = lax.rem(ix, 2), lax.rem(iy, 2)
    inner = (ix + px > 0) & (ix + px < nx)
    return px == 0, py == 0, inner, ix * ny + iy, (ix - px) * ny + iy, ny


def odd_side():
    ny, iy = lax.axis_size("gy"), lax.axis_index("gy")
    py = lax.rem(iy, 2)
    return (iy + py > 0) & (iy + py < ny)


def split(value):
    high = value.astype(BF16)
    low = (value - high.astype(F32)).astype(BF16)
    return high, low


def dot3(a_high, a_low, b_high, b_low):
    def one(a, b):
        return jnp.dot(a, b, preferred_element_type=F32)

    return one(a_high, b_high) + (one(a_high, b_low) + one(a_low, b_high))


def dot3_last(a_high, a_low, b_high, b_low):
    def one(a, b):
        return lax.dot_general(a, b, (((1,), (1,)), ((), ())), preferred_element_type=F32)

    return one(a_high, b_high) + (one(a_high, b_low) + one(a_low, b_high))


def reduce_list(items, op):
    result = items[0]
    for item in items[1:]:
        result = op(result, item)
    return result


def pack_body(v_ref, spin_hbm, *rest):
    params, (pay_c, pay_d, blk_ref, held, held_int, spin_ref, sems) = rest[:5], rest[5:]
    _, even_y, _, brick, _, _ = place()

    def faces(first, second):
        made = []
        for k, (ref, y) in enumerate(((pay_c, first), (pay_d, second))):
            for c in range(3):
                made.append(pltpu.make_async_copy(v_ref.at[c, :, y], ref.at[pl.ds(c * CX, CX)], sems.at[3 * k + c]))
        return made

    @pl.when(even_y)
    def _():
        for copy in faces(CY - 1, 0):
            copy.start()

    @pl.when(jnp.logical_not(even_y))
    def _():
        for copy in faces(0, CY - 1):
            copy.start()

    small = [pltpu.make_async_copy(spin_hbm, spin_ref, sems.at[6])]
    small += [pltpu.make_async_copy(p, held.at[k], sems.at[7 + k]) for k, p in enumerate(params[:4])]
    small.append(pltpu.make_async_copy(params[4], held_int, sems.at[11]))
    for copy in small:
        copy.start()
    for copy in small:
        copy.wait()
    radius, chord, twist, angle = [held[k] for k in range(4)]
    parts = [
        radius,
        chord,
        jnp.cos(twist),
        jnp.sin(twist),
        jnp.cos(angle),
        jnp.sin(angle),
        held_int[...].astype(F32),
        jnp.broadcast_to(spin_ref[...], (1, CZ)),
        jnp.full((1, CZ), brick.astype(F32), F32),
    ]
    block = jnp.concatenate(parts, axis=0)
    blk_ref[...] = block
    pay_c[FACE_Y:] = block
    pay_d[FACE_Y:] = block
    for copy in faces(0, 0):
        copy.wait()


def stencil_body(start, v_ref, out_ref):
    row = lax.broadcasted_iota(jnp.int32, (CY, CZ), 0)
    lane = lax.broadcasted_iota(jnp.int32, (CY, CZ), 1)
    half = 0.5 * DT_STEP
    visc = DT_STEP * NU_VISC
    not_last_y, not_first_y = row < CY - 1, row > 0
    not_last_z, not_first_z = lane < CZ - 1, lane > 0

    def step(k, carry):
        x = start + k
        up = jnp.minimum(x + 1, CX - 1)
        down = jnp.maximum(x - 1, 0)
        v0, v1, v2 = v_ref[0, x], v_ref[1, x], v_ref[2, x]
        a_x = jnp.where(x < CX - 1, visc - half * v0, 0.0)
        b_x = jnp.where(x > 0, visc + half * v0, 0.0)
        a_y = jnp.where(not_last_y, visc - half * v1, 0.0)
        b_y = jnp.where(not_first_y, visc + half * v1, 0.0)
        a_z = jnp.where(not_last_z, visc - half * v2, 0.0)
        b_z = jnp.where(not_first_z, visc + half * v2, 0.0)
        for c in range(3):
            mid = (v0, v1, v2)[c]
            along_x = a_x * v_ref[c, up] + b_x * v_ref[c, down]
            along_y = a_y * pltpu.roll(mid, CY - 1, 0) + b_y * pltpu.roll(mid, 1, 0)
            along_z = a_z * pltpu.roll(mid, CZ - 1, 1) + b_z * pltpu.roll(mid, 1, 1)
            out_ref[c, k] = (1.0 - 6.0 * visc) * mid + along_x + (along_y + along_z)
        return carry

    lax.fori_loop(0, out_ref.shape[1], step, 0, unroll=2)


def weight(coord, base, frac):
    return jnp.where(coord == base, 1.0 - frac, jnp.where(coord == base + 1, frac, 0.0))


def sample_part(start, v_ref, table, acc):
    x_col, y_col = [table[:, k : k + 1].astype(jnp.int32) for k in range(2)]
    fx, fy = [table[:, k : k + 1] for k in range(3, 5)]
    lane = lax.broadcasted_iota(jnp.int32, (HOST, CZ), 1)
    wy = weight(lane % CY, y_col, fy)
    x_lane = (lane // CY + start - x_col).astype(F32).astype(BF16)
    near, far = split((1.0 - fx) * wy), split(fx * wy)
    zero = jnp.zeros((HOST, CZ), BF16)
    per = 4
    nx = CZ * per // CY
    for j in range(CX // 2 // nx):
        highs, lows = [], []
        for i in range(per):
            shift = (CZ // CY) * (j * per + i)
            at_base, at_next = x_lane == jnp.bfloat16(-shift), x_lane == jnp.bfloat16(1 - shift)
            highs.append(jnp.where(at_base, near[0], jnp.where(at_next, far[0], zero)))
            lows.append(jnp.where(at_base, near[1], jnp.where(at_next, far[1], zero)))
        w_high, w_low = jnp.concatenate(highs, axis=1), jnp.concatenate(lows, axis=1)
        first = start + j * nx
        field = [v_ref[c, first : first + nx].reshape(nx * CY, CZ) for c in range(3)]
        f_high, f_low = split(jnp.concatenate(field, axis=1))
        part = dot3(w_high, w_low, f_high, f_low)
        acc = part if acc is None else acc + part
    return acc


def sample_low_body(v_ref, cell_ref, frac_ref, tab_ref, acc_ref, x_ref, y_ref):
    for c in range(3):
        x_ref[c] = v_ref[c, 0]
        x_ref[c + 3] = v_ref[c, CX - 1]
    y_ref[0] = v_ref[1, :, 0, :]
    y_ref[1] = v_ref[1, :, CY - 1, :]
    rows = jnp.concatenate([cell_ref[...].astype(F32), frac_ref[...], jnp.zeros((CZ - 6, HOST), F32)], axis=0)
    table = rows.T
    tab_ref[...] = table
    acc_ref[...] = sample_part(0, v_ref, table, None)


def sample_high_body(v_ref, tab_ref, low_ref, acc_ref, edge_ref, wz_ref):
    table = tab_ref[...]
    acc_ref[...] = sample_part(CX // 2, v_ref, table, low_ref[...])
    lane = lax.broadcasted_iota(jnp.int32, (HOST, CZ), 1)
    x_col, y_col, z_col = [table[:, k : k + 1].astype(jnp.int32) for k in range(3)]
    fx, fy, fz = [table[:, k : k + 1] for k in range(3, 6)]
    on_line = lane >= CX
    edge_x = jnp.where(on_line, lane - CX, CX)
    edge_y = jnp.where(on_line, CY, lane)
    both = weight(edge_x, x_col, fx) * weight(edge_y, y_col, fy)
    edge_ref[...] = jnp.where(on_line | (lane <= CY), both, 0.0)
    wz_ref[...] = weight(lane, z_col, fz)


def split_blocks(sources):
    return [
        ref[first + k * ROWS : first + (k + 1) * ROWS]
        for ref, first in sources
        for k in range((ref.shape[0] - first) // ROWS)
    ]


def pick_pair(values, b0, ny):
    keys = [value[12:13, 0:1] for value in values]
    members = []
    for key in keys:
        home = jnp.floor(key * (1.0 / HOST)).astype(jnp.int32)
        members.append((home == b0) | (home == b0 + ny))
    low_key = reduce_list([jnp.where(m, k, 1e9) for k, m in zip(keys, members)], jnp.minimum)
    high_key = reduce_list([jnp.where(m, k, -9.0) for k, m in zip(keys, members)], jnp.maximum)
    low = jnp.full((ROWS, CZ), -1.0, F32)
    high = low
    for key, value in zip(keys, values):
        low = jnp.where(key == low_key, value, low)
        high = jnp.where(key == high_key, value, high)
    return low, high


def xpack_body(n_blk, x_ref, rec_c, rec_d, *rest):
    pieces, (pay_a, pay_b, own_ref, *others) = rest[:n_blk], rest[n_blk:]
    even_x, even_y, inner, _, b0, ny = place()
    for c in range(3):
        at = c * CX
        y_high = jnp.where(even_y, rec_c[at : at + 1], jnp.where(odd_side(), rec_d[at : at + 1], 0.0))
        tail = jnp.concatenate([y_high, jnp.zeros((XROWS - CY - 1, CZ), F32)], axis=0)
        low, high = x_ref[c], x_ref[c + 3]
        at = c * XROWS
        pay_a[at : at + CY] = jnp.where(even_x, high, low)
        pay_b[at : at + CY] = jnp.where(even_x, low, high)
        pay_a[at + CY : at + XROWS] = tail
        pay_b[at + CY : at + XROWS] = tail
    if not others:
        own_ref[...] = jnp.concatenate([p[...] for p in pieces], axis=0)
        return
    values = split_blocks([(p, 0) for p in pieces])
    chips = ny * 2
    side = jnp.where(even_x, -chips, chips)
    total = lax.axis_size("gx") * ny
    own_ref[...] = jnp.concatenate(pick_pair(values, b0, ny), axis=0)
    beside = jnp.concatenate(pick_pair(values, lax.rem(b0 + side + total, total), ny), axis=0)
    pay_b[FACE_X:] = beside
    others[1][...] = beside
    others[0][...] = jnp.concatenate(pick_pair(values, lax.rem(b0 + 2 * chips, total), ny), axis=0)


def select_body(n_blk, tab_ref, acc_ref, edge_ref, wz_ref, face_a, face_b, rec_c, rec_d, blk_ref, *rest):
    others, (samp_ref, sel_ref, pts_ref) = rest[:n_blk], rest[n_blk:]
    even_x, even_y, inner, brick, b0, ny = place()
    sources = [(blk_ref, 0), (face_b, FACE_X)] + [(o, 0) for o in others]
    turbine_a, turbine_b = pick_pair(split_blocks(sources), b0, ny)
    sel = jnp.concatenate([turbine_a, turbine_b], axis=0)
    sel_ref[...] = sel
    turned = jnp.concatenate([sel, jnp.zeros((CZ - 2 * ROWS, CZ), F32)], axis=0).T

    def column(k):
        picks = (2 * k, 2 * k + 1, ROWS + 2 * k, ROWS + 2 * k + 1)
        return jnp.concatenate([turned[:, j : j + 1] for j in picks], axis=0)

    table = tab_ref[...]
    lane = lax.broadcasted_iota(jnp.int32, (PTS, CZ), 1)
    field = []
    for c in range(3):
        at = c * XROWS
        past = jnp.where(inner, face_b[at : at + XROWS], 0.0)
        plane = jnp.where(even_x, face_a[at : at + XROWS], past)
        at = c * CX
        line = jnp.where(even_y, rec_c[at : at + CX], jnp.where(odd_side(), rec_d[at : at + CX], 0.0))
        field.append(jnp.concatenate([plane, jnp.zeros((CX - XROWS, CZ), F32), line], axis=0))
    w_high, w_low = split(edge_ref[...])
    f_high, f_low = split(jnp.concatenate(field, axis=1))
    acc = acc_ref[...] + dot3(w_high, w_low, f_high, f_low)
    wz = wz_ref[...]
    for c in range(3):
        value = jnp.sum(acc[:, c * CZ : (c + 1) * CZ] * wz, axis=1, keepdims=True)
        table = table + jnp.where(lane == 6 + c, value, 0.0)
    slot = column(6).astype(jnp.int32)
    mine = (slot // HOST) == brick
    local = jnp.where(mine, slot % HOST, -1)
    hit = (lax.broadcasted_iota(jnp.int32, (PTS, HOST), 1) == local).astype(F32).astype(BF16)
    first, second = split(table)
    third = (table - first.astype(F32) - second.astype(F32)).astype(BF16)
    pulled = [jnp.dot(hit, part, preferred_element_type=F32) for part in (first, second, third)]
    points = pulled[0] + pulled[1] + pulled[2]
    points = jnp.where(lane == 9, column(0), points)
    pts_ref[...] = jnp.where((lane == 0) & jnp.logical_not(mine), -100.0, points)
    samp_ref[...] = points.T[6:14]


def offsets(frac):
    raw = [jnp.exp(-((o - frac) ** 2) / EPS_SQ) for o in (-1.0, 0.0, 1.0, 2.0)]
    total = (raw[0] + raw[1]) + (raw[2] + raw[3])
    return [value / total for value in raw]


def profile(rows, inner, base, frac):
    index = lax.broadcasted_iota(jnp.int32, (rows, PTS), 0)
    late = index - inner
    index = jnp.where(index < inner, index, jnp.where(late < 2, late - 2, late - 2 + inner))
    rel = index - base.astype(jnp.int32)
    result = jnp.zeros((rows, PTS), F32)
    for k, w in enumerate(offsets(frac)):
        result = jnp.where(rel == k - 1, w, result)
    return result


def weights_body(pts_ref, sel_ref, gx_ref, gy_ref, pz_ref, pos_ref, pair_ref, edge_ref):
    table = pts_ref[...].T
    gx = profile(YROWS, CX, table[0:1], table[3:4])
    gy = profile(CY, CY, table[1:2], table[4:5])
    gx_ref[...] = gx
    gy_ref[...] = gy
    pz_ref[...] = profile(CZ, CZ, table[2:3], table[5:6]) * DT_STEP
    pos_ref[...] = jnp.concatenate([table[q : q + 1, k * CZ : (k + 1) * CZ] for q in range(6) for k in range(4)], axis=0)
    for t in range(2):
        at = t * ROWS
        radius = jnp.concatenate([sel_ref[at : at + 1], sel_ref[at + 1 : at + 2]], axis=1)
        spacing = radius - pts_ref[t * P_SIZE : (t + 1) * P_SIZE, 9:10]
        pair_ref[t] = spacing / (spacing * spacing + CORE_SQ)
    for k in range(4):
        edge_ref[k * CY : (k + 1) * CY] = gx[CX + k : CX + k + 1] * gy


def attack(axial_flow, tangent, cos_twist, sin_twist):
    rel_speed = jnp.sqrt(axial_flow * axial_flow + tangent * tangent + 1.0)
    cos_phi = tangent / rel_speed
    sin_phi = axial_flow / rel_speed
    sin_alpha = sin_phi * cos_twist - cos_phi * sin_twist
    cos_alpha = cos_phi * cos_twist + sin_phi * sin_twist
    lift_coef = 2.0 * jnp.pi * sin_alpha * cos_alpha / (1.0 + 4.0 * sin_alpha * sin_alpha)
    drag_coef = 0.02 + 0.8 * sin_alpha * sin_alpha
    return rel_speed, cos_phi, sin_phi, lift_coef, drag_coef


def loads_body(samp_ref, other_ref, sel_ref, pz_ref, pos_ref, pair_ref, edge_ref, lh_ref, pay_ref, xrim_ref):
    def row(k):
        picks = (2 * k, 2 * k + 1, ROWS + 2 * k, ROWS + 2 * k + 1)
        return jnp.concatenate([sel_ref[j : j + 1] for j in picks], axis=1)

    radius, chord, cos_t, sin_t, cos_a, sin_a = [row(k) for k in range(6)]
    spin = radius * jnp.concatenate([sel_ref[j : j + 1] for j in (14, 14, ROWS + 14, ROWS + 14)], axis=1)
    flow = samp_ref[...] + other_ref[...]
    axial = flow[0:1]
    tangent = spin - (cos_a * flow[2:3] - sin_a * flow[1:2])
    rel_speed, cos_phi, sin_phi, lift_coef, drag_coef = attack(axial, tangent, cos_t, sin_t)
    circ = 0.5 * chord * rel_speed * lift_coef
    parts = []
    for t in range(2):
        seg = slice(t * P_SIZE, (t + 1) * P_SIZE)
        lhs = jnp.concatenate([cos_a[:, seg] * circ[:, seg], sin_a[:, seg] * circ[:, seg], jnp.zeros((6, P_SIZE), F32)], axis=0)
        both = jnp.dot(lhs, pair_ref[t], preferred_element_type=F32, precision=lax.Precision.HIGHEST)
        parts.append((cos_a[:, seg] * both[0:1] + sin_a[:, seg] * both[1:2]) / (4.0 * math.pi))
    induced = jnp.concatenate(parts, axis=1)
    rel_speed, cos_phi, sin_phi, lift_coef, drag_coef = attack(axial + induced, tangent, cos_t, sin_t)
    dynamic = 0.5 * chord * rel_speed * rel_speed
    lift = dynamic * lift_coef
    drag = dynamic * drag_coef
    thrust = lift * cos_phi + drag * sin_phi
    torque = lift * sin_phi - drag * cos_phi
    force = [-thrust, torque * sin_a, -torque * cos_a]
    pieces = []
    for t in range(2):
        for c in range(3):
            for h in range(2):
                at = t * P_SIZE + h * CZ
                pieces.append(force[c][:, at : at + CZ])
        pieces += [sel_ref[t * ROWS + 15 : t * ROWS + 16]] * 2
    blocks = jnp.concatenate(pieces, axis=0)
    pay_ref[0 : 2 * BACK] = blocks
    pay_ref[2 * BACK :] = pos_ref[...]
    pz = pz_ref[...]
    lines = jnp.concatenate([f * pz for f in force], axis=0)
    l_high, l_low = split(lines)
    lh_ref[...] = lines
    w_high, w_low = split(edge_ref[...])
    rim = dot3_last(w_high, w_low, l_high, l_low)
    for k in range(4):
        for c in range(3):
            at = (k * 3 + c) * CY
            xrim_ref[at : at + CY] = rim[k * CY : (k + 1) * CY, c * CZ : (c + 1) * CZ]


def near_body(rec_c, rec_d, low_ref, high_ref):
    _, even_y, _, _, _, _ = place()
    c_all, d_all = rec_c[...], jnp.where(odd_side(), rec_d[...], 0.0)
    for side, out_ref in ((0, low_ref), (1, high_ref)):
        got = jnp.where(even_y, d_all, c_all) if side == 0 else jnp.where(even_y, c_all, d_all)

        def wide(first, picks):
            return jnp.concatenate([got[first + j : first + j + 1] for j in picks], axis=1)

        x, y, z, fx, fy, fz = [wide(2 * BACK + 4 * q, range(4)) for q in range(6)]
        force = [wide(2 * c, (0, 1, BACK, BACK + 1)) * DT_STEP for c in range(3)]
        pz = profile(CZ, CZ, z, fz)
        l_high, l_low = split(jnp.concatenate([f * pz for f in force], axis=0))
        gx = profile(YROWS, CX, x, fx)
        wy = offsets(fy)
        planes = []
        for i in range(2):
            rel = (CY + i if side == 0 else i - 2) - y.astype(jnp.int32)
            gy = jnp.zeros((1, PTS), F32)
            for k in range(4):
                gy = jnp.where(rel == k - 1, wy[k], gy)
            planes.append(gx * gy)
        w_high, w_low = split(jnp.concatenate(planes, axis=0))
        rim = dot3_last(w_high, w_low, l_high, l_low)
        for i in range(2):
            for c in range(3):
                at = (i * 3 + c) * YROWS
                out_ref[at : at + YROWS] = rim[i * YROWS : (i + 1) * YROWS, c * CZ : (c + 1) * CZ]


SPREAD_X = 8


def spread_body(start, lines_ref, gx_ref, gy_ref, *rest):
    bases, out_ref = rest[:-1], rest[-1]
    l_high, l_low = split(lines_ref[...])
    gy = gy_ref[0:CY]
    held = [(ref, k) for ref in bases for k in range(0, ref.shape[1], SPREAD_X)]
    for k in range(out_ref.shape[1] // SPREAD_X):
        at = k * SPREAD_X
        first = start + at
        planes = jnp.concatenate([gx_ref[first + i : first + i + 1] * gy for i in range(SPREAD_X)], axis=0)
        w_high, w_low = split(planes)
        value = dot3_last(w_high, w_low, l_high, l_low)
        base, inner = held[k]
        for c in range(3):
            part = value[:, c * CZ : (c + 1) * CZ].reshape(SPREAD_X, CY, CZ)
            out_ref[c, at : at + SPREAD_X] = base[c, inner : inner + SPREAD_X] + part


def rimpack_body(n_blk, xrim_ref, low_ref, high_ref, *rest):
    pieces, (pay_a, pay_b, back_ref, *others) = rest[:n_blk], rest[n_blk:]
    even_x, even_y, inner, _, b0, ny = place()
    zero = jnp.zeros((CY - 4, CZ), F32)
    for k in range(2):
        for c in range(3):
            sides = []
            for s in range(2):
                near, far = [], []
                for y in range(2):
                    at = (y * 3 + c) * YROWS + CX + 2 * s + k
                    near.append(low_ref[at : at + 1])
                    far.append(high_ref[at : at + 1])
                at = ((2 * s + k) * 3 + c) * CY
                sides.append(xrim_ref[at : at + CY] + jnp.concatenate(near + [zero] + far, axis=0))
            at = (k * 3 + c) * CY
            pay_a[at : at + CY] = jnp.where(even_x, sides[1], sides[0])
            pay_b[at : at + CY] = jnp.where(even_x, sides[0], sides[1])
    back = jnp.concatenate([p[...] for p in pieces], axis=0)
    back_ref[...] = back
    if others:
        chips = ny * 2
        side = jnp.where(even_x, -chips, chips)
        total = lax.axis_size("gx") * ny
        for ref, at, target in (
            (pay_b, RIM_X, lax.rem(b0 + side + total, total)),
            (others[0], 0, lax.rem(b0 + 2 * chips, total)),
        ):
            for core in range(2):
                wanted = (target + core * ny).astype(F32)
                found = jnp.full((BACK, CZ), -1.0, F32)
                for k in range(back.shape[0] // BACK):
                    value = back[k * BACK : (k + 1) * BACK]
                    found = jnp.where(value[6:7, 0:1] == wanted, value, found)
                ref[at + core * BACK : at + (core + 1) * BACK] = found


def face_terms(buf, at, first, size, main_low, main_high, y_ref, rec_c, rec_d, rim_low, rim_high, even_y):
    half = 0.5 * DT_STEP
    visc = DT_STEP * NU_VISC
    part = slice(first, first + size)
    here = slice(at, at + size)
    half_of = main_low if first < CX // 2 else main_high
    inner = first % (CX // 2)
    for c in range(3):
        buf[c, here] = half_of[c, inner : inner + size]
        rows = slice(c * CX + first, c * CX + first + size)
        a, b = rec_c[rows], jnp.where(odd_side(), rec_d[rows], 0.0)
        low = [jnp.where(even_y, b, a) * (visc + half * y_ref[0, part]), 0.0]
        high = [0.0, jnp.where(even_y, a, b) * (visc - half * y_ref[1, part])]
        for i in range(2):
            row = (i * 3 + c) * YROWS + first
            buf[c, here, i, :] += rim_low[row : row + size] + low[i]
            buf[c, here, CY - 2 + i, :] += rim_high[row : row + size] + high[i]


INNER = [(2, CHUNK - 2)] + [(k * CHUNK, CHUNK) for k in range(1, N_CHUNK - 1)] + [(CX - CHUNK, CHUNK - 2)]


def chunk_copy(buf, at, out_ref, first, size, sem):
    return pltpu.make_async_copy(buf.at[:, pl.ds(at, size)], out_ref.at[:, pl.ds(first, size)], sem)


def inside_body(main_low, main_high, y_ref, rec_c, rec_d, rim_low, rim_high, out_ref, buf, sems):
    _, even_y, _, _, _, _ = place()
    copies = []
    for k, (first, size) in enumerate(INNER):
        face_terms(buf, first - 2, first, size, main_low, main_high, y_ref, rec_c, rec_d, rim_low, rim_high, even_y)
        copies.append(chunk_copy(buf, first - 2, out_ref, first, size, sems.at[k]))
        copies[-1].start()
    for copy in copies:
        copy.wait()


def final_body(n_ret, _, main_low, main_high, x_ref, y_ref, face_a, face_b, rec_c, rec_d, rim_a, rim_b, rim_low, rim_high, back_ref, *rest):
    rets, (out_ref, pf_ref, buf, pf_buf, sems) = rest[:n_ret], rest[n_ret:]
    even_x, even_y, inner, brick, _, _ = place()
    half = 0.5 * DT_STEP
    visc = DT_STEP * NU_VISC
    mine = brick.astype(F32)
    found = jnp.zeros((BACK, CZ), F32)
    for ref, first in [(back_ref, 0), (rim_b, RIM_X)] + [(r, 0) for r in rets]:
        for k in range((ref.shape[0] - first) // BACK):
            value = ref[first + BACK * k : first + BACK * k + BACK]
            found = jnp.where(value[6:7, 0:1] == mine, value, found)
    for c in range(3):
        pf_buf[c : c + 1] = jnp.concatenate([found[2 * c : 2 * c + 1], found[2 * c + 1 : 2 * c + 2]], axis=1)
    copies = [pltpu.make_async_copy(pf_buf, pf_ref, sems.at[2])]
    copies[0].start()
    for k in range(2):
        first, at = k * (CX - 2), k * 2
        face_terms(buf, at, first, 2, main_low, main_high, y_ref, rec_c, rec_d, rim_low, rim_high, even_y)
        for c in range(3):
            a = face_a[c * XROWS : c * XROWS + CY]
            b = jnp.where(inner, face_b[c * XROWS : c * XROWS + CY], 0.0)
            if k == 0:
                buf[c, 0] += jnp.where(even_x, b, a) * (visc + half * x_ref[0])
            else:
                buf[c, 3] += jnp.where(even_x, a, b) * (visc - half * x_ref[3])
            for i in range(2):
                rows = slice((i * 3 + c) * CY, (i * 3 + c + 1) * CY)
                a, b = rim_a[rows], jnp.where(inner, rim_b[rows], 0.0)
                if k == 0:
                    buf[c, i] += jnp.where(even_x, b, a)
                else:
                    buf[c, 2 + i] += jnp.where(even_x, a, b)
        copies.append(chunk_copy(buf, at, out_ref, first, 2, sems.at[k]))
        copies[-1].start()
    for copy in copies:
        copy.wait()


def per_device(
    velocity,
    host_cell,
    host_frac,
    host_dst,
    owner_src,
    rotor_speed,
    blade_radius,
    blade_chord,
    blade_twist,
    blade_angle,
):
    nx, ny = lax.axis_size("gx"), lax.axis_size("gy")
    ring, short = nx == 8, ny == 4

    def flip(n, bits):
        return [(i, i ^ bits) for i in range(n)]

    def odd_pairs(n, closed=False):
        up = [(i, (i + 1) % n) for i in range(1, n if closed else n - 1, 2)]
        return up + [(t, s) for s, t in up]

    def same_side(n):
        return [(i, (i + (2 if i % 2 else n - 2)) % n) for i in range(n)]

    def across_x(blocks):
        return [lax.ppermute(b, "gx", p) for b, p in zip(blocks, (flip(nx, 4), same_side(nx)))]

    def swap(block):
        return lax.ppermute(block, "gx", flip(nx, 1))

    def join(pieces):
        return pieces[0] if len(pieces) == 1 else jnp.concatenate(pieces, axis=0)

    def after(values, other):
        return lax.optimization_barrier((values, other))

    def gather_y(first):
        pieces = [first]
        for bit in [b for b in (2, 4, 8) if b < ny]:
            pieces.append(lax.ppermute(join(pieces), "gy", flip(ny, bit)))
        return pieces

    def exchange_y(to_c, to_d, block):
        from_c = lax.ppermute(to_c, "gy", flip(ny, 1))
        from_d = lax.ppermute(to_d, "gy", flip(ny, 3) if short else odd_pairs(ny))
        return from_c, from_d, [lax.ppermute(block, "gy", flip(ny, 2))] if short else []

    def blocks_y(block, from_c, from_d, far, size, at):
        got = join([block, from_c[at : at + size]])
        if short:
            return [join([got, from_d[at : at + size]] + far)]
        return gather_y(got)

    def gather_x(blocks):
        pieces = []
        for bit in [b for b in (2, 4, 8, 16) if b < nx]:
            pieces.append(lax.ppermute(join([blocks] + pieces), "gx", flip(nx, bit)))
        return pieces

    dma = pltpu.SemaphoreType.DMA
    pay_c, pay_d, block = call(
        pack_body,
        [(FACE_Y + ROWS, CZ)] * 2 + [(ROWS, CZ)],
        7,
        "pack",
        scratch=[pltpu.VMEM((4, 2, CZ), F32), pltpu.VMEM((2, CZ), jnp.int32), pltpu.VMEM((1, 1), F32), dma((12,))],
        in_specs=[HB] * 7,
        vmem=56,
    )(velocity, rotor_speed.reshape(1, 1), *[a.reshape(2, CZ) for a in (blade_radius, blade_chord, blade_twist, blade_angle, owner_src)])
    rec_c, rec_d, far = exchange_y(pay_c, pay_d, block)

    def stencil(start, count):
        return call(lambda *refs: stencil_body(start, *refs), [(3, count, CY, CZ)], 1, "stencil")(velocity)[0]

    base_low = stencil(0, CX // 2)
    table, sums, x_faces, y_faces = call(
        sample_low_body, [(HOST, CZ), (HOST, 3 * CZ), (6, CY, CZ), (2, CX, CZ)], 3, "sample_low", vmem=24
    )(velocity, host_cell, host_frac)
    (rec_c, rec_d, far), (base_low, sums) = after((rec_c, rec_d, far), (base_low, sums))
    pieces = blocks_y(block, rec_c, rec_d, far, ROWS, FACE_Y)
    beside = [swap(p) for p in pieces]
    beside, base_third = after(beside, stencil(CX // 2, CX // 4))
    pieces = pieces + beside
    n_rows = 2 * ny * ROWS
    pair = (2 * ROWS, CZ)
    pay_a, pay_b, blocks, *across = call(
        lambda *refs: xpack_body(len(pieces), *refs),
        [(FACE_X, CZ), (FACE_X + 2 * ROWS, CZ), pair, pair, pair] if ring else [(FACE_X, CZ), (FACE_X, CZ), (n_rows, CZ)],
        3 + len(pieces),
        "xpack",
    )(x_faces, rec_c, rec_d, *pieces)
    face_b = lax.ppermute(pay_b, "gx", odd_pairs(nx, ring))
    from_x = across_x(across) if ring else gather_x(blocks)
    face_a = swap(pay_a)
    sums, edge, wz = call(
        sample_high_body, [(HOST, 3 * CZ), (HOST, CZ), (HOST, CZ)], 3, "sample_high", vmem=24
    )(velocity, table, sums)
    (face_a, face_b, from_x), sums = after((face_a, face_b, from_x), sums)
    samp, sel, pts = call(
        lambda *refs: select_body(len(from_x), *refs),
        [(8, PTS), (2 * ROWS, CZ), (PTS, CZ)],
        9 + len(from_x),
        "select",
    )(table, sums, edge, wz, face_a, face_b, rec_c, rec_d, blocks, *from_x)
    other = swap(samp)
    gx, gy, pz, pos, pair_kernel, edge = call(
        weights_body,
        [(YROWS, PTS), (CY, PTS), (CZ, PTS), (24, CZ), (2, P_SIZE, P_SIZE), (4 * CY, PTS)],
        2,
        "weights",
    )(pts, sel)
    other, base_next = after(other, stencil(6 * CX // 8, CX // 8))
    lines, points, xrim = call(
        loads_body,
        [(3 * CZ, PTS), (2 * BACK + 24, CZ), (2 * RIM_X, CZ)],
        7,
        "loads",
    )(samp, other, sel, pz, pos, pair_kernel, edge)
    ret = points[: 2 * BACK]
    near_c, near_d, far = exchange_y(points, points, ret)

    def spread(start, *bases):
        return call(
            lambda *refs: spread_body(start, *refs), [(3, CX // 2, CY, CZ)], 3 + len(bases), "spread"
        )(lines, gx, gy, *bases)[0]

    (near_c, near_d), main_low = after((near_c, near_d), spread(0, base_low))
    rim_low, rim_high = call(near_body, [(RIM_Y, CZ)] * 2, 2, "near")(near_c, near_d)
    far, rim_low = after(far, rim_low)
    pieces = blocks_y(ret, near_c, near_d, far, 2 * BACK, 0)
    n_rows = 2 * ny * BACK
    pair = (2 * BACK, CZ)
    pay_a, pay_b, back, *across = call(
        lambda *refs: rimpack_body(len(pieces), *refs),
        [(RIM_X, CZ), (RIM_X + 2 * BACK, CZ), (n_rows, CZ), pair] if ring else [(RIM_X, CZ), (RIM_X, CZ), (n_rows, CZ)],
        3 + len(pieces),
        "rimpack",
    )(xrim, rim_low, rim_high, *pieces)
    rim_b = lax.ppermute(pay_b, "gx", odd_pairs(nx, ring))
    rets = [lax.ppermute(across[0], "gx", flip(nx, 4))] if ring else gather_x(back)
    rim_a = swap(pay_a)
    main_high = spread(CX // 2, base_third, base_next, stencil(7 * CX // 8, CX // 8))
    (rim_a, rim_b), (main_low, main_high) = after((rim_a, rim_b), (main_low, main_high))
    if ring:
        rets.append(swap(rim_b[RIM_X:]))
    inside = call(
        inside_body,
        [velocity.shape],
        7,
        "inside",
        scratch=[pltpu.VMEM((3, CX - 4, CY, CZ), F32), dma((N_CHUNK,))],
        out_specs=[HB],
        vmem=16,
    )(main_low, main_high, y_faces, rec_c, rec_d, rim_low, rim_high)[0]
    rets, inside = after(rets, inside)
    return tuple(
        call(
            lambda *refs: final_body(len(rets), *refs),
            [velocity.shape, (3, P_SIZE)],
            14 + len(rets),
            "final",
            scratch=[pltpu.VMEM((3, 4, CY, CZ), F32), pltpu.VMEM((3, P_SIZE), F32), dma((3,))],
            first=HB,
            out_specs=[HB, HB],
            aliases={0: 0},
        )(inside, main_low, main_high, x_faces, y_faces, face_a, face_b, rec_c, rec_d, rim_a, rim_b, rim_low, rim_high, back, *rets)
    )


def solution(mesh):
    return jax.shard_map(
        per_device,
        mesh=mesh,
        in_specs=(
            P(None, "gx", "gy", None),
            P(None, ("gx", "gy")),
            P(None, ("gx", "gy")),
            P(("gx", "gy")),
            P(("gx", "gy")),
            P(("gx", "gy")),
            P(("gx", "gy")),
            P(("gx", "gy")),
            P(("gx", "gy")),
            P(("gx", "gy")),
        ),
        out_specs=(P(None, "gx", "gy", None), P(None, ("gx", "gy"))),
        check_vma=False,
    )
```

```python
import math

import jax
import jax.numpy as jnp
from jax import lax
from jax.experimental import pallas as pl
from jax.experimental.pallas import tpu as pltpu
from jax.sharding import PartitionSpec as P

CX = 64
CY = 32
CZ = 128
P_SIZE = 256
HOST = 512
PTS = 2 * P_SIZE

DT_STEP = 0.2
NU_VISC = 0.5
EPS_SQ = 1.44
CORE_SQ = 0.01

ROWS = 16
BACK = 8
YROWS = 72
XROWS = 40
FACE_Y = 3 * CX
FACE_X = 3 * XROWS
RIM_Y = 2 * 3 * YROWS
RIM_X = 2 * 3 * CY
CHUNK = 8
N_CHUNK = CX // CHUNK

F32 = jnp.float32
BF16 = jnp.bfloat16
VM = pl.BlockSpec(memory_space=pltpu.MemorySpace.VMEM)
SM = pl.BlockSpec(memory_space=pltpu.MemorySpace.SMEM)
HB = pl.BlockSpec(memory_space=pltpu.MemorySpace.HBM)
MIB = 1024 * 1024


def call(body, outs, n_in, name, scratch=(), first=VM, second=VM, out_specs=None, in_specs=None, vmem=12, aliases=None):
    return pl.pallas_call(
        body,
        out_shape=[jax.ShapeDtypeStruct(s, F32) for s in outs],
        in_specs=in_specs or ([first, second] + [VM] * n_in)[:n_in],
        out_specs=out_specs or [VM] * len(outs),
        scratch_shapes=list(scratch),
        input_output_aliases=aliases or {},
        compiler_params=pltpu.CompilerParams(vmem_limit_bytes=vmem * MIB),
        name=name,
    )


def place():
    nx, ny = lax.axis_size("gx"), lax.axis_size("gy")
    ix, iy = lax.axis_index("gx"), lax.axis_index("gy")
    px, py = lax.rem(ix, 2), lax.rem(iy, 2)
    inner = (ix + px > 0) & (ix + px < nx)
    return px == 0, py == 0, inner, ix * ny + iy, (ix - px) * ny + iy, ny


def odd_side():
    ny, iy = lax.axis_size("gy"), lax.axis_index("gy")
    py = lax.rem(iy, 2)
    return (iy + py > 0) & (iy + py < ny)


def split(value):
    high = value.astype(BF16)
    low = (value - high.astype(F32)).astype(BF16)
    return high, low


def dot3(a_high, a_low, b_high, b_low):
    def one(a, b):
        return jnp.dot(a, b, preferred_element_type=F32)

    return one(a_high, b_high) + (one(a_high, b_low) + one(a_low, b_high))


def dot3_last(a_high, a_low, b_high, b_low):
    def one(a, b):
        return lax.dot_general(a, b, (((1,), (1,)), ((), ())), preferred_element_type=F32)

    return one(a_high, b_high) + (one(a_high, b_low) + one(a_low, b_high))


def reduce_list(items, op):
    result = items[0]
    for item in items[1:]:
        result = op(result, item)
    return result


def pack_body(v_ref, spin_hbm, *rest):
    params, (pay_c, pay_d, blk_ref, held, held_int, spin_ref, sems) = rest[:5], rest[5:]
    _, even_y, _, brick, _, _ = place()

    def faces(first, second):
        made = []
        for k, (ref, y) in enumerate(((pay_c, first), (pay_d, second))):
            for c in range(3):
                made.append(pltpu.make_async_copy(v_ref.at[c, :, y], ref.at[pl.ds(c * CX, CX)], sems.at[3 * k + c]))
        return made

    @pl.when(even_y)
    def _():
        for copy in faces(CY - 1, 0):
            copy.start()

    @pl.when(jnp.logical_not(even_y))
    def _():
        for copy in faces(0, CY - 1):
            copy.start()

    small = [pltpu.make_async_copy(spin_hbm, spin_ref, sems.at[6])]
    small += [pltpu.make_async_copy(p, held.at[k], sems.at[7 + k]) for k, p in enumerate(params[:4])]
    small.append(pltpu.make_async_copy(params[4], held_int, sems.at[11]))
    for copy in small:
        copy.start()
    for copy in small:
        copy.wait()
    radius, chord, twist, angle = [held[k] for k in range(4)]
    parts = [
        radius,
        chord,
        jnp.cos(twist),
        jnp.sin(twist),
        jnp.cos(angle),
        jnp.sin(angle),
        held_int[...].astype(F32),
        jnp.broadcast_to(spin_ref[...], (1, CZ)),
        jnp.full((1, CZ), brick.astype(F32), F32),
    ]
    block = jnp.concatenate(parts, axis=0)
    blk_ref[...] = block
    pay_c[FACE_Y:] = block
    pay_d[FACE_Y:] = block
    for copy in faces(0, 0):
        copy.wait()


def stencil_body(start, v_ref, out_ref):
    row = lax.broadcasted_iota(jnp.int32, (CY, CZ), 0)
    lane = lax.broadcasted_iota(jnp.int32, (CY, CZ), 1)
    half = 0.5 * DT_STEP
    visc = DT_STEP * NU_VISC
    not_last_y, not_first_y = row < CY - 1, row > 0
    not_last_z, not_first_z = lane < CZ - 1, lane > 0

    def step(k, carry):
        x = start + k
        up = jnp.minimum(x + 1, CX - 1)
        down = jnp.maximum(x - 1, 0)
        v0, v1, v2 = v_ref[0, x], v_ref[1, x], v_ref[2, x]
        a_x = jnp.where(x < CX - 1, visc - half * v0, 0.0)
        b_x = jnp.where(x > 0, visc + half * v0, 0.0)
        a_y = jnp.where(not_last_y, visc - half * v1, 0.0)
        b_y = jnp.where(not_first_y, visc + half * v1, 0.0)
        a_z = jnp.where(not_last_z, visc - half * v2, 0.0)
        b_z = jnp.where(not_first_z, visc + half * v2, 0.0)
        for c in range(3):
            mid = (v0, v1, v2)[c]
            along_x = a_x * v_ref[c, up] + b_x * v_ref[c, down]
            along_y = a_y * pltpu.roll(mid, CY - 1, 0) + b_y * pltpu.roll(mid, 1, 0)
            along_z = a_z * pltpu.roll(mid, CZ - 1, 1) + b_z * pltpu.roll(mid, 1, 1)
            out_ref[c, k] = (1.0 - 6.0 * visc) * mid + along_x + (along_y + along_z)
        return carry

    lax.fori_loop(0, out_ref.shape[1], step, 0, unroll=2)


def weight(coord, base, frac):
    return jnp.where(coord == base, 1.0 - frac, jnp.where(coord == base + 1, frac, 0.0))


def sample_part(start, v_ref, table, acc):
    x_col, y_col = [table[:, k : k + 1].astype(jnp.int32) for k in range(2)]
    fx, fy = [table[:, k : k + 1] for k in range(3, 5)]
    lane = lax.broadcasted_iota(jnp.int32, (HOST, CZ), 1)
    wy = weight(lane % CY, y_col, fy)
    x_lane = (lane // CY + start - x_col).astype(F32).astype(BF16)
    near, far = split((1.0 - fx) * wy), split(fx * wy)
    zero = jnp.zeros((HOST, CZ), BF16)
    per = 4
    nx = CZ * per // CY
    for j in range(CX // 2 // nx):
        highs, lows = [], []
        for i in range(per):
            shift = (CZ // CY) * (j * per + i)
            at_base, at_next = x_lane == jnp.bfloat16(-shift), x_lane == jnp.bfloat16(1 - shift)
            highs.append(jnp.where(at_base, near[0], jnp.where(at_next, far[0], zero)))
            lows.append(jnp.where(at_base, near[1], jnp.where(at_next, far[1], zero)))
        w_high, w_low = jnp.concatenate(highs, axis=1), jnp.concatenate(lows, axis=1)
        first = start + j * nx
        field = [v_ref[c, first : first + nx].reshape(nx * CY, CZ) for c in range(3)]
        f_high, f_low = split(jnp.concatenate(field, axis=1))
        part = dot3(w_high, w_low, f_high, f_low)
        acc = part if acc is None else acc + part
    return acc


def sample_low_body(v_ref, cell_ref, frac_ref, tab_ref, acc_ref, x_ref, y_ref):
    for c in range(3):
        x_ref[c] = v_ref[c, 0]
        x_ref[c + 3] = v_ref[c, CX - 1]
    y_ref[0] = v_ref[1, :, 0, :]
    y_ref[1] = v_ref[1, :, CY - 1, :]
    rows = jnp.concatenate([cell_ref[...].astype(F32), frac_ref[...], jnp.zeros((CZ - 6, HOST), F32)], axis=0)
    table = rows.T
    tab_ref[...] = table
    acc_ref[...] = sample_part(0, v_ref, table, None)


def sample_high_body(v_ref, tab_ref, low_ref, acc_ref, edge_ref, wz_ref):
    table = tab_ref[...]
    acc_ref[...] = sample_part(CX // 2, v_ref, table, low_ref[...])
    lane = lax.broadcasted_iota(jnp.int32, (HOST, CZ), 1)
    x_col, y_col, z_col = [table[:, k : k + 1].astype(jnp.int32) for k in range(3)]
    fx, fy, fz = [table[:, k : k + 1] for k in range(3, 6)]
    on_line = lane >= CX
    edge_x = jnp.where(on_line, lane - CX, CX)
    edge_y = jnp.where(on_line, CY, lane)
    both = weight(edge_x, x_col, fx) * weight(edge_y, y_col, fy)
    edge_ref[...] = jnp.where(on_line | (lane <= CY), both, 0.0)
    wz_ref[...] = weight(lane, z_col, fz)


def split_blocks(sources):
    return [
        ref[first + k * ROWS : first + (k + 1) * ROWS]
        for ref, first in sources
        for k in range((ref.shape[0] - first) // ROWS)
    ]


def pick_pair(values, b0, ny):
    keys = [value[12:13, 0:1] for value in values]
    members = []
    for key in keys:
        home = jnp.floor(key * (1.0 / HOST)).astype(jnp.int32)
        members.append((home == b0) | (home == b0 + ny))
    low_key = reduce_list([jnp.where(m, k, 1e9) for k, m in zip(keys, members)], jnp.minimum)
    high_key = reduce_list([jnp.where(m, k, -9.0) for k, m in zip(keys, members)], jnp.maximum)
    low = jnp.full((ROWS, CZ), -1.0, F32)
    high = low
    for key, value in zip(keys, values):
        low = jnp.where(key == low_key, value, low)
        high = jnp.where(key == high_key, value, high)
    return low, high


def xpack_body(n_blk, x_ref, rec_c, rec_d, *rest):
    pieces, (pay_a, pay_b, own_ref, *others) = rest[:n_blk], rest[n_blk:]
    even_x, even_y, inner, _, b0, ny = place()
    for c in range(3):
        at = c * CX
        y_high = jnp.where(even_y, rec_c[at : at + 1], jnp.where(odd_side(), rec_d[at : at + 1], 0.0))
        tail = jnp.concatenate([y_high, jnp.zeros((XROWS - CY - 1, CZ), F32)], axis=0)
        low, high = x_ref[c], x_ref[c + 3]
        at = c * XROWS
        pay_a[at : at + CY] = jnp.where(even_x, high, low)
        pay_b[at : at + CY] = jnp.where(even_x, low, high)
        pay_a[at + CY : at + XROWS] = tail
        pay_b[at + CY : at + XROWS] = tail
    if not others:
        own_ref[...] = jnp.concatenate([p[...] for p in pieces], axis=0)
        return
    values = split_blocks([(p, 0) for p in pieces])
    chips = ny * 2
    side = jnp.where(even_x, -chips, chips)
    total = lax.axis_size("gx") * ny
    own_ref[...] = jnp.concatenate(pick_pair(values, b0, ny), axis=0)
    beside = jnp.concatenate(pick_pair(values, lax.rem(b0 + side + total, total), ny), axis=0)
    pay_b[FACE_X:] = beside
    others[1][...] = beside
    others[0][...] = jnp.concatenate(pick_pair(values, lax.rem(b0 + 2 * chips, total), ny), axis=0)


def select_body(n_blk, tab_ref, acc_ref, edge_ref, wz_ref, face_a, face_b, rec_c, rec_d, blk_ref, *rest):
    others, (samp_ref, sel_ref, pts_ref) = rest[:n_blk], rest[n_blk:]
    even_x, even_y, inner, brick, b0, ny = place()
    sources = [(blk_ref, 0), (face_b, FACE_X)] + [(o, 0) for o in others]
    turbine_a, turbine_b = pick_pair(split_blocks(sources), b0, ny)
    sel = jnp.concatenate([turbine_a, turbine_b], axis=0)
    sel_ref[...] = sel
    turned = jnp.concatenate([sel, jnp.zeros((CZ - 2 * ROWS, CZ), F32)], axis=0).T

    def column(k):
        picks = (2 * k, 2 * k + 1, ROWS + 2 * k, ROWS + 2 * k + 1)
        return jnp.concatenate([turned[:, j : j + 1] for j in picks], axis=0)

    table = tab_ref[...]
    lane = lax.broadcasted_iota(jnp.int32, (PTS, CZ), 1)
    field = []
    for c in range(3):
        at = c * XROWS
        past = jnp.where(inner, face_b[at : at + XROWS], 0.0)
        plane = jnp.where(even_x, face_a[at : at + XROWS], past)
        at = c * CX
        line = jnp.where(even_y, rec_c[at : at + CX], jnp.where(odd_side(), rec_d[at : at + CX], 0.0))
        field.append(jnp.concatenate([plane, jnp.zeros((CX - XROWS, CZ), F32), line], axis=0))
    w_high, w_low = split(edge_ref[...])
    f_high, f_low = split(jnp.concatenate(field, axis=1))
    acc = acc_ref[...] + dot3(w_high, w_low, f_high, f_low)
    wz = wz_ref[...]
    for c in range(3):
        value = jnp.sum(acc[:, c * CZ : (c + 1) * CZ] * wz, axis=1, keepdims=True)
        table = table + jnp.where(lane == 6 + c, value, 0.0)
    slot = column(6).astype(jnp.int32)
    mine = (slot // HOST) == brick
    local = jnp.where(mine, slot % HOST, -1)
    hit = (lax.broadcasted_iota(jnp.int32, (PTS, HOST), 1) == local).astype(F32).astype(BF16)
    first, second = split(table)
    third = (table - first.astype(F32) - second.astype(F32)).astype(BF16)
    pulled = [jnp.dot(hit, part, preferred_element_type=F32) for part in (first, second, third)]
    points = pulled[0] + pulled[1] + pulled[2]
    points = jnp.where(lane == 9, column(0), points)
    pts_ref[...] = jnp.where((lane == 0) & jnp.logical_not(mine), -100.0, points)
    samp_ref[...] = points.T[6:14]


def offsets(frac):
    raw = [jnp.exp(-((o - frac) ** 2) / EPS_SQ) for o in (-1.0, 0.0, 1.0, 2.0)]
    total = (raw[0] + raw[1]) + (raw[2] + raw[3])
    return [value / total for value in raw]


def profile(rows, inner, base, frac):
    index = lax.broadcasted_iota(jnp.int32, (rows, PTS), 0)
    late = index - inner
    index = jnp.where(index < inner, index, jnp.where(late < 2, late - 2, late - 2 + inner))
    rel = index - base.astype(jnp.int32)
    result = jnp.zeros((rows, PTS), F32)
    for k, w in enumerate(offsets(frac)):
        result = jnp.where(rel == k - 1, w, result)
    return result


def weights_body(pts_ref, sel_ref, gx_ref, gy_ref, pz_ref, pos_ref, pair_ref, edge_ref):
    table = pts_ref[...].T
    gx = profile(YROWS, CX, table[0:1], table[3:4])
    gy = profile(CY, CY, table[1:2], table[4:5])
    gx_ref[...] = gx
    gy_ref[...] = gy
    pz_ref[...] = profile(CZ, CZ, table[2:3], table[5:6]) * DT_STEP
    pos_ref[...] = jnp.concatenate([table[q : q + 1, k * CZ : (k + 1) * CZ] for q in range(6) for k in range(4)], axis=0)
    for t in range(2):
        at = t * ROWS
        radius = jnp.concatenate([sel_ref[at : at + 1], sel_ref[at + 1 : at + 2]], axis=1)
        spacing = radius - pts_ref[t * P_SIZE : (t + 1) * P_SIZE, 9:10]
        pair_ref[t] = spacing / (spacing * spacing + CORE_SQ)
    for k in range(4):
        edge_ref[k * CY : (k + 1) * CY] = gx[CX + k : CX + k + 1] * gy


def attack(axial_flow, tangent, cos_twist, sin_twist):
    rel_speed = jnp.sqrt(axial_flow * axial_flow + tangent * tangent + 1.0)
    cos_phi = tangent / rel_speed
    sin_phi = axial_flow / rel_speed
    sin_alpha = sin_phi * cos_twist - cos_phi * sin_twist
    cos_alpha = cos_phi * cos_twist + sin_phi * sin_twist
    lift_coef = 2.0 * jnp.pi * sin_alpha * cos_alpha / (1.0 + 4.0 * sin_alpha * sin_alpha)
    drag_coef = 0.02 + 0.8 * sin_alpha * sin_alpha
    return rel_speed, cos_phi, sin_phi, lift_coef, drag_coef


def loads_body(samp_ref, other_ref, sel_ref, pz_ref, pos_ref, pair_ref, edge_ref, lh_ref, pay_ref, xrim_ref):
    def row(k):
        picks = (2 * k, 2 * k + 1, ROWS + 2 * k, ROWS + 2 * k + 1)
        return jnp.concatenate([sel_ref[j : j + 1] for j in picks], axis=1)

    radius, chord, cos_t, sin_t, cos_a, sin_a = [row(k) for k in range(6)]
    spin = radius * jnp.concatenate([sel_ref[j : j + 1] for j in (14, 14, ROWS + 14, ROWS + 14)], axis=1)
    flow = samp_ref[...] + other_ref[...]
    axial = flow[0:1]
    tangent = spin - (cos_a * flow[2:3] - sin_a * flow[1:2])
    rel_speed, cos_phi, sin_phi, lift_coef, drag_coef = attack(axial, tangent, cos_t, sin_t)
    circ = 0.5 * chord * rel_speed * lift_coef
    parts = []
    for t in range(2):
        seg = slice(t * P_SIZE, (t + 1) * P_SIZE)
        lhs = jnp.concatenate([cos_a[:, seg] * circ[:, seg], sin_a[:, seg] * circ[:, seg], jnp.zeros((6, P_SIZE), F32)], axis=0)
        both = jnp.dot(lhs, pair_ref[t], preferred_element_type=F32, precision=lax.Precision.HIGHEST)
        parts.append((cos_a[:, seg] * both[0:1] + sin_a[:, seg] * both[1:2]) / (4.0 * math.pi))
    induced = jnp.concatenate(parts, axis=1)
    rel_speed, cos_phi, sin_phi, lift_coef, drag_coef = attack(axial + induced, tangent, cos_t, sin_t)
    dynamic = 0.5 * chord * rel_speed * rel_speed
    lift = dynamic * lift_coef
    drag = dynamic * drag_coef
    thrust = lift * cos_phi + drag * sin_phi
    torque = lift * sin_phi - drag * cos_phi
    force = [-thrust, torque * sin_a, -torque * cos_a]
    pieces = []
    for t in range(2):
        for c in range(3):
            for h in range(2):
                at = t * P_SIZE + h * CZ
                pieces.append(force[c][:, at : at + CZ])
        pieces += [sel_ref[t * ROWS + 15 : t * ROWS + 16]] * 2
    blocks = jnp.concatenate(pieces, axis=0)
    pay_ref[0 : 2 * BACK] = blocks
    pay_ref[2 * BACK :] = pos_ref[...]
    pz = pz_ref[...]
    lines = jnp.concatenate([f * pz for f in force], axis=0)
    l_high, l_low = split(lines)
    lh_ref[...] = lines
    w_high, w_low = split(edge_ref[...])
    rim = dot3_last(w_high, w_low, l_high, l_low)
    for k in range(4):
        for c in range(3):
            at = (k * 3 + c) * CY
            xrim_ref[at : at + CY] = rim[k * CY : (k + 1) * CY, c * CZ : (c + 1) * CZ]


def near_body(rec_c, rec_d, low_ref, high_ref):
    _, even_y, _, _, _, _ = place()
    c_all, d_all = rec_c[...], jnp.where(odd_side(), rec_d[...], 0.0)
    for side, out_ref in ((0, low_ref), (1, high_ref)):
        got = jnp.where(even_y, d_all, c_all) if side == 0 else jnp.where(even_y, c_all, d_all)

        def wide(first, picks):
            return jnp.concatenate([got[first + j : first + j + 1] for j in picks], axis=1)

        x, y, z, fx, fy, fz = [wide(2 * BACK + 4 * q, range(4)) for q in range(6)]
        force = [wide(2 * c, (0, 1, BACK, BACK + 1)) * DT_STEP for c in range(3)]
        pz = profile(CZ, CZ, z, fz)
        l_high, l_low = split(jnp.concatenate([f * pz for f in force], axis=0))
        gx = profile(YROWS, CX, x, fx)
        wy = offsets(fy)
        planes = []
        for i in range(2):
            rel = (CY + i if side == 0 else i - 2) - y.astype(jnp.int32)
            gy = jnp.zeros((1, PTS), F32)
            for k in range(4):
                gy = jnp.where(rel == k - 1, wy[k], gy)
            planes.append(gx * gy)
        w_high, w_low = split(jnp.concatenate(planes, axis=0))
        rim = dot3_last(w_high, w_low, l_high, l_low)
        for i in range(2):
            for c in range(3):
                at = (i * 3 + c) * YROWS
                out_ref[at : at + YROWS] = rim[i * YROWS : (i + 1) * YROWS, c * CZ : (c + 1) * CZ]


SPREAD_X = 8


def spread_body(start, lines_ref, gx_ref, gy_ref, *rest):
    bases, out_ref = rest[:-1], rest[-1]
    l_high, l_low = split(lines_ref[...])
    gy = gy_ref[0:CY]
    held = [(ref, k) for ref in bases for k in range(0, ref.shape[1], SPREAD_X)]
    for k in range(out_ref.shape[1] // SPREAD_X):
        at = k * SPREAD_X
        first = start + at
        planes = jnp.concatenate([gx_ref[first + i : first + i + 1] * gy for i in range(SPREAD_X)], axis=0)
        w_high, w_low = split(planes)
        value = dot3_last(w_high, w_low, l_high, l_low)
        base, inner = held[k]
        for c in range(3):
            part = value[:, c * CZ : (c + 1) * CZ].reshape(SPREAD_X, CY, CZ)
            out_ref[c, at : at + SPREAD_X] = base[c, inner : inner + SPREAD_X] + part


def rimpack_body(n_blk, xrim_ref, low_ref, high_ref, *rest):
    pieces, (pay_a, pay_b, back_ref, *others) = rest[:n_blk], rest[n_blk:]
    even_x, even_y, inner, _, b0, ny = place()
    zero = jnp.zeros((CY - 4, CZ), F32)
    for k in range(2):
        for c in range(3):
            sides = []
            for s in range(2):
                near, far = [], []
                for y in range(2):
                    at = (y * 3 + c) * YROWS + CX + 2 * s + k
                    near.append(low_ref[at : at + 1])
                    far.append(high_ref[at : at + 1])
                at = ((2 * s + k) * 3 + c) * CY
                sides.append(xrim_ref[at : at + CY] + jnp.concatenate(near + [zero] + far, axis=0))
            at = (k * 3 + c) * CY
            pay_a[at : at + CY] = jnp.where(even_x, sides[1], sides[0])
            pay_b[at : at + CY] = jnp.where(even_x, sides[0], sides[1])
    back = jnp.concatenate([p[...] for p in pieces], axis=0)
    back_ref[...] = back
    if others:
        chips = ny * 2
        side = jnp.where(even_x, -chips, chips)
        total = lax.axis_size("gx") * ny
        for ref, at, target in (
            (pay_b, RIM_X, lax.rem(b0 + side + total, total)),
            (others[0], 0, lax.rem(b0 + 2 * chips, total)),
        ):
            for core in range(2):
                wanted = (target + core * ny).astype(F32)
                found = jnp.full((BACK, CZ), -1.0, F32)
                for k in range(back.shape[0] // BACK):
                    value = back[k * BACK : (k + 1) * BACK]
                    found = jnp.where(value[6:7, 0:1] == wanted, value, found)
                ref[at + core * BACK : at + (core + 1) * BACK] = found


def face_terms(buf, at, first, size, main_low, main_high, y_ref, rec_c, rec_d, rim_low, rim_high, even_y):
    half = 0.5 * DT_STEP
    visc = DT_STEP * NU_VISC
    part = slice(first, first + size)
    here = slice(at, at + size)
    half_of = main_low if first < CX // 2 else main_high
    inner = first % (CX // 2)
    for c in range(3):
        buf[c, here] = half_of[c, inner : inner + size]
        rows = slice(c * CX + first, c * CX + first + size)
        a, b = rec_c[rows], jnp.where(odd_side(), rec_d[rows], 0.0)
        low = [jnp.where(even_y, b, a) * (visc + half * y_ref[0, part]), 0.0]
        high = [0.0, jnp.where(even_y, a, b) * (visc - half * y_ref[1, part])]
        for i in range(2):
            row = (i * 3 + c) * YROWS + first
            buf[c, here, i, :] += rim_low[row : row + size] + low[i]
            buf[c, here, CY - 2 + i, :] += rim_high[row : row + size] + high[i]


INNER = [(2, CHUNK - 2)] + [(k * CHUNK, CHUNK) for k in range(1, N_CHUNK - 1)] + [(CX - CHUNK, CHUNK - 2)]


def chunk_copy(buf, at, out_ref, first, size, sem):
    return pltpu.make_async_copy(buf.at[:, pl.ds(at, size)], out_ref.at[:, pl.ds(first, size)], sem)


def inside_body(main_low, main_high, y_ref, rec_c, rec_d, rim_low, rim_high, out_ref, buf, sems):
    _, even_y, _, _, _, _ = place()
    copies = []
    for k, (first, size) in enumerate(INNER):
        face_terms(buf, first - 2, first, size, main_low, main_high, y_ref, rec_c, rec_d, rim_low, rim_high, even_y)
        copies.append(chunk_copy(buf, first - 2, out_ref, first, size, sems.at[k]))
        copies[-1].start()
    for copy in copies:
        copy.wait()


def final_body(n_ret, _, main_low, main_high, x_ref, y_ref, face_a, face_b, rec_c, rec_d, rim_a, rim_b, rim_low, rim_high, back_ref, *rest):
    rets, (out_ref, pf_ref, buf, pf_buf, sems) = rest[:n_ret], rest[n_ret:]
    even_x, even_y, inner, brick, _, _ = place()
    half = 0.5 * DT_STEP
    visc = DT_STEP * NU_VISC
    mine = brick.astype(F32)
    found = jnp.zeros((BACK, CZ), F32)
    for ref, first in [(back_ref, 0), (rim_b, RIM_X)] + [(r, 0) for r in rets]:
        for k in range((ref.shape[0] - first) // BACK):
            value = ref[first + BACK * k : first + BACK * k + BACK]
            found = jnp.where(value[6:7, 0:1] == mine, value, found)
    for c in range(3):
        pf_buf[c : c + 1] = jnp.concatenate([found[2 * c : 2 * c + 1], found[2 * c + 1 : 2 * c + 2]], axis=1)
    copies = [pltpu.make_async_copy(pf_buf, pf_ref, sems.at[2])]
    copies[0].start()
    for k in range(2):
        first, at = k * (CX - 2), k * 2
        face_terms(buf, at, first, 2, main_low, main_high, y_ref, rec_c, rec_d, rim_low, rim_high, even_y)
        for c in range(3):
            a = face_a[c * XROWS : c * XROWS + CY]
            b = jnp.where(inner, face_b[c * XROWS : c * XROWS + CY], 0.0)
            if k == 0:
                buf[c, 0] += jnp.where(even_x, b, a) * (visc + half * x_ref[0])
            else:
                buf[c, 3] += jnp.where(even_x, a, b) * (visc - half * x_ref[3])
            for i in range(2):
                rows = slice((i * 3 + c) * CY, (i * 3 + c + 1) * CY)
                a, b = rim_a[rows], jnp.where(inner, rim_b[rows], 0.0)
                if k == 0:
                    buf[c, i] += jnp.where(even_x, b, a)
                else:
                    buf[c, 2 + i] += jnp.where(even_x, a, b)
        copies.append(chunk_copy(buf, at, out_ref, first, 2, sems.at[k]))
        copies[-1].start()
    for copy in copies:
        copy.wait()


def per_device(
    velocity,
    host_cell,
    host_frac,
    host_dst,
    owner_src,
    rotor_speed,
    blade_radius,
    blade_chord,
    blade_twist,
    blade_angle,
):
    nx, ny = lax.axis_size("gx"), lax.axis_size("gy")
    ring, short = nx == 8, ny == 4

    def flip(n, bits):
        return [(i, i ^ bits) for i in range(n)]

    def odd_pairs(n, closed=False):
        up = [(i, (i + 1) % n) for i in range(1, n if closed else n - 1, 2)]
        return up + [(t, s) for s, t in up]

    def same_side(n):
        return [(i, (i + (2 if i % 2 else n - 2)) % n) for i in range(n)]

    def across_x(blocks):
        return [lax.ppermute(b, "gx", p) for b, p in zip(blocks, (flip(nx, 4), same_side(nx)))]

    def swap(block):
        return lax.ppermute(block, "gx", flip(nx, 1))

    def join(pieces):
        return pieces[0] if len(pieces) == 1 else jnp.concatenate(pieces, axis=0)

    def after(values, other):
        return lax.optimization_barrier((values, other))

    def gather_y(first):
        pieces = [first]
        for bit in [b for b in (2, 4, 8) if b < ny]:
            pieces.append(lax.ppermute(join(pieces), "gy", flip(ny, bit)))
        return pieces

    def exchange_y(to_c, to_d, block):
        from_c = lax.ppermute(to_c, "gy", flip(ny, 1))
        from_d = lax.ppermute(to_d, "gy", flip(ny, 3) if short else odd_pairs(ny))
        return from_c, from_d, [lax.ppermute(block, "gy", flip(ny, 2))] if short else []

    def blocks_y(block, from_c, from_d, far, size, at):
        got = join([block, from_c[at : at + size]])
        if short:
            return [join([got, from_d[at : at + size]] + far)]
        return gather_y(got)

    def gather_x(blocks):
        pieces = []
        for bit in [b for b in (2, 4, 8, 16) if b < nx]:
            pieces.append(lax.ppermute(join([blocks] + pieces), "gx", flip(nx, bit)))
        return pieces

    def pin(array):
        return pltpu.with_memory_space_constraint(array, pltpu.MemorySpace.HBM)

    dma = pltpu.SemaphoreType.DMA
    pay_c, pay_d, block = call(
        pack_body,
        [(FACE_Y + ROWS, CZ)] * 2 + [(ROWS, CZ)],
        7,
        "pack",
        scratch=[pltpu.VMEM((4, 2, CZ), F32), pltpu.VMEM((2, CZ), jnp.int32), pltpu.VMEM((1, 1), F32), dma((12,))],
        in_specs=[HB] * 7,
    )(pin(velocity), rotor_speed.reshape(1, 1), *[pin(a.reshape(2, CZ)) for a in (blade_radius, blade_chord, blade_twist, blade_angle, owner_src)])
    rec_c, rec_d, far = exchange_y(pay_c, pay_d, block)

    def stencil(start, count):
        return call(lambda *refs: stencil_body(start, *refs), [(3, count, CY, CZ)], 1, "stencil")(velocity)[0]

    base_low = stencil(0, 3 * CX // 8)
    table, sums, x_faces, y_faces = call(
        sample_low_body, [(HOST, CZ), (HOST, 3 * CZ), (6, CY, CZ), (2, CX, CZ)], 3, "sample_low", vmem=24
    )(velocity, host_cell, host_frac)
    (rec_c, rec_d, far), (base_low, sums) = after((rec_c, rec_d, far), (base_low, sums))
    pieces = blocks_y(block, rec_c, rec_d, far, ROWS, FACE_Y)
    beside = [swap(p) for p in pieces]
    beside, base_third = after(beside, stencil(CX // 2, CX // 4))
    pieces = pieces + beside
    n_rows = 2 * ny * ROWS
    pair = (2 * ROWS, CZ)
    pay_a, pay_b, blocks, *across = call(
        lambda *refs: xpack_body(len(pieces), *refs),
        [(FACE_X, CZ), (FACE_X + 2 * ROWS, CZ), pair, pair, pair] if ring else [(FACE_X, CZ), (FACE_X, CZ), (n_rows, CZ)],
        3 + len(pieces),
        "xpack",
    )(x_faces, rec_c, rec_d, *pieces)
    face_b = lax.ppermute(pay_b, "gx", odd_pairs(nx, ring))
    from_x = across_x(across) if ring else gather_x(blocks)
    face_a = swap(pay_a)
    sums, edge, wz = call(
        sample_high_body, [(HOST, 3 * CZ), (HOST, CZ), (HOST, CZ)], 3, "sample_high", vmem=24
    )(velocity, table, sums)
    base_more = stencil(3 * CX // 8, CX // 8)
    (face_a, face_b, from_x), (sums, base_more) = after((face_a, face_b, from_x), (sums, base_more))
    samp, sel, pts = call(
        lambda *refs: select_body(len(from_x), *refs),
        [(8, PTS), (2 * ROWS, CZ), (PTS, CZ)],
        9 + len(from_x),
        "select",
    )(table, sums, edge, wz, face_a, face_b, rec_c, rec_d, blocks, *from_x)
    other = swap(samp)
    gx, gy, pz, pos, pair_kernel, edge = call(
        weights_body,
        [(YROWS, PTS), (CY, PTS), (CZ, PTS), (24, CZ), (2, P_SIZE, P_SIZE), (4 * CY, PTS)],
        2,
        "weights",
    )(pts, sel)
    other, base_next = after(other, stencil(6 * CX // 8, CX // 8))
    lines, points, xrim = call(
        loads_body,
        [(3 * CZ, PTS), (2 * BACK + 24, CZ), (2 * RIM_X, CZ)],
        7,
        "loads",
    )(samp, other, sel, pz, pos, pair_kernel, edge)
    ret = points[: 2 * BACK]
    near_c, near_d, far = exchange_y(points, points, ret)

    def spread(start, *bases):
        return call(
            lambda *refs: spread_body(start, *refs), [(3, CX // 2, CY, CZ)], 3 + len(bases), "spread"
        )(lines, gx, gy, *bases)[0]

    (near_c, near_d), main_low = after((near_c, near_d), spread(0, base_low, base_more))
    rim_low, rim_high = call(near_body, [(RIM_Y, CZ)] * 2, 2, "near")(near_c, near_d)
    far, rim_low = after(far, rim_low)
    pieces = blocks_y(ret, near_c, near_d, far, 2 * BACK, 0)
    n_rows = 2 * ny * BACK
    pair = (2 * BACK, CZ)
    pay_a, pay_b, back, *across = call(
        lambda *refs: rimpack_body(len(pieces), *refs),
        [(RIM_X, CZ), (RIM_X + 2 * BACK, CZ), (n_rows, CZ), pair] if ring else [(RIM_X, CZ), (RIM_X, CZ), (n_rows, CZ)],
        3 + len(pieces),
        "rimpack",
    )(xrim, rim_low, rim_high, *pieces)
    rim_b = lax.ppermute(pay_b, "gx", odd_pairs(nx, ring))
    rets = [lax.ppermute(across[0], "gx", flip(nx, 4))] if ring else gather_x(back)
    rim_a = swap(pay_a)
    main_high = spread(CX // 2, base_third, base_next, stencil(7 * CX // 8, CX // 8))
    (rim_a, rim_b), (main_low, main_high) = after((rim_a, rim_b), (main_low, main_high))
    if ring:
        rets.append(swap(rim_b[RIM_X:]))
    inside = call(
        inside_body,
        [velocity.shape],
        7,
        "inside",
        scratch=[pltpu.VMEM((3, CX - 4, CY, CZ), F32), dma((N_CHUNK,))],
        out_specs=[HB],
        vmem=16,
    )(main_low, main_high, y_faces, rec_c, rec_d, rim_low, rim_high)[0]
    rets, inside = after(rets, inside)
    return tuple(
        call(
            lambda *refs: final_body(len(rets), *refs),
            [velocity.shape, (3, P_SIZE)],
            14 + len(rets),
            "final",
            scratch=[pltpu.VMEM((3, 4, CY, CZ), F32), pltpu.VMEM((3, P_SIZE), F32), dma((3,))],
            first=HB,
            out_specs=[HB, HB],
            aliases={0: 0},
        )(inside, main_low, main_high, x_faces, y_faces, face_a, face_b, rec_c, rec_d, rim_a, rim_b, rim_low, rim_high, back, *rets)
    )


def solution(mesh):
    return jax.shard_map(
        per_device,
        mesh=mesh,
        in_specs=(
            P(None, "gx", "gy", None),
            P(None, ("gx", "gy")),
            P(None, ("gx", "gy")),
            P(("gx", "gy")),
            P(("gx", "gy")),
            P(("gx", "gy")),
            P(("gx", "gy")),
            P(("gx", "gy")),
            P(("gx", "gy")),
            P(("gx", "gy")),
        ),
        out_specs=(P(None, "gx", "gy", None), P(None, ("gx", "gy"))),
        check_vma=False,
    )
```

```python
import math

import jax
import jax.numpy as jnp
from jax import lax
from jax.experimental import pallas as pl
from jax.experimental.pallas import tpu as pltpu
from jax.sharding import PartitionSpec as P

CX = 64
CY = 32
CZ = 128
P_SIZE = 256
HOST = 512
PTS = 2 * P_SIZE

DT_STEP = 0.2
NU_VISC = 0.5
EPS_SQ = 1.44
CORE_SQ = 0.01

ROWS = 16
BACK = 8
YROWS = 72
XROWS = 40
FACE_Y = 3 * CX
FACE_X = 3 * XROWS
RIM_Y = 2 * 3 * YROWS
RIM_X = 2 * 3 * CY
CHUNK = 8
N_CHUNK = CX // CHUNK

F32 = jnp.float32
BF16 = jnp.bfloat16
VM = pl.BlockSpec(memory_space=pltpu.MemorySpace.VMEM)
SM = pl.BlockSpec(memory_space=pltpu.MemorySpace.SMEM)
HB = pl.BlockSpec(memory_space=pltpu.MemorySpace.HBM)
MIB = 1024 * 1024


def call(body, outs, n_in, name, scratch=(), first=VM, second=VM, out_specs=None, in_specs=None, vmem=12, aliases=None):
    return pl.pallas_call(
        body,
        out_shape=[jax.ShapeDtypeStruct(s, F32) for s in outs],
        in_specs=in_specs or ([first, second] + [VM] * n_in)[:n_in],
        out_specs=out_specs or [VM] * len(outs),
        scratch_shapes=list(scratch),
        input_output_aliases=aliases or {},
        compiler_params=pltpu.CompilerParams(vmem_limit_bytes=vmem * MIB),
        name=name,
    )


def place():
    nx, ny = lax.axis_size("gx"), lax.axis_size("gy")
    ix, iy = lax.axis_index("gx"), lax.axis_index("gy")
    px, py = lax.rem(ix, 2), lax.rem(iy, 2)
    inner = (ix + px > 0) & (ix + px < nx)
    return px == 0, py == 0, inner, ix * ny + iy, (ix - px) * ny + iy, ny


def odd_side():
    ny, iy = lax.axis_size("gy"), lax.axis_index("gy")
    py = lax.rem(iy, 2)
    return (iy + py > 0) & (iy + py < ny)


def split(value):
    high = value.astype(BF16)
    low = (value - high.astype(F32)).astype(BF16)
    return high, low


def dot3(a_high, a_low, b_high, b_low):
    def one(a, b):
        return jnp.dot(a, b, preferred_element_type=F32)

    return one(a_high, b_high) + (one(a_high, b_low) + one(a_low, b_high))


def dot3_last(a_high, a_low, b_high, b_low):
    def one(a, b):
        return lax.dot_general(a, b, (((1,), (1,)), ((), ())), preferred_element_type=F32)

    return one(a_high, b_high) + (one(a_high, b_low) + one(a_low, b_high))


def reduce_list(items, op):
    result = items[0]
    for item in items[1:]:
        result = op(result, item)
    return result


def pack_body(v_ref, spin_hbm, *rest):
    params, (pay_c, pay_d, blk_ref, held, held_int, spin_ref, sems) = rest[:5], rest[5:]
    _, even_y, _, brick, _, _ = place()

    def faces(first, second):
        made = []
        for k, (ref, y) in enumerate(((pay_c, first), (pay_d, second))):
            for c in range(3):
                made.append(pltpu.make_async_copy(v_ref.at[c, :, y], ref.at[pl.ds(c * CX, CX)], sems.at[3 * k + c]))
        return made

    @pl.when(even_y)
    def _():
        for copy in faces(CY - 1, 0):
            copy.start()

    @pl.when(jnp.logical_not(even_y))
    def _():
        for copy in faces(0, CY - 1):
            copy.start()

    small = [pltpu.make_async_copy(spin_hbm, spin_ref, sems.at[6])]
    small += [pltpu.make_async_copy(p, held.at[k], sems.at[7 + k]) for k, p in enumerate(params[:4])]
    small.append(pltpu.make_async_copy(params[4], held_int, sems.at[11]))
    for copy in small:
        copy.start()
    for copy in small:
        copy.wait()
    radius, chord, twist, angle = [held[k] for k in range(4)]
    parts = [
        radius,
        chord,
        jnp.cos(twist),
        jnp.sin(twist),
        jnp.cos(angle),
        jnp.sin(angle),
        held_int[...].astype(F32),
        jnp.broadcast_to(spin_ref[...], (1, CZ)),
        jnp.full((1, CZ), brick.astype(F32), F32),
    ]
    block = jnp.concatenate(parts, axis=0)
    blk_ref[...] = block
    pay_c[FACE_Y:] = block
    pay_d[FACE_Y:] = block
    for copy in faces(0, 0):
        copy.wait()


def stencil_body(start, v_ref, out_ref):
    row = lax.broadcasted_iota(jnp.int32, (CY, CZ), 0)
    lane = lax.broadcasted_iota(jnp.int32, (CY, CZ), 1)
    half = 0.5 * DT_STEP
    visc = DT_STEP * NU_VISC
    not_last_y, not_first_y = row < CY - 1, row > 0
    not_last_z, not_first_z = lane < CZ - 1, lane > 0

    def step(k, carry):
        x = start + k
        up = jnp.minimum(x + 1, CX - 1)
        down = jnp.maximum(x - 1, 0)
        v0, v1, v2 = v_ref[0, x], v_ref[1, x], v_ref[2, x]
        a_x = jnp.where(x < CX - 1, visc - half * v0, 0.0)
        b_x = jnp.where(x > 0, visc + half * v0, 0.0)
        a_y = jnp.where(not_last_y, visc - half * v1, 0.0)
        b_y = jnp.where(not_first_y, visc + half * v1, 0.0)
        a_z = jnp.where(not_last_z, visc - half * v2, 0.0)
        b_z = jnp.where(not_first_z, visc + half * v2, 0.0)
        for c in range(3):
            mid = (v0, v1, v2)[c]
            along_x = a_x * v_ref[c, up] + b_x * v_ref[c, down]
            along_y = a_y * pltpu.roll(mid, CY - 1, 0) + b_y * pltpu.roll(mid, 1, 0)
            along_z = a_z * pltpu.roll(mid, CZ - 1, 1) + b_z * pltpu.roll(mid, 1, 1)
            out_ref[c, k] = (1.0 - 6.0 * visc) * mid + along_x + (along_y + along_z)
        return carry

    lax.fori_loop(0, out_ref.shape[1], step, 0, unroll=2)


def weight(coord, base, frac):
    return jnp.where(coord == base, 1.0 - frac, jnp.where(coord == base + 1, frac, 0.0))


def sample_part(start, v_ref, table, acc):
    x_col, y_col = [table[:, k : k + 1].astype(jnp.int32) for k in range(2)]
    fx, fy = [table[:, k : k + 1] for k in range(3, 5)]
    lane = lax.broadcasted_iota(jnp.int32, (HOST, CZ), 1)
    wy = weight(lane % CY, y_col, fy)
    x_lane = (lane // CY + start - x_col).astype(F32).astype(BF16)
    near, far = split((1.0 - fx) * wy), split(fx * wy)
    zero = jnp.zeros((HOST, CZ), BF16)
    per = 4
    nx = CZ * per // CY
    for j in range(CX // 2 // nx):
        highs, lows = [], []
        for i in range(per):
            shift = (CZ // CY) * (j * per + i)
            at_base, at_next = x_lane == jnp.bfloat16(-shift), x_lane == jnp.bfloat16(1 - shift)
            highs.append(jnp.where(at_base, near[0], jnp.where(at_next, far[0], zero)))
            lows.append(jnp.where(at_base, near[1], jnp.where(at_next, far[1], zero)))
        w_high, w_low = jnp.concatenate(highs, axis=1), jnp.concatenate(lows, axis=1)
        first = start + j * nx
        field = [v_ref[c, first : first + nx].reshape(nx * CY, CZ) for c in range(3)]
        f_high, f_low = split(jnp.concatenate(field, axis=1))
        part = dot3(w_high, w_low, f_high, f_low)
        acc = part if acc is None else acc + part
    return acc


def sample_low_body(v_ref, cell_ref, frac_ref, tab_ref, acc_ref, x_ref, y_ref):
    for c in range(3):
        x_ref[c] = v_ref[c, 0]
        x_ref[c + 3] = v_ref[c, CX - 1]
    y_ref[0] = v_ref[1, :, 0, :]
    y_ref[1] = v_ref[1, :, CY - 1, :]
    rows = jnp.concatenate([cell_ref[...].astype(F32), frac_ref[...], jnp.zeros((CZ - 6, HOST), F32)], axis=0)
    table = rows.T
    tab_ref[...] = table
    acc_ref[...] = sample_part(0, v_ref, table, None)


def sample_high_body(v_ref, tab_ref, low_ref, acc_ref, edge_ref, wz_ref):
    table = tab_ref[...]
    acc_ref[...] = sample_part(CX // 2, v_ref, table, low_ref[...])
    lane = lax.broadcasted_iota(jnp.int32, (HOST, CZ), 1)
    x_col, y_col, z_col = [table[:, k : k + 1].astype(jnp.int32) for k in range(3)]
    fx, fy, fz = [table[:, k : k + 1] for k in range(3, 6)]
    on_line = lane >= CX
    edge_x = jnp.where(on_line, lane - CX, CX)
    edge_y = jnp.where(on_line, CY, lane)
    both = weight(edge_x, x_col, fx) * weight(edge_y, y_col, fy)
    edge_ref[...] = jnp.where(on_line | (lane <= CY), both, 0.0)
    wz_ref[...] = weight(lane, z_col, fz)


def split_blocks(sources):
    return [
        ref[first + k * ROWS : first + (k + 1) * ROWS]
        for ref, first in sources
        for k in range((ref.shape[0] - first) // ROWS)
    ]


def pick_pair(values, b0, ny):
    keys = [value[12:13, 0:1] for value in values]
    members = []
    for key in keys:
        home = jnp.floor(key * (1.0 / HOST)).astype(jnp.int32)
        members.append((home == b0) | (home == b0 + ny))
    low_key = reduce_list([jnp.where(m, k, 1e9) for k, m in zip(keys, members)], jnp.minimum)
    high_key = reduce_list([jnp.where(m, k, -9.0) for k, m in zip(keys, members)], jnp.maximum)
    low = jnp.full((ROWS, CZ), -1.0, F32)
    high = low
    for key, value in zip(keys, values):
        low = jnp.where(key == low_key, value, low)
        high = jnp.where(key == high_key, value, high)
    return low, high


def xpack_body(n_blk, x_ref, rec_c, rec_d, *rest):
    pieces, (pay_a, pay_b, own_ref, *others) = rest[:n_blk], rest[n_blk:]
    even_x, even_y, inner, _, b0, ny = place()
    for c in range(3):
        at = c * CX
        y_high = jnp.where(even_y, rec_c[at : at + 1], jnp.where(odd_side(), rec_d[at : at + 1], 0.0))
        tail = jnp.concatenate([y_high, jnp.zeros((XROWS - CY - 1, CZ), F32)], axis=0)
        low, high = x_ref[c], x_ref[c + 3]
        at = c * XROWS
        pay_a[at : at + CY] = jnp.where(even_x, high, low)
        pay_b[at : at + CY] = jnp.where(even_x, low, high)
        pay_a[at + CY : at + XROWS] = tail
        pay_b[at + CY : at + XROWS] = tail
    if not others:
        own_ref[...] = jnp.concatenate([p[...] for p in pieces], axis=0)
        return
    values = split_blocks([(p, 0) for p in pieces])
    chips = ny * 2
    side = jnp.where(even_x, -chips, chips)
    total = lax.axis_size("gx") * ny
    own_ref[...] = jnp.concatenate(pick_pair(values, b0, ny), axis=0)
    beside = jnp.concatenate(pick_pair(values, lax.rem(b0 + side + total, total), ny), axis=0)
    pay_b[FACE_X:] = beside
    others[1][...] = beside
    others[0][...] = jnp.concatenate(pick_pair(values, lax.rem(b0 + 2 * chips, total), ny), axis=0)


def select_body(n_blk, tab_ref, acc_ref, edge_ref, wz_ref, face_a, face_b, rec_c, rec_d, blk_ref, *rest):
    others, (samp_ref, sel_ref, pts_ref) = rest[:n_blk], rest[n_blk:]
    even_x, even_y, inner, brick, b0, ny = place()
    sources = [(blk_ref, 0), (face_b, FACE_X)] + [(o, 0) for o in others]
    turbine_a, turbine_b = pick_pair(split_blocks(sources), b0, ny)
    sel = jnp.concatenate([turbine_a, turbine_b], axis=0)
    sel_ref[...] = sel
    table = tab_ref[...]
    lane = lax.broadcasted_iota(jnp.int32, (PTS, CZ), 1)
    field = []
    for c in range(3):
        at = c * XROWS
        past = jnp.where(inner, face_b[at : at + XROWS], 0.0)
        plane = jnp.where(even_x, face_a[at : at + XROWS], past)
        at = c * CX
        line = jnp.where(even_y, rec_c[at : at + CX], jnp.where(odd_side(), rec_d[at : at + CX], 0.0))
        field.append(jnp.concatenate([plane, jnp.zeros((CX - XROWS, CZ), F32), line], axis=0))
    w_high, w_low = split(edge_ref[...])
    f_high, f_low = split(jnp.concatenate(field, axis=1))
    acc = acc_ref[...] + dot3(w_high, w_low, f_high, f_low)
    wz = wz_ref[...]
    for c in range(3):
        value = jnp.sum(acc[:, c * CZ : (c + 1) * CZ] * wz, axis=1, keepdims=True)
        table = table + jnp.where(lane == 6 + c, value, 0.0)
    slot = jnp.concatenate([sel[j : j + 1] for j in (12, 13, ROWS + 12, ROWS + 13)], axis=1).astype(jnp.int32)
    mine = (slot // HOST) == brick
    local = jnp.where(mine, slot % HOST, -1)
    hit = (lax.broadcasted_iota(jnp.int32, (HOST, PTS), 0) == local).astype(F32).astype(BF16)
    by_slot = table.T[0:16]
    first, second = split(by_slot)
    third = (by_slot - first.astype(F32) - second.astype(F32)).astype(BF16)
    pulled = jnp.dot(jnp.concatenate([first, second, third], axis=0), hit, preferred_element_type=F32)
    points = pulled[0:16] + pulled[16:32] + pulled[32:48]
    row = lax.broadcasted_iota(jnp.int32, (16, PTS), 0)
    pts_ref[...] = jnp.where((row == 0) & jnp.logical_not(mine), -100.0, points)
    samp_ref[...] = points[6:14]


def offsets(frac):
    raw = [jnp.exp(-((o - frac) ** 2) / EPS_SQ) for o in (-1.0, 0.0, 1.0, 2.0)]
    total = (raw[0] + raw[1]) + (raw[2] + raw[3])
    return [value / total for value in raw]


def profile(rows, inner, base, frac):
    index = lax.broadcasted_iota(jnp.int32, (rows, PTS), 0)
    late = index - inner
    index = jnp.where(index < inner, index, jnp.where(late < 2, late - 2, late - 2 + inner))
    rel = index - base.astype(jnp.int32)
    result = jnp.zeros((rows, PTS), F32)
    for k, w in enumerate(offsets(frac)):
        result = jnp.where(rel == k - 1, w, result)
    return result


def weights_body(pts_ref, sel_ref, gx_ref, gy_ref, pz_ref, pos_ref, pair_ref, edge_ref):
    table = pts_ref[...]
    sel = sel_ref[...]
    turned = jnp.concatenate([sel, jnp.zeros((CZ - 2 * ROWS, CZ), F32)], axis=0).T
    gx = profile(YROWS, CX, table[0:1], table[3:4])
    gy = profile(CY, CY, table[1:2], table[4:5])
    gx_ref[...] = gx
    gy_ref[...] = gy
    pz_ref[...] = profile(CZ, CZ, table[2:3], table[5:6]) * DT_STEP
    pos_ref[...] = jnp.concatenate([table[q : q + 1, k * CZ : (k + 1) * CZ] for q in range(6) for k in range(4)], axis=0)
    for t in range(2):
        at = t * ROWS
        radius = jnp.concatenate([sel_ref[at : at + 1], sel_ref[at + 1 : at + 2]], axis=1)
        column = jnp.concatenate([turned[:, at : at + 1], turned[:, at + 1 : at + 2]], axis=0)
        spacing = radius - column
        pair_ref[t] = spacing / (spacing * spacing + CORE_SQ)
    for k in range(4):
        edge_ref[k * CY : (k + 1) * CY] = gx[CX + k : CX + k + 1] * gy


def attack(axial_flow, tangent, cos_twist, sin_twist):
    rel_speed = jnp.sqrt(axial_flow * axial_flow + tangent * tangent + 1.0)
    cos_phi = tangent / rel_speed
    sin_phi = axial_flow / rel_speed
    sin_alpha = sin_phi * cos_twist - cos_phi * sin_twist
    cos_alpha = cos_phi * cos_twist + sin_phi * sin_twist
    lift_coef = 2.0 * jnp.pi * sin_alpha * cos_alpha / (1.0 + 4.0 * sin_alpha * sin_alpha)
    drag_coef = 0.02 + 0.8 * sin_alpha * sin_alpha
    return rel_speed, cos_phi, sin_phi, lift_coef, drag_coef


def loads_body(samp_ref, other_ref, sel_ref, pz_ref, pos_ref, pair_ref, edge_ref, lh_ref, pay_ref, xrim_ref):
    def row(k):
        picks = (2 * k, 2 * k + 1, ROWS + 2 * k, ROWS + 2 * k + 1)
        return jnp.concatenate([sel_ref[j : j + 1] for j in picks], axis=1)

    radius, chord, cos_t, sin_t, cos_a, sin_a = [row(k) for k in range(6)]
    spin = radius * jnp.concatenate([sel_ref[j : j + 1] for j in (14, 14, ROWS + 14, ROWS + 14)], axis=1)
    flow = samp_ref[...] + other_ref[...]
    axial = flow[0:1]
    tangent = spin - (cos_a * flow[2:3] - sin_a * flow[1:2])
    rel_speed, cos_phi, sin_phi, lift_coef, drag_coef = attack(axial, tangent, cos_t, sin_t)
    circ = 0.5 * chord * rel_speed * lift_coef
    parts = []
    for t in range(2):
        seg = slice(t * P_SIZE, (t + 1) * P_SIZE)
        lhs = jnp.concatenate([cos_a[:, seg] * circ[:, seg], sin_a[:, seg] * circ[:, seg], jnp.zeros((6, P_SIZE), F32)], axis=0)
        both = jnp.dot(lhs, pair_ref[t], preferred_element_type=F32, precision=lax.Precision.HIGHEST)
        parts.append((cos_a[:, seg] * both[0:1] + sin_a[:, seg] * both[1:2]) / (4.0 * math.pi))
    induced = jnp.concatenate(parts, axis=1)
    rel_speed, cos_phi, sin_phi, lift_coef, drag_coef = attack(axial + induced, tangent, cos_t, sin_t)
    dynamic = 0.5 * chord * rel_speed * rel_speed
    lift = dynamic * lift_coef
    drag = dynamic * drag_coef
    thrust = lift * cos_phi + drag * sin_phi
    torque = lift * sin_phi - drag * cos_phi
    force = [-thrust, torque * sin_a, -torque * cos_a]
    pieces = []
    for t in range(2):
        for c in range(3):
            for h in range(2):
                at = t * P_SIZE + h * CZ
                pieces.append(force[c][:, at : at + CZ])
        pieces += [sel_ref[t * ROWS + 15 : t * ROWS + 16]] * 2
    blocks = jnp.concatenate(pieces, axis=0)
    pay_ref[0 : 2 * BACK] = blocks
    pay_ref[2 * BACK :] = pos_ref[...]
    pz = pz_ref[...]
    lines = jnp.concatenate([f * pz for f in force], axis=0)
    l_high, l_low = split(lines)
    lh_ref[...] = lines
    w_high, w_low = split(edge_ref[...])
    rim = dot3_last(w_high, w_low, l_high, l_low)
    for k in range(4):
        for c in range(3):
            at = (k * 3 + c) * CY
            xrim_ref[at : at + CY] = rim[k * CY : (k + 1) * CY, c * CZ : (c + 1) * CZ]


def near_body(rec_c, rec_d, low_ref, high_ref):
    _, even_y, _, _, _, _ = place()
    c_all, d_all = rec_c[...], jnp.where(odd_side(), rec_d[...], 0.0)
    for side, out_ref in ((0, low_ref), (1, high_ref)):
        got = jnp.where(even_y, d_all, c_all) if side == 0 else jnp.where(even_y, c_all, d_all)

        def wide(first, picks):
            return jnp.concatenate([got[first + j : first + j + 1] for j in picks], axis=1)

        x, y, z, fx, fy, fz = [wide(2 * BACK + 4 * q, range(4)) for q in range(6)]
        force = [wide(2 * c, (0, 1, BACK, BACK + 1)) * DT_STEP for c in range(3)]
        pz = profile(CZ, CZ, z, fz)
        l_high, l_low = split(jnp.concatenate([f * pz for f in force], axis=0))
        gx = profile(YROWS, CX, x, fx)
        wy = offsets(fy)
        planes = []
        for i in range(2):
            rel = (CY + i if side == 0 else i - 2) - y.astype(jnp.int32)
            gy = jnp.zeros((1, PTS), F32)
            for k in range(4):
                gy = jnp.where(rel == k - 1, wy[k], gy)
            planes.append(gx * gy)
        w_high, w_low = split(jnp.concatenate(planes, axis=0))
        rim = dot3_last(w_high, w_low, l_high, l_low)
        for i in range(2):
            for c in range(3):
                at = (i * 3 + c) * YROWS
                out_ref[at : at + YROWS] = rim[i * YROWS : (i + 1) * YROWS, c * CZ : (c + 1) * CZ]


SPREAD_X = 8


def spread_body(start, lines_ref, gx_ref, gy_ref, *rest):
    bases, out_ref = rest[:-1], rest[-1]
    l_high, l_low = split(lines_ref[...])
    gy = gy_ref[0:CY]
    held = [(ref, k) for ref in bases for k in range(0, ref.shape[1], SPREAD_X)]
    for k in range(out_ref.shape[1] // SPREAD_X):
        at = k * SPREAD_X
        first = start + at
        planes = jnp.concatenate([gx_ref[first + i : first + i + 1] * gy for i in range(SPREAD_X)], axis=0)
        w_high, w_low = split(planes)
        value = dot3_last(w_high, w_low, l_high, l_low)
        base, inner = held[k]
        for c in range(3):
            part = value[:, c * CZ : (c + 1) * CZ].reshape(SPREAD_X, CY, CZ)
            out_ref[c, at : at + SPREAD_X] = base[c, inner : inner + SPREAD_X] + part


def rimpack_body(n_blk, xrim_ref, low_ref, high_ref, *rest):
    pieces, (pay_a, pay_b, back_ref, *others) = rest[:n_blk], rest[n_blk:]
    even_x, even_y, inner, _, b0, ny = place()
    zero = jnp.zeros((CY - 4, CZ), F32)
    for k in range(2):
        for c in range(3):
            sides = []
            for s in range(2):
                near, far = [], []
                for y in range(2):
                    at = (y * 3 + c) * YROWS + CX + 2 * s + k
                    near.append(low_ref[at : at + 1])
                    far.append(high_ref[at : at + 1])
                at = ((2 * s + k) * 3 + c) * CY
                sides.append(xrim_ref[at : at + CY] + jnp.concatenate(near + [zero] + far, axis=0))
            at = (k * 3 + c) * CY
            pay_a[at : at + CY] = jnp.where(even_x, sides[1], sides[0])
            pay_b[at : at + CY] = jnp.where(even_x, sides[0], sides[1])
    back = jnp.concatenate([p[...] for p in pieces], axis=0)
    back_ref[...] = back
    if others:
        chips = ny * 2
        side = jnp.where(even_x, -chips, chips)
        total = lax.axis_size("gx") * ny
        for ref, at, target in (
            (pay_b, RIM_X, lax.rem(b0 + side + total, total)),
            (others[0], 0, lax.rem(b0 + 2 * chips, total)),
        ):
            for core in range(2):
                wanted = (target + core * ny).astype(F32)
                found = jnp.full((BACK, CZ), -1.0, F32)
                for k in range(back.shape[0] // BACK):
                    value = back[k * BACK : (k + 1) * BACK]
                    found = jnp.where(value[6:7, 0:1] == wanted, value, found)
                ref[at + core * BACK : at + (core + 1) * BACK] = found


def face_terms(buf, at, first, size, main_low, main_high, y_ref, rec_c, rec_d, rim_low, rim_high, even_y):
    half = 0.5 * DT_STEP
    visc = DT_STEP * NU_VISC
    part = slice(first, first + size)
    here = slice(at, at + size)
    half_of = main_low if first < CX // 2 else main_high
    inner = first % (CX // 2)
    for c in range(3):
        buf[c, here] = half_of[c, inner : inner + size]
        rows = slice(c * CX + first, c * CX + first + size)
        a, b = rec_c[rows], jnp.where(odd_side(), rec_d[rows], 0.0)
        low = [jnp.where(even_y, b, a) * (visc + half * y_ref[0, part]), 0.0]
        high = [0.0, jnp.where(even_y, a, b) * (visc - half * y_ref[1, part])]
        for i in range(2):
            row = (i * 3 + c) * YROWS + first
            buf[c, here, i, :] += rim_low[row : row + size] + low[i]
            buf[c, here, CY - 2 + i, :] += rim_high[row : row + size] + high[i]


INNER = [(2, CHUNK - 2)] + [(k * CHUNK, CHUNK) for k in range(1, N_CHUNK - 1)] + [(CX - CHUNK, CHUNK - 2)]


def chunk_copy(buf, at, out_ref, first, size, sem):
    return pltpu.make_async_copy(buf.at[:, pl.ds(at, size)], out_ref.at[:, pl.ds(first, size)], sem)


def inside_body(main_low, main_high, y_ref, rec_c, rec_d, rim_low, rim_high, out_ref, buf, sems):
    _, even_y, _, _, _, _ = place()
    copies = []
    for k, (first, size) in enumerate(INNER):
        face_terms(buf, first - 2, first, size, main_low, main_high, y_ref, rec_c, rec_d, rim_low, rim_high, even_y)
        copies.append(chunk_copy(buf, first - 2, out_ref, first, size, sems.at[k]))
        copies[-1].start()
    for copy in copies:
        copy.wait()


def final_body(n_ret, _, main_low, main_high, x_ref, y_ref, face_a, face_b, rec_c, rec_d, rim_a, rim_b, rim_low, rim_high, back_ref, *rest):
    rets, (out_ref, pf_ref, buf, pf_buf, sems) = rest[:n_ret], rest[n_ret:]
    even_x, even_y, inner, brick, _, _ = place()
    half = 0.5 * DT_STEP
    visc = DT_STEP * NU_VISC
    mine = brick.astype(F32)
    found = jnp.zeros((BACK, CZ), F32)
    for ref, first in [(back_ref, 0), (rim_b, RIM_X)] + [(r, 0) for r in rets]:
        for k in range((ref.shape[0] - first) // BACK):
            value = ref[first + BACK * k : first + BACK * k + BACK]
            found = jnp.where(value[6:7, 0:1] == mine, value, found)
    for c in range(3):
        pf_buf[c : c + 1] = jnp.concatenate([found[2 * c : 2 * c + 1], found[2 * c + 1 : 2 * c + 2]], axis=1)
    copies = [pltpu.make_async_copy(pf_buf, pf_ref, sems.at[2])]
    copies[0].start()
    for k in range(2):
        first, at = k * (CX - 2), k * 2
        face_terms(buf, at, first, 2, main_low, main_high, y_ref, rec_c, rec_d, rim_low, rim_high, even_y)
        for c in range(3):
            a = face_a[c * XROWS : c * XROWS + CY]
            b = jnp.where(inner, face_b[c * XROWS : c * XROWS + CY], 0.0)
            if k == 0:
                buf[c, 0] += jnp.where(even_x, b, a) * (visc + half * x_ref[0])
            else:
                buf[c, 3] += jnp.where(even_x, a, b) * (visc - half * x_ref[3])
            for i in range(2):
                rows = slice((i * 3 + c) * CY, (i * 3 + c + 1) * CY)
                a, b = rim_a[rows], jnp.where(inner, rim_b[rows], 0.0)
                if k == 0:
                    buf[c, i] += jnp.where(even_x, b, a)
                else:
                    buf[c, 2 + i] += jnp.where(even_x, a, b)
        copies.append(chunk_copy(buf, at, out_ref, first, 2, sems.at[k]))
        copies[-1].start()
    for copy in copies:
        copy.wait()


def per_device(
    velocity,
    host_cell,
    host_frac,
    host_dst,
    owner_src,
    rotor_speed,
    blade_radius,
    blade_chord,
    blade_twist,
    blade_angle,
):
    nx, ny = lax.axis_size("gx"), lax.axis_size("gy")
    ring, short = nx == 8, ny == 4

    def flip(n, bits):
        return [(i, i ^ bits) for i in range(n)]

    def odd_pairs(n, closed=False):
        up = [(i, (i + 1) % n) for i in range(1, n if closed else n - 1, 2)]
        return up + [(t, s) for s, t in up]

    def same_side(n):
        return [(i, (i + (2 if i % 2 else n - 2)) % n) for i in range(n)]

    def across_x(blocks):
        return [lax.ppermute(b, "gx", p) for b, p in zip(blocks, (flip(nx, 4), same_side(nx)))]

    def swap(block):
        return lax.ppermute(block, "gx", flip(nx, 1))

    def join(pieces):
        return pieces[0] if len(pieces) == 1 else jnp.concatenate(pieces, axis=0)

    def after(values, other):
        return lax.optimization_barrier((values, other))

    def gather_y(first):
        pieces = [first]
        for bit in [b for b in (2, 4, 8) if b < ny]:
            pieces.append(lax.ppermute(join(pieces), "gy", flip(ny, bit)))
        return pieces

    def exchange_y(to_c, to_d, block):
        from_c = lax.ppermute(to_c, "gy", flip(ny, 1))
        from_d = lax.ppermute(to_d, "gy", flip(ny, 3) if short else odd_pairs(ny))
        return from_c, from_d, [lax.ppermute(block, "gy", flip(ny, 2))] if short else []

    def blocks_y(block, from_c, from_d, far, size, at):
        got = join([block, from_c[at : at + size]])
        if short:
            return [join([got, from_d[at : at + size]] + far)]
        return gather_y(got)

    def gather_x(blocks):
        pieces = []
        for bit in [b for b in (2, 4, 8, 16) if b < nx]:
            pieces.append(lax.ppermute(join([blocks] + pieces), "gx", flip(nx, bit)))
        return pieces

    def pin(array):
        return pltpu.with_memory_space_constraint(array, pltpu.MemorySpace.HBM)

    dma = pltpu.SemaphoreType.DMA
    pay_c, pay_d, block = call(
        pack_body,
        [(FACE_Y + ROWS, CZ)] * 2 + [(ROWS, CZ)],
        7,
        "pack",
        scratch=[pltpu.VMEM((4, 2, CZ), F32), pltpu.VMEM((2, CZ), jnp.int32), pltpu.VMEM((1, 1), F32), dma((12,))],
        in_specs=[HB] * 7,
    )(pin(velocity), rotor_speed.reshape(1, 1), *[pin(a.reshape(2, CZ)) for a in (blade_radius, blade_chord, blade_twist, blade_angle, owner_src)])
    rec_c, rec_d, far = exchange_y(pay_c, pay_d, block)

    def stencil(start, count):
        return call(lambda *refs: stencil_body(start, *refs), [(3, count, CY, CZ)], 1, "stencil")(velocity)[0]

    base_low = stencil(0, 3 * CX // 8)
    table, sums, x_faces, y_faces = call(
        sample_low_body, [(HOST, CZ), (HOST, 3 * CZ), (6, CY, CZ), (2, CX, CZ)], 3, "sample_low", vmem=24
    )(velocity, host_cell, host_frac)
    (rec_c, rec_d, far), (base_low, sums) = after((rec_c, rec_d, far), (base_low, sums))
    pieces = blocks_y(block, rec_c, rec_d, far, ROWS, FACE_Y)
    beside = [swap(p) for p in pieces]
    beside, base_third = after(beside, stencil(CX // 2, CX // 4))
    pieces = pieces + beside
    n_rows = 2 * ny * ROWS
    pair = (2 * ROWS, CZ)
    pay_a, pay_b, blocks, *across = call(
        lambda *refs: xpack_body(len(pieces), *refs),
        [(FACE_X, CZ), (FACE_X + 2 * ROWS, CZ), pair, pair, pair] if ring else [(FACE_X, CZ), (FACE_X, CZ), (n_rows, CZ)],
        3 + len(pieces),
        "xpack",
    )(x_faces, rec_c, rec_d, *pieces)
    face_b = lax.ppermute(pay_b, "gx", odd_pairs(nx, ring))
    from_x = across_x(across) if ring else gather_x(blocks)
    face_a = swap(pay_a)
    sums, edge, wz = call(
        sample_high_body, [(HOST, 3 * CZ), (HOST, CZ), (HOST, CZ)], 3, "sample_high", vmem=24
    )(velocity, table, sums)
    base_more = stencil(3 * CX // 8, CX // 8)
    (face_a, face_b, from_x), (sums, base_more) = after((face_a, face_b, from_x), (sums, base_more))
    samp, sel, pts = call(
        lambda *refs: select_body(len(from_x), *refs),
        [(8, PTS), (2 * ROWS, CZ), (16, PTS)],
        9 + len(from_x),
        "select",
    )(table, sums, edge, wz, face_a, face_b, rec_c, rec_d, blocks, *from_x)
    other = swap(samp)
    gx, gy, pz, pos, pair_kernel, edge = call(
        weights_body,
        [(YROWS, PTS), (CY, PTS), (CZ, PTS), (24, CZ), (2, P_SIZE, P_SIZE), (4 * CY, PTS)],
        2,
        "weights",
    )(pts, sel)
    other, base_next = after(other, stencil(6 * CX // 8, CX // 8))
    lines, points, xrim = call(
        loads_body,
        [(3 * CZ, PTS), (2 * BACK + 24, CZ), (2 * RIM_X, CZ)],
        7,
        "loads",
    )(samp, other, sel, pz, pos, pair_kernel, edge)
    ret = points[: 2 * BACK]
    near_c, near_d, far = exchange_y(points, points, ret)

    def spread(start, *bases):
        return call(
            lambda *refs: spread_body(start, *refs), [(3, CX // 2, CY, CZ)], 3 + len(bases), "spread"
        )(lines, gx, gy, *bases)[0]

    (near_c, near_d), main_low = after((near_c, near_d), spread(0, base_low, base_more))
    rim_low, rim_high = call(near_body, [(RIM_Y, CZ)] * 2, 2, "near")(near_c, near_d)
    far, rim_low = after(far, rim_low)
    pieces = blocks_y(ret, near_c, near_d, far, 2 * BACK, 0)
    n_rows = 2 * ny * BACK
    pair = (2 * BACK, CZ)
    pay_a, pay_b, back, *across = call(
        lambda *refs: rimpack_body(len(pieces), *refs),
        [(RIM_X, CZ), (RIM_X + 2 * BACK, CZ), (n_rows, CZ), pair] if ring else [(RIM_X, CZ), (RIM_X, CZ), (n_rows, CZ)],
        3 + len(pieces),
        "rimpack",
    )(xrim, rim_low, rim_high, *pieces)
    rim_b = lax.ppermute(pay_b, "gx", odd_pairs(nx, ring))
    rets = [lax.ppermute(across[0], "gx", flip(nx, 4))] if ring else gather_x(back)
    rim_a = swap(pay_a)
    main_high = spread(CX // 2, base_third, base_next, stencil(7 * CX // 8, CX // 8))
    (rim_a, rim_b), (main_low, main_high) = after((rim_a, rim_b), (main_low, main_high))
    if ring:
        rets.append(swap(rim_b[RIM_X:]))
    inside = call(
        inside_body,
        [velocity.shape],
        7,
        "inside",
        scratch=[pltpu.VMEM((3, CX - 4, CY, CZ), F32), dma((N_CHUNK,))],
        out_specs=[HB],
        vmem=16,
    )(main_low, main_high, y_faces, rec_c, rec_d, rim_low, rim_high)[0]
    rets, inside = after(rets, inside)
    return tuple(
        call(
            lambda *refs: final_body(len(rets), *refs),
            [velocity.shape, (3, P_SIZE)],
            14 + len(rets),
            "final",
            scratch=[pltpu.VMEM((3, 4, CY, CZ), F32), pltpu.VMEM((3, P_SIZE), F32), dma((3,))],
            first=HB,
            out_specs=[HB, HB],
            aliases={0: 0},
        )(inside, main_low, main_high, x_faces, y_faces, face_a, face_b, rec_c, rec_d, rim_a, rim_b, rim_low, rim_high, back, *rets)
    )


def solution(mesh):
    return jax.shard_map(
        per_device,
        mesh=mesh,
        in_specs=(
            P(None, "gx", "gy", None),
            P(None, ("gx", "gy")),
            P(None, ("gx", "gy")),
            P(("gx", "gy")),
            P(("gx", "gy")),
            P(("gx", "gy")),
            P(("gx", "gy")),
            P(("gx", "gy")),
            P(("gx", "gy")),
            P(("gx", "gy")),
        ),
        out_specs=(P(None, "gx", "gy", None), P(None, ("gx", "gy"))),
        check_vma=False,
    )
```

```python
import math

import jax
import jax.numpy as jnp
from jax import lax
from jax.experimental import pallas as pl
from jax.experimental.pallas import tpu as pltpu
from jax.sharding import PartitionSpec as P

CX = 64
CY = 32
CZ = 128
P_SIZE = 256
HOST = 512
PTS = 2 * P_SIZE

DT_STEP = 0.2
NU_VISC = 0.5
EPS_SQ = 1.44
CORE_SQ = 0.01

ROWS = 16
BACK = 8
YROWS = 72
XROWS = 40
FACE_Y = 3 * CX
FACE_X = 3 * XROWS
RIM_Y = 2 * 3 * YROWS
RIM_X = 2 * 3 * CY
CHUNK = 8
N_CHUNK = CX // CHUNK

F32 = jnp.float32
BF16 = jnp.bfloat16
VM = pl.BlockSpec(memory_space=pltpu.MemorySpace.VMEM)
SM = pl.BlockSpec(memory_space=pltpu.MemorySpace.SMEM)
HB = pl.BlockSpec(memory_space=pltpu.MemorySpace.HBM)
MIB = 1024 * 1024


def call(body, outs, n_in, name, scratch=(), first=VM, second=VM, out_specs=None, in_specs=None, vmem=12, aliases=None):
    return pl.pallas_call(
        body,
        out_shape=[jax.ShapeDtypeStruct(s, F32) for s in outs],
        in_specs=in_specs or ([first, second] + [VM] * n_in)[:n_in],
        out_specs=out_specs or [VM] * len(outs),
        scratch_shapes=list(scratch),
        input_output_aliases=aliases or {},
        compiler_params=pltpu.CompilerParams(vmem_limit_bytes=vmem * MIB),
        name=name,
    )


def place():
    nx, ny = lax.axis_size("gx"), lax.axis_size("gy")
    ix, iy = lax.axis_index("gx"), lax.axis_index("gy")
    px, py = lax.rem(ix, 2), lax.rem(iy, 2)
    inner = (ix + px > 0) & (ix + px < nx)
    return px == 0, py == 0, inner, ix * ny + iy, (ix - px) * ny + iy, ny


def odd_side():
    ny, iy = lax.axis_size("gy"), lax.axis_index("gy")
    py = lax.rem(iy, 2)
    return (iy + py > 0) & (iy + py < ny)


def split(value):
    high = value.astype(BF16)
    low = (value - high.astype(F32)).astype(BF16)
    return high, low


def dot3(a_high, a_low, b_high, b_low):
    def one(a, b):
        return jnp.dot(a, b, preferred_element_type=F32)

    return one(a_high, b_high) + (one(a_high, b_low) + one(a_low, b_high))


def dot3_last(a_high, a_low, b_high, b_low):
    def one(a, b):
        return lax.dot_general(a, b, (((1,), (1,)), ((), ())), preferred_element_type=F32)

    return one(a_high, b_high) + (one(a_high, b_low) + one(a_low, b_high))


def reduce_list(items, op):
    result = items[0]
    for item in items[1:]:
        result = op(result, item)
    return result


def pack_body(v_ref, spin_hbm, *rest):
    params, (pay_c, pay_d, blk_ref, held, held_int, spin_ref, sems) = rest[:5], rest[5:]
    _, even_y, _, brick, _, _ = place()

    def faces(first, second):
        made = []
        for k, (ref, y) in enumerate(((pay_c, first), (pay_d, second))):
            for c in range(3):
                made.append(pltpu.make_async_copy(v_ref.at[c, :, y], ref.at[pl.ds(c * CX, CX)], sems.at[3 * k + c]))
        return made

    @pl.when(even_y)
    def _():
        for copy in faces(CY - 1, 0):
            copy.start()

    @pl.when(jnp.logical_not(even_y))
    def _():
        for copy in faces(0, CY - 1):
            copy.start()

    small = [pltpu.make_async_copy(spin_hbm, spin_ref, sems.at[6])]
    small += [pltpu.make_async_copy(p, held.at[k], sems.at[7 + k]) for k, p in enumerate(params[:4])]
    small.append(pltpu.make_async_copy(params[4], held_int, sems.at[11]))
    for copy in small:
        copy.start()
    for copy in small:
        copy.wait()
    radius, chord, twist, angle = [held[k] for k in range(4)]
    parts = [
        radius,
        chord,
        jnp.cos(twist),
        jnp.sin(twist),
        jnp.cos(angle),
        jnp.sin(angle),
        held_int[...].astype(F32),
        jnp.broadcast_to(spin_ref[...], (1, CZ)),
        jnp.full((1, CZ), brick.astype(F32), F32),
    ]
    block = jnp.concatenate(parts, axis=0)
    blk_ref[...] = block
    pay_c[FACE_Y:] = block
    pay_d[FACE_Y:] = block
    for copy in faces(0, 0):
        copy.wait()


def stencil_body(start, v_ref, out_ref):
    row = lax.broadcasted_iota(jnp.int32, (CY, CZ), 0)
    lane = lax.broadcasted_iota(jnp.int32, (CY, CZ), 1)
    half = 0.5 * DT_STEP
    visc = DT_STEP * NU_VISC
    not_last_y, not_first_y = row < CY - 1, row > 0
    not_last_z, not_first_z = lane < CZ - 1, lane > 0

    def step(k, carry):
        x = start + k
        up = jnp.minimum(x + 1, CX - 1)
        down = jnp.maximum(x - 1, 0)
        v0, v1, v2 = v_ref[0, x], v_ref[1, x], v_ref[2, x]
        a_x = jnp.where(x < CX - 1, visc - half * v0, 0.0)
        b_x = jnp.where(x > 0, visc + half * v0, 0.0)
        a_y = jnp.where(not_last_y, visc - half * v1, 0.0)
        b_y = jnp.where(not_first_y, visc + half * v1, 0.0)
        a_z = jnp.where(not_last_z, visc - half * v2, 0.0)
        b_z = jnp.where(not_first_z, visc + half * v2, 0.0)
        for c in range(3):
            mid = (v0, v1, v2)[c]
            along_x = a_x * v_ref[c, up] + b_x * v_ref[c, down]
            along_y = a_y * pltpu.roll(mid, CY - 1, 0) + b_y * pltpu.roll(mid, 1, 0)
            along_z = a_z * pltpu.roll(mid, CZ - 1, 1) + b_z * pltpu.roll(mid, 1, 1)
            out_ref[c, k] = (1.0 - 6.0 * visc) * mid + along_x + (along_y + along_z)
        return carry

    lax.fori_loop(0, out_ref.shape[1], step, 0, unroll=2)


def weight(coord, base, frac):
    return jnp.where(coord == base, 1.0 - frac, jnp.where(coord == base + 1, frac, 0.0))


def sample_part(start, v_ref, table, acc):
    x_col, y_col = [table[:, k : k + 1].astype(jnp.int32) for k in range(2)]
    fx, fy = [table[:, k : k + 1] for k in range(3, 5)]
    lane = lax.broadcasted_iota(jnp.int32, (HOST, CZ), 1)
    wy = weight(lane % CY, y_col, fy)
    x_lane = (lane // CY + start - x_col).astype(F32).astype(BF16)
    near, far = split((1.0 - fx) * wy), split(fx * wy)
    zero = jnp.zeros((HOST, CZ), BF16)
    per = 4
    nx = CZ * per // CY
    for j in range(CX // 2 // nx):
        highs, lows = [], []
        for i in range(per):
            shift = (CZ // CY) * (j * per + i)
            at_base, at_next = x_lane == jnp.bfloat16(-shift), x_lane == jnp.bfloat16(1 - shift)
            highs.append(jnp.where(at_base, near[0], jnp.where(at_next, far[0], zero)))
            lows.append(jnp.where(at_base, near[1], jnp.where(at_next, far[1], zero)))
        w_high, w_low = jnp.concatenate(highs, axis=1), jnp.concatenate(lows, axis=1)
        first = start + j * nx
        field = [v_ref[c, first : first + nx].reshape(nx * CY, CZ) for c in range(3)]
        f_high, f_low = split(jnp.concatenate(field, axis=1))
        part = dot3(w_high, w_low, f_high, f_low)
        acc = part if acc is None else acc + part
    return acc


def sample_low_body(v_ref, cell_ref, frac_ref, tab_ref, acc_ref, x_ref, y_ref):
    for c in range(3):
        x_ref[c] = v_ref[c, 0]
        x_ref[c + 3] = v_ref[c, CX - 1]
    y_ref[0] = v_ref[1, :, 0, :]
    y_ref[1] = v_ref[1, :, CY - 1, :]
    rows = jnp.concatenate([cell_ref[...].astype(F32), frac_ref[...], jnp.zeros((CZ - 6, HOST), F32)], axis=0)
    table = rows.T
    tab_ref[...] = table
    acc_ref[...] = sample_part(0, v_ref, table, None)


def sample_high_body(v_ref, tab_ref, low_ref, acc_ref, edge_ref, wz_ref):
    table = tab_ref[...]
    acc_ref[...] = sample_part(CX // 2, v_ref, table, low_ref[...])
    lane = lax.broadcasted_iota(jnp.int32, (HOST, CZ), 1)
    x_col, y_col, z_col = [table[:, k : k + 1].astype(jnp.int32) for k in range(3)]
    fx, fy, fz = [table[:, k : k + 1] for k in range(3, 6)]
    on_line = lane >= CX
    edge_x = jnp.where(on_line, lane - CX, CX)
    edge_y = jnp.where(on_line, CY, lane)
    both = weight(edge_x, x_col, fx) * weight(edge_y, y_col, fy)
    edge_ref[...] = jnp.where(on_line | (lane <= CY), both, 0.0)
    wz_ref[...] = weight(lane, z_col, fz)


def split_blocks(sources):
    return [
        ref[first + k * ROWS : first + (k + 1) * ROWS]
        for ref, first in sources
        for k in range((ref.shape[0] - first) // ROWS)
    ]


def pick_pair(values, b0, ny):
    keys = [value[12:13, 0:1] for value in values]
    members = []
    for key in keys:
        home = jnp.floor(key * (1.0 / HOST)).astype(jnp.int32)
        members.append((home == b0) | (home == b0 + ny))
    low_key = reduce_list([jnp.where(m, k, 1e9) for k, m in zip(keys, members)], jnp.minimum)
    high_key = reduce_list([jnp.where(m, k, -9.0) for k, m in zip(keys, members)], jnp.maximum)
    low = jnp.full((ROWS, CZ), -1.0, F32)
    high = low
    for key, value in zip(keys, values):
        low = jnp.where(key == low_key, value, low)
        high = jnp.where(key == high_key, value, high)
    return low, high


def xpack_body(n_blk, x_ref, rec_c, rec_d, *rest):
    pieces, (pay_a, pay_b, own_ref, *others) = rest[:n_blk], rest[n_blk:]
    even_x, even_y, inner, _, b0, ny = place()
    for c in range(3):
        at = c * CX
        y_high = jnp.where(even_y, rec_c[at : at + 1], jnp.where(odd_side(), rec_d[at : at + 1], 0.0))
        tail = jnp.concatenate([y_high, jnp.zeros((XROWS - CY - 1, CZ), F32)], axis=0)
        low, high = x_ref[c], x_ref[c + 3]
        at = c * XROWS
        pay_a[at : at + CY] = jnp.where(even_x, high, low)
        pay_b[at : at + CY] = jnp.where(even_x, low, high)
        pay_a[at + CY : at + XROWS] = tail
        pay_b[at + CY : at + XROWS] = tail
    if not others:
        own_ref[...] = jnp.concatenate([p[...] for p in pieces], axis=0)
        return
    values = split_blocks([(p, 0) for p in pieces])
    chips = ny * 2
    side = jnp.where(even_x, -chips, chips)
    total = lax.axis_size("gx") * ny
    own_ref[...] = jnp.concatenate(pick_pair(values, b0, ny), axis=0)
    beside = jnp.concatenate(pick_pair(values, lax.rem(b0 + side + total, total), ny), axis=0)
    pay_b[FACE_X:] = beside
    others[1][...] = beside
    others[0][...] = jnp.concatenate(pick_pair(values, lax.rem(b0 + 2 * chips, total), ny), axis=0)


def select_body(n_blk, tab_ref, acc_ref, edge_ref, wz_ref, face_a, face_b, rec_c, rec_d, blk_ref, *rest):
    others, (samp_ref, sel_ref, pts_ref) = rest[:n_blk], rest[n_blk:]
    even_x, even_y, inner, brick, b0, ny = place()
    sources = [(blk_ref, 0), (face_b, FACE_X)] + [(o, 0) for o in others]
    turbine_a, turbine_b = pick_pair(split_blocks(sources), b0, ny)
    sel = jnp.concatenate([turbine_a, turbine_b], axis=0)
    sel_ref[...] = sel
    table = tab_ref[...]
    lane = lax.broadcasted_iota(jnp.int32, (PTS, CZ), 1)
    field = []
    for c in range(3):
        at = c * XROWS
        past = jnp.where(inner, face_b[at : at + XROWS], 0.0)
        plane = jnp.where(even_x, face_a[at : at + XROWS], past)
        at = c * CX
        line = jnp.where(even_y, rec_c[at : at + CX], jnp.where(odd_side(), rec_d[at : at + CX], 0.0))
        field.append(jnp.concatenate([plane, jnp.zeros((CX - XROWS, CZ), F32), line], axis=0))
    w_high, w_low = split(edge_ref[...])
    f_high, f_low = split(jnp.concatenate(field, axis=1))
    acc = acc_ref[...] + dot3(w_high, w_low, f_high, f_low)
    wz = wz_ref[...]
    for c in range(3):
        value = jnp.sum(acc[:, c * CZ : (c + 1) * CZ] * wz, axis=1, keepdims=True)
        table = table + jnp.where(lane == 6 + c, value, 0.0)
    slot = jnp.concatenate([sel[j : j + 1] for j in (12, 13, ROWS + 12, ROWS + 13)], axis=1).astype(jnp.int32)
    mine = (slot // HOST) == brick
    local = jnp.where(mine, slot % HOST, -1)
    hit = (lax.broadcasted_iota(jnp.int32, (HOST, PTS), 0) == local).astype(F32).astype(BF16)
    by_slot = table.T[0:16]
    first, second = split(by_slot)
    third = (by_slot - first.astype(F32) - second.astype(F32)).astype(BF16)
    pulled = jnp.dot(jnp.concatenate([first, second, third], axis=0), hit, preferred_element_type=F32)
    points = pulled[0:16] + pulled[16:32] + pulled[32:48]
    row = lax.broadcasted_iota(jnp.int32, (16, PTS), 0)
    pts_ref[...] = jnp.where((row == 0) & jnp.logical_not(mine), -100.0, points)
    samp_ref[...] = points[6:14]


def offsets(frac):
    raw = [jnp.exp(-((o - frac) ** 2) / EPS_SQ) for o in (-1.0, 0.0, 1.0, 2.0)]
    total = (raw[0] + raw[1]) + (raw[2] + raw[3])
    return [value / total for value in raw]


def profile(rows, inner, base, frac):
    index = lax.broadcasted_iota(jnp.int32, (rows, PTS), 0)
    late = index - inner
    index = jnp.where(index < inner, index, jnp.where(late < 2, late - 2, late - 2 + inner))
    rel = index - base.astype(jnp.int32)
    result = jnp.zeros((rows, PTS), F32)
    for k, w in enumerate(offsets(frac)):
        result = jnp.where(rel == k - 1, w, result)
    return result


def weights_body(pts_ref, sel_ref, gx_ref, gy_ref, pz_ref, pos_ref, pair_ref, edge_ref):
    table = pts_ref[...]
    sel = sel_ref[...]
    turned = jnp.concatenate([sel, jnp.zeros((CZ - 2 * ROWS, CZ), F32)], axis=0).T
    gx = profile(YROWS, CX, table[0:1], table[3:4])
    gy = profile(CY, CY, table[1:2], table[4:5])
    gx_ref[...] = gx
    gy_ref[...] = gy
    pz_ref[...] = profile(CZ, CZ, table[2:3], table[5:6]) * DT_STEP
    pos_ref[...] = jnp.concatenate([table[q : q + 1, k * CZ : (k + 1) * CZ] for q in range(6) for k in range(4)], axis=0)
    for t in range(2):
        at = t * ROWS
        radius = jnp.concatenate([sel_ref[at : at + 1], sel_ref[at + 1 : at + 2]], axis=1)
        column = jnp.concatenate([turned[:, at : at + 1], turned[:, at + 1 : at + 2]], axis=0)
        spacing = radius - column
        pair_ref[t] = spacing / (spacing * spacing + CORE_SQ)
    for k in range(4):
        edge_ref[k * CY : (k + 1) * CY] = gx[CX + k : CX + k + 1] * gy


def attack(axial_flow, tangent, cos_twist, sin_twist):
    rel_speed = jnp.sqrt(axial_flow * axial_flow + tangent * tangent + 1.0)
    cos_phi = tangent / rel_speed
    sin_phi = axial_flow / rel_speed
    sin_alpha = sin_phi * cos_twist - cos_phi * sin_twist
    cos_alpha = cos_phi * cos_twist + sin_phi * sin_twist
    lift_coef = 2.0 * jnp.pi * sin_alpha * cos_alpha / (1.0 + 4.0 * sin_alpha * sin_alpha)
    drag_coef = 0.02 + 0.8 * sin_alpha * sin_alpha
    return rel_speed, cos_phi, sin_phi, lift_coef, drag_coef


def loads_body(samp_ref, other_ref, sel_ref, pz_ref, pos_ref, pair_ref, edge_ref, lh_ref, pay_ref, xrim_ref):
    def row(k):
        picks = (2 * k, 2 * k + 1, ROWS + 2 * k, ROWS + 2 * k + 1)
        return jnp.concatenate([sel_ref[j : j + 1] for j in picks], axis=1)

    radius, chord, cos_t, sin_t, cos_a, sin_a = [row(k) for k in range(6)]
    spin = radius * jnp.concatenate([sel_ref[j : j + 1] for j in (14, 14, ROWS + 14, ROWS + 14)], axis=1)
    flow = samp_ref[...] + other_ref[...]
    axial = flow[0:1]
    tangent = spin - (cos_a * flow[2:3] - sin_a * flow[1:2])
    rel_speed, cos_phi, sin_phi, lift_coef, drag_coef = attack(axial, tangent, cos_t, sin_t)
    circ = 0.5 * chord * rel_speed * lift_coef
    parts = []
    for t in range(2):
        seg = slice(t * P_SIZE, (t + 1) * P_SIZE)
        lhs = jnp.concatenate([cos_a[:, seg] * circ[:, seg], sin_a[:, seg] * circ[:, seg], jnp.zeros((6, P_SIZE), F32)], axis=0)
        both = jnp.dot(lhs, pair_ref[t], preferred_element_type=F32, precision=lax.Precision.HIGHEST)
        parts.append((cos_a[:, seg] * both[0:1] + sin_a[:, seg] * both[1:2]) / (4.0 * math.pi))
    induced = jnp.concatenate(parts, axis=1)
    rel_speed, cos_phi, sin_phi, lift_coef, drag_coef = attack(axial + induced, tangent, cos_t, sin_t)
    dynamic = 0.5 * chord * rel_speed * rel_speed
    lift = dynamic * lift_coef
    drag = dynamic * drag_coef
    thrust = lift * cos_phi + drag * sin_phi
    torque = lift * sin_phi - drag * cos_phi
    force = [-thrust, torque * sin_a, -torque * cos_a]
    pieces = []
    for t in range(2):
        for c in range(3):
            for h in range(2):
                at = t * P_SIZE + h * CZ
                pieces.append(force[c][:, at : at + CZ])
        pieces += [sel_ref[t * ROWS + 15 : t * ROWS + 16]] * 2
    blocks = jnp.concatenate(pieces, axis=0)
    pay_ref[0 : 2 * BACK] = blocks
    pay_ref[2 * BACK :] = pos_ref[...]
    pz = pz_ref[...]
    lines = jnp.concatenate([f * pz for f in force], axis=0)
    l_high, l_low = split(lines)
    lh_ref[...] = lines
    w_high, w_low = split(edge_ref[...])
    rim = dot3_last(w_high, w_low, l_high, l_low)
    for k in range(4):
        for c in range(3):
            at = (k * 3 + c) * CY
            xrim_ref[at : at + CY] = rim[k * CY : (k + 1) * CY, c * CZ : (c + 1) * CZ]


def near_body(rec_c, rec_d, low_ref, high_ref):
    _, even_y, _, _, _, _ = place()
    c_all, d_all = rec_c[...], jnp.where(odd_side(), rec_d[...], 0.0)
    for side, out_ref in ((0, low_ref), (1, high_ref)):
        got = jnp.where(even_y, d_all, c_all) if side == 0 else jnp.where(even_y, c_all, d_all)

        def wide(first, picks):
            return jnp.concatenate([got[first + j : first + j + 1] for j in picks], axis=1)

        x, y, z, fx, fy, fz = [wide(2 * BACK + 4 * q, range(4)) for q in range(6)]
        force = [wide(2 * c, (0, 1, BACK, BACK + 1)) * DT_STEP for c in range(3)]
        pz = profile(CZ, CZ, z, fz)
        l_high, l_low = split(jnp.concatenate([f * pz for f in force], axis=0))
        gx = profile(YROWS, CX, x, fx)
        wy = offsets(fy)
        planes = []
        for i in range(2):
            rel = (CY + i if side == 0 else i - 2) - y.astype(jnp.int32)
            gy = jnp.zeros((1, PTS), F32)
            for k in range(4):
                gy = jnp.where(rel == k - 1, wy[k], gy)
            planes.append(gx * gy)
        w_high, w_low = split(jnp.concatenate(planes, axis=0))
        rim = dot3_last(w_high, w_low, l_high, l_low)
        for i in range(2):
            for c in range(3):
                at = (i * 3 + c) * YROWS
                out_ref[at : at + YROWS] = rim[i * YROWS : (i + 1) * YROWS, c * CZ : (c + 1) * CZ]


SPREAD_X = 8


def spread_body(start, lines_ref, gx_ref, gy_ref, *rest):
    bases, out_ref = rest[:-1], rest[-1]
    l_high, l_low = split(lines_ref[...])
    gy = gy_ref[0:CY]
    held = [(ref, k) for ref in bases for k in range(0, ref.shape[1], SPREAD_X)]
    for k in range(out_ref.shape[1] // SPREAD_X):
        at = k * SPREAD_X
        first = start + at
        planes = jnp.concatenate([gx_ref[first + i : first + i + 1] * gy for i in range(SPREAD_X)], axis=0)
        w_high, w_low = split(planes)
        value = dot3_last(w_high, w_low, l_high, l_low)
        base, inner = held[k]
        for c in range(3):
            part = value[:, c * CZ : (c + 1) * CZ].reshape(SPREAD_X, CY, CZ)
            out_ref[c, at : at + SPREAD_X] = base[c, inner : inner + SPREAD_X] + part


def rimpack_body(n_blk, xrim_ref, low_ref, high_ref, *rest):
    pieces, (pay_a, pay_b, back_ref, *others) = rest[:n_blk], rest[n_blk:]
    even_x, even_y, inner, _, b0, ny = place()
    zero = jnp.zeros((CY - 4, CZ), F32)
    for k in range(2):
        for c in range(3):
            sides = []
            for s in range(2):
                near, far = [], []
                for y in range(2):
                    at = (y * 3 + c) * YROWS + CX + 2 * s + k
                    near.append(low_ref[at : at + 1])
                    far.append(high_ref[at : at + 1])
                at = ((2 * s + k) * 3 + c) * CY
                sides.append(xrim_ref[at : at + CY] + jnp.concatenate(near + [zero] + far, axis=0))
            at = (k * 3 + c) * CY
            pay_a[at : at + CY] = jnp.where(even_x, sides[1], sides[0])
            pay_b[at : at + CY] = jnp.where(even_x, sides[0], sides[1])
    back = jnp.concatenate([p[...] for p in pieces], axis=0)
    back_ref[...] = back
    if others:
        chips = ny * 2
        side = jnp.where(even_x, -chips, chips)
        total = lax.axis_size("gx") * ny
        for ref, at, target in (
            (pay_b, RIM_X, lax.rem(b0 + side + total, total)),
            (others[0], 0, lax.rem(b0 + 2 * chips, total)),
        ):
            for core in range(2):
                wanted = (target + core * ny).astype(F32)
                found = jnp.full((BACK, CZ), -1.0, F32)
                for k in range(back.shape[0] // BACK):
                    value = back[k * BACK : (k + 1) * BACK]
                    found = jnp.where(value[6:7, 0:1] == wanted, value, found)
                ref[at + core * BACK : at + (core + 1) * BACK] = found


def face_terms(buf, at, first, size, main_low, main_high, y_ref, rec_c, rec_d, rim_low, rim_high, even_y):
    half = 0.5 * DT_STEP
    visc = DT_STEP * NU_VISC
    part = slice(first, first + size)
    here = slice(at, at + size)
    half_of = main_low if first < CX // 2 else main_high
    inner = first % (CX // 2)
    for c in range(3):
        buf[c, here] = half_of[c, inner : inner + size]
        rows = slice(c * CX + first, c * CX + first + size)
        a, b = rec_c[rows], jnp.where(odd_side(), rec_d[rows], 0.0)
        low = [jnp.where(even_y, b, a) * (visc + half * y_ref[0, part]), 0.0]
        high = [0.0, jnp.where(even_y, a, b) * (visc - half * y_ref[1, part])]
        for i in range(2):
            row = (i * 3 + c) * YROWS + first
            buf[c, here, i, :] += rim_low[row : row + size] + low[i]
            buf[c, here, CY - 2 + i, :] += rim_high[row : row + size] + high[i]


INNER = [(2, CHUNK - 2)] + [(k * CHUNK, CHUNK) for k in range(1, N_CHUNK - 1)] + [(CX - CHUNK, CHUNK - 2)]


def chunk_copy(buf, at, out_ref, first, size, sem):
    return pltpu.make_async_copy(buf.at[:, pl.ds(at, size)], out_ref.at[:, pl.ds(first, size)], sem)


def inside_body(chunks, *refs):
    main_low, main_high, y_ref, rec_c, rec_d, rim_low, rim_high, out_ref, buf, sems = refs[-10:]
    _, even_y, _, _, _, _ = place()
    copies = []
    for k, (first, size) in enumerate(chunks):
        face_terms(buf, first - 2, first, size, main_low, main_high, y_ref, rec_c, rec_d, rim_low, rim_high, even_y)
        copies.append(chunk_copy(buf, first - 2, out_ref, first, size, sems.at[k]))
        copies[-1].start()
    for copy in copies:
        copy.wait()


def final_body(n_ret, _, main_low, main_high, x_ref, y_ref, face_a, face_b, rec_c, rec_d, rim_a, rim_b, rim_low, rim_high, back_ref, *rest):
    rets, (out_ref, pf_ref, buf, pf_buf, sems) = rest[:n_ret], rest[n_ret:]
    even_x, even_y, inner, brick, _, _ = place()
    half = 0.5 * DT_STEP
    visc = DT_STEP * NU_VISC
    mine = brick.astype(F32)
    found = jnp.zeros((BACK, CZ), F32)
    for ref, first in [(back_ref, 0), (rim_b, RIM_X)] + [(r, 0) for r in rets]:
        for k in range((ref.shape[0] - first) // BACK):
            value = ref[first + BACK * k : first + BACK * k + BACK]
            found = jnp.where(value[6:7, 0:1] == mine, value, found)
    for c in range(3):
        pf_buf[c : c + 1] = jnp.concatenate([found[2 * c : 2 * c + 1], found[2 * c + 1 : 2 * c + 2]], axis=1)
    copies = [pltpu.make_async_copy(pf_buf, pf_ref, sems.at[2])]
    copies[0].start()
    for k in range(2):
        first, at = k * (CX - 2), k * 2
        face_terms(buf, at, first, 2, main_low, main_high, y_ref, rec_c, rec_d, rim_low, rim_high, even_y)
        for c in range(3):
            a = face_a[c * XROWS : c * XROWS + CY]
            b = jnp.where(inner, face_b[c * XROWS : c * XROWS + CY], 0.0)
            if k == 0:
                buf[c, 0] += jnp.where(even_x, b, a) * (visc + half * x_ref[0])
            else:
                buf[c, 3] += jnp.where(even_x, a, b) * (visc - half * x_ref[3])
            for i in range(2):
                rows = slice((i * 3 + c) * CY, (i * 3 + c + 1) * CY)
                a, b = rim_a[rows], jnp.where(inner, rim_b[rows], 0.0)
                if k == 0:
                    buf[c, i] += jnp.where(even_x, b, a)
                else:
                    buf[c, 2 + i] += jnp.where(even_x, a, b)
        copies.append(chunk_copy(buf, at, out_ref, first, 2, sems.at[k]))
        copies[-1].start()
    for copy in copies:
        copy.wait()


def per_device(
    velocity,
    host_cell,
    host_frac,
    host_dst,
    owner_src,
    rotor_speed,
    blade_radius,
    blade_chord,
    blade_twist,
    blade_angle,
):
    nx, ny = lax.axis_size("gx"), lax.axis_size("gy")
    ring, short = nx == 8, ny == 4

    def flip(n, bits):
        return [(i, i ^ bits) for i in range(n)]

    def odd_pairs(n, closed=False):
        up = [(i, (i + 1) % n) for i in range(1, n if closed else n - 1, 2)]
        return up + [(t, s) for s, t in up]

    def same_side(n):
        return [(i, (i + (2 if i % 2 else n - 2)) % n) for i in range(n)]

    def across_x(blocks):
        return [lax.ppermute(b, "gx", p) for b, p in zip(blocks, (flip(nx, 4), same_side(nx)))]

    def swap(block):
        return lax.ppermute(block, "gx", flip(nx, 1))

    def join(pieces):
        return pieces[0] if len(pieces) == 1 else jnp.concatenate(pieces, axis=0)

    def after(values, other):
        return lax.optimization_barrier((values, other))

    def gather_y(first):
        pieces = [first]
        for bit in [b for b in (2, 4, 8) if b < ny]:
            pieces.append(lax.ppermute(join(pieces), "gy", flip(ny, bit)))
        return pieces

    def exchange_y(to_c, to_d, block):
        from_c = lax.ppermute(to_c, "gy", flip(ny, 1))
        from_d = lax.ppermute(to_d, "gy", flip(ny, 3) if short else odd_pairs(ny))
        return from_c, from_d, [lax.ppermute(block, "gy", flip(ny, 2))] if short else []

    def blocks_y(block, from_c, from_d, far, size, at):
        got = join([block, from_c[at : at + size]])
        if short:
            return [join([got, from_d[at : at + size]] + far)]
        return gather_y(got)

    def gather_x(blocks):
        pieces = []
        for bit in [b for b in (2, 4, 8, 16) if b < nx]:
            pieces.append(lax.ppermute(join([blocks] + pieces), "gx", flip(nx, bit)))
        return pieces

    def pin(array):
        return pltpu.with_memory_space_constraint(array, pltpu.MemorySpace.HBM)

    dma = pltpu.SemaphoreType.DMA
    pay_c, pay_d, block = call(
        pack_body,
        [(FACE_Y + ROWS, CZ)] * 2 + [(ROWS, CZ)],
        7,
        "pack",
        scratch=[pltpu.VMEM((4, 2, CZ), F32), pltpu.VMEM((2, CZ), jnp.int32), pltpu.VMEM((1, 1), F32), dma((12,))],
        in_specs=[HB] * 7,
    )(pin(velocity), rotor_speed.reshape(1, 1), *[pin(a.reshape(2, CZ)) for a in (blade_radius, blade_chord, blade_twist, blade_angle, owner_src)])
    rec_c, rec_d, far = exchange_y(pay_c, pay_d, block)

    def stencil(start, count):
        return call(lambda *refs: stencil_body(start, *refs), [(3, count, CY, CZ)], 1, "stencil")(velocity)[0]

    base_low = stencil(0, 3 * CX // 8)
    table, sums, x_faces, y_faces = call(
        sample_low_body, [(HOST, CZ), (HOST, 3 * CZ), (6, CY, CZ), (2, CX, CZ)], 3, "sample_low", vmem=24
    )(velocity, host_cell, host_frac)
    (rec_c, rec_d, far), (base_low, sums) = after((rec_c, rec_d, far), (base_low, sums))
    pieces = blocks_y(block, rec_c, rec_d, far, ROWS, FACE_Y)
    beside = [swap(p) for p in pieces]
    beside, base_third = after(beside, stencil(CX // 2, CX // 4))
    pieces = pieces + beside
    n_rows = 2 * ny * ROWS
    pair = (2 * ROWS, CZ)
    pay_a, pay_b, blocks, *across = call(
        lambda *refs: xpack_body(len(pieces), *refs),
        [(FACE_X, CZ), (FACE_X + 2 * ROWS, CZ), pair, pair, pair] if ring else [(FACE_X, CZ), (FACE_X, CZ), (n_rows, CZ)],
        3 + len(pieces),
        "xpack",
    )(x_faces, rec_c, rec_d, *pieces)
    face_b = lax.ppermute(pay_b, "gx", odd_pairs(nx, ring))
    from_x = across_x(across) if ring else gather_x(blocks)
    face_a = swap(pay_a)
    sums, edge, wz = call(
        sample_high_body, [(HOST, 3 * CZ), (HOST, CZ), (HOST, CZ)], 3, "sample_high", vmem=24
    )(velocity, table, sums)
    base_more = stencil(3 * CX // 8, CX // 8)
    (face_a, face_b, from_x), (sums, base_more) = after((face_a, face_b, from_x), (sums, base_more))
    samp, sel, pts = call(
        lambda *refs: select_body(len(from_x), *refs),
        [(8, PTS), (2 * ROWS, CZ), (16, PTS)],
        9 + len(from_x),
        "select",
    )(table, sums, edge, wz, face_a, face_b, rec_c, rec_d, blocks, *from_x)
    other = swap(samp)
    gx, gy, pz, pos, pair_kernel, edge = call(
        weights_body,
        [(YROWS, PTS), (CY, PTS), (CZ, PTS), (24, CZ), (2, P_SIZE, P_SIZE), (4 * CY, PTS)],
        2,
        "weights",
    )(pts, sel)
    other, base_next = after(other, stencil(6 * CX // 8, CX // 8))
    lines, points, xrim = call(
        loads_body,
        [(3 * CZ, PTS), (2 * BACK + 24, CZ), (2 * RIM_X, CZ)],
        7,
        "loads",
    )(samp, other, sel, pz, pos, pair_kernel, edge)
    ret = points[: 2 * BACK]
    near_c, near_d, far = exchange_y(points, points, ret)

    def spread(start, *bases):
        return call(
            lambda *refs: spread_body(start, *refs), [(3, CX // 2, CY, CZ)], 3 + len(bases), "spread"
        )(lines, gx, gy, *bases)[0]

    (near_c, near_d), main_low = after((near_c, near_d), spread(0, base_low, base_more))
    rim_low, rim_high = call(near_body, [(RIM_Y, CZ)] * 2, 2, "near")(near_c, near_d)
    far, rim_low = after(far, rim_low)
    pieces = blocks_y(ret, near_c, near_d, far, 2 * BACK, 0)
    n_rows = 2 * ny * BACK
    pair = (2 * BACK, CZ)
    pay_a, pay_b, back, *across = call(
        lambda *refs: rimpack_body(len(pieces), *refs),
        [(RIM_X, CZ), (RIM_X + 2 * BACK, CZ), (n_rows, CZ), pair] if ring else [(RIM_X, CZ), (RIM_X, CZ), (n_rows, CZ)],
        3 + len(pieces),
        "rimpack",
    )(xrim, rim_low, rim_high, *pieces)
    rim_b = lax.ppermute(pay_b, "gx", odd_pairs(nx, ring))
    rets = [lax.ppermute(across[0], "gx", flip(nx, 4))] if ring else gather_x(back)
    rim_a = swap(pay_a)
    main_high = spread(CX // 2, base_third, base_next, stencil(7 * CX // 8, CX // 8))
    faces = (main_low, main_high, y_faces, rec_c, rec_d, rim_low, rim_high)
    room = [pltpu.VMEM((3, CX - 4, CY, CZ), F32), dma((N_CHUNK,))]
    inside = call(
        lambda *refs: inside_body(INNER[:2], *refs), [velocity.shape], 7, "inside", scratch=room, out_specs=[HB], vmem=16
    )(*faces)[0]
    (rim_a, rim_b), inside = after((rim_a, rim_b), inside)
    if ring:
        rets.append(swap(rim_b[RIM_X:]))
    inside = call(
        lambda *refs: inside_body(INNER[2:], *refs),
        [velocity.shape],
        8,
        "inside",
        scratch=room,
        first=HB,
        out_specs=[HB],
        vmem=16,
        aliases={0: 0},
    )(inside, *faces)[0]
    rets, inside = after(rets, inside)
    return tuple(
        call(
            lambda *refs: final_body(len(rets), *refs),
            [velocity.shape, (3, P_SIZE)],
            14 + len(rets),
            "final",
            scratch=[pltpu.VMEM((3, 4, CY, CZ), F32), pltpu.VMEM((3, P_SIZE), F32), dma((3,))],
            first=HB,
            out_specs=[HB, HB],
            aliases={0: 0},
        )(inside, main_low, main_high, x_faces, y_faces, face_a, face_b, rec_c, rec_d, rim_a, rim_b, rim_low, rim_high, back, *rets)
    )


def solution(mesh):
    return jax.shard_map(
        per_device,
        mesh=mesh,
        in_specs=(
            P(None, "gx", "gy", None),
            P(None, ("gx", "gy")),
            P(None, ("gx", "gy")),
            P(("gx", "gy")),
            P(("gx", "gy")),
            P(("gx", "gy")),
            P(("gx", "gy")),
            P(("gx", "gy")),
            P(("gx", "gy")),
            P(("gx", "gy")),
        ),
        out_specs=(P(None, "gx", "gy", None), P(None, ("gx", "gy"))),
        check_vma=False,
    )
```

```python
import math

import jax
import jax.numpy as jnp
from jax import lax
from jax.experimental import pallas as pl
from jax.experimental.pallas import tpu as pltpu
from jax.sharding import PartitionSpec as P

CX = 64
CY = 32
CZ = 128
P_SIZE = 256
HOST = 512
PTS = 2 * P_SIZE

DT_STEP = 0.2
NU_VISC = 0.5
EPS_SQ = 1.44
CORE_SQ = 0.01

ROWS = 16
BACK = 8
YROWS = 72
XROWS = 40
FACE_Y = 3 * CX
FACE_X = 3 * XROWS
RIM_Y = 2 * 3 * YROWS
RIM_X = 2 * 3 * CY
CHUNK = 8
N_CHUNK = CX // CHUNK

F32 = jnp.float32
BF16 = jnp.bfloat16
VM = pl.BlockSpec(memory_space=pltpu.MemorySpace.VMEM)
SM = pl.BlockSpec(memory_space=pltpu.MemorySpace.SMEM)
HB = pl.BlockSpec(memory_space=pltpu.MemorySpace.HBM)
MIB = 1024 * 1024


def call(body, outs, n_in, name, scratch=(), first=VM, second=VM, out_specs=None, in_specs=None, vmem=12, aliases=None):
    return pl.pallas_call(
        body,
        out_shape=[jax.ShapeDtypeStruct(s, F32) for s in outs],
        in_specs=in_specs or ([first, second] + [VM] * n_in)[:n_in],
        out_specs=out_specs or [VM] * len(outs),
        scratch_shapes=list(scratch),
        input_output_aliases=aliases or {},
        compiler_params=pltpu.CompilerParams(vmem_limit_bytes=vmem * MIB),
        name=name,
    )


def place():
    nx, ny = lax.axis_size("gx"), lax.axis_size("gy")
    ix, iy = lax.axis_index("gx"), lax.axis_index("gy")
    px, py = lax.rem(ix, 2), lax.rem(iy, 2)
    inner = (ix + px > 0) & (ix + px < nx)
    return px == 0, py == 0, inner, ix * ny + iy, (ix - px) * ny + iy, ny


def odd_side():
    ny, iy = lax.axis_size("gy"), lax.axis_index("gy")
    py = lax.rem(iy, 2)
    return (iy + py > 0) & (iy + py < ny)


def split(value):
    high = value.astype(BF16)
    low = (value - high.astype(F32)).astype(BF16)
    return high, low


def dot3(a_high, a_low, b_high, b_low):
    def one(a, b):
        return jnp.dot(a, b, preferred_element_type=F32)

    return one(a_high, b_high) + (one(a_high, b_low) + one(a_low, b_high))


def dot3_last(a_high, a_low, b_high, b_low):
    def one(a, b):
        return lax.dot_general(a, b, (((1,), (1,)), ((), ())), preferred_element_type=F32)

    return one(a_high, b_high) + (one(a_high, b_low) + one(a_low, b_high))


def reduce_list(items, op):
    result = items[0]
    for item in items[1:]:
        result = op(result, item)
    return result


def pack_body(v_ref, spin_hbm, *rest):
    params, (pay_c, pay_d, blk_ref, held, held_int, spin_ref, sems) = rest[:5], rest[5:]
    _, even_y, _, brick, _, _ = place()

    def faces(first, second):
        made = []
        for k, (ref, y) in enumerate(((pay_c, first), (pay_d, second))):
            for c in range(3):
                made.append(pltpu.make_async_copy(v_ref.at[c, :, y], ref.at[pl.ds(c * CX, CX)], sems.at[3 * k + c]))
        return made

    @pl.when(even_y)
    def _():
        for copy in faces(CY - 1, 0):
            copy.start()

    @pl.when(jnp.logical_not(even_y))
    def _():
        for copy in faces(0, CY - 1):
            copy.start()

    small = [pltpu.make_async_copy(spin_hbm, spin_ref, sems.at[6])]
    small += [pltpu.make_async_copy(p, held.at[k], sems.at[7 + k]) for k, p in enumerate(params[:4])]
    small.append(pltpu.make_async_copy(params[4], held_int, sems.at[11]))
    for copy in small:
        copy.start()
    for copy in small:
        copy.wait()
    radius, chord, twist, angle = [held[k] for k in range(4)]
    parts = [
        radius,
        chord,
        jnp.cos(twist),
        jnp.sin(twist),
        jnp.cos(angle),
        jnp.sin(angle),
        held_int[...].astype(F32),
        jnp.broadcast_to(spin_ref[...], (1, CZ)),
        jnp.full((1, CZ), brick.astype(F32), F32),
    ]
    block = jnp.concatenate(parts, axis=0)
    blk_ref[...] = block
    pay_c[FACE_Y:] = block
    pay_d[FACE_Y:] = block
    for copy in faces(0, 0):
        copy.wait()


def stencil_body(start, v_ref, out_ref):
    row = lax.broadcasted_iota(jnp.int32, (CY, CZ), 0)
    lane = lax.broadcasted_iota(jnp.int32, (CY, CZ), 1)
    half = 0.5 * DT_STEP
    visc = DT_STEP * NU_VISC
    not_last_y, not_first_y = row < CY - 1, row > 0
    not_last_z, not_first_z = lane < CZ - 1, lane > 0

    def step(k, carry):
        x = start + k
        up = jnp.minimum(x + 1, CX - 1)
        down = jnp.maximum(x - 1, 0)
        v0, v1, v2 = v_ref[0, x], v_ref[1, x], v_ref[2, x]
        a_x = jnp.where(x < CX - 1, visc - half * v0, 0.0)
        b_x = jnp.where(x > 0, visc + half * v0, 0.0)
        a_y = jnp.where(not_last_y, visc - half * v1, 0.0)
        b_y = jnp.where(not_first_y, visc + half * v1, 0.0)
        a_z = jnp.where(not_last_z, visc - half * v2, 0.0)
        b_z = jnp.where(not_first_z, visc + half * v2, 0.0)
        for c in range(3):
            mid = (v0, v1, v2)[c]
            along_x = a_x * v_ref[c, up] + b_x * v_ref[c, down]
            along_y = a_y * pltpu.roll(mid, CY - 1, 0) + b_y * pltpu.roll(mid, 1, 0)
            along_z = a_z * pltpu.roll(mid, CZ - 1, 1) + b_z * pltpu.roll(mid, 1, 1)
            out_ref[c, k] = (1.0 - 6.0 * visc) * mid + along_x + (along_y + along_z)
        return carry

    lax.fori_loop(0, out_ref.shape[1], step, 0, unroll=2)


def weight(coord, base, frac):
    return jnp.where(coord == base, 1.0 - frac, jnp.where(coord == base + 1, frac, 0.0))


def sample_part(start, v_ref, table, acc):
    x_col, y_col = [table[:, k : k + 1].astype(jnp.int32) for k in range(2)]
    fx, fy = [table[:, k : k + 1] for k in range(3, 5)]
    lane = lax.broadcasted_iota(jnp.int32, (HOST, CZ), 1)
    wy = weight(lane % CY, y_col, fy)
    x_lane = (lane // CY + start - x_col).astype(F32).astype(BF16)
    near, far = split((1.0 - fx) * wy), split(fx * wy)
    zero = jnp.zeros((HOST, CZ), BF16)
    per = 4
    nx = CZ * per // CY
    for j in range(CX // 2 // nx):
        highs, lows = [], []
        for i in range(per):
            shift = (CZ // CY) * (j * per + i)
            at_base, at_next = x_lane == jnp.bfloat16(-shift), x_lane == jnp.bfloat16(1 - shift)
            highs.append(jnp.where(at_base, near[0], jnp.where(at_next, far[0], zero)))
            lows.append(jnp.where(at_base, near[1], jnp.where(at_next, far[1], zero)))
        w_high, w_low = jnp.concatenate(highs, axis=1), jnp.concatenate(lows, axis=1)
        first = start + j * nx
        field = [v_ref[c, first : first + nx].reshape(nx * CY, CZ) for c in range(3)]
        f_high, f_low = split(jnp.concatenate(field, axis=1))
        part = dot3(w_high, w_low, f_high, f_low)
        acc = part if acc is None else acc + part
    return acc


def sample_low_body(v_ref, cell_ref, frac_ref, tab_ref, acc_ref, x_ref, y_ref):
    for c in range(3):
        x_ref[c] = v_ref[c, 0]
        x_ref[c + 3] = v_ref[c, CX - 1]
    y_ref[0] = v_ref[1, :, 0, :]
    y_ref[1] = v_ref[1, :, CY - 1, :]
    rows = jnp.concatenate([cell_ref[...].astype(F32), frac_ref[...], jnp.zeros((CZ - 6, HOST), F32)], axis=0)
    table = rows.T
    tab_ref[...] = table
    acc_ref[...] = sample_part(0, v_ref, table, None)


def sample_high_body(v_ref, tab_ref, low_ref, acc_ref, edge_ref, wz_ref):
    table = tab_ref[...]
    acc_ref[...] = sample_part(CX // 2, v_ref, table, low_ref[...])
    lane = lax.broadcasted_iota(jnp.int32, (HOST, CZ), 1)
    x_col, y_col, z_col = [table[:, k : k + 1].astype(jnp.int32) for k in range(3)]
    fx, fy, fz = [table[:, k : k + 1] for k in range(3, 6)]
    on_line = lane >= CX
    edge_x = jnp.where(on_line, lane - CX, CX)
    edge_y = jnp.where(on_line, CY, lane)
    both = weight(edge_x, x_col, fx) * weight(edge_y, y_col, fy)
    edge_ref[...] = jnp.where(on_line | (lane <= CY), both, 0.0)
    wz_ref[...] = weight(lane, z_col, fz)


def split_blocks(sources):
    return [
        ref[first + k * ROWS : first + (k + 1) * ROWS]
        for ref, first in sources
        for k in range((ref.shape[0] - first) // ROWS)
    ]


def pick_pair(values, b0, ny):
    keys = [value[12:13, 0:1] for value in values]
    members = []
    for key in keys:
        home = jnp.floor(key * (1.0 / HOST)).astype(jnp.int32)
        members.append((home == b0) | (home == b0 + ny))
    low_key = reduce_list([jnp.where(m, k, 1e9) for k, m in zip(keys, members)], jnp.minimum)
    high_key = reduce_list([jnp.where(m, k, -9.0) for k, m in zip(keys, members)], jnp.maximum)
    low = jnp.full((ROWS, CZ), -1.0, F32)
    high = low
    for key, value in zip(keys, values):
        low = jnp.where(key == low_key, value, low)
        high = jnp.where(key == high_key, value, high)
    return low, high


def xpack_body(n_blk, x_ref, rec_c, rec_d, *rest):
    pieces, (pay_a, pay_b, own_ref, *others) = rest[:n_blk], rest[n_blk:]
    even_x, even_y, inner, _, b0, ny = place()
    for c in range(3):
        at = c * CX
        y_high = jnp.where(even_y, rec_c[at : at + 1], jnp.where(odd_side(), rec_d[at : at + 1], 0.0))
        tail = jnp.concatenate([y_high, jnp.zeros((XROWS - CY - 1, CZ), F32)], axis=0)
        low, high = x_ref[c], x_ref[c + 3]
        at = c * XROWS
        pay_a[at : at + CY] = jnp.where(even_x, high, low)
        pay_b[at : at + CY] = jnp.where(even_x, low, high)
        pay_a[at + CY : at + XROWS] = tail
        pay_b[at + CY : at + XROWS] = tail
    if not others:
        own_ref[...] = jnp.concatenate([p[...] for p in pieces], axis=0)
        return
    values = split_blocks([(p, 0) for p in pieces])
    chips = ny * 2
    side = jnp.where(even_x, -chips, chips)
    total = lax.axis_size("gx") * ny
    own_ref[...] = jnp.concatenate(pick_pair(values, b0, ny), axis=0)
    beside = jnp.concatenate(pick_pair(values, lax.rem(b0 + side + total, total), ny), axis=0)
    pay_b[FACE_X:] = beside
    others[1][...] = beside
    others[0][...] = jnp.concatenate(pick_pair(values, lax.rem(b0 + 2 * chips, total), ny), axis=0)


def select_body(n_blk, tab_ref, acc_ref, edge_ref, wz_ref, face_a, face_b, rec_c, rec_d, blk_ref, *rest):
    others, (samp_ref, sel_ref, pts_ref) = rest[:n_blk], rest[n_blk:]
    even_x, even_y, inner, brick, b0, ny = place()
    sources = [(blk_ref, 0), (face_b, FACE_X)] + [(o, 0) for o in others]
    turbine_a, turbine_b = pick_pair(split_blocks(sources), b0, ny)
    sel = jnp.concatenate([turbine_a, turbine_b], axis=0)
    sel_ref[...] = sel
    table = tab_ref[...]
    lane = lax.broadcasted_iota(jnp.int32, (PTS, CZ), 1)
    field = []
    for c in range(3):
        at = c * XROWS
        past = jnp.where(inner, face_b[at : at + XROWS], 0.0)
        plane = jnp.where(even_x, face_a[at : at + XROWS], past)
        at = c * CX
        line = jnp.where(even_y, rec_c[at : at + CX], jnp.where(odd_side(), rec_d[at : at + CX], 0.0))
        field.append(jnp.concatenate([plane, jnp.zeros((CX - XROWS, CZ), F32), line], axis=0))
    w_high, w_low = split(edge_ref[...])
    f_high, f_low = split(jnp.concatenate(field, axis=1))
    acc = acc_ref[...] + dot3(w_high, w_low, f_high, f_low)
    wz = wz_ref[...]
    for c in range(3):
        value = jnp.sum(acc[:, c * CZ : (c + 1) * CZ] * wz, axis=1, keepdims=True)
        table = table + jnp.where(lane == 6 + c, value, 0.0)
    slot = jnp.concatenate([sel[j : j + 1] for j in (12, 13, ROWS + 12, ROWS + 13)], axis=1).astype(jnp.int32)
    mine = (slot // HOST) == brick
    local = jnp.where(mine, slot % HOST, -1)
    hit = (lax.broadcasted_iota(jnp.int32, (HOST, PTS), 0) == local).astype(F32).astype(BF16)
    by_slot = table.T[0:16]
    first, second = split(by_slot)
    third = (by_slot - first.astype(F32) - second.astype(F32)).astype(BF16)
    pulled = jnp.dot(jnp.concatenate([first, second, third], axis=0), hit, preferred_element_type=F32)
    points = pulled[0:16] + pulled[16:32] + pulled[32:48]
    row = lax.broadcasted_iota(jnp.int32, (16, PTS), 0)
    pts_ref[...] = jnp.where((row == 0) & jnp.logical_not(mine), -100.0, points)
    samp_ref[...] = points[6:14]


def offsets(frac):
    raw = [jnp.exp(-((o - frac) ** 2) / EPS_SQ) for o in (-1.0, 0.0, 1.0, 2.0)]
    total = (raw[0] + raw[1]) + (raw[2] + raw[3])
    return [value / total for value in raw]


def profile(rows, inner, base, frac):
    index = lax.broadcasted_iota(jnp.int32, (rows, PTS), 0)
    late = index - inner
    index = jnp.where(index < inner, index, jnp.where(late < 2, late - 2, late - 2 + inner))
    rel = index - base.astype(jnp.int32)
    result = jnp.zeros((rows, PTS), F32)
    for k, w in enumerate(offsets(frac)):
        result = jnp.where(rel == k - 1, w, result)
    return result


def weights_body(pts_ref, sel_ref, gx_ref, gy_ref, pz_ref, pos_ref, pair_ref, edge_ref):
    table = pts_ref[...]
    sel = sel_ref[...]
    turned = jnp.concatenate([sel, jnp.zeros((CZ - 2 * ROWS, CZ), F32)], axis=0).T
    gx = profile(YROWS, CX, table[0:1], table[3:4])
    gy = profile(CY, CY, table[1:2], table[4:5])
    gx_ref[...] = gx
    gy_ref[...] = gy
    pz_ref[...] = profile(CZ, CZ, table[2:3], table[5:6]) * DT_STEP
    pos_ref[...] = jnp.concatenate([table[q : q + 1, k * CZ : (k + 1) * CZ] for q in range(6) for k in range(4)], axis=0)
    for t in range(2):
        at = t * ROWS
        radius = jnp.concatenate([sel_ref[at : at + 1], sel_ref[at + 1 : at + 2]], axis=1)
        column = jnp.concatenate([turned[:, at : at + 1], turned[:, at + 1 : at + 2]], axis=0)
        spacing = radius - column
        pair_ref[t] = spacing / (spacing * spacing + CORE_SQ)
    for k in range(4):
        edge_ref[k * CY : (k + 1) * CY] = gx[CX + k : CX + k + 1] * gy


def attack(axial_flow, tangent, cos_twist, sin_twist):
    rel_speed = jnp.sqrt(axial_flow * axial_flow + tangent * tangent + 1.0)
    cos_phi = tangent / rel_speed
    sin_phi = axial_flow / rel_speed
    sin_alpha = sin_phi * cos_twist - cos_phi * sin_twist
    cos_alpha = cos_phi * cos_twist + sin_phi * sin_twist
    lift_coef = 2.0 * jnp.pi * sin_alpha * cos_alpha / (1.0 + 4.0 * sin_alpha * sin_alpha)
    drag_coef = 0.02 + 0.8 * sin_alpha * sin_alpha
    return rel_speed, cos_phi, sin_phi, lift_coef, drag_coef


def loads_body(samp_ref, other_ref, sel_ref, pz_ref, pos_ref, pair_ref, edge_ref, lh_ref, pay_ref, xrim_ref):
    def row(k):
        picks = (2 * k, 2 * k + 1, ROWS + 2 * k, ROWS + 2 * k + 1)
        return jnp.concatenate([sel_ref[j : j + 1] for j in picks], axis=1)

    radius, chord, cos_t, sin_t, cos_a, sin_a = [row(k) for k in range(6)]
    spin = radius * jnp.concatenate([sel_ref[j : j + 1] for j in (14, 14, ROWS + 14, ROWS + 14)], axis=1)
    flow = samp_ref[...] + other_ref[...]
    axial = flow[0:1]
    tangent = spin - (cos_a * flow[2:3] - sin_a * flow[1:2])
    rel_speed, cos_phi, sin_phi, lift_coef, drag_coef = attack(axial, tangent, cos_t, sin_t)
    circ = 0.5 * chord * rel_speed * lift_coef
    parts = []
    for t in range(2):
        seg = slice(t * P_SIZE, (t + 1) * P_SIZE)
        lhs = jnp.concatenate([cos_a[:, seg] * circ[:, seg], sin_a[:, seg] * circ[:, seg], jnp.zeros((6, P_SIZE), F32)], axis=0)
        both = dot3(*split(lhs), *split(pair_ref[t]))
        parts.append((cos_a[:, seg] * both[0:1] + sin_a[:, seg] * both[1:2]) / (4.0 * math.pi))
    induced = jnp.concatenate(parts, axis=1)
    rel_speed, cos_phi, sin_phi, lift_coef, drag_coef = attack(axial + induced, tangent, cos_t, sin_t)
    dynamic = 0.5 * chord * rel_speed * rel_speed
    lift = dynamic * lift_coef
    drag = dynamic * drag_coef
    thrust = lift * cos_phi + drag * sin_phi
    torque = lift * sin_phi - drag * cos_phi
    force = [-thrust, torque * sin_a, -torque * cos_a]
    pieces = []
    for t in range(2):
        for c in range(3):
            for h in range(2):
                at = t * P_SIZE + h * CZ
                pieces.append(force[c][:, at : at + CZ])
        pieces += [sel_ref[t * ROWS + 15 : t * ROWS + 16]] * 2
    blocks = jnp.concatenate(pieces, axis=0)
    pay_ref[0 : 2 * BACK] = blocks
    pay_ref[2 * BACK :] = pos_ref[...]
    pz = pz_ref[...]
    lines = jnp.concatenate([f * pz for f in force], axis=0)
    l_high, l_low = split(lines)
    lh_ref[...] = lines
    w_high, w_low = split(edge_ref[...])
    rim = dot3_last(w_high, w_low, l_high, l_low)
    for k in range(4):
        for c in range(3):
            at = (k * 3 + c) * CY
            xrim_ref[at : at + CY] = rim[k * CY : (k + 1) * CY, c * CZ : (c + 1) * CZ]


def near_body(rec_c, rec_d, low_ref, high_ref):
    _, even_y, _, _, _, _ = place()
    c_all, d_all = rec_c[...], jnp.where(odd_side(), rec_d[...], 0.0)
    for side, out_ref in ((0, low_ref), (1, high_ref)):
        got = jnp.where(even_y, d_all, c_all) if side == 0 else jnp.where(even_y, c_all, d_all)

        def wide(first, picks):
            return jnp.concatenate([got[first + j : first + j + 1] for j in picks], axis=1)

        x, y, z, fx, fy, fz = [wide(2 * BACK + 4 * q, range(4)) for q in range(6)]
        force = [wide(2 * c, (0, 1, BACK, BACK + 1)) * DT_STEP for c in range(3)]
        pz = profile(CZ, CZ, z, fz)
        l_high, l_low = split(jnp.concatenate([f * pz for f in force], axis=0))
        gx = profile(YROWS, CX, x, fx)
        wy = offsets(fy)
        planes = []
        for i in range(2):
            rel = (CY + i if side == 0 else i - 2) - y.astype(jnp.int32)
            gy = jnp.zeros((1, PTS), F32)
            for k in range(4):
                gy = jnp.where(rel == k - 1, wy[k], gy)
            planes.append(gx * gy)
        w_high, w_low = split(jnp.concatenate(planes, axis=0))
        rim = dot3_last(w_high, w_low, l_high, l_low)
        for i in range(2):
            for c in range(3):
                at = (i * 3 + c) * YROWS
                out_ref[at : at + YROWS] = rim[i * YROWS : (i + 1) * YROWS, c * CZ : (c + 1) * CZ]


SPREAD_X = 8


def spread_body(start, lines_ref, gx_ref, gy_ref, *rest):
    bases, out_ref = rest[:-1], rest[-1]
    l_high, l_low = split(lines_ref[...])
    gy = gy_ref[0:CY]
    held = [(ref, k) for ref in bases for k in range(0, ref.shape[1], SPREAD_X)]
    for k in range(out_ref.shape[1] // SPREAD_X):
        at = k * SPREAD_X
        first = start + at
        planes = jnp.concatenate([gx_ref[first + i : first + i + 1] * gy for i in range(SPREAD_X)], axis=0)
        w_high, w_low = split(planes)
        value = dot3_last(w_high, w_low, l_high, l_low)
        base, inner = held[k]
        for c in range(3):
            part = value[:, c * CZ : (c + 1) * CZ].reshape(SPREAD_X, CY, CZ)
            out_ref[c, at : at + SPREAD_X] = base[c, inner : inner + SPREAD_X] + part


def rimpack_body(n_blk, xrim_ref, low_ref, high_ref, *rest):
    pieces, (pay_a, pay_b, back_ref, *others) = rest[:n_blk], rest[n_blk:]
    even_x, even_y, inner, _, b0, ny = place()
    zero = jnp.zeros((CY - 4, CZ), F32)
    for k in range(2):
        for c in range(3):
            sides = []
            for s in range(2):
                near, far = [], []
                for y in range(2):
                    at = (y * 3 + c) * YROWS + CX + 2 * s + k
                    near.append(low_ref[at : at + 1])
                    far.append(high_ref[at : at + 1])
                at = ((2 * s + k) * 3 + c) * CY
                sides.append(xrim_ref[at : at + CY] + jnp.concatenate(near + [zero] + far, axis=0))
            at = (k * 3 + c) * CY
            pay_a[at : at + CY] = jnp.where(even_x, sides[1], sides[0])
            pay_b[at : at + CY] = jnp.where(even_x, sides[0], sides[1])
    back = jnp.concatenate([p[...] for p in pieces], axis=0)
    back_ref[...] = back
    if others:
        chips = ny * 2
        side = jnp.where(even_x, -chips, chips)
        total = lax.axis_size("gx") * ny
        for ref, at, target in (
            (pay_b, RIM_X, lax.rem(b0 + side + total, total)),
            (others[0], 0, lax.rem(b0 + 2 * chips, total)),
        ):
            for core in range(2):
                wanted = (target + core * ny).astype(F32)
                found = jnp.full((BACK, CZ), -1.0, F32)
                for k in range(back.shape[0] // BACK):
                    value = back[k * BACK : (k + 1) * BACK]
                    found = jnp.where(value[6:7, 0:1] == wanted, value, found)
                ref[at + core * BACK : at + (core + 1) * BACK] = found


def face_terms(buf, at, first, size, main_low, main_high, y_ref, rec_c, rec_d, rim_low, rim_high, even_y):
    half = 0.5 * DT_STEP
    visc = DT_STEP * NU_VISC
    part = slice(first, first + size)
    here = slice(at, at + size)
    half_of = main_low if first < CX // 2 else main_high
    inner = first % (CX // 2)
    for c in range(3):
        buf[c, here] = half_of[c, inner : inner + size]
        rows = slice(c * CX + first, c * CX + first + size)
        a, b = rec_c[rows], jnp.where(odd_side(), rec_d[rows], 0.0)
        low = [jnp.where(even_y, b, a) * (visc + half * y_ref[0, part]), 0.0]
        high = [0.0, jnp.where(even_y, a, b) * (visc - half * y_ref[1, part])]
        for i in range(2):
            row = (i * 3 + c) * YROWS + first
            buf[c, here, i, :] += rim_low[row : row + size] + low[i]
            buf[c, here, CY - 2 + i, :] += rim_high[row : row + size] + high[i]


INNER = [(2, CHUNK - 2)] + [(k * CHUNK, CHUNK) for k in range(1, N_CHUNK - 1)] + [(CX - CHUNK, CHUNK - 2)]


def chunk_copy(buf, at, out_ref, first, size, sem):
    return pltpu.make_async_copy(buf.at[:, pl.ds(at, size)], out_ref.at[:, pl.ds(first, size)], sem)


def inside_body(main_low, main_high, y_ref, rec_c, rec_d, rim_low, rim_high, out_ref, buf, sems):
    _, even_y, _, _, _, _ = place()
    copies = []
    for k, (first, size) in enumerate(INNER):
        face_terms(buf, first - 2, first, size, main_low, main_high, y_ref, rec_c, rec_d, rim_low, rim_high, even_y)
        copies.append(chunk_copy(buf, first - 2, out_ref, first, size, sems.at[k]))
        copies[-1].start()
    for copy in copies:
        copy.wait()


def final_body(n_ret, _, main_low, main_high, x_ref, y_ref, face_a, face_b, rec_c, rec_d, rim_a, rim_b, rim_low, rim_high, back_ref, *rest):
    rets, (out_ref, pf_ref, buf, pf_buf, sems) = rest[:n_ret], rest[n_ret:]
    even_x, even_y, inner, brick, _, _ = place()
    half = 0.5 * DT_STEP
    visc = DT_STEP * NU_VISC
    mine = brick.astype(F32)
    found = jnp.zeros((BACK, CZ), F32)
    for ref, first in [(back_ref, 0), (rim_b, RIM_X)] + [(r, 0) for r in rets]:
        for k in range((ref.shape[0] - first) // BACK):
            value = ref[first + BACK * k : first + BACK * k + BACK]
            found = jnp.where(value[6:7, 0:1] == mine, value, found)
    for c in range(3):
        pf_buf[c : c + 1] = jnp.concatenate([found[2 * c : 2 * c + 1], found[2 * c + 1 : 2 * c + 2]], axis=1)
    copies = [pltpu.make_async_copy(pf_buf, pf_ref, sems.at[2])]
    copies[0].start()
    for k in range(2):
        first, at = k * (CX - 2), k * 2
        face_terms(buf, at, first, 2, main_low, main_high, y_ref, rec_c, rec_d, rim_low, rim_high, even_y)
        for c in range(3):
            a = face_a[c * XROWS : c * XROWS + CY]
            b = jnp.where(inner, face_b[c * XROWS : c * XROWS + CY], 0.0)
            if k == 0:
                buf[c, 0] += jnp.where(even_x, b, a) * (visc + half * x_ref[0])
            else:
                buf[c, 3] += jnp.where(even_x, a, b) * (visc - half * x_ref[3])
            for i in range(2):
                rows = slice((i * 3 + c) * CY, (i * 3 + c + 1) * CY)
                a, b = rim_a[rows], jnp.where(inner, rim_b[rows], 0.0)
                if k == 0:
                    buf[c, i] += jnp.where(even_x, b, a)
                else:
                    buf[c, 2 + i] += jnp.where(even_x, a, b)
        copies.append(chunk_copy(buf, at, out_ref, first, 2, sems.at[k]))
        copies[-1].start()
    for copy in copies:
        copy.wait()


def per_device(
    velocity,
    host_cell,
    host_frac,
    host_dst,
    owner_src,
    rotor_speed,
    blade_radius,
    blade_chord,
    blade_twist,
    blade_angle,
):
    nx, ny = lax.axis_size("gx"), lax.axis_size("gy")
    ring, short = nx == 8, ny == 4

    def flip(n, bits):
        return [(i, i ^ bits) for i in range(n)]

    def odd_pairs(n, closed=False):
        up = [(i, (i + 1) % n) for i in range(1, n if closed else n - 1, 2)]
        return up + [(t, s) for s, t in up]

    def same_side(n):
        return [(i, (i + (2 if i % 2 else n - 2)) % n) for i in range(n)]

    def across_x(blocks):
        return [lax.ppermute(b, "gx", p) for b, p in zip(blocks, (flip(nx, 4), same_side(nx)))]

    def swap(block):
        return lax.ppermute(block, "gx", flip(nx, 1))

    def join(pieces):
        return pieces[0] if len(pieces) == 1 else jnp.concatenate(pieces, axis=0)

    def after(values, other):
        return lax.optimization_barrier((values, other))

    def gather_y(first):
        pieces = [first]
        for bit in [b for b in (2, 4, 8) if b < ny]:
            pieces.append(lax.ppermute(join(pieces), "gy", flip(ny, bit)))
        return pieces

    def exchange_y(to_c, to_d, block):
        from_c = lax.ppermute(to_c, "gy", flip(ny, 1))
        from_d = lax.ppermute(to_d, "gy", flip(ny, 3) if short else odd_pairs(ny))
        return from_c, from_d, [lax.ppermute(block, "gy", flip(ny, 2))] if short else []

    def blocks_y(block, from_c, from_d, far, size, at):
        got = join([block, from_c[at : at + size]])
        if short:
            return [join([got, from_d[at : at + size]] + far)]
        return gather_y(got)

    def gather_x(blocks):
        pieces = []
        for bit in [b for b in (2, 4, 8, 16) if b < nx]:
            pieces.append(lax.ppermute(join([blocks] + pieces), "gx", flip(nx, bit)))
        return pieces

    def pin(array):
        return pltpu.with_memory_space_constraint(array, pltpu.MemorySpace.HBM)

    dma = pltpu.SemaphoreType.DMA
    pay_c, pay_d, block = call(
        pack_body,
        [(FACE_Y + ROWS, CZ)] * 2 + [(ROWS, CZ)],
        7,
        "pack",
        scratch=[pltpu.VMEM((4, 2, CZ), F32), pltpu.VMEM((2, CZ), jnp.int32), pltpu.VMEM((1, 1), F32), dma((12,))],
        in_specs=[HB] * 7,
    )(pin(velocity), rotor_speed.reshape(1, 1), *[pin(a.reshape(2, CZ)) for a in (blade_radius, blade_chord, blade_twist, blade_angle, owner_src)])
    rec_c, rec_d, far = exchange_y(pay_c, pay_d, block)

    def stencil(start, count):
        return call(lambda *refs: stencil_body(start, *refs), [(3, count, CY, CZ)], 1, "stencil")(velocity)[0]

    base_low = stencil(0, 3 * CX // 8)
    table, sums, x_faces, y_faces = call(
        sample_low_body, [(HOST, CZ), (HOST, 3 * CZ), (6, CY, CZ), (2, CX, CZ)], 3, "sample_low", vmem=24
    )(velocity, host_cell, host_frac)
    (rec_c, rec_d, far), (base_low, sums) = after((rec_c, rec_d, far), (base_low, sums))
    pieces = blocks_y(block, rec_c, rec_d, far, ROWS, FACE_Y)
    beside = [swap(p) for p in pieces]
    beside, base_third = after(beside, stencil(CX // 2, CX // 4))
    pieces = pieces + beside
    n_rows = 2 * ny * ROWS
    pair = (2 * ROWS, CZ)
    pay_a, pay_b, blocks, *across = call(
        lambda *refs: xpack_body(len(pieces), *refs),
        [(FACE_X, CZ), (FACE_X + 2 * ROWS, CZ), pair, pair, pair] if ring else [(FACE_X, CZ), (FACE_X, CZ), (n_rows, CZ)],
        3 + len(pieces),
        "xpack",
    )(x_faces, rec_c, rec_d, *pieces)
    face_b = lax.ppermute(pay_b, "gx", odd_pairs(nx, ring))
    from_x = across_x(across) if ring else gather_x(blocks)
    face_a = swap(pay_a)
    sums, edge, wz = call(
        sample_high_body, [(HOST, 3 * CZ), (HOST, CZ), (HOST, CZ)], 3, "sample_high", vmem=24
    )(velocity, table, sums)
    base_more = stencil(3 * CX // 8, CX // 8)
    (face_a, face_b, from_x), (sums, base_more) = after((face_a, face_b, from_x), (sums, base_more))
    samp, sel, pts = call(
        lambda *refs: select_body(len(from_x), *refs),
        [(8, PTS), (2 * ROWS, CZ), (16, PTS)],
        9 + len(from_x),
        "select",
    )(table, sums, edge, wz, face_a, face_b, rec_c, rec_d, blocks, *from_x)
    other = swap(samp)
    gx, gy, pz, pos, pair_kernel, edge = call(
        weights_body,
        [(YROWS, PTS), (CY, PTS), (CZ, PTS), (24, CZ), (2, P_SIZE, P_SIZE), (4 * CY, PTS)],
        2,
        "weights",
    )(pts, sel)
    other, base_next = after(other, stencil(6 * CX // 8, CX // 8))
    lines, points, xrim = call(
        loads_body,
        [(3 * CZ, PTS), (2 * BACK + 24, CZ), (2 * RIM_X, CZ)],
        7,
        "loads",
    )(samp, other, sel, pz, pos, pair_kernel, edge)
    ret = points[: 2 * BACK]
    near_c, near_d, far = exchange_y(points, points, ret)

    def spread(start, *bases):
        return call(
            lambda *refs: spread_body(start, *refs), [(3, CX // 2, CY, CZ)], 3 + len(bases), "spread"
        )(lines, gx, gy, *bases)[0]

    (near_c, near_d), main_low = after((near_c, near_d), spread(0, base_low, base_more))
    rim_low, rim_high = call(near_body, [(RIM_Y, CZ)] * 2, 2, "near")(near_c, near_d)
    far, rim_low = after(far, rim_low)
    pieces = blocks_y(ret, near_c, near_d, far, 2 * BACK, 0)
    n_rows = 2 * ny * BACK
    pair = (2 * BACK, CZ)
    pay_a, pay_b, back, *across = call(
        lambda *refs: rimpack_body(len(pieces), *refs),
        [(RIM_X, CZ), (RIM_X + 2 * BACK, CZ), (n_rows, CZ), pair] if ring else [(RIM_X, CZ), (RIM_X, CZ), (n_rows, CZ)],
        3 + len(pieces),
        "rimpack",
    )(xrim, rim_low, rim_high, *pieces)
    rim_b = lax.ppermute(pay_b, "gx", odd_pairs(nx, ring))
    rets = [lax.ppermute(across[0], "gx", flip(nx, 4))] if ring else gather_x(back)
    rim_a = swap(pay_a)
    main_high = spread(CX // 2, base_third, base_next, stencil(7 * CX // 8, CX // 8))
    (rim_a, rim_b), (main_low, main_high) = after((rim_a, rim_b), (main_low, main_high))
    if ring:
        rets.append(swap(rim_b[RIM_X:]))
    inside = call(
        inside_body,
        [velocity.shape],
        7,
        "inside",
        scratch=[pltpu.VMEM((3, CX - 4, CY, CZ), F32), dma((N_CHUNK,))],
        out_specs=[HB],
        vmem=16,
    )(main_low, main_high, y_faces, rec_c, rec_d, rim_low, rim_high)[0]
    rets, inside = after(rets, inside)
    return tuple(
        call(
            lambda *refs: final_body(len(rets), *refs),
            [velocity.shape, (3, P_SIZE)],
            14 + len(rets),
            "final",
            scratch=[pltpu.VMEM((3, 4, CY, CZ), F32), pltpu.VMEM((3, P_SIZE), F32), dma((3,))],
            first=HB,
            out_specs=[HB, HB],
            aliases={0: 0},
        )(inside, main_low, main_high, x_faces, y_faces, face_a, face_b, rec_c, rec_d, rim_a, rim_b, rim_low, rim_high, back, *rets)
    )


def solution(mesh):
    return jax.shard_map(
        per_device,
        mesh=mesh,
        in_specs=(
            P(None, "gx", "gy", None),
            P(None, ("gx", "gy")),
            P(None, ("gx", "gy")),
            P(("gx", "gy")),
            P(("gx", "gy")),
            P(("gx", "gy")),
            P(("gx", "gy")),
            P(("gx", "gy")),
            P(("gx", "gy")),
            P(("gx", "gy")),
        ),
        out_specs=(P(None, "gx", "gy", None), P(None, ("gx", "gy"))),
        check_vma=False,
    )
```
